32 devices in a mesh: section: 4 (over x, core), dp: 8 (over z, y).
Axes of the slice: x: 2, y: 2, z: 4, core: 2. Of those that a mesh axis runs over, the one named last changes fastest.
Arguments:
- tokens: bfloat16 [16, 1024, 768], P('dp'), may hold values from -6 to 6
- doc_ids: int32 [16, 1024], P('dp'), may hold values from 0 to 3, never falling along the last dimension, each value on 1 to 512 neighbouring positions
- reset_flags: int32 [16, 1], P('dp'), may hold values 0 or 1
- first_weights: bfloat16 [4, 768, 3072], P('section'), may hold values from -2 to 2
- down_halves: bfloat16 [4, 1536, 768], P('section'), may hold values from -0.109375 to 0.109375
- norm_gain: float32 [4, 768], P('section'), may hold values from 0.5 to 1.5
- norm_bias: float32 [4, 768], P('section'), may hold values from -2.5 to 2.5
- cotangent: bfloat16 [16, 1024, 768], P('dp'), may hold values from -6 to 6
Outputs:
- section_out: bfloat16 [4, 16, 1024, 768], P('section', 'dp')
- section_in_grad: bfloat16 [4, 16, 1024, 768], P('section', 'dp')
- first_grad: float32 [4, 768, 3072], P('section')
- down_grad: float32 [4, 1536, 768], P('section')
- gain_grad: float32 [4, 768], P('section')
- bias_grad: float32 [4, 768], P('section')
The draws below stay inside these ranges and needn't reach their ends.
Inputs may be any that keep to these rules, and one draw needn't show every extreme that they name: doc_ids never fall along a sequence.
All inputs are finite; a program needn't handle non-finite values. No bound on the sum of `reset_flags` on one device may be relied on, other than what follows from the above.
Results may differ from the reference program's by a relative error of at most 0.023.
Values may be sent and summed in bfloat16 or wider, within the bound.
A program may use at most 192 MiB of HBM per device.

```python
import math
import jax
import jax.numpy as jnp
import numpy as np
from jax import lax

D = 768
H = 12
HD = 64
FF = 3072
M = 20
SEG = 512
NSEG = 2
LEN = 1024
SEQS = 16
N_SECTION = 4


def draw_first_weights(key, part):
    full_shape = (N_SECTION, D, FF)
    normal_draw = jax.random.truncated_normal(key, -6.0, 6.0, full_shape, jnp.float32)
    column_ids = lax.broadcasted_iota(jnp.int32, full_shape, 2)
    section_ids = lax.broadcasted_iota(jnp.int32, full_shape, 0)
    out_boost = jnp.where((section_ids % 2 == 0) & (column_ids >= 3 * D), math.sqrt(M + SEG) / 3.0, 1.0)
    return (normal_draw * out_boost * D ** (-0.5)).astype(jnp.bfloat16)


def place_ends(result, own_key, low, high):
    longest = result.shape.index(max(result.shape))
    spots = []
    for shift in (0, 1):
        where = [jax.random.randint(jax.random.fold_in(own_key, axis), (), 0, length) for axis, length in enumerate(result.shape)]
        where[longest] = (where[longest] + shift) % result.shape[longest]
        spots.append(tuple(where))
    return result.at[spots[0]].set(low).at[spots[1]].set(high)


def block_scale(key, shape, shards, low, high):
    gain = 1.0
    for position, shards_of in shards:
        draws = jax.random.uniform(jax.random.fold_in(jax.random.fold_in(key, 6), position), (shards_of,), jnp.float32, low / len(shards), high / len(shards))
        gain = gain * jnp.repeat(jnp.exp(draws), shape[position] // shards_of).reshape((-1,) + (1,) * (len(shape) - 1 - position))
    return gain


def split_up(count, total, reach, lean):
    portions = [(1 << 20) // math.isqrt(grade ** lean) + 1 for grade in range(2, count + 1)]
    spare, given = total - reach - (count - 1), [1] * (count - 1)
    while spare > 0:
        movable = [i for i in range(count - 1) if given[i] < reach]
        whole, left = sum([portions[i] for i in movable]), spare
        for i in movable:
            addition = min(reach - given[i], max(1, left * portions[i] // whole), spare)
            given[i] = given[i] + addition
            spare = spare - addition
    return np.array([reach] + given)


def ragged(own_key, amount, total, bound, slope):
    if amount == 2:
        one = jax.random.randint(own_key, (), max(1, total - bound), min(bound, total - 1) + 1)
        return jnp.stack([one, total - one])
    lengths = jnp.asarray(split_up(amount, total, bound, slope), jnp.int32)
    twos = (amount - 1) // 2
    source_of, sink = lengths[1:1 + 2 * twos:2], lengths[2:2 + 2 * twos:2]
    slack = jnp.minimum(source_of - 1, bound - sink)
    moved = jax.random.randint(jax.random.fold_in(own_key, 1), (twos,), 0, 1 << 20) % (slack + 1)
    lengths = lengths.at[1:1 + 2 * twos:2].set(source_of - moved).at[2:2 + 2 * twos:2].set(sink + moved)
    return lengths[jax.random.permutation(jax.random.fold_in(own_key, 2), amount)]


def bell_draw(rng, dims, deviation, reach, cuts=(), held_as=jnp.bfloat16):
    factor_of = block_scale(rng, dims, cuts, -0.22, 0.18) if cuts else 1.0
    array = jax.random.normal(rng, dims, jnp.float32) * deviation * factor_of
    return jnp.minimum(jnp.maximum(array, -reach), reach).astype(held_as)


def setup_inputs(seed: int = 0) -> dict:
    key_of = jax.random.split(jax.random.key(seed), 9)
    return {
        "tokens": bell_draw(key_of[0], (SEQS, LEN, D), 1.0, 6.0, ((0, 8),)),
        "doc_ids": jax.vmap(lambda own: jnp.searchsorted(jnp.cumsum(ragged(own, 2 * NSEG, LEN, SEG, 1)), jnp.arange(LEN), side="right"))(jax.random.split(key_of[1], SEQS)).reshape((SEQS, LEN)).astype(jnp.int32),
        "reset_flags": place_ends((jax.random.randint(key_of[2], (SEQS, NSEG - 1), 0, 4) < 1).astype(jnp.int32), jax.random.fold_in(key_of[2], 1), 0, 1),
        "first_weights": draw_first_weights(jax.random.fold_in(key_of[8], 71), 0),
        "down_halves": bell_draw(key_of[4], (N_SECTION, FF // 2, D), FF ** -0.5, 0.109375, ((0, 4),)),
        "norm_gain": jnp.clip(1.0 + 0.1 * jax.random.normal(key_of[5], (N_SECTION, D), jnp.float32), 0.5, 1.5),
        "norm_bias": bell_draw(key_of[6], (N_SECTION, D), 0.3, 2.5, ((0, 4),), jnp.float32),
        "cotangent": bell_draw(key_of[7], (SEQS, LEN, D), 1.0, 6.0, ((0, 8),)),
    }


NORM_EPSILON = 1e-05
MASKED_SCORE = -1000000000.0
HIGHEST = lax.Precision.HIGHEST

@jax.custom_vjp
def low(v):
    return lax.optimization_barrier(v.astype(jnp.bfloat16)).astype(jnp.float32)

@jax.custom_vjp
def low_back(v):
    return v

def low_keep(v):
    return (low(v), None)

def low_pass(kept, grad):
    return (grad,)

def back_keep(v):
    return (v, None)

def back_low(kept, grad):
    return (low(grad),)
low.defvjp(low_keep, low_pass)
low_back.defvjp(back_keep, back_low)

def product(left, right):
    return jnp.dot(left, right, precision=HIGHEST, preferred_element_type=jnp.float32)

def norm_rows(summed, norm_scale, norm_shift):
    row_mean = lax.optimization_barrier(jnp.mean(summed, axis=-1, keepdims=True))
    centered = summed - row_mean
    row_var = lax.optimization_barrier(jnp.mean(centered * centered, axis=-1, keepdims=True))
    return centered * lax.rsqrt(row_var + NORM_EPSILON) * norm_scale + norm_shift

def allowed_mask(doc_rows):
    marks = jnp.concatenate([jnp.full((M,), -1, jnp.int32), doc_rows.astype(jnp.int32)])
    is_memory = jnp.arange(M + SEG) < M
    return is_memory[:, None] | is_memory[None, :] | (marks[:, None] == marks[None, :])

def attend(queries, keys, values, allowed):
    row_count = queries.shape[0]
    head_queries = queries.reshape(row_count, H, HD)
    head_keys = keys.reshape(row_count, H, HD)
    head_values = values.reshape(row_count, H, HD)
    scores = jnp.einsum('rhd,khd->hrk', head_queries, head_keys, precision=HIGHEST) * HD ** (-0.5)
    scores = low_back(scores)
    scores = jnp.where(allowed[None], scores, MASKED_SCORE)
    log_total = jax.nn.logsumexp(scores, axis=2, keepdims=True)
    attn_probs = low(jnp.exp(scores - log_total))
    context = jnp.einsum('hrk,khd->rhd', attn_probs, head_values, precision=HIGHEST)
    return context.reshape(row_count, H * HD)

def attention_section(inputs, first_matrix, norm_scale, norm_shift, allowed):
    inputs = low_back(inputs)
    queries = low_back(low(product(inputs, first_matrix[:, :D])))
    keys = low_back(low(product(inputs, first_matrix[:, D:2 * D])))
    values = low_back(low(product(inputs, first_matrix[:, 2 * D:3 * D])))
    context = low_back(low(jax.checkpoint(attend)(queries, keys, values, allowed)))
    branch = low_back(product(context, first_matrix[:, 3 * D:]))
    return low(norm_rows(inputs + branch, norm_scale, norm_shift))

def feed_section(inputs, up_matrix, down_matrix, norm_scale, norm_shift):
    inputs = low_back(inputs)
    pre_act = low_back(product(inputs, up_matrix))
    hidden = low(jax.nn.gelu(pre_act, approximate=False))
    branch = low_back(product(hidden, down_matrix))
    return low(norm_rows(inputs + branch, norm_scale, norm_shift))

def sequence_forward(firsts, downs, gains, biases, probes, seq_tokens, seq_docs, seq_flags):
    memory = jnp.zeros((M, D), jnp.float32)
    memory_pad = jnp.zeros((M, D), jnp.float32)
    collected = [[] for section_number in range(N_SECTION)]
    for segment in range(NSEG):
        row_start = segment * SEG
        if segment > 0:
            memory = jnp.where(seq_flags[segment - 1] > 0, 0.0, memory)
        allowed = allowed_mask(seq_docs[row_start:row_start + SEG])
        current = jnp.concatenate([memory, seq_tokens[row_start:row_start + SEG] + probes[0, row_start:row_start + SEG]], axis=0)
        for section_number in range(N_SECTION):
            if section_number > 0:
                current = current + jnp.concatenate([memory_pad, probes[section_number, row_start:row_start + SEG]], axis=0)
            if section_number % 2 == 0:
                current = attention_section(current, firsts[section_number], gains[section_number], biases[section_number], allowed)
            else:
                down_matrix = jnp.concatenate([downs[section_number - 1], downs[section_number]], axis=0)
                current = feed_section(current, firsts[section_number], down_matrix, gains[section_number], biases[section_number])
            collected[section_number].append(current[M:])
        memory = current[:M]
    stacked = jnp.stack([jnp.concatenate(pieces, axis=0) for pieces in collected])
    return (stacked[N_SECTION - 1], stacked)

def reference(tokens, doc_ids, reset_flags, first_weights, down_halves, norm_gain, norm_bias, cotangent):
    firsts = first_weights.astype(jnp.float32)
    downs = down_halves.astype(jnp.float32)
    gains = norm_gain.astype(jnp.float32)
    biases = norm_bias.astype(jnp.float32)
    probes = jnp.zeros((N_SECTION, LEN, D), jnp.float32)

    def one_sequence(totals, inputs):
        seq_tokens, seq_docs, seq_flags, seq_cot = inputs

        def run(first_part, down_part, gain_part, bias_part, probe_part):
            return sequence_forward(first_part, down_part, gain_part, bias_part, probe_part, seq_tokens.astype(jnp.float32), seq_docs, seq_flags)
        final, backward, stacked = jax.vjp(run, firsts, downs, gains, biases, probes, has_aux=True)
        grads = backward(seq_cot.astype(jnp.float32))
        totals = (totals[0] + grads[0], totals[1] + grads[1], totals[2] + grads[2], totals[3] + grads[3])
        return (totals, (stacked.astype(jnp.bfloat16), grads[4].astype(jnp.bfloat16)))
    initial = (jnp.zeros_like(firsts), jnp.zeros_like(downs), jnp.zeros_like(gains), jnp.zeros_like(biases))
    totals, (outputs, input_grads) = lax.scan(one_sequence, initial, (tokens, doc_ids, reset_flags, cotangent))
    section_out = jnp.transpose(outputs, (1, 0, 2, 3))
    section_in_grad = jnp.transpose(input_grads, (1, 0, 2, 3))
    return (section_out, section_in_grad, totals[0], totals[1], totals[2], totals[3])
```

```python
from functools import partial

import jax
import jax.numpy as jnp
from jax import lax
from jax.experimental import pallas as pl
from jax.experimental.pallas import tpu as pltpu
from jax.sharding import PartitionSpec as P

H = 12
M = 20
NSEG = 2
MEM_PAD = 16
NORM_EPSILON = 1e-05
MASKED_SCORE = -1000000000.0
ABSENT_SCORE = -3e38
MESH = pl.DeviceIdType.MESH
BF16 = jnp.bfloat16
F32 = jnp.float32

OUT_ATT, OUT_FF, GIN_ATT, GIN_FF = 0, 1, 2, 3
S_X0, S_CTX, S_DQ, S_DKV, S_DATT, S_GLO, S_DFF0 = 4, 5, 6, 7, 8, 9, 10
S_Y1, S_Y2, S_DU, S_GHI, S_DFF1 = 11, 12, 13, 14, 15
KINDS = 16


def dot(a, b, lhs_dim=1, rhs_dim=0):
    return lax.dot_general(
        a, b, (((lhs_dim,), (rhs_dim,)), ((), ())), preferred_element_type=F32
    )


def normalize(summed):
    mean = jnp.mean(summed, axis=-1, keepdims=True)
    centered = summed - mean
    var = jnp.mean(centered * centered, axis=-1, keepdims=True)
    inv = lax.rsqrt(var + NORM_EPSILON)
    return centered * inv, inv


def layers_kernel(
    n, nseg, heads,
    tokens, cotangent, first, down, bias, gain_bias, keep,
    out, gin, sx1, sx2, sr, sg, sd, norm_grad,
    wf, wd, nrm, x0, q, kv, ctx, natt, yatt, nff, yd, gy, g, gp, stats, biasb,
    memin, mgin, dkvs, dkvin, dhb, dctx, acc, accp,
    wl, ws, wr, tok_sem, cot_sem, bias_sem, kvs_sem, kvr_sem, xs_sem, xr_sem,
    ms_sem, mr_sem, gs_sem, gr_sem, hs_sem, hr_sem, ds_sem, dr_sem, as_sem, ar_sem,
    lsem, ssem, rsem,
):
    items = n * nseg
    section = lax.axis_index("section")
    c = lax.rem(section, 2)
    x = lax.div(section, 2)
    core_peer = {"section": x * 2 + (1 - c)}
    chip_peer = {"section": (1 - x) * 2 + c}
    rows, width = x0.shape[1:]
    toks = rows - MEM_PAD
    seg_len = 2 * toks
    hidden_half = wd.shape[1]
    hidden = 2 * hidden_half
    wide = 3 * width
    lanes = 128
    chunk = 512 if hidden_half % 512 == 0 else 256
    per_half = hidden_half // chunk
    ncol = 256

    def remote(src, dst, send, recv, peer):
        return pltpu.make_async_remote_copy(
            src_ref=src, dst_ref=dst, send_sem=send, recv_sem=recv,
            device_id=peer, device_id_type=MESH,
        )

    barrier = pltpu.get_barrier_semaphore()
    pl.semaphore_signal(barrier, inc=1, device_id=core_peer, device_id_type=MESH)
    pl.semaphore_signal(barrier, inc=1, device_id=chip_peer, device_id_type=MESH)
    pl.semaphore_wait(barrier, 2)

    def weight_piece(k):
        if k == 0:
            return first.at[:, width:wide], wf.at[c, :, width:wide]
        if k == 1:
            return first.at[:, 0:width], wf.at[c, :, 0:width]
        if k == 2:
            return first.at[:, wide:], wf.at[c, :, wide:]
        return down, wd.at[c]

    nrm[c] = gain_bias[...]
    nrm_copy = remote(nrm.at[c], nrm.at[c], ws.at[4], wr.at[4], core_peer)
    for k in range(4):
        src, dst = weight_piece(k)
        remote(src, dst, ws.at[k], wr.at[k], core_peer).start()
        pltpu.make_async_copy(src, dst, wl.at[k]).start()
    nrm_copy.start()

    def wait_local(k):
        src, dst = weight_piece(k)
        pltpu.make_async_copy(src, dst, wl.at[k]).wait()

    def wait_remote(k):
        if k == 4:
            nrm_copy.wait_recv()
        else:
            src, dst = weight_piece(k)
            remote(src, dst, ws.at[k], wr.at[k], core_peer).wait_recv()

    def wait_first_of(core, ks):
        @pl.when(c == core)
        def _():
            for k in ks:
                wait_local(k)

        @pl.when(c != core)
        def _():
            for k in ks:
                wait_remote(k)

    def bias_copy(i):
        return pltpu.make_async_copy(bias.at[i], biasb.at[i], bias_sem.at[i])

    def token_rows(ref, i):
        return ref.at[lax.rem(i, n), pl.ds(lax.div(i, n) * seg_len + c * toks, toks), :]

    def token_copy(i):
        return pltpu.make_async_copy(
            token_rows(tokens, i), x0.at[i, 0:toks, :], tok_sem.at[i]
        )

    def cot_copy(i):
        return pltpu.make_async_copy(
            token_rows(cotangent, i), gy.at[i, 0:toks, :], cot_sem.at[i]
        )

    for i in range(items):
        @pl.when(x == 0)
        def _():
            token_copy(i).start()

        bias_copy(i).start()

    for i in range(items):
        @pl.when(x == 1)
        def _():
            cot_copy(i).start()

    def routed(kind, i):
        block = i * 2 + c
        sec = 0
        if kind == OUT_ATT:
            src, dst = yatt.at[i, 0:toks, :], token_rows(out, i)
        elif kind == OUT_FF:
            src, dst, sec = yd.at[i, 0:toks, :], token_rows(out, i), 1
        elif kind == GIN_ATT:
            src, dst = yd.at[i, 0:toks, :], token_rows(gin, i)
        elif kind == GIN_FF:
            src, dst, sec = gy.at[i, 0:toks, :], token_rows(gin, i), 1
        elif kind == S_X0:
            src, dst = x0.at[i], sx1.at[block]
        elif kind == S_CTX:
            src, dst = ctx.at[i], sx2.at[block]
        elif kind == S_DQ:
            src, dst = q.at[i], sr.at[block, :, 0:width]
        elif kind == S_DKV:
            src, dst = kv.at[i, c], sr.at[block, :, width:wide]
        elif kind == S_DATT:
            src, dst = natt.at[i], sr.at[block, :, wide:]
        elif kind == S_GLO:
            src, dst = g.at[i, :, 0:hidden_half], sg.at[block]
        elif kind == S_DFF0:
            src, dst = nff.at[i], sd.at[block]
        elif kind == S_Y1:
            src, dst, sec = yatt.at[i], sx1.at[block], 1
        elif kind == S_Y2:
            src, dst, sec = yatt.at[i], sx2.at[block], 1
        elif kind == S_DU:
            src, dst, sec = gp.at[i], sr.at[block], 1
        elif kind == S_GHI:
            src, dst, sec = g.at[i, :, hidden_half:], sg.at[block], 1
        else:
            src, dst, sec = nff.at[i], sd.at[block], 1
        return src, dst, sec

    def route_local(kind, i):
        src, dst, _ = routed(kind, i)
        return pltpu.make_async_copy(src, dst, lsem.at[kind, i])

    def route_away(kind, i):
        src, dst, _ = routed(kind, i)
        return remote(src, dst, ssem.at[kind, i], rsem.at[kind, i], core_peer)

    def route(kind, i):
        sec = routed(kind, i)[2]

        @pl.when(c == sec)
        def _():
            route_local(kind, i).start()

        @pl.when(c != sec)
        def _():
            route_away(kind, i).start()

    def route_sent(kind, i):
        sec = routed(kind, i)[2]

        @pl.when(c == sec)
        def _():
            route_local(kind, i).wait()

        @pl.when(c != sec)
        def _():
            route_away(kind, i).wait_send()

    def route_received(kind, i):
        @pl.when(c == routed(kind, i)[2])
        def _():
            route_away(kind, i).wait_recv()

    def kv_copy(i):
        return remote(kv.at[i, c], kv.at[i, c], kvs_sem.at[i], kvr_sem.at[i], core_peer)

    def x_copy(i):
        return remote(yd.at[i], x0.at[i], xs_sem.at[i], xr_sem.at[i], chip_peer)

    def mem_copy(i):
        return remote(
            yd.at[i, toks:rows, :], memin.at[i], ms_sem.at[i], mr_sem.at[i], chip_peer
        )

    def gy_copy(i):
        return remote(yd.at[i], gy.at[i], gs_sem.at[i], gr_sem.at[i], chip_peer)

    def mg_copy(i):
        return remote(
            yd.at[i, toks:rows, :], mgin.at[i], hs_sem.at[i], hr_sem.at[i], chip_peer
        )

    def dkv_copy(i, slot):
        return remote(
            dkvs.at[1 - c], dkvin.at[slot], ds_sem.at[i], dr_sem.at[i], core_peer
        )

    lane = lax.broadcasted_iota(jnp.int32, (rows, lanes), 1)
    first_head = lane < lanes // 2
    stat_lane = lax.broadcasted_iota(jnp.int32, (rows, lanes), 1)
    key_first_head = lax.broadcasted_iota(jnp.int32, (2 * rows, lanes), 1) < lanes // 2

    def lane_block(j, base=0):
        return pl.ds(pl.multiple_of(base + j * lanes, lanes), lanes)

    def masked_scores(qm, k2, i):
        s = dot(qm, k2, 1, 1)
        b = biasb[i]
        return jnp.where(b == 0.0, s, b)

    def both_keys(i, cols):
        return jnp.concatenate([kv[i, 0, :, cols], kv[i, 1, :, cols]], axis=0)

    def forward_tick(t, carry):
        i = t - x

        @pl.when((i >= 0) & (i < items))
        def _():
            @pl.when(x == 0)
            def _():
                token_copy(i).wait()

                @pl.when(i < n)
                def _():
                    x0[i, toks:rows, :] = jnp.zeros((MEM_PAD, width), BF16)

                @pl.when(i >= n)
                def _():
                    mem_copy(i - n).wait_recv()
                    x0[i, toks:rows, :] = jnp.where(
                        keep[i][:, 0:1] > 0.0, memin[i - n], jnp.zeros((), BF16)
                    )

            @pl.when(x == 1)
            def _():
                x_copy(i).wait_recv()

            @pl.when(i == 0)
            def _():
                wait_first_of(0, (0,))

            xb = x0[i]
            for col in range(width, wide, ncol):
                kv[i, c, :, col - width : col - width + ncol] = dot(
                    xb, wf[0, :, col : col + ncol]
                ).astype(BF16)
            kv_copy(i).start()
            route(S_X0, i)

            @pl.when(i == 0)
            def _():
                wait_first_of(0, (1,))

            for col in range(0, width, ncol):
                q[i, :, col : col + ncol] = (
                    dot(xb, wf[0, :, col : col + ncol]).astype(BF16) * BF16(0.125)
                )
            bias_copy(i).wait()
            kv_copy(i).wait_recv()
            stats[i] = jnp.zeros((rows, lanes), F32)

            def head_pair(j, carry):
                cols = lane_block(j)
                q2 = q[i, :, cols]
                k2 = both_keys(i, cols)
                v2 = both_keys(i, lane_block(j, width))
                outs = []
                for e in range(2):
                    mine = first_head if e == 0 else ~first_head
                    s = masked_scores(jnp.where(mine, q2, BF16(0)), k2, i)
                    peak = jnp.max(s, axis=1, keepdims=True)
                    p = jnp.exp(s - peak)
                    total = jnp.sum(p, axis=1, keepdims=True)
                    outs.append(dot(p.astype(BF16), v2) * (1.0 / total))
                    lse = peak + jnp.log(total)
                    stats[i] = jnp.where(stat_lane == 2 * j + e, lse, stats[i])
                ctx[i, :, cols] = jnp.where(first_head, outs[0], outs[1]).astype(BF16)
                return carry

            lax.fori_loop(0, heads // 2, head_pair, 0)
            route(S_CTX, i)

            @pl.when(i == 0)
            def _():
                wait_first_of(0, (2,))

                @pl.when(c == 0)
                def _():
                    wait_remote(4)

                @pl.when(c == 1)
                def _():
                    wait_remote(4)

            for col in range(0, width, ncol):
                dhb[:, col : col + ncol] = dot(
                    ctx[i], wf[0, :, wide + col : wide + col + ncol]
                ) + x0[i, :, col : col + ncol].astype(F32)
            normed, inv = normalize(dhb[...])
            natt[i] = normed.astype(BF16)
            stats[i] = jnp.where(stat_lane == heads, inv, stats[i])
            yatt[i] = (normed * nrm[0, 0:1, :] + nrm[0, 1:2, :]).astype(BF16)
            route(OUT_ATT, i)
            route(S_Y1, i)
            route(S_Y2, i)

            @pl.when(i == 0)
            def _():
                wait_first_of(1, (0, 1, 2))

            def up(k, carry):
                cols = pl.ds(pl.multiple_of(k * chunk, chunk), chunk)
                u = dot(yatt[i], wf[1, :, cols])
                cdf = 0.5 + 0.5 * lax.erf(u * 0.7071067811865476)
                pdf = 0.3989422804014327 * jnp.exp(-0.5 * u * u)
                g[i, :, cols] = (u * cdf).astype(BF16)
                gp[i, :, cols] = (cdf + u * pdf).astype(BF16)
                return carry

            lax.fori_loop(0, hidden // chunk, up, 0)
            route(S_GLO, i)
            route(S_GHI, i)

            @pl.when(i == 0)
            def _():
                wait_first_of(0, (3,))
                wait_first_of(1, (3,))

            for col in range(0, width, ncol):
                dhb[:, col : col + ncol] = (
                    dot(g[i, :, 0:hidden_half], wd[0, :, col : col + ncol])
                    + dot(g[i, :, hidden_half:], wd[1, :, col : col + ncol])
                    + yatt[i, :, col : col + ncol].astype(F32)
                )
            normed, inv = normalize(dhb[...])
            nff[i] = normed.astype(BF16)
            stats[i] = jnp.where(stat_lane == heads + 1, inv, stats[i])
            yd[i] = (normed * nrm[1, 0:1, :] + nrm[1, 1:2, :]).astype(BF16)

            @pl.when(x == 0)
            def _():
                x_copy(i).start()

            @pl.when((x == 1) & (i < items - n))
            def _():
                mem_copy(i).start()

            route(OUT_FF, i)

        return carry

    lax.fori_loop(0, items + 1, forward_tick, 0)

    def forward_drain(i, carry):
        kv_copy(i).wait_send()
        route_sent(OUT_FF, i)

        @pl.when(x == 0)
        def _():
            x_copy(i).wait_send()

        @pl.when((x == 1) & (i < items - n))
        def _():
            mem_copy(i).wait_send()

        return carry

    lax.fori_loop(0, items, forward_drain, 0)
    acc[...] = jnp.zeros_like(acc)

    def norm_back(s, i, normed_ref):
        grad = gy[i].astype(F32)
        normed = normed_ref[i].astype(F32)
        inv = jnp.sum(jnp.where(stat_lane == heads + s, stats[i], 0.0), axis=1, keepdims=True)
        acc[s, 0:1, :] += jnp.sum(grad * normed, axis=0, keepdims=True)
        acc[s, 1:2, :] += jnp.sum(grad, axis=0, keepdims=True)
        scaled = grad * nrm[s, 0:1, :]
        row_term = jnp.mean(scaled, axis=1, keepdims=True)
        row_cross = jnp.mean(scaled * normed, axis=1, keepdims=True)
        dh = inv * (scaled - row_term - normed * row_cross)
        dhb[...] = dh
        normed_ref[i] = dh.astype(BF16)

    def backward_tick(t, carry):
        r = t - (1 - x)

        @pl.when((r >= 0) & (r < items))
        def _():
            i = (nseg - 1 - lax.div(r, n)) * n + lax.rem(r, n)
            slot = lax.rem(r, 2)

            @pl.when(x == 1)
            def _():
                cot_copy(i).wait()

                @pl.when(i >= items - n)
                def _():
                    gy[i, toks:rows, :] = jnp.zeros((MEM_PAD, width), BF16)

                @pl.when(i < items - n)
                def _():
                    mg_copy(i + n).wait_recv()
                    gy[i, toks:rows, :] = jnp.where(
                        keep[i + n][:, 0:1] > 0.0, mgin[i + n], jnp.zeros((), BF16)
                    )

            @pl.when(x == 0)
            def _():
                gy_copy(i).wait_recv()

            norm_back(1, i, nff)
            route(S_DFF0, i)
            route(S_DFF1, i)

            def down_back(k, carry):
                cols = pl.ds(pl.multiple_of(k * chunk, chunk), chunk)
                part = pl.ds(pl.multiple_of(lax.rem(k, per_half) * chunk, chunk), chunk)
                dg = dot(nff[i], wd[lax.div(k, per_half), part, :], 1, 1)
                gp[i, :, cols] = (dg * gp[i, :, cols].astype(F32)).astype(BF16)
                return carry

            lax.fori_loop(0, hidden // chunk, down_back, 0)
            route(S_DU, i)
            for col in range(0, width, ncol):
                gy[i, :, col : col + ncol] = (
                    dot(gp[i], wf[1, col : col + ncol, :], 1, 1) + dhb[:, col : col + ncol]
                ).astype(BF16)
            route(GIN_FF, i)

            norm_back(0, i, natt)
            route(S_DATT, i)
            for col in range(0, width, ncol):
                dctx[:, col : col + ncol] = dot(
                    natt[i], wf[0, col : col + ncol, wide:], 1, 1
                ).astype(BF16)

            def head_pair(j, carry):
                cols = lane_block(j)
                q2 = q[i, :, cols]
                k2 = both_keys(i, cols)
                v2 = both_keys(i, lane_block(j, width))
                c2 = dctx[:, cols]
                t2 = c2.astype(F32) * ctx[i, :, cols].astype(F32)
                dq2, dk2, dv2 = 0.0, 0.0, 0.0
                for e in range(2):
                    mine = first_head if e == 0 else ~first_head
                    key_mine = key_first_head if e == 0 else ~key_first_head
                    qm = jnp.where(mine, q2, BF16(0))
                    cm = jnp.where(mine, c2, BF16(0))
                    km = jnp.where(key_mine, k2, BF16(0))
                    lse = jnp.sum(
                        jnp.where(stat_lane == 2 * j + e, stats[i], 0.0), axis=1, keepdims=True
                    )
                    inner = jnp.sum(jnp.where(mine, t2, 0.0), axis=1, keepdims=True)
                    p = jnp.exp(masked_scores(qm, k2, i) - lse)
                    dp = dot(cm, v2, 1, 1)
                    ds = (p * (dp - inner)).astype(BF16)
                    dv2 = dv2 + dot(p.astype(BF16), cm, 0, 0)
                    dk2 = dk2 + dot(ds, qm, 0, 0)
                    dq2 = dq2 + dot(ds, km)
                q[i, :, cols] = (dq2 * 0.125).astype(BF16)
                vcols = lane_block(j, width)
                dkvs[0, :, cols] = dk2[0:rows].astype(BF16)
                dkvs[1, :, cols] = dk2[rows:].astype(BF16)
                dkvs[0, :, vcols] = dv2[0:rows].astype(BF16)
                dkvs[1, :, vcols] = dv2[rows:].astype(BF16)
                return carry

            lax.fori_loop(0, heads // 2, head_pair, 0)
            dkv_copy(i, slot).start()
            route(S_DQ, i)
            for col in range(0, width, ncol):
                dhb[:, col : col + ncol] += dot(q[i], wf[0, col : col + ncol, 0:width], 1, 1)
            dkv_copy(i, slot).wait_recv()
            kv[i, c] = (dkvs[c].astype(F32) + dkvin[slot].astype(F32)).astype(BF16)
            route(S_DKV, i)
            for col in range(0, width, ncol):
                yd[i, :, col : col + ncol] = (
                    dot(kv[i, c], wf[0, col : col + ncol, width:wide], 1, 1)
                    + dhb[:, col : col + ncol]
                ).astype(BF16)

            @pl.when(x == 1)
            def _():
                gy_copy(i).start()

            @pl.when((x == 0) & (i >= n))
            def _():
                mg_copy(i).start()

            route(GIN_ATT, i)
            dkv_copy(i, slot).wait_send()

        return carry

    lax.fori_loop(0, items + 1, backward_tick, 0)

    acc_copy = remote(acc.at[1 - c], accp, as_sem, ar_sem, core_peer)
    acc_copy.start()

    def backward_drain(i, carry):
        @pl.when(x == 1)
        def _():
            gy_copy(i).wait_send()

        @pl.when((x == 0) & (i >= n))
        def _():
            mg_copy(i).wait_send()

        for kind in range(KINDS):
            if kind != OUT_FF:
                route_sent(kind, i)
            route_received(kind, i)
        return carry

    lax.fori_loop(0, items, backward_drain, 0)
    for k in range(4):
        src, dst = weight_piece(k)
        remote(src, dst, ws.at[k], wr.at[k], core_peer).wait_send()
    nrm_copy.wait_send()
    acc_copy.wait()
    norm_grad[...] = acc[c] + accp[...]


def run_layers(n, nseg, heads, tokens, cotangent, first, down, bias, gain_bias, keep):
    length, width = tokens.shape[1:]
    toks = length // nseg // 2
    rows = toks + MEM_PAD
    items = n * nseg
    hidden_half = down.shape[0]
    any_spec = pl.BlockSpec(memory_space=pl.ANY)
    vmem_spec = pl.BlockSpec(memory_space=pltpu.VMEM)
    dma = pltpu.SemaphoreType.DMA
    item_rows = pltpu.VMEM((items, rows, width), BF16)
    return pl.pallas_call(
        partial(layers_kernel, n, nseg, heads),
        out_shape=(
            jax.ShapeDtypeStruct((n, length, width), BF16),
            jax.ShapeDtypeStruct((n, length, width), BF16),
            jax.ShapeDtypeStruct((2 * items, rows, width), BF16),
            jax.ShapeDtypeStruct((2 * items, rows, width), BF16),
            jax.ShapeDtypeStruct((2 * items, rows, 4 * width), BF16),
            jax.ShapeDtypeStruct((2 * items, rows, hidden_half), BF16),
            jax.ShapeDtypeStruct((2 * items, rows, width), BF16),
            jax.ShapeDtypeStruct((2, width), F32),
        ),
        in_specs=[any_spec] * 5 + [vmem_spec] * 2,
        out_specs=[any_spec] * 7 + [vmem_spec],
        scratch_shapes=[
            pltpu.VMEM((2, width, 4 * width), BF16),
            pltpu.VMEM((2, hidden_half, width), BF16),
            pltpu.VMEM((2, 2, width), F32),
            item_rows,
            item_rows,
            pltpu.VMEM((items, 2, rows, 2 * width), BF16),
            item_rows,
            item_rows,
            item_rows,
            item_rows,
            item_rows,
            item_rows,
            pltpu.VMEM((items, rows, 2 * hidden_half), BF16),
            pltpu.VMEM((items, rows, 2 * hidden_half), BF16),
            pltpu.VMEM((items, rows, 128), F32),
            pltpu.VMEM((items, rows, 2 * rows), F32),
            pltpu.VMEM((items, MEM_PAD, width), BF16),
            pltpu.VMEM((items, MEM_PAD, width), BF16),
            pltpu.VMEM((2, rows, 2 * width), BF16),
            pltpu.VMEM((2, rows, 2 * width), BF16),
            pltpu.VMEM((rows, width), F32),
            pltpu.VMEM((rows, width), BF16),
            pltpu.VMEM((2, 2, width), F32),
            pltpu.VMEM((2, width), F32),
            dma((4,)), dma((5,)), dma((5,)),
        ]
        + [dma((items,))] * 15
        + [dma(()), dma(())]
        + [dma((KINDS, items))] * 3,
        compiler_params=pltpu.CompilerParams(
            collective_id=0, has_side_effects=True, vmem_limit_bytes=60 * 1024 * 1024
        ),
    )(tokens, cotangent, first, down, bias, gain_bias, keep)


def shards(
    tokens, doc_ids, reset_flags, first_weights, down_halves, norm_gain, norm_bias, cotangent
):
    c = lax.rem(lax.axis_index("section"), 2)
    n, length, width = tokens.shape
    nseg = NSEG
    seg_len = length // nseg
    toks = seg_len // 2
    items = n * nseg
    mem_half = M // 2
    rows = toks + MEM_PAD

    docs = doc_ids.reshape(n, nseg, 2, toks).transpose(1, 0, 2, 3).reshape(items, 2, toks)
    tail = jnp.where(lax.iota(jnp.int32, MEM_PAD) < mem_half, -1, -2)
    tail = jnp.broadcast_to(tail, (items, 2, MEM_PAD))
    marks = jnp.concatenate([docs, tail], axis=2)
    own = lax.dynamic_index_in_dim(marks, c, 1, keepdims=False)
    keys = marks.reshape(items, 1, 2 * rows)
    own = own[:, :, None]
    allowed = (own == keys) | (keys == -1) | (own < 0)
    bias = jnp.where(keys == -2, ABSENT_SCORE, jnp.where(allowed, 0.0, MASKED_SCORE))
    bias = bias.astype(F32)
    resets = jnp.concatenate([jnp.ones((n, 1), jnp.int32), reset_flags], axis=1)
    keep = (1 - resets).astype(F32).T.reshape(items, 1, 1)
    keep = jnp.broadcast_to(keep, (items, MEM_PAD, 128))
    gain_bias = jnp.concatenate([norm_gain, norm_bias], axis=0)

    out, gin, sx1, sx2, sr, sg, sd, norm_grad = run_layers(
        n, nseg, H, tokens, cotangent, first_weights[0], down_halves[0], bias, gain_bias, keep
    )
    total = 2 * items * rows
    sx1, sx2, sd = (a.reshape(total, width) for a in (sx1, sx2, sd))
    sr = sr.reshape(total, 4 * width)
    sg = sg.reshape(total, -1)

    def weight_grad(left, right):
        return jnp.einsum("rd,re->de", left, right, preferred_element_type=F32).astype(BF16)

    first_grad = jnp.concatenate(
        [weight_grad(sx1, sr[:, : 3 * width]), weight_grad(sx2, sr[:, 3 * width :])], axis=1
    )
    down_grad = weight_grad(sg, sd)
    first_grad, down_grad = lax.psum((first_grad, down_grad), "dp")
    norm_grad = lax.psum(norm_grad, "dp")
    return (
        out[None],
        gin[None],
        first_grad.astype(F32)[None],
        down_grad.astype(F32)[None],
        norm_grad[0:1],
        norm_grad[1:2],
    )


def solution(mesh):
    in_specs = (
        P("dp", None, None),
        P("dp", None),
        P("dp", None),
        P("section", None, None),
        P("section", None, None),
        P("section", None),
        P("section", None),
        P("dp", None, None),
    )
    out_specs = (
        P("section", "dp", None, None),
        P("section", "dp", None, None),
        P("section", None, None),
        P("section", None, None),
        P("section", None),
        P("section", None),
    )
    return jax.shard_map(shards, mesh=mesh, in_specs=in_specs, out_specs=out_specs, check_vma=False)
```

```python
from functools import partial

import jax
import jax.numpy as jnp
from jax import lax
from jax.experimental import pallas as pl
from jax.experimental.pallas import tpu as pltpu
from jax.sharding import PartitionSpec as P

H = 12
M = 20
NSEG = 2
MEM_PAD = 16
NORM_EPSILON = 1e-05
MASKED_SCORE = -1000000000.0
ABSENT_SCORE = -3e38
MESH = pl.DeviceIdType.MESH
BF16 = jnp.bfloat16
F32 = jnp.float32

OUT_ATT, OUT_FF, GIN_ATT, GIN_FF = 0, 1, 2, 3
S_X0, S_CTX, S_DQ, S_DKV, S_DATT, S_GLO, S_DFF0 = 4, 5, 6, 7, 8, 9, 10
S_Y1, S_Y2, S_DU, S_GHI, S_DFF1 = 11, 12, 13, 14, 15
KINDS = 16


def dot(a, b, lhs_dim=1, rhs_dim=0):
    return lax.dot_general(
        a, b, (((lhs_dim,), (rhs_dim,)), ((), ())), preferred_element_type=F32
    )


def normalize(summed):
    mean = jnp.mean(summed, axis=-1, keepdims=True)
    centered = summed - mean
    var = jnp.mean(centered * centered, axis=-1, keepdims=True)
    inv = lax.rsqrt(var + NORM_EPSILON)
    return centered * inv, inv


def layers_kernel(
    n, nseg, heads,
    tokens, cotangent, first, down, bias, gain_bias, keep,
    out, gin, sx1, sx2, sr, sg, sd, norm_grad,
    wf, wd, nrm, x0, q, kv, ctx, natt, yatt, nff, yd, gy, g, gp, stats, biasb,
    memin, mgin, dkvs, dkvin, dhb, dctx, acc, accp,
    wl, ws, wr, tok_sem, cot_sem, bias_sem, kvs_sem, kvr_sem, xs_sem, xr_sem,
    ms_sem, mr_sem, gs_sem, gr_sem, hs_sem, hr_sem, ds_sem, dr_sem, as_sem, ar_sem,
    lsem, ssem, rsem,
):
    items = n * nseg
    section = lax.axis_index("section")
    c = lax.rem(section, 2)
    x = lax.div(section, 2)
    core_peer = {"section": x * 2 + (1 - c)}
    chip_peer = {"section": (1 - x) * 2 + c}
    rows, width = x0.shape[1:]
    toks = rows - MEM_PAD
    seg_len = 2 * toks
    hidden_half = wd.shape[1]
    hidden = 2 * hidden_half
    wide = 3 * width
    lanes = 128
    chunk = 512 if hidden_half % 512 == 0 else 256
    per_half = hidden_half // chunk
    ncol = 256

    def remote(src, dst, send, recv, peer):
        return pltpu.make_async_remote_copy(
            src_ref=src, dst_ref=dst, send_sem=send, recv_sem=recv,
            device_id=peer, device_id_type=MESH,
        )

    barrier = pltpu.get_barrier_semaphore()
    pl.semaphore_signal(barrier, inc=1, device_id=core_peer, device_id_type=MESH)
    pl.semaphore_signal(barrier, inc=1, device_id=chip_peer, device_id_type=MESH)
    pl.semaphore_wait(barrier, 2)

    def weight_piece(k):
        if k == 0:
            return first.at[:, width:wide], wf.at[c, :, width:wide]
        if k == 1:
            return first.at[:, 0:width], wf.at[c, :, 0:width]
        if k == 2:
            return first.at[:, wide:], wf.at[c, :, wide:]
        return down, wd.at[c]

    nrm[c] = gain_bias[...]
    nrm_copy = remote(nrm.at[c], nrm.at[c], ws.at[4], wr.at[4], core_peer)
    for k in range(4):
        src, dst = weight_piece(k)
        remote(src, dst, ws.at[k], wr.at[k], core_peer).start()
        pltpu.make_async_copy(src, dst, wl.at[k]).start()
    nrm_copy.start()

    def wait_local(k):
        src, dst = weight_piece(k)
        pltpu.make_async_copy(src, dst, wl.at[k]).wait()

    def wait_remote(k):
        if k == 4:
            nrm_copy.wait_recv()
        else:
            src, dst = weight_piece(k)
            remote(src, dst, ws.at[k], wr.at[k], core_peer).wait_recv()

    def wait_first_of(core, ks):
        @pl.when(c == core)
        def _():
            for k in ks:
                wait_local(k)

        @pl.when(c != core)
        def _():
            for k in ks:
                wait_remote(k)

    def bias_copy(i):
        return pltpu.make_async_copy(bias.at[i], biasb.at[i], bias_sem.at[i])

    def token_rows(ref, i):
        return ref.at[lax.rem(i, n), pl.ds(lax.div(i, n) * seg_len + c * toks, toks), :]

    def token_copy(i):
        return pltpu.make_async_copy(
            token_rows(tokens, i), x0.at[i, 0:toks, :], tok_sem.at[i]
        )

    def cot_copy(i):
        return pltpu.make_async_copy(
            token_rows(cotangent, i), gy.at[i, 0:toks, :], cot_sem.at[i]
        )

    for i in range(items):
        @pl.when(x == 0)
        def _():
            token_copy(i).start()

        bias_copy(i).start()

    for i in range(items):
        @pl.when(x == 1)
        def _():
            cot_copy(i).start()

    def routed(kind, i):
        block = i * 2 + c
        sec = 0
        if kind == OUT_ATT:
            src, dst = yatt.at[i, 0:toks, :], token_rows(out, i)
        elif kind == OUT_FF:
            src, dst, sec = yd.at[i, 0:toks, :], token_rows(out, i), 1
        elif kind == GIN_ATT:
            src, dst = yd.at[i, 0:toks, :], token_rows(gin, i)
        elif kind == GIN_FF:
            src, dst, sec = gy.at[i, 0:toks, :], token_rows(gin, i), 1
        elif kind == S_X0:
            src, dst = x0.at[i], sx1.at[block]
        elif kind == S_CTX:
            src, dst = ctx.at[i], sx2.at[block]
        elif kind == S_DQ:
            src, dst = q.at[i], sr.at[block, :, 0:width]
        elif kind == S_DKV:
            src, dst = kv.at[i, c], sr.at[block, :, width:wide]
        elif kind == S_DATT:
            src, dst = natt.at[i], sr.at[block, :, wide:]
        elif kind == S_GLO:
            src, dst = g.at[i, :, 0:hidden_half], sg.at[block]
        elif kind == S_DFF0:
            src, dst = nff.at[i], sd.at[block]
        elif kind == S_Y1:
            src, dst, sec = yatt.at[i], sx1.at[block], 1
        elif kind == S_Y2:
            src, dst, sec = yatt.at[i], sx2.at[block], 1
        elif kind == S_DU:
            src, dst, sec = gp.at[i], sr.at[block], 1
        elif kind == S_GHI:
            src, dst, sec = g.at[i, :, hidden_half:], sg.at[block], 1
        else:
            src, dst, sec = nff.at[i], sd.at[block], 1
        return src, dst, sec

    def route_local(kind, i):
        src, dst, _ = routed(kind, i)
        return pltpu.make_async_copy(src, dst, lsem.at[kind, i])

    def route_away(kind, i):
        src, dst, _ = routed(kind, i)
        return remote(src, dst, ssem.at[kind, i], rsem.at[kind, i], core_peer)

    def route(kind, i):
        sec = routed(kind, i)[2]

        @pl.when(c == sec)
        def _():
            route_local(kind, i).start()

        @pl.when(c != sec)
        def _():
            route_away(kind, i).start()

    def route_sent(kind, i):
        sec = routed(kind, i)[2]

        @pl.when(c == sec)
        def _():
            route_local(kind, i).wait()

        @pl.when(c != sec)
        def _():
            route_away(kind, i).wait_send()

    def route_received(kind, i):
        @pl.when(c == routed(kind, i)[2])
        def _():
            route_away(kind, i).wait_recv()

    def kv_copy(i):
        return remote(kv.at[i, c], kv.at[i, c], kvs_sem.at[i], kvr_sem.at[i], core_peer)

    def x_copy(i):
        return remote(yd.at[i], x0.at[i], xs_sem.at[i], xr_sem.at[i], chip_peer)

    def mem_copy(i):
        return remote(
            yd.at[i, toks:rows, :], memin.at[i], ms_sem.at[i], mr_sem.at[i], chip_peer
        )

    def gy_copy(i):
        return remote(yd.at[i], gy.at[i], gs_sem.at[i], gr_sem.at[i], chip_peer)

    def mg_copy(i):
        return remote(
            yd.at[i, toks:rows, :], mgin.at[i], hs_sem.at[i], hr_sem.at[i], chip_peer
        )

    def dkv_copy(i, slot):
        return remote(
            dkvs.at[1 - c], dkvin.at[slot], ds_sem.at[i], dr_sem.at[i], core_peer
        )

    lane = lax.broadcasted_iota(jnp.int32, (rows, lanes), 1)
    first_head = lane < lanes // 2
    stat_lane = lax.broadcasted_iota(jnp.int32, (rows, lanes), 1)
    key_first_head = lax.broadcasted_iota(jnp.int32, (2 * rows, lanes), 1) < lanes // 2

    def lane_block(j, base=0):
        return pl.ds(pl.multiple_of(base + j * lanes, lanes), lanes)

    def masked_scores(qm, k2, i):
        s = dot(qm, k2, 1, 1)
        b = biasb[i]
        return jnp.where(b == 0.0, s, b)

    def both_keys(i, cols):
        return jnp.concatenate([kv[i, 0, :, cols], kv[i, 1, :, cols]], axis=0)

    def forward_tick(t, carry):
        i = t - x

        @pl.when((i >= 0) & (i < items))
        def _():
            @pl.when(x == 0)
            def _():
                token_copy(i).wait()

                @pl.when(i < n)
                def _():
                    x0[i, toks:rows, :] = jnp.zeros((MEM_PAD, width), BF16)

                @pl.when(i >= n)
                def _():
                    mem_copy(i - n).wait_recv()
                    x0[i, toks:rows, :] = jnp.where(
                        keep[i][:, 0:1] > 0.0, memin[i - n], jnp.zeros((), BF16)
                    )

            @pl.when(x == 1)
            def _():
                x_copy(i).wait_recv()

            @pl.when(i == 0)
            def _():
                wait_first_of(0, (0,))

            xb = x0[i]
            for col in range(width, wide, ncol):
                kv[i, c, :, col - width : col - width + ncol] = dot(
                    xb, wf[0, :, col : col + ncol]
                ).astype(BF16)
            kv_copy(i).start()
            route(S_X0, i)

            @pl.when(i == 0)
            def _():
                wait_first_of(0, (1,))

            for col in range(0, width, ncol):
                q[i, :, col : col + ncol] = (
                    dot(xb, wf[0, :, col : col + ncol]).astype(BF16) * BF16(0.125)
                )
            bias_copy(i).wait()
            kv_copy(i).wait_recv()
            stats[i] = jnp.zeros((rows, lanes), F32)

            def head_pair(j, carry):
                cols = lane_block(j)
                q2 = q[i, :, cols]
                k2 = both_keys(i, cols)
                v2 = both_keys(i, lane_block(j, width))
                outs = []
                for e in range(2):
                    mine = first_head if e == 0 else ~first_head
                    s = masked_scores(jnp.where(mine, q2, BF16(0)), k2, i)
                    peak = jnp.max(s, axis=1, keepdims=True)
                    p = jnp.exp(s - peak)
                    total = jnp.sum(p, axis=1, keepdims=True)
                    outs.append(dot(p.astype(BF16), v2) * (1.0 / total))
                    lse = peak + jnp.log(total)
                    stats[i] = jnp.where(stat_lane == 2 * j + e, lse, stats[i])
                ctx[i, :, cols] = jnp.where(first_head, outs[0], outs[1]).astype(BF16)
                return carry

            lax.fori_loop(0, heads // 2, head_pair, 0)
            route(S_CTX, i)

            @pl.when(i == 0)
            def _():
                wait_first_of(0, (2,))

                @pl.when(c == 0)
                def _():
                    wait_remote(4)

                @pl.when(c == 1)
                def _():
                    wait_remote(4)

            for col in range(0, width, ncol):
                dhb[:, col : col + ncol] = dot(
                    ctx[i], wf[0, :, wide + col : wide + col + ncol]
                ) + x0[i, :, col : col + ncol].astype(F32)
            normed, inv = normalize(dhb[...])
            natt[i] = normed.astype(BF16)
            stats[i] = jnp.where(stat_lane == heads, inv, stats[i])
            yatt[i] = (normed * nrm[0, 0:1, :] + nrm[0, 1:2, :]).astype(BF16)
            route(OUT_ATT, i)
            route(S_Y1, i)
            route(S_Y2, i)

            @pl.when(i == 0)
            def _():
                wait_first_of(1, (0, 1, 2))

            def up(k, carry):
                cols = pl.ds(pl.multiple_of(k * chunk, chunk), chunk)
                u = dot(yatt[i], wf[1, :, cols])
                cdf = 0.5 + 0.5 * lax.erf(u * 0.7071067811865476)
                pdf = 0.3989422804014327 * jnp.exp(-0.5 * u * u)
                g[i, :, cols] = (u * cdf).astype(BF16)
                gp[i, :, cols] = (cdf + u * pdf).astype(BF16)
                return carry

            lax.fori_loop(0, hidden // chunk, up, 0)
            route(S_GLO, i)
            route(S_GHI, i)

            @pl.when(i == 0)
            def _():
                wait_first_of(0, (3,))
                wait_first_of(1, (3,))

            for col in range(0, width, ncol):
                dhb[:, col : col + ncol] = (
                    dot(g[i, :, 0:hidden_half], wd[0, :, col : col + ncol])
                    + dot(g[i, :, hidden_half:], wd[1, :, col : col + ncol])
                    + yatt[i, :, col : col + ncol].astype(F32)
                )
            normed, inv = normalize(dhb[...])
            nff[i] = normed.astype(BF16)
            stats[i] = jnp.where(stat_lane == heads + 1, inv, stats[i])
            yd[i] = (normed * nrm[1, 0:1, :] + nrm[1, 1:2, :]).astype(BF16)

            @pl.when(x == 0)
            def _():
                x_copy(i).start()

            @pl.when((x == 1) & (i < items - n))
            def _():
                mem_copy(i).start()

            route(OUT_FF, i)

        return carry

    lax.fori_loop(0, items + 1, forward_tick, 0)

    def forward_drain(i, carry):
        kv_copy(i).wait_send()
        route_sent(OUT_FF, i)

        @pl.when(x == 0)
        def _():
            x_copy(i).wait_send()

        @pl.when((x == 1) & (i < items - n))
        def _():
            mem_copy(i).wait_send()

        return carry

    lax.fori_loop(0, items, forward_drain, 0)
    acc[...] = jnp.zeros_like(acc)

    def norm_back(s, i, normed_ref):
        grad = gy[i].astype(F32)
        normed = normed_ref[i].astype(F32)
        inv = jnp.sum(jnp.where(stat_lane == heads + s, stats[i], 0.0), axis=1, keepdims=True)
        acc[s, 0:1, :] += jnp.sum(grad * normed, axis=0, keepdims=True)
        acc[s, 1:2, :] += jnp.sum(grad, axis=0, keepdims=True)
        scaled = grad * nrm[s, 0:1, :]
        row_term = jnp.mean(scaled, axis=1, keepdims=True)
        row_cross = jnp.mean(scaled * normed, axis=1, keepdims=True)
        dh = inv * (scaled - row_term - normed * row_cross)
        dhb[...] = dh
        normed_ref[i] = dh.astype(BF16)

    def backward_tick(t, carry):
        r = t - (1 - x)

        @pl.when((r >= 0) & (r < items))
        def _():
            i = (nseg - 1 - lax.div(r, n)) * n + lax.rem(r, n)
            slot = lax.rem(r, 2)

            @pl.when(x == 1)
            def _():
                cot_copy(i).wait()

                @pl.when(i >= items - n)
                def _():
                    gy[i, toks:rows, :] = jnp.zeros((MEM_PAD, width), BF16)

                @pl.when(i < items - n)
                def _():
                    mg_copy(i + n).wait_recv()
                    gy[i, toks:rows, :] = jnp.where(
                        keep[i + n][:, 0:1] > 0.0, mgin[i + n], jnp.zeros((), BF16)
                    )

            @pl.when(x == 0)
            def _():
                gy_copy(i).wait_recv()

            norm_back(1, i, nff)
            route(S_DFF0, i)
            route(S_DFF1, i)

            def down_back(k, carry):
                cols = pl.ds(pl.multiple_of(k * chunk, chunk), chunk)
                part = pl.ds(pl.multiple_of(lax.rem(k, per_half) * chunk, chunk), chunk)
                dg = dot(nff[i], wd[lax.div(k, per_half), part, :], 1, 1)
                gp[i, :, cols] = (dg * gp[i, :, cols].astype(F32)).astype(BF16)
                return carry

            lax.fori_loop(0, hidden // chunk, down_back, 0)
            route(S_DU, i)
            for col in range(0, width, ncol):
                gy[i, :, col : col + ncol] = (
                    dot(gp[i], wf[1, col : col + ncol, :], 1, 1) + dhb[:, col : col + ncol]
                ).astype(BF16)
            route(GIN_FF, i)

            norm_back(0, i, natt)
            route(S_DATT, i)
            for col in range(0, width, ncol):
                dctx[:, col : col + ncol] = dot(
                    natt[i], wf[0, col : col + ncol, wide:], 1, 1
                ).astype(BF16)

            def head_pair(j, carry):
                cols = lane_block(j)
                q2 = q[i, :, cols]
                k2 = both_keys(i, cols)
                v2 = both_keys(i, lane_block(j, width))
                c2 = dctx[:, cols]
                t2 = c2.astype(F32) * ctx[i, :, cols].astype(F32)
                dq2, dk2, dv2 = 0.0, 0.0, 0.0
                for e in range(2):
                    mine = first_head if e == 0 else ~first_head
                    key_mine = key_first_head if e == 0 else ~key_first_head
                    qm = jnp.where(mine, q2, BF16(0))
                    cm = jnp.where(mine, c2, BF16(0))
                    km = jnp.where(key_mine, k2, BF16(0))
                    lse = jnp.sum(
                        jnp.where(stat_lane == 2 * j + e, stats[i], 0.0), axis=1, keepdims=True
                    )
                    inner = jnp.sum(jnp.where(mine, t2, 0.0), axis=1, keepdims=True)
                    p = jnp.exp(masked_scores(qm, k2, i) - lse)
                    dp = dot(cm, v2, 1, 1)
                    ds = (p * (dp - inner)).astype(BF16)
                    dv2 = dv2 + dot(p.astype(BF16), cm, 0, 0)
                    dk2 = dk2 + dot(ds, qm, 0, 0)
                    dq2 = dq2 + dot(ds, km)
                q[i, :, cols] = (dq2 * 0.125).astype(BF16)
                vcols = lane_block(j, width)
                dkvs[0, :, cols] = dk2[0:rows].astype(BF16)
                dkvs[1, :, cols] = dk2[rows:].astype(BF16)
                dkvs[0, :, vcols] = dv2[0:rows].astype(BF16)
                dkvs[1, :, vcols] = dv2[rows:].astype(BF16)
                return carry

            lax.fori_loop(0, heads // 2, head_pair, 0)
            dkv_copy(i, slot).start()
            route(S_DQ, i)
            for col in range(0, width, ncol):
                dhb[:, col : col + ncol] += dot(q[i], wf[0, col : col + ncol, 0:width], 1, 1)
            dkv_copy(i, slot).wait_recv()
            kv[i, c] = (dkvs[c].astype(F32) + dkvin[slot].astype(F32)).astype(BF16)
            route(S_DKV, i)
            for col in range(0, width, ncol):
                yd[i, :, col : col + ncol] = (
                    dot(kv[i, c], wf[0, col : col + ncol, width:wide], 1, 1)
                    + dhb[:, col : col + ncol]
                ).astype(BF16)

            @pl.when(x == 1)
            def _():
                gy_copy(i).start()

            @pl.when((x == 0) & (i >= n))
            def _():
                mg_copy(i).start()

            route(GIN_ATT, i)
            dkv_copy(i, slot).wait_send()

        return carry

    lax.fori_loop(0, items + 1, backward_tick, 0)

    acc_copy = remote(acc.at[1 - c], accp, as_sem, ar_sem, core_peer)
    acc_copy.start()

    def backward_drain(i, carry):
        @pl.when(x == 1)
        def _():
            gy_copy(i).wait_send()

        @pl.when((x == 0) & (i >= n))
        def _():
            mg_copy(i).wait_send()

        for kind in range(KINDS):
            if kind != OUT_FF:
                route_sent(kind, i)
            route_received(kind, i)
        return carry

    lax.fori_loop(0, items, backward_drain, 0)
    for k in range(4):
        src, dst = weight_piece(k)
        remote(src, dst, ws.at[k], wr.at[k], core_peer).wait_send()
    nrm_copy.wait_send()
    acc_copy.wait()
    norm_grad[...] = acc[c] + accp[...]


def run_layers(n, nseg, heads, tokens, cotangent, first, down, bias, gain_bias, keep):
    length, width = tokens.shape[1:]
    toks = length // nseg // 2
    rows = toks + MEM_PAD
    items = n * nseg
    hidden_half = down.shape[0]
    any_spec = pl.BlockSpec(memory_space=pl.ANY)
    vmem_spec = pl.BlockSpec(memory_space=pltpu.VMEM)
    dma = pltpu.SemaphoreType.DMA
    item_rows = pltpu.VMEM((items, rows, width), BF16)
    return pl.pallas_call(
        partial(layers_kernel, n, nseg, heads),
        out_shape=(
            jax.ShapeDtypeStruct((n, length, width), BF16),
            jax.ShapeDtypeStruct((n, length, width), BF16),
            jax.ShapeDtypeStruct((2 * items, rows, width), BF16),
            jax.ShapeDtypeStruct((2 * items, rows, width), BF16),
            jax.ShapeDtypeStruct((2 * items, rows, 4 * width), BF16),
            jax.ShapeDtypeStruct((2 * items, rows, hidden_half), BF16),
            jax.ShapeDtypeStruct((2 * items, rows, width), BF16),
            jax.ShapeDtypeStruct((2, width), F32),
        ),
        in_specs=[any_spec] * 5 + [vmem_spec] * 2,
        out_specs=[any_spec] * 7 + [vmem_spec],
        scratch_shapes=[
            pltpu.VMEM((2, width, 4 * width), BF16),
            pltpu.VMEM((2, hidden_half, width), BF16),
            pltpu.VMEM((2, 2, width), F32),
            item_rows,
            item_rows,
            pltpu.VMEM((items, 2, rows, 2 * width), BF16),
            item_rows,
            item_rows,
            item_rows,
            item_rows,
            item_rows,
            item_rows,
            pltpu.VMEM((items, rows, 2 * hidden_half), BF16),
            pltpu.VMEM((items, rows, 2 * hidden_half), BF16),
            pltpu.VMEM((items, rows, 128), F32),
            pltpu.VMEM((items, rows, 2 * rows), F32),
            pltpu.VMEM((items, MEM_PAD, width), BF16),
            pltpu.VMEM((items, MEM_PAD, width), BF16),
            pltpu.VMEM((2, rows, 2 * width), BF16),
            pltpu.VMEM((2, rows, 2 * width), BF16),
            pltpu.VMEM((rows, width), F32),
            pltpu.VMEM((rows, width), BF16),
            pltpu.VMEM((2, 2, width), F32),
            pltpu.VMEM((2, width), F32),
            dma((4,)), dma((5,)), dma((5,)),
        ]
        + [dma((items,))] * 15
        + [dma(()), dma(())]
        + [dma((KINDS, items))] * 3,
        compiler_params=pltpu.CompilerParams(
            collective_id=0, has_side_effects=True, vmem_limit_bytes=60 * 1024 * 1024
        ),
    )(tokens, cotangent, first, down, bias, gain_bias, keep)


def reduce_kernel(
    chunks,
    sx1, sx2, sr, sg, sd, norm_part,
    first_out, down_out, norm_out,
    x1, x2, rr, gg, dd, work, done, got_u, got_uz, got_vz, got_vy, stage, norms,
    in_sem, out_sem, u_s, u_r, uz_s, uz_r, vz_s, vz_r, vy_s, vy_r, vg_s, vg_r,
    uzg_s, uzg_r, vzg_s, vzg_r, ug_s, ug_r, n_s, n_r,
):
    lines = 4
    d = lax.axis_index("dp")
    y = lax.rem(d, 2)
    z = lax.div(d, 2)
    dp = lax.axis_size("dp")
    width = sd.shape[1]
    half = width // 2
    part = width // chunks
    hr = part // 2
    lane_group = 128
    per_group = lane_group // part
    y_peer = {"dp": z * 2 + (1 - y)}

    def remote(src, dst, send, recv, peer):
        return pltpu.make_async_remote_copy(
            src_ref=src, dst_ref=dst, send_sem=send, recv_sem=recv,
            device_id=peer, device_id_type=MESH,
        )

    def other(step):
        return {"dp": lax.rem(d + step, dp)}

    barrier = pltpu.get_barrier_semaphore()
    for step in range(1, dp):
        pl.semaphore_signal(barrier, inc=1, device_id=other(step), device_id_type=MESH)

    loads = [
        (sd, dd),
        (sg.at[:, 0:width], gg.at[:, 0:width]),
        (sg.at[:, width:], gg.at[:, width:]),
        (sx2, x2),
        (sr.at[:, 3 * width :], rr.at[:, 3 * width :]),
        (sx1, x1),
        (sr.at[:, 0 : 3 * width], rr.at[:, 0 : 3 * width]),
    ]
    for k, (src, dst) in enumerate(loads):
        pltpu.make_async_copy(src, dst, in_sem.at[k]).start()

    norms[d] = norm_part[...]
    pl.semaphore_wait(barrier, dp - 1)

    def norm_copy(step):
        return remote(norms.at[d], norms.at[d], n_s.at[step - 1], n_r.at[step - 1], other(step))

    def norm_arrival(step):
        source = lax.rem(d + dp - step, dp)
        return remote(
            norms.at[source], norms.at[source], n_s.at[step - 1], n_r.at[step - 1], other(step)
        )

    for step in range(1, dp):
        norm_copy(step).start()

    def column_half(h):
        return pl.ds(pl.multiple_of(h * half, 128), half)

    mine, theirs = column_half(y), column_half(1 - y)

    def place(flow):
        return z if flow == 0 else lines - 1 - z

    def onward(flow):
        step = -1 if flow == 0 else 1
        return {"dp": (z + step) * 2 + y}

    def back(flow):
        step = 1 if flow == 0 else -1
        return {"dp": (z + step) * 2 + y}

    def rows_of(flow):
        return slice(flow * hr, (flow + 1) * hr)

    def u_copy(k):
        return remote(
            work.at[k, 0:3, :, theirs], got_u.at[k], u_s.at[k], u_r.at[k], y_peer
        )

    def uz_copy(flow, k):
        return remote(
            work.at[k, 0:3, rows_of(flow), mine], got_uz.at[flow, k],
            uz_s.at[flow, k], uz_r.at[flow, k], onward(flow),
        )

    def vz_copy(flow, k):
        return remote(
            work.at[k, 3:6, rows_of(flow), :], got_vz.at[flow, k],
            vz_s.at[flow, k], vz_r.at[flow, k], onward(flow),
        )

    def vy_copy(flow, k):
        return remote(
            work.at[k, 3:6, rows_of(flow), theirs], got_vy.at[k], vy_s.at[k], vy_r.at[k], y_peer
        )

    def vg_copy(flow, k, cols):
        spot = done.at[k, 3:6, rows_of(flow), cols]
        return remote(spot, spot, vg_s.at[k], vg_r.at[k], y_peer)

    def uzg_copy(flow, k):
        spot = done.at[k, 0:3, rows_of(flow), mine]
        return remote(spot, spot, uzg_s.at[flow, k], uzg_r.at[flow, k], back(flow))

    def vzg_copy(flow, k):
        spot = done.at[k, 3:6, rows_of(flow), :]
        return remote(spot, spot, vzg_s.at[flow, k], vzg_r.at[flow, k], back(flow))

    def ug_copy(flow, k, cols):
        spot = done.at[k, 0:3, rows_of(flow), cols]
        return remote(spot, spot, ug_s.at[flow, k], ug_r.at[flow, k], y_peer)

    def out_copies(k, slot):
        rows = pl.ds(pl.multiple_of(k * part, part), part)
        copies = []
        for b in range(6):
            if b < 4:
                dst = first_out.at[rows, b * width : (b + 1) * width]
            else:
                low = pl.ds(pl.multiple_of((b - 4) * width + k * part, part), part)
                dst = down_out.at[low, :]
            copies.append(
                pltpu.make_async_copy(stage.at[slot, b], dst, out_sem.at[slot, b])
            )
        return copies

    def plus(a, b):
        return (a.astype(F32) + b.astype(F32)).astype(BF16)

    def wait_load(k):
        src, dst = loads[k]
        pltpu.make_async_copy(src, dst, in_sem.at[k]).wait()

    def ready(k, low=0):
        return (k >= low) & (k < chunks)

    def store_chunks(group, block, value):
        for e in range(per_group):
            work[group * per_group + e, block] = value[e * part : (e + 1) * part]

    def round_step(r, carry):
        group = lax.div(r, per_group)

        @pl.when((lax.rem(r, per_group) == 0) & (r < chunks))
        def _():
            cols = pl.ds(pl.multiple_of(group * lane_group, lane_group), lane_group)
            gcols = pl.ds(pl.multiple_of(width + group * lane_group, lane_group), lane_group)

            @pl.when(r == 0)
            def _():
                wait_load(0)
                wait_load(1)

            store_chunks(group, 4, dot(gg[:, cols], dd[...], 0, 0).astype(BF16))

            @pl.when(r == 0)
            def _():
                wait_load(2)

            store_chunks(group, 5, dot(gg[:, gcols], dd[...], 0, 0).astype(BF16))

            @pl.when(r == 0)
            def _():
                wait_load(3)
                wait_load(4)

            store_chunks(group, 3, dot(x2[:, cols], rr[:, 3 * width :], 0, 0).astype(BF16))

            @pl.when(r == 0)
            def _():
                wait_load(5)
                wait_load(6)

            for b in range(3):
                store_chunks(
                    group, b,
                    dot(x1[:, cols], rr[:, b * width : (b + 1) * width], 0, 0).astype(BF16),
                )

        @pl.when(ready(r))
        def _():
            u_copy(r).start()

        for flow in range(2):
            p = place(flow)
            k = r - (lines - 1 - p)
            rows = rows_of(flow)

            @pl.when(ready(k))
            def _():
                @pl.when(p < lines - 1)
                def _():
                    vz_copy(flow, k).wait_recv()
                    work[k, 3:6, rows, :] = plus(work[k, 3:6, rows, :], got_vz[flow, k])

                @pl.when(p > 0)
                def _():
                    vz_copy(flow, k).start()

                @pl.when(p == 0)
                def _():
                    vy_copy(flow, k).start()

        @pl.when(ready(r - 1))
        def _():
            k = r - 1
            u_copy(k).wait_recv()
            work[k, 0:3, :, mine] = plus(work[k, 0:3, :, mine], got_u[k])

        for flow in range(2):
            p = place(flow)
            k = r - 1 - (lines - 1 - p)
            rows = rows_of(flow)

            @pl.when(ready(k))
            def _():
                @pl.when(p < lines - 1)
                def _():
                    uz_copy(flow, k).wait_recv()
                    total = plus(work[k, 0:3, rows, mine], got_uz[flow, k])

                    @pl.when(p > 0)
                    def _():
                        work[k, 0:3, rows, mine] = total

                    @pl.when(p == 0)
                    def _():
                        done[k, 0:3, rows, mine] = total

                @pl.when(p > 0)
                def _():
                    uz_copy(flow, k).start()

                @pl.when(p == 0)
                def _():
                    uzg_copy(flow, k).start()
                    ug_copy(flow, k, mine).start()

        for flow in range(2):
            p = place(flow)
            rows = rows_of(flow)

            @pl.when((p == 0) & ready(r - lines))
            def _():
                k = r - lines
                vy_copy(flow, k).wait_recv()
                done[k, 3:6, rows, mine] = plus(work[k, 3:6, rows, mine], got_vy[k])
                vg_copy(flow, k, mine).start()

            @pl.when((p == 0) & ready(r - lines - 1))
            def _():
                k = r - lines - 1
                vg_copy(flow, k, theirs).wait_recv()
                vzg_copy(flow, k).start()

        for flow in range(2):
            p = place(flow)
            k = r - lines - p

            @pl.when((p > 0) & ready(k))
            def _():
                uzg_copy(flow, k).wait_recv()

                @pl.when(p < lines - 1)
                def _():
                    uzg_copy(flow, k).start()

                ug_copy(flow, k, mine).start()

        for flow in range(2):
            p = place(flow)
            k = r - lines - 1 - p

            @pl.when((p > 0) & ready(k))
            def _():
                vzg_copy(flow, k).wait_recv()

                @pl.when(p < lines - 1)
                def _():
                    vzg_copy(flow, k).start()

            @pl.when(ready(k))
            def _():
                ug_copy(flow, k, theirs).wait_recv()

        k = r - 2 * lines

        @pl.when(ready(k))
        def _():
            slot = lax.rem(k, 2)

            @pl.when(k >= 2)
            def _():
                for copy in out_copies(k - 2, slot):
                    copy.wait()

            stage[slot] = done[k].astype(F32)
            for copy in out_copies(k, slot):
                copy.start()

        return carry

    lax.fori_loop(0, chunks + 2 * lines, round_step, 0)

    for step in range(1, dp):
        norm_arrival(step).wait_recv()
    total = norms[0]
    for e in range(1, dp):
        total = total + norms[e]
    norm_out[...] = total

    def drain(k, carry):
        u_copy(k).wait_send()
        for flow in range(2):
            p = place(flow)
            ug_copy(flow, k, mine).wait_send()

            @pl.when(p > 0)
            def _():
                vz_copy(flow, k).wait_send()
                uz_copy(flow, k).wait_send()

            @pl.when(p < lines - 1)
            def _():
                uzg_copy(flow, k).wait_send()
                vzg_copy(flow, k).wait_send()

            @pl.when(p == 0)
            def _():
                vy_copy(flow, k).wait_send()
                vg_copy(flow, k, mine).wait_send()

        return carry

    lax.fori_loop(0, chunks, drain, 0)
    for k in (chunks - 2, chunks - 1):
        for copy in out_copies(k, k % 2):
            copy.wait()
    for step in range(1, dp):
        norm_copy(step).wait_send()


def sum_weights(dp, sx1, sx2, sr, sg, sd, norm_part):
    total, width = sx1.shape
    chunks = 12
    part = width // chunks
    half = width // 2
    any_spec = pl.BlockSpec(memory_space=pl.ANY)
    vmem_spec = pl.BlockSpec(memory_space=pltpu.VMEM)
    dma = pltpu.SemaphoreType.DMA
    one, two = dma((chunks,)), dma((2, chunks))
    return pl.pallas_call(
        partial(reduce_kernel, chunks),
        out_shape=(
            jax.ShapeDtypeStruct((width, 4 * width), F32),
            jax.ShapeDtypeStruct((2 * width, width), F32),
            jax.ShapeDtypeStruct((2, width), F32),
        ),
        in_specs=[any_spec] * 5 + [vmem_spec],
        out_specs=[any_spec] * 2 + [vmem_spec],
        scratch_shapes=[
            pltpu.VMEM((total, width), BF16),
            pltpu.VMEM((total, width), BF16),
            pltpu.VMEM((total, 4 * width), BF16),
            pltpu.VMEM((total, 2 * width), BF16),
            pltpu.VMEM((total, width), BF16),
            pltpu.VMEM((chunks, 6, part, width), BF16),
            pltpu.VMEM((chunks, 6, part, width), BF16),
            pltpu.VMEM((chunks, 3, part, half), BF16),
            pltpu.VMEM((2, chunks, 3, part // 2, half), BF16),
            pltpu.VMEM((2, chunks, 3, part // 2, width), BF16),
            pltpu.VMEM((chunks, 3, part // 2, half), BF16),
            pltpu.VMEM((2, 6, part, width), F32),
            pltpu.VMEM((dp, 2, width), F32),
            dma((7,)),
            dma((2, 6)),
            one, one,
            two, two,
            two, two,
            one, one,
            one, one,
            two, two,
            two, two,
            two, two,
            dma((dp - 1,)), dma((dp - 1,)),
        ],
        compiler_params=pltpu.CompilerParams(
            collective_id=1, has_side_effects=True, vmem_limit_bytes=60 * 1024 * 1024
        ),
    )(sx1, sx2, sr, sg, sd, norm_part)


def shards(
    tokens, doc_ids, reset_flags, first_weights, down_halves, norm_gain, norm_bias, cotangent
):
    c = lax.rem(lax.axis_index("section"), 2)
    n, length, width = tokens.shape
    nseg = NSEG
    seg_len = length // nseg
    toks = seg_len // 2
    items = n * nseg
    mem_half = M // 2
    rows = toks + MEM_PAD

    docs = doc_ids.reshape(n, nseg, 2, toks).transpose(1, 0, 2, 3).reshape(items, 2, toks)
    tail = jnp.where(lax.iota(jnp.int32, MEM_PAD) < mem_half, -1, -2)
    tail = jnp.broadcast_to(tail, (items, 2, MEM_PAD))
    marks = jnp.concatenate([docs, tail], axis=2)
    own = lax.dynamic_index_in_dim(marks, c, 1, keepdims=False)
    keys = marks.reshape(items, 1, 2 * rows)
    own = own[:, :, None]
    allowed = (own == keys) | (keys == -1) | (own < 0)
    bias = jnp.where(keys == -2, ABSENT_SCORE, jnp.where(allowed, 0.0, MASKED_SCORE))
    bias = bias.astype(F32)
    resets = jnp.concatenate([jnp.ones((n, 1), jnp.int32), reset_flags], axis=1)
    keep = (1 - resets).astype(F32).T.reshape(items, 1, 1)
    keep = jnp.broadcast_to(keep, (items, MEM_PAD, 128))
    gain_bias = jnp.concatenate([norm_gain, norm_bias], axis=0)

    out, gin, sx1, sx2, sr, sg, sd, norm_grad = run_layers(
        n, nseg, H, tokens, cotangent, first_weights[0], down_halves[0], bias, gain_bias, keep
    )
    total = 2 * items * rows
    sx1, sx2, sd = (a.reshape(total, width) for a in (sx1, sx2, sd))
    sr = sr.reshape(total, 4 * width)
    sg = sg.reshape(total, -1)

    dp = lax.axis_size("dp")
    if dp == 8:
        first_grad, down_grad, norm_grad = sum_weights(dp, sx1, sx2, sr, sg, sd, norm_grad)
    else:

        def weight_grad(left, right):
            return jnp.einsum("rd,re->de", left, right, preferred_element_type=F32).astype(BF16)

        first_grad = jnp.concatenate(
            [weight_grad(sx1, sr[:, : 3 * width]), weight_grad(sx2, sr[:, 3 * width :])], axis=1
        )
        down_grad = weight_grad(sg, sd)
        first_grad, down_grad = lax.psum((first_grad, down_grad), "dp")
        norm_grad = lax.psum(norm_grad, "dp")
    return (
        out[None],
        gin[None],
        first_grad.astype(F32)[None],
        down_grad.astype(F32)[None],
        norm_grad[0:1],
        norm_grad[1:2],
    )


def solution(mesh):
    in_specs = (
        P("dp", None, None),
        P("dp", None),
        P("dp", None),
        P("section", None, None),
        P("section", None, None),
        P("section", None),
        P("section", None),
        P("dp", None, None),
    )
    out_specs = (
        P("section", "dp", None, None),
        P("section", "dp", None, None),
        P("section", None, None),
        P("section", None, None),
        P("section", None),
        P("section", None),
    )
    return jax.shard_map(shards, mesh=mesh, in_specs=in_specs, out_specs=out_specs, check_vma=False)
```

```python
from functools import partial

import jax
import jax.numpy as jnp
from jax import lax
from jax.experimental import pallas as pl
from jax.experimental.pallas import tpu as pltpu
from jax.sharding import PartitionSpec as P

H = 12
M = 20
NSEG = 2
MEM_PAD = 16
NORM_EPSILON = 1e-05
MASKED_SCORE = -1000000000.0
ABSENT_SCORE = -3e38
MESH = pl.DeviceIdType.MESH
BF16 = jnp.bfloat16
F32 = jnp.float32

OUT_ATT, OUT_FF, GIN_ATT, GIN_FF = 0, 1, 2, 3
S_X0, S_CTX, S_DQ, S_DKV, S_DATT, S_GLO, S_DFF0 = 4, 5, 6, 7, 8, 9, 10
S_Y1, S_Y2, S_DU, S_GHI, S_DFF1 = 11, 12, 13, 14, 15
KINDS = 16


def dot(a, b, lhs_dim=1, rhs_dim=0):
    return lax.dot_general(
        a, b, (((lhs_dim,), (rhs_dim,)), ((), ())), preferred_element_type=F32
    )


def normalize(summed):
    mean = jnp.mean(summed, axis=-1, keepdims=True)
    centered = summed - mean
    var = jnp.mean(centered * centered, axis=-1, keepdims=True)
    inv = lax.rsqrt(var + NORM_EPSILON)
    return centered * inv, inv


def group_of(shape, dim, size):
    index = lax.broadcasted_iota(jnp.int32, shape, dim)
    return lax.shift_right_logical(index, size.bit_length() - 1)


def spread(values, groups):
    result = values[-1]
    for h in range(len(values) - 1):
        result = jnp.where(groups == h, values[h], result)
    return result


def layers_kernel(
    n, nseg, heads,
    tokens, cotangent, first, down, docs, resets, gain, shift,
    out, gin, sx1, sx2, sr, sg, sd, norm_grad,
    wf, wd, nrm, x0, q, kv, ctx, natt, yatt, nff, yd, gy, g, gp, stats, qdoc, kdoc, keep,
    memin, mgin, dkvs, dkvin, dhb, dctx, acc, accp,
    wl, ws, wr, tok_sem, cot_sem, kvs_sem, kvr_sem, xs_sem, xr_sem,
    ms_sem, mr_sem, gs_sem, gr_sem, hs_sem, hr_sem, ds_sem, dr_sem, as_sem, ar_sem,
    lsem, ssem, rsem,
):
    items = n * nseg
    section = lax.axis_index("section")
    c = lax.rem(section, 2)
    x = lax.div(section, 2)
    core_peer = {"section": x * 2 + (1 - c)}
    chip_peer = {"section": (1 - x) * 2 + c}
    rows, width = x0.shape[1:]
    toks = rows - MEM_PAD
    seg_len = 2 * toks
    hidden_half = wd.shape[1]
    wide = 3 * width
    head_dim = width // heads
    quad = 4 * head_dim
    quads = heads // 4
    mem_keys = 2 * MEM_PAD
    scale = head_dim ** (-0.5)

    def remote(src, dst, send, recv, peer):
        return pltpu.make_async_remote_copy(
            src_ref=src, dst_ref=dst, send_sem=send, recv_sem=recv,
            device_id=peer, device_id_type=MESH,
        )

    barrier = pltpu.get_barrier_semaphore()
    pl.semaphore_signal(barrier, inc=1, device_id=core_peer, device_id_type=MESH)
    pl.semaphore_signal(barrier, inc=1, device_id=chip_peer, device_id_type=MESH)

    def token_rows(ref, i):
        return ref.at[lax.rem(i, n), pl.ds(lax.div(i, n) * seg_len + c * toks, toks), :]

    def token_copy(i):
        return pltpu.make_async_copy(
            token_rows(tokens, i), x0.at[i, 0:toks, :], tok_sem.at[i]
        )

    def cot_copy(i):
        return pltpu.make_async_copy(
            token_rows(cotangent, i), gy.at[i, 0:toks, :], cot_sem.at[i]
        )

    def weight_piece(k):
        if k == 0:
            return first.at[0, :, width:wide], wf.at[c, :, width:wide]
        if k == 1:
            return first.at[0, :, 0:width], wf.at[c, :, 0:width]
        if k == 2:
            return first.at[0, :, wide:], wf.at[c, :, wide:]
        return down.at[0], wd.at[c]

    def weight_local(k):
        src, dst = weight_piece(k)
        return pltpu.make_async_copy(src, dst, wl.at[k])

    def weight_remote(k):
        if k == 4:
            return remote(nrm.at[c], nrm.at[c], ws.at[4], wr.at[4], core_peer)
        src, dst = weight_piece(k)
        return remote(src, dst, ws.at[k], wr.at[k], core_peer)

    nrm[c, 0:1, :] = gain[...]
    nrm[c, 1:2, :] = shift[...]
    weight_local(0).start()

    @pl.when(x == 0)
    def _():
        token_copy(0).start()

    pl.semaphore_wait(barrier, 2)
    for k in range(5):
        weight_remote(k).start()
    for k in range(1, 4):
        weight_local(k).start()
    for i in range(items):
        if i > 0:

            @pl.when(x == 0)
            def _():
                token_copy(i).start()

        @pl.when(x == 1)
        def _():
            cot_copy(i).start()

    def wait_first_of(core, ks):
        @pl.when(c == core)
        def _():
            for k in ks:
                weight_local(k).wait()

        @pl.when(c != core)
        def _():
            for k in ks:
                weight_remote(k).wait_recv()

    for i in range(items):
        seq, seg = i % n, i // n
        kdoc[i] = docs[seq : seq + 1, seg * seg_len : (seg + 1) * seg_len].astype(F32)
        own = pl.ds(pl.multiple_of(seg * seg_len + c * toks, toks), toks)
        own_row = docs[seq : seq + 1, own].astype(F32)
        qdoc[i] = jnp.transpose(jnp.broadcast_to(own_row, (128, toks)))
        if seg > 0:
            flag = resets[seq : seq + 1, seg - 1 : seg].astype(F32)
            keep[i] = jnp.broadcast_to(1.0 - flag, (MEM_PAD, 128))

    def routed(kind, i):
        block = i * 2 + c
        sec = 0
        if kind == OUT_ATT:
            src, dst = yatt.at[i, 0:toks, :], token_rows(out, i)
        elif kind == OUT_FF:
            src, dst, sec = yd.at[i, 0:toks, :], token_rows(out, i), 1
        elif kind == GIN_ATT:
            src, dst = yd.at[i, 0:toks, :], token_rows(gin, i)
        elif kind == GIN_FF:
            src, dst, sec = gy.at[i, 0:toks, :], token_rows(gin, i), 1
        elif kind == S_X0:
            src, dst = x0.at[i], sx1.at[block]
        elif kind == S_CTX:
            src, dst = ctx.at[i], sx2.at[block]
        elif kind == S_DQ:
            src, dst = q.at[i], sr.at[block, :, 0:width]
        elif kind == S_DKV:
            src, dst = kv.at[i, c], sr.at[block, :, width:wide]
        elif kind == S_DATT:
            src, dst = natt.at[i], sr.at[block, :, wide:]
        elif kind == S_GLO:
            src, dst = g.at[i, :, 0:hidden_half], sg.at[block]
        elif kind == S_DFF0:
            src, dst = nff.at[i], sd.at[block]
        elif kind == S_Y1:
            src, dst, sec = yatt.at[i], sx1.at[block], 1
        elif kind == S_Y2:
            src, dst, sec = yatt.at[i], sx2.at[block], 1
        elif kind == S_DU:
            src, dst, sec = gp.at[i], sr.at[block], 1
        elif kind == S_GHI:
            src, dst, sec = g.at[i, :, hidden_half:], sg.at[block], 1
        else:
            src, dst, sec = nff.at[i], sd.at[block], 1
        return src, dst, sec

    def route_local(kind, i):
        src, dst, _ = routed(kind, i)
        return pltpu.make_async_copy(src, dst, lsem.at[kind, i])

    def route_away(kind, i):
        src, dst, _ = routed(kind, i)
        return remote(src, dst, ssem.at[kind, i], rsem.at[kind, i], core_peer)

    def route(kind, i):
        sec = routed(kind, i)[2]

        @pl.when(c == sec)
        def _():
            route_local(kind, i).start()

        @pl.when(c != sec)
        def _():
            route_away(kind, i).start()

    def route_sent(kind, i):
        sec = routed(kind, i)[2]

        @pl.when(c == sec)
        def _():
            route_local(kind, i).wait()

        @pl.when(c != sec)
        def _():
            route_away(kind, i).wait_send()

    def route_received(kind, i):
        @pl.when(c == routed(kind, i)[2])
        def _():
            route_away(kind, i).wait_recv()

    def kv_copy(part, i):
        piece = kv.at[i, c, :, part * width : (part + 1) * width]
        return remote(piece, piece, kvs_sem.at[part, i], kvr_sem.at[part, i], core_peer)

    def x_copy(i):
        return remote(yd.at[i], x0.at[i], xs_sem.at[i], xr_sem.at[i], chip_peer)

    def mem_copy(i):
        return remote(
            yd.at[i, toks:rows, :], memin.at[i], ms_sem.at[i], mr_sem.at[i], chip_peer
        )

    def gy_copy(i):
        return remote(yd.at[i], gy.at[i], gs_sem.at[i], gr_sem.at[i], chip_peer)

    def mg_copy(i):
        return remote(
            yd.at[i, toks:rows, :], mgin.at[i], hs_sem.at[i], hr_sem.at[i], chip_peer
        )

    def dkv_copy(j, i, slot):
        return remote(
            dkvs.at[1 - c, j], dkvin.at[slot, j], ds_sem.at[j, i], dr_sem.at[j, i], core_peer
        )

    head_lanes = group_of((rows, quad), 1, head_dim)
    mem_lanes = group_of((rows, 4 * mem_keys), 1, mem_keys)
    key_lane = lax.broadcasted_iota(jnp.int32, (rows, 4 * mem_keys), 1)
    mem_valid = lax.rem(key_lane, MEM_PAD) < M // 2
    diagonal = group_of((4 * mem_keys, quad), 0, mem_keys) == group_of(
        (4 * mem_keys, quad), 1, head_dim
    )
    stat_lane = lax.broadcasted_iota(jnp.int32, (rows, 128), 1)

    def stacked(block):
        return jnp.concatenate(
            [jnp.where(head_lanes == h, block, BF16(0)) for h in range(4)], axis=0
        )

    def head_rows(block):
        return [block[h * rows : (h + 1) * rows] for h in range(4)]

    def token_and_memory(i, low):
        cols = slice(low, low + quad)
        tok = jnp.concatenate([kv[i, 0, 0:toks, cols], kv[i, 1, 0:toks, cols]], axis=0)
        mem = jnp.concatenate([kv[i, 0, toks:, cols], kv[i, 1, toks:, cols]], axis=0)
        return tok, jnp.where(diagonal, jnp.concatenate([mem] * 4, axis=0), BF16(0))

    def only_same_document(s, i):
        mine = jnp.concatenate([qdoc[i]] * (seg_len // 128), axis=1)
        same = jnp.where(mine == kdoc[i], s[0:toks], MASKED_SCORE)
        return jnp.concatenate([same, s[toks:]], axis=0)

    def memory_scores(q4, mem_k):
        return jnp.where(mem_valid, dot(q4, mem_k, 1, 1), ABSENT_SCORE)

    def attend(i):
        st = jnp.zeros((rows, 128), F32)
        for j in range(quads):
            cols = slice(j * quad, (j + 1) * quad)
            q4 = q[i, :, cols]
            if j == 0:
                kv_copy(0, i).wait_recv()
            tok_k, mem_k = token_and_memory(i, j * quad)
            s = head_rows(dot(stacked(q4), tok_k, 1, 1))
            sm = memory_scores(q4, mem_k)
            peaks, totals, probs = [], [], []
            for h in range(4):
                sh = only_same_document(s[h], i)
                own_mem = jnp.where(mem_lanes == h, sm, ABSENT_SCORE)
                peak = jnp.maximum(
                    jnp.max(sh, axis=1, keepdims=True), jnp.max(own_mem, axis=1, keepdims=True)
                )
                p = jnp.exp(sh - peak)
                peaks.append(peak)
                totals.append(jnp.sum(p, axis=1, keepdims=True))
                probs.append(p.astype(BF16))
            pm = jnp.exp(sm - spread(peaks, mem_lanes))
            for h in range(4):
                totals[h] += jnp.sum(jnp.where(mem_lanes == h, pm, 0.0), axis=1, keepdims=True)
                lse = peaks[h] + jnp.log(totals[h])
                st = jnp.where(stat_lane == 4 * j + h, lse, st)
            if j == 0:
                kv_copy(1, i).wait_recv()
            tok_v, mem_v = token_and_memory(i, width + j * quad)
            o = spread(head_rows(dot(jnp.concatenate(probs, axis=0), tok_v)), head_lanes)
            o = o + dot(pm.astype(BF16), mem_v)
            inverse = spread([1.0 / total for total in totals], head_lanes)
            ctx[i, :, cols] = (o * inverse).astype(BF16)
        stats[i] = st

    def forward_tick(t, carry):
        i = t - x

        @pl.when((i >= 0) & (i < items))
        def _():
            @pl.when(x == 0)
            def _():
                token_copy(i).wait()

                @pl.when(i < n)
                def _():
                    x0[i, toks:rows, :] = jnp.zeros((MEM_PAD, width), BF16)

                @pl.when(i >= n)
                def _():
                    mem_copy(i - n).wait_recv()
                    x0[i, toks:rows, :] = jnp.where(
                        keep[i][:, 0:1] > 0.0, memin[i - n], jnp.zeros((), BF16)
                    )

            @pl.when(x == 1)
            def _():
                x_copy(i).wait_recv()

            @pl.when(i == 0)
            def _():
                wait_first_of(0, (0,))

            for part in range(2):
                kv[i, c, :, part * width : (part + 1) * width] = dot(
                    x0[i], wf[0, :, (part + 1) * width : (part + 2) * width]
                ).astype(BF16)
                kv_copy(part, i).start()

            @pl.when(i == 0)
            def _():
                wait_first_of(0, (1,))

            q[i] = dot(x0[i], wf[0, :, 0:width]).astype(BF16) * BF16(scale)
            attend(i)
            route(S_X0, i)
            route(S_CTX, i)

            @pl.when(i == 0)
            def _():
                wait_first_of(0, (2,))
                weight_remote(4).wait_recv()

            normed, inv = normalize(dot(ctx[i], wf[0, :, wide:]) + x0[i].astype(F32))
            natt[i] = normed.astype(BF16)
            stats[i] = jnp.where(stat_lane == heads, inv, stats[i])
            yatt[i] = (normed * nrm[0, 0:1, :] + nrm[0, 1:2, :]).astype(BF16)

            @pl.when(i == 0)
            def _():
                wait_first_of(1, (0, 1, 2))

            for part in range(2):
                cols = slice(part * hidden_half, (part + 1) * hidden_half)
                u = dot(yatt[i], wf[1, :, cols])
                cdf = 0.5 + 0.5 * lax.erf(u * 0.7071067811865476)
                pdf = 0.3989422804014327 * jnp.exp(-0.5 * u * u)
                g[i, :, cols] = (u * cdf).astype(BF16)
                gp[i, :, cols] = (cdf + u * pdf).astype(BF16)
            route(OUT_ATT, i)
            route(S_Y1, i)
            route(S_Y2, i)
            route(S_GLO, i)
            route(S_GHI, i)

            @pl.when(i == 0)
            def _():
                wait_first_of(0, (3,))
                wait_first_of(1, (3,))

            normed, inv = normalize(
                dot(g[i, :, 0:hidden_half], wd[0])
                + dot(g[i, :, hidden_half:], wd[1])
                + yatt[i].astype(F32)
            )
            yd[i] = (normed * nrm[1, 0:1, :] + nrm[1, 1:2, :]).astype(BF16)

            @pl.when(x == 0)
            def _():
                x_copy(i).start()

            @pl.when((x == 1) & (i < items - n))
            def _():
                mem_copy(i).start()

            nff[i] = normed.astype(BF16)
            stats[i] = jnp.where(stat_lane == heads + 1, inv, stats[i])
            route(OUT_FF, i)

        return carry

    lax.fori_loop(0, items + 1, forward_tick, 0)

    def forward_drain(i, carry):
        kv_copy(0, i).wait_send()
        kv_copy(1, i).wait_send()
        route_sent(OUT_FF, i)

        @pl.when(x == 0)
        def _():
            x_copy(i).wait_send()

        @pl.when((x == 1) & (i < items - n))
        def _():
            mem_copy(i).wait_send()

        return carry

    lax.fori_loop(0, items, forward_drain, 0)
    acc[...] = jnp.zeros_like(acc)

    def norm_back(s, i, normed_ref):
        grad = gy[i].astype(F32)
        normed = normed_ref[i].astype(F32)
        inv = stats[i][:, heads + s : heads + s + 1]
        acc[s, 0:1, :] += jnp.sum(grad * normed, axis=0, keepdims=True)
        acc[s, 1:2, :] += jnp.sum(grad, axis=0, keepdims=True)
        scaled = grad * nrm[s, 0:1, :]
        row_term = jnp.mean(scaled, axis=1, keepdims=True)
        row_cross = jnp.mean(scaled * normed, axis=1, keepdims=True)
        dh = inv * (scaled - row_term - normed * row_cross)
        dhb[...] = dh
        normed_ref[i] = dh.astype(BF16)

    def attend_back(i, slot):
        for j in range(quads):
            cols = slice(j * quad, (j + 1) * quad)
            q4 = q[i, :, cols]
            c4 = dctx[:, cols]
            tok_k, mem_k = token_and_memory(i, j * quad)
            tok_v, mem_v = token_and_memory(i, width + j * quad)
            products = c4.astype(F32) * ctx[i, :, cols].astype(F32)
            qs, cs = stacked(q4), stacked(c4)
            s = head_rows(dot(qs, tok_k, 1, 1))
            dp = head_rows(dot(cs, tok_v, 1, 1))
            sm = memory_scores(q4, mem_k)
            dpm = dot(c4, mem_v, 1, 1)
            lse = [stats[i][:, 4 * j + h : 4 * j + h + 1] for h in range(4)]
            inner = [
                jnp.sum(jnp.where(head_lanes == h, products, 0.0), axis=1, keepdims=True)
                for h in range(4)
            ]
            probs, dscores = [], []
            for h in range(4):
                p = jnp.exp(only_same_document(s[h], i) - lse[h])
                probs.append(p.astype(BF16))
                dscores.append((p * (dp[h] - inner[h])).astype(BF16))
            pm = jnp.exp(sm - spread(lse, mem_lanes))
            dsm = (pm * (dpm - spread(inner, mem_lanes))).astype(BF16)
            probs = jnp.concatenate(probs, axis=0)
            dscores = jnp.concatenate(dscores, axis=0)
            dv = dot(probs, cs, 0, 0)
            dk = dot(dscores, qs, 0, 0)
            dq = spread(head_rows(dot(dscores, tok_k)), head_lanes) + dot(dsm, mem_k)
            q[i, :, cols] = (dq * scale).astype(BF16)
            dvm = jnp.where(diagonal, dot(pm.astype(BF16), c4, 0, 0), 0.0)
            dkm = jnp.where(diagonal, dot(dsm, q4, 0, 0), 0.0)
            dvm = sum(dvm[h * mem_keys : (h + 1) * mem_keys] for h in range(4))
            dkm = sum(dkm[h * mem_keys : (h + 1) * mem_keys] for h in range(4))
            for half, (tok_part, mem_part) in enumerate(((dk, dkm), (dv, dvm))):
                cols = slice(half * quad, (half + 1) * quad)
                for core in range(2):
                    dkvs[core, j, 0:toks, cols] = tok_part[
                        core * toks : (core + 1) * toks
                    ].astype(BF16)
                    dkvs[core, j, toks:rows, cols] = mem_part[
                        core * MEM_PAD : (core + 1) * MEM_PAD
                    ].astype(BF16)
            dkv_copy(j, i, slot).start()

    def gather_dkv(j, i, slot):
        dkv_copy(j, i, slot).wait_recv()
        both = (dkvs[c, j].astype(F32) + dkvin[slot, j].astype(F32)).astype(BF16)
        kv[i, c, :, j * quad : (j + 1) * quad] = both[:, 0:quad]
        kv[i, c, :, width + j * quad : width + (j + 1) * quad] = both[:, quad:]

    def dkv_back(i, low, high):
        return dot(kv[i, c, :, low:high], wf[0, :, width + low : width + high], 1, 1) + dot(
            kv[i, c, :, width + low : width + high],
            wf[0, :, 2 * width + low : 2 * width + high], 1, 1,
        )

    def backward_tick(t, carry):
        r = t - (1 - x)

        @pl.when((r >= 0) & (r < items))
        def _():
            i = (nseg - 1 - lax.div(r, n)) * n + lax.rem(r, n)
            slot = lax.rem(r, 2)

            @pl.when(x == 1)
            def _():
                cot_copy(i).wait()

                @pl.when(i >= items - n)
                def _():
                    gy[i, toks:rows, :] = jnp.zeros((MEM_PAD, width), BF16)

                @pl.when(i < items - n)
                def _():
                    mg_copy(i + n).wait_recv()
                    gy[i, toks:rows, :] = jnp.where(
                        keep[i + n][:, 0:1] > 0.0, mgin[i + n], jnp.zeros((), BF16)
                    )

            @pl.when(x == 0)
            def _():
                gy_copy(i).wait_recv()

            norm_back(1, i, nff)
            for part in range(2):
                cols = slice(part * hidden_half, (part + 1) * hidden_half)
                dg = dot(nff[i], wd[part], 1, 1)
                gp[i, :, cols] = (dg * gp[i, :, cols].astype(F32)).astype(BF16)
            gy[i] = (dot(gp[i], wf[1], 1, 1) + dhb[...]).astype(BF16)
            norm_back(0, i, natt)
            dctx[...] = dot(natt[i], wf[0, :, wide:], 1, 1).astype(BF16)
            route(S_DFF0, i)
            route(S_DFF1, i)
            route(S_DU, i)
            route(GIN_FF, i)
            route(S_DATT, i)
            attend_back(i, slot)
            for j in range(quads - 1):
                gather_dkv(j, i, slot)
            early = (quads - 1) * quad
            partial_sum = dot(q[i], wf[0, :, 0:width], 1, 1) + dhb[...]
            if early:
                partial_sum = partial_sum + dkv_back(i, 0, early)
            dhb[...] = partial_sum
            gather_dkv(quads - 1, i, slot)
            yd[i] = (dkv_back(i, early, width) + dhb[...]).astype(BF16)

            @pl.when(x == 1)
            def _():
                gy_copy(i).start()

            @pl.when((x == 0) & (i >= n))
            def _():
                mg_copy(i).start()

            route(S_DQ, i)
            route(S_DKV, i)
            route(GIN_ATT, i)
            for j in range(quads):
                dkv_copy(j, i, slot).wait_send()

        return carry

    lax.fori_loop(0, items + 1, backward_tick, 0)

    acc_copy = remote(acc.at[1 - c], accp, as_sem, ar_sem, core_peer)
    acc_copy.start()

    def backward_drain(i, carry):
        @pl.when(x == 1)
        def _():
            gy_copy(i).wait_send()

        @pl.when((x == 0) & (i >= n))
        def _():
            mg_copy(i).wait_send()

        for kind in range(KINDS):
            if kind != OUT_FF:
                route_sent(kind, i)
            route_received(kind, i)
        return carry

    lax.fori_loop(0, items, backward_drain, 0)
    for k in range(5):
        weight_remote(k).wait_send()
    acc_copy.wait()
    norm_grad[...] = acc[c] + accp[...]


def run_layers(n, nseg, heads, tokens, cotangent, first, down, docs, resets, gain, shift):
    length, width = tokens.shape[1:]
    toks = length // nseg // 2
    rows = toks + MEM_PAD
    items = n * nseg
    hidden_half = down.shape[1]
    quads = heads // 4
    quad = width // quads
    any_spec = pl.BlockSpec(memory_space=pl.ANY)
    vmem_spec = pl.BlockSpec(memory_space=pltpu.VMEM)
    dma = pltpu.SemaphoreType.DMA
    item_rows = pltpu.VMEM((items, rows, width), BF16)
    one = dma((items,))
    return pl.pallas_call(
        partial(layers_kernel, n, nseg, heads),
        out_shape=(
            jax.ShapeDtypeStruct((n, length, width), BF16),
            jax.ShapeDtypeStruct((n, length, width), BF16),
            jax.ShapeDtypeStruct((2 * items, rows, width), BF16),
            jax.ShapeDtypeStruct((2 * items, rows, width), BF16),
            jax.ShapeDtypeStruct((2 * items, rows, 4 * width), BF16),
            jax.ShapeDtypeStruct((2 * items, rows, hidden_half), BF16),
            jax.ShapeDtypeStruct((2 * items, rows, width), BF16),
            jax.ShapeDtypeStruct((2, width), F32),
        ),
        in_specs=[any_spec] * 4 + [vmem_spec] * 4,
        out_specs=[any_spec] * 7 + [vmem_spec],
        scratch_shapes=[
            pltpu.VMEM((2, width, 4 * width), BF16),
            pltpu.VMEM((2, hidden_half, width), BF16),
            pltpu.VMEM((2, 2, width), F32),
            item_rows,
            item_rows,
            pltpu.VMEM((items, 2, rows, 2 * width), BF16),
            item_rows,
            item_rows,
            item_rows,
            item_rows,
            item_rows,
            item_rows,
            pltpu.VMEM((items, rows, 2 * hidden_half), BF16),
            pltpu.VMEM((items, rows, 2 * hidden_half), BF16),
            pltpu.VMEM((items, rows, 128), F32),
            pltpu.VMEM((items, toks, 128), F32),
            pltpu.VMEM((items, 1, 2 * toks), F32),
            pltpu.VMEM((items, MEM_PAD, 128), F32),
            pltpu.VMEM((items, MEM_PAD, width), BF16),
            pltpu.VMEM((items, MEM_PAD, width), BF16),
            pltpu.VMEM((2, quads, rows, 2 * quad), BF16),
            pltpu.VMEM((2, quads, rows, 2 * quad), BF16),
            pltpu.VMEM((rows, width), F32),
            pltpu.VMEM((rows, width), BF16),
            pltpu.VMEM((2, 2, width), F32),
            pltpu.VMEM((2, width), F32),
            dma((4,)), dma((5,)), dma((5,)),
            one, one,
            dma((2, items)), dma((2, items)),
            one, one, one, one, one, one, one, one,
            dma((quads, items)), dma((quads, items)),
            dma(()), dma(()),
        ]
        + [dma((KINDS, items))] * 3,
        compiler_params=pltpu.CompilerParams(
            collective_id=0, has_side_effects=True, vmem_limit_bytes=61 * 1024 * 1024
        ),
    )(tokens, cotangent, first, down, docs, resets, gain, shift)


def reduce_kernel(
    chunks,
    sx1, sx2, sr, sg, sd, norm_part,
    first_out, down_out, norm_out,
    x1, x2, rr, gg, dd, work, done, got_u, got_uz, got_vz, got_vy, stage, norms,
    in_sem, out_sem, u_s, u_r, uz_s, uz_r, vz_s, vz_r, vy_s, vy_r, vg_s, vg_r,
    uzg_s, uzg_r, vzg_s, vzg_r, ug_s, ug_r, n_s, n_r,
):
    lines = 4
    d = lax.axis_index("dp")
    y = lax.rem(d, 2)
    z = lax.div(d, 2)
    dp = lax.axis_size("dp")
    width = sd.shape[1]
    half = width // 2
    part = width // chunks
    hr = part // 2
    lane_group = 128
    per_group = lane_group // part
    y_peer = {"dp": z * 2 + (1 - y)}

    def remote(src, dst, send, recv, peer):
        return pltpu.make_async_remote_copy(
            src_ref=src, dst_ref=dst, send_sem=send, recv_sem=recv,
            device_id=peer, device_id_type=MESH,
        )

    def other(step):
        return {"dp": lax.rem(d + step, dp)}

    barrier = pltpu.get_barrier_semaphore()
    for step in range(1, dp):
        pl.semaphore_signal(barrier, inc=1, device_id=other(step), device_id_type=MESH)

    loads = [
        (sd, dd),
        (sg.at[:, 0:width], gg.at[:, 0:width]),
        (sg.at[:, width:], gg.at[:, width:]),
        (sx2, x2),
        (sr.at[:, 3 * width :], rr.at[:, 3 * width :]),
        (sx1, x1),
        (sr.at[:, 0 : 3 * width], rr.at[:, 0 : 3 * width]),
    ]
    for k, (src, dst) in enumerate(loads):
        pltpu.make_async_copy(src, dst, in_sem.at[k]).start()

    norms[d] = norm_part[...]
    pl.semaphore_wait(barrier, dp - 1)

    def norm_copy(step):
        return remote(norms.at[d], norms.at[d], n_s.at[step - 1], n_r.at[step - 1], other(step))

    def norm_arrival(step):
        source = lax.rem(d + dp - step, dp)
        return remote(
            norms.at[source], norms.at[source], n_s.at[step - 1], n_r.at[step - 1], other(step)
        )

    for step in range(1, dp):
        norm_copy(step).start()

    def column_half(h):
        return pl.ds(pl.multiple_of(h * half, 128), half)

    mine, theirs = column_half(y), column_half(1 - y)

    def place(flow):
        return z if flow == 0 else lines - 1 - z

    def onward(flow):
        step = -1 if flow == 0 else 1
        return {"dp": (z + step) * 2 + y}

    def back(flow):
        step = 1 if flow == 0 else -1
        return {"dp": (z + step) * 2 + y}

    def rows_of(flow):
        return slice(flow * hr, (flow + 1) * hr)

    def u_copy(k):
        return remote(
            work.at[k, 0:3, :, theirs], got_u.at[k], u_s.at[k], u_r.at[k], y_peer
        )

    def uz_copy(flow, k):
        return remote(
            work.at[k, 0:3, rows_of(flow), mine], got_uz.at[flow, k],
            uz_s.at[flow, k], uz_r.at[flow, k], onward(flow),
        )

    def vz_copy(flow, k):
        return remote(
            work.at[k, 3:6, rows_of(flow), :], got_vz.at[flow, k],
            vz_s.at[flow, k], vz_r.at[flow, k], onward(flow),
        )

    def vy_copy(flow, k):
        return remote(
            work.at[k, 3:6, rows_of(flow), theirs], got_vy.at[k], vy_s.at[k], vy_r.at[k], y_peer
        )

    def vg_copy(flow, k, cols):
        spot = done.at[k, 3:6, rows_of(flow), cols]
        return remote(spot, spot, vg_s.at[k], vg_r.at[k], y_peer)

    def uzg_copy(flow, k):
        spot = done.at[k, 0:3, rows_of(flow), mine]
        return remote(spot, spot, uzg_s.at[flow, k], uzg_r.at[flow, k], back(flow))

    def vzg_copy(flow, k):
        spot = done.at[k, 3:6, rows_of(flow), :]
        return remote(spot, spot, vzg_s.at[flow, k], vzg_r.at[flow, k], back(flow))

    def ug_copy(flow, k, cols):
        spot = done.at[k, 0:3, rows_of(flow), cols]
        return remote(spot, spot, ug_s.at[flow, k], ug_r.at[flow, k], y_peer)

    def out_copies(k, slot):
        rows = pl.ds(pl.multiple_of(k * part, part), part)
        copies = []
        for b in range(6):
            if b < 4:
                dst = first_out.at[rows, b * width : (b + 1) * width]
            else:
                low = pl.ds(pl.multiple_of((b - 4) * width + k * part, part), part)
                dst = down_out.at[low, :]
            copies.append(
                pltpu.make_async_copy(stage.at[slot, b], dst, out_sem.at[slot, b])
            )
        return copies

    def plus(a, b):
        return (a.astype(F32) + b.astype(F32)).astype(BF16)

    def wait_load(k):
        src, dst = loads[k]
        pltpu.make_async_copy(src, dst, in_sem.at[k]).wait()

    def ready(k, low=0):
        return (k >= low) & (k < chunks)

    def store_chunks(group, block, value):
        for e in range(per_group):
            work[group * per_group + e, block] = value[e * part : (e + 1) * part]

    def round_step(r, carry):
        group = lax.div(r, per_group)

        @pl.when((lax.rem(r, per_group) == 0) & (r < chunks))
        def _():
            cols = pl.ds(pl.multiple_of(group * lane_group, lane_group), lane_group)
            gcols = pl.ds(pl.multiple_of(width + group * lane_group, lane_group), lane_group)

            @pl.when(r == 0)
            def _():
                wait_load(0)
                wait_load(1)

            store_chunks(group, 4, dot(gg[:, cols], dd[...], 0, 0).astype(BF16))

            @pl.when(r == 0)
            def _():
                wait_load(2)

            store_chunks(group, 5, dot(gg[:, gcols], dd[...], 0, 0).astype(BF16))

            @pl.when(r == 0)
            def _():
                wait_load(3)
                wait_load(4)

            store_chunks(group, 3, dot(x2[:, cols], rr[:, 3 * width :], 0, 0).astype(BF16))

        for flow in range(2):
            p = place(flow)
            k = r - (lines - 1 - p)
            rows = rows_of(flow)

            @pl.when(ready(k))
            def _():
                @pl.when(p < lines - 1)
                def _():
                    vz_copy(flow, k).wait_recv()
                    work[k, 3:6, rows, :] = plus(work[k, 3:6, rows, :], got_vz[flow, k])

                @pl.when(p > 0)
                def _():
                    vz_copy(flow, k).start()

                @pl.when(p == 0)
                def _():
                    vy_copy(flow, k).start()

        @pl.when((lax.rem(r, per_group) == 0) & (r < chunks))
        def _():
            cols = pl.ds(pl.multiple_of(group * lane_group, lane_group), lane_group)

            @pl.when(r == 0)
            def _():
                wait_load(5)
                wait_load(6)

            for b in range(3):
                store_chunks(
                    group, b,
                    dot(x1[:, cols], rr[:, b * width : (b + 1) * width], 0, 0).astype(BF16),
                )

        @pl.when(ready(r))
        def _():
            u_copy(r).start()

        @pl.when(ready(r - 1))
        def _():
            k = r - 1
            u_copy(k).wait_recv()
            work[k, 0:3, :, mine] = plus(work[k, 0:3, :, mine], got_u[k])

        for flow in range(2):
            p = place(flow)
            k = r - 1 - (lines - 1 - p)
            rows = rows_of(flow)

            @pl.when(ready(k))
            def _():
                @pl.when(p < lines - 1)
                def _():
                    uz_copy(flow, k).wait_recv()
                    total = plus(work[k, 0:3, rows, mine], got_uz[flow, k])

                    @pl.when(p > 0)
                    def _():
                        work[k, 0:3, rows, mine] = total

                    @pl.when(p == 0)
                    def _():
                        done[k, 0:3, rows, mine] = total

                @pl.when(p > 0)
                def _():
                    uz_copy(flow, k).start()

                @pl.when(p == 0)
                def _():
                    uzg_copy(flow, k).start()
                    ug_copy(flow, k, mine).start()

        for flow in range(2):
            p = place(flow)
            rows = rows_of(flow)

            @pl.when((p == 0) & ready(r - lines))
            def _():
                k = r - lines
                vy_copy(flow, k).wait_recv()
                done[k, 3:6, rows, mine] = plus(work[k, 3:6, rows, mine], got_vy[k])
                vg_copy(flow, k, mine).start()

            @pl.when((p == 0) & ready(r - lines - 1))
            def _():
                k = r - lines - 1
                vg_copy(flow, k, theirs).wait_recv()
                vzg_copy(flow, k).start()

        for flow in range(2):
            p = place(flow)
            k = r - lines - p

            @pl.when((p > 0) & ready(k))
            def _():
                uzg_copy(flow, k).wait_recv()

                @pl.when(p < lines - 1)
                def _():
                    uzg_copy(flow, k).start()

                ug_copy(flow, k, mine).start()

        for flow in range(2):
            p = place(flow)
            k = r - lines - 1 - p

            @pl.when((p > 0) & ready(k))
            def _():
                vzg_copy(flow, k).wait_recv()

                @pl.when(p < lines - 1)
                def _():
                    vzg_copy(flow, k).start()

            @pl.when(ready(k))
            def _():
                ug_copy(flow, k, theirs).wait_recv()

        k = r - 2 * lines

        @pl.when(ready(k))
        def _():
            slot = lax.rem(k, 2)

            @pl.when(k >= 2)
            def _():
                for copy in out_copies(k - 2, slot):
                    copy.wait()

            stage[slot] = done[k].astype(F32)
            for copy in out_copies(k, slot):
                copy.start()

        return carry

    lax.fori_loop(0, chunks + 2 * lines, round_step, 0)

    for step in range(1, dp):
        norm_arrival(step).wait_recv()
    total = norms[0]
    for e in range(1, dp):
        total = total + norms[e]
    norm_out[...] = total

    def drain(k, carry):
        u_copy(k).wait_send()
        for flow in range(2):
            p = place(flow)
            ug_copy(flow, k, mine).wait_send()

            @pl.when(p > 0)
            def _():
                vz_copy(flow, k).wait_send()
                uz_copy(flow, k).wait_send()

            @pl.when(p < lines - 1)
            def _():
                uzg_copy(flow, k).wait_send()
                vzg_copy(flow, k).wait_send()

            @pl.when(p == 0)
            def _():
                vy_copy(flow, k).wait_send()
                vg_copy(flow, k, mine).wait_send()

        return carry

    lax.fori_loop(0, chunks, drain, 0)
    for k in (chunks - 2, chunks - 1):
        for copy in out_copies(k, k % 2):
            copy.wait()
    for step in range(1, dp):
        norm_copy(step).wait_send()


def sum_weights(dp, sx1, sx2, sr, sg, sd, norm_part):
    total, width = sx1.shape
    chunks = 12
    part = width // chunks
    half = width // 2
    any_spec = pl.BlockSpec(memory_space=pl.ANY)
    vmem_spec = pl.BlockSpec(memory_space=pltpu.VMEM)
    dma = pltpu.SemaphoreType.DMA
    one, two = dma((chunks,)), dma((2, chunks))
    return pl.pallas_call(
        partial(reduce_kernel, chunks),
        out_shape=(
            jax.ShapeDtypeStruct((width, 4 * width), F32),
            jax.ShapeDtypeStruct((2 * width, width), F32),
            jax.ShapeDtypeStruct((2, width), F32),
        ),
        in_specs=[any_spec] * 5 + [vmem_spec],
        out_specs=[any_spec] * 2 + [vmem_spec],
        scratch_shapes=[
            pltpu.VMEM((total, width), BF16),
            pltpu.VMEM((total, width), BF16),
            pltpu.VMEM((total, 4 * width), BF16),
            pltpu.VMEM((total, 2 * width), BF16),
            pltpu.VMEM((total, width), BF16),
            pltpu.VMEM((chunks, 6, part, width), BF16),
            pltpu.VMEM((chunks, 6, part, width), BF16),
            pltpu.VMEM((chunks, 3, part, half), BF16),
            pltpu.VMEM((2, chunks, 3, part // 2, half), BF16),
            pltpu.VMEM((2, chunks, 3, part // 2, width), BF16),
            pltpu.VMEM((chunks, 3, part // 2, half), BF16),
            pltpu.VMEM((2, 6, part, width), F32),
            pltpu.VMEM((dp, 2, width), F32),
            dma((7,)),
            dma((2, 6)),
            one, one,
            two, two,
            two, two,
            one, one,
            one, one,
            two, two,
            two, two,
            two, two,
            dma((dp - 1,)), dma((dp - 1,)),
        ],
        compiler_params=pltpu.CompilerParams(
            collective_id=1, has_side_effects=True, vmem_limit_bytes=60 * 1024 * 1024
        ),
    )(sx1, sx2, sr, sg, sd, norm_part)


def shards(
    tokens, doc_ids, reset_flags, first_weights, down_halves, norm_gain, norm_bias, cotangent
):
    n, length, width = tokens.shape
    items = n * NSEG
    rows = length // NSEG // 2 + MEM_PAD
    out, gin, sx1, sx2, sr, sg, sd, norm_grad = run_layers(
        n, NSEG, H, tokens, cotangent, first_weights, down_halves,
        doc_ids, reset_flags, norm_gain, norm_bias,
    )
    total = 2 * items * rows
    sx1, sx2, sd = (a.reshape(total, width) for a in (sx1, sx2, sd))
    sr = sr.reshape(total, 4 * width)
    sg = sg.reshape(total, -1)

    dp = lax.axis_size("dp")
    if dp == 8:
        first_grad, down_grad, norm_grad = sum_weights(dp, sx1, sx2, sr, sg, sd, norm_grad)
    else:

        def weight_grad(left, right):
            return jnp.einsum("rd,re->de", left, right, preferred_element_type=F32).astype(BF16)

        first_grad = jnp.concatenate(
            [weight_grad(sx1, sr[:, : 3 * width]), weight_grad(sx2, sr[:, 3 * width :])], axis=1
        )
        down_grad = weight_grad(sg, sd)
        first_grad, down_grad = lax.psum((first_grad, down_grad), "dp")
        norm_grad = lax.psum(norm_grad, "dp")
    return (
        out[None],
        gin[None],
        first_grad.astype(F32)[None],
        down_grad.astype(F32)[None],
        norm_grad[0:1],
        norm_grad[1:2],
    )


def solution(mesh):
    in_specs = (
        P("dp", None, None),
        P("dp", None),
        P("dp", None),
        P("section", None, None),
        P("section", None, None),
        P("section", None),
        P("section", None),
        P("dp", None, None),
    )
    out_specs = (
        P("section", "dp", None, None),
        P("section", "dp", None, None),
        P("section", None, None),
        P("section", None, None),
        P("section", None),
        P("section", None),
    )
    return jax.shard_map(shards, mesh=mesh, in_specs=in_specs, out_specs=out_specs, check_vma=False)
```

```python
from functools import partial

import jax
import jax.numpy as jnp
from jax import lax
from jax.experimental import pallas as pl
from jax.experimental.pallas import tpu as pltpu
from jax.sharding import PartitionSpec as P

H = 12
M = 20
NSEG = 2
MEM_PAD = 16
NORM_EPSILON = 1e-05
MASKED_SCORE = -1000000000.0
ABSENT_SCORE = -3e38
MESH = pl.DeviceIdType.MESH
BF16 = jnp.bfloat16
F32 = jnp.float32

OUT_ATT, OUT_FF, GIN_ATT, GIN_FF = 0, 1, 2, 3
S_X0, S_CTX, S_DQ, S_DKV, S_DATT, S_GLO, S_DFF0 = 4, 5, 6, 7, 8, 9, 10
S_Y1, S_Y2, S_DU, S_GHI, S_DFF1 = 11, 12, 13, 14, 15
KINDS = 16


def dot(a, b, lhs_dim=1, rhs_dim=0):
    return lax.dot_general(
        a, b, (((lhs_dim,), (rhs_dim,)), ((), ())), preferred_element_type=F32
    )


def normalize(summed):
    mean = jnp.mean(summed, axis=-1, keepdims=True)
    centered = summed - mean
    var = jnp.mean(centered * centered, axis=-1, keepdims=True)
    inv = lax.rsqrt(var + NORM_EPSILON)
    return centered * inv, inv


def group_of(shape, dim, size):
    index = lax.broadcasted_iota(jnp.int32, shape, dim)
    return lax.shift_right_logical(index, size.bit_length() - 1)


def spread(values, groups):
    result = values[-1]
    for h in range(len(values) - 1):
        result = jnp.where(groups == h, values[h], result)
    return result


def layers_kernel(
    n, nseg, heads,
    tokens, cotangent, first, down, docs, resets, gain, shift,
    out, gin, sx1, sx2, sr, sg, sd, norm_grad,
    wf, wd, nrm, x0, xo, q, kv, ctx, natt, yatt, nff, yd, gy, g, gpb, gp, stats, qdoc, kdoc, keep,
    memin, mgin, dkvs, dkvin, dhb, dctx, acc, accp,
    wl, ws, wr, tok_sem, cot_sem, gp_sem, fs_sem, fr_sem, xs_sem, xr_sem,
    ms_sem, mr_sem, gs_sem, gr_sem, hs_sem, hr_sem, ds_sem, dr_sem, as_sem, ar_sem,
    lsem, ssem, rsem,
):
    items = n * nseg
    section = lax.axis_index("section")
    c = lax.rem(section, 2)
    x = lax.div(section, 2)
    core_peer = {"section": x * 2 + (1 - c)}
    chip_peer = {"section": (1 - x) * 2 + c}
    cross_peer = {"section": (1 - x) * 2 + (1 - c)}
    rows, width = x0.shape[1:]
    toks = rows - MEM_PAD
    seg_len = 2 * toks
    hidden_half = wd.shape[1]
    wide = 3 * width
    head_dim = width // heads
    quad = 4 * head_dim
    quads = heads // 4
    mem_keys = 2 * MEM_PAD
    scale = head_dim ** (-0.5)

    def remote(src, dst, send, recv, peer):
        return pltpu.make_async_remote_copy(
            src_ref=src, dst_ref=dst, send_sem=send, recv_sem=recv,
            device_id=peer, device_id_type=MESH,
        )

    barrier = pltpu.get_barrier_semaphore()
    pl.semaphore_signal(barrier, inc=1, device_id=core_peer, device_id_type=MESH)
    pl.semaphore_signal(barrier, inc=1, device_id=chip_peer, device_id_type=MESH)
    pl.semaphore_signal(barrier, inc=1, device_id=cross_peer, device_id_type=MESH)

    def token_rows(ref, i, core=None):
        core = c if core is None else core
        return ref.at[lax.rem(i, n), pl.ds(lax.div(i, n) * seg_len + core * toks, toks), :]

    def token_copy(which, i):
        if which == 0:
            src, dst = token_rows(tokens, i), x0.at[i, 0:toks, :]
        else:
            src, dst = token_rows(tokens, i, 1 - c), xo.at[i, 0:toks, :]
        return pltpu.make_async_copy(src, dst, tok_sem.at[which, i])

    def cot_copy(i):
        return pltpu.make_async_copy(
            token_rows(cotangent, i), gy.at[i, 0:toks, :], cot_sem.at[i]
        )

    def weight_piece(k):
        if k == 0:
            return first.at[0, :, width:wide], wf.at[c, :, width:wide]
        if k == 1:
            return first.at[0, :, 0:width], wf.at[c, :, 0:width]
        if k == 2:
            return first.at[0, :, wide:], wf.at[c, :, wide:]
        return down.at[0], wd.at[c]

    def weight_local(k):
        src, dst = weight_piece(k)
        return pltpu.make_async_copy(src, dst, wl.at[k])

    def weight_remote(k):
        if k == 4:
            return remote(nrm.at[c], nrm.at[c], ws.at[4], wr.at[4], core_peer)
        src, dst = weight_piece(k)
        return remote(src, dst, ws.at[k], wr.at[k], core_peer)

    nrm[c, 0:1, :] = gain[...]
    nrm[c, 1:2, :] = shift[...]
    weight_local(0).start()

    @pl.when(x == 0)
    def _():
        token_copy(0, 0).start()
        token_copy(1, 0).start()

    pl.semaphore_wait(barrier, 3)
    for k in range(5):
        weight_remote(k).start()
    for k in range(1, 4):
        weight_local(k).start()
    for i in range(items):
        if i > 0:

            @pl.when(x == 0)
            def _():
                token_copy(0, i).start()
                token_copy(1, i).start()

        @pl.when(x == 1)
        def _():
            cot_copy(i).start()

    def wait_first_of(core, ks):
        @pl.when(c == core)
        def _():
            for k in ks:
                weight_local(k).wait()

        @pl.when(c != core)
        def _():
            for k in ks:
                weight_remote(k).wait_recv()

    for i in range(items):
        seq, seg = i % n, i // n
        kdoc[i] = docs[seq : seq + 1, seg * seg_len : (seg + 1) * seg_len].astype(F32)
        own = pl.ds(pl.multiple_of(seg * seg_len + c * toks, toks), toks)
        own_row = docs[seq : seq + 1, own].astype(F32)
        qdoc[i] = jnp.transpose(jnp.broadcast_to(own_row, (128, toks)))
        if seg > 0:
            flag = resets[seq : seq + 1, seg - 1 : seg].astype(F32)
            keep[i] = jnp.broadcast_to(1.0 - flag, (MEM_PAD, 128))

    def routed(kind, i):
        block = i * 2 + c
        sec = 0
        if kind == OUT_ATT:
            src, dst = yatt.at[i, 0:toks, :], token_rows(out, i)
        elif kind == OUT_FF:
            src, dst, sec = yd.at[i, 0:toks, :], token_rows(out, i), 1
        elif kind == GIN_ATT:
            src, dst = yd.at[i, 0:toks, :], token_rows(gin, i)
        elif kind == GIN_FF:
            src, dst, sec = gy.at[i, 0:toks, :], token_rows(gin, i), 1
        elif kind == S_X0:
            src, dst = x0.at[i], sx1.at[block]
        elif kind == S_CTX:
            src, dst = ctx.at[i], sx2.at[block]
        elif kind == S_DQ:
            src, dst = q.at[i], sr.at[block, :, 0:width]
        elif kind == S_DKV:
            src, dst = kv.at[i, c], sr.at[block, :, width:wide]
        elif kind == S_DATT:
            src, dst = natt.at[i], sr.at[block, :, wide:]
        elif kind == S_GLO:
            src, dst = g.at[:, 0:hidden_half], sg.at[block]
        elif kind == S_DFF0:
            src, dst = nff.at[i], sd.at[block]
        elif kind == S_Y1:
            src, dst, sec = yatt.at[i], sx1.at[block], 1
        elif kind == S_Y2:
            src, dst, sec = yatt.at[i], sx2.at[block], 1
        elif kind == S_DU:
            src, dst, sec = gp.at[i], sr.at[block], 1
        elif kind == S_GHI:
            src, dst, sec = g.at[:, hidden_half:], sg.at[block], 1
        else:
            src, dst, sec = nff.at[i], sd.at[block], 1
        return src, dst, sec

    def route_local(kind, i):
        src, dst, _ = routed(kind, i)
        return pltpu.make_async_copy(src, dst, lsem.at[kind, i])

    def route_away(kind, i):
        src, dst, _ = routed(kind, i)
        return remote(src, dst, ssem.at[kind, i], rsem.at[kind, i], core_peer)

    def route(kind, i):
        sec = routed(kind, i)[2]

        @pl.when(c == sec)
        def _():
            route_local(kind, i).start()

        @pl.when(c != sec)
        def _():
            route_away(kind, i).start()

    def route_sent(kind, i):
        sec = routed(kind, i)[2]

        @pl.when(c == sec)
        def _():
            route_local(kind, i).wait()

        @pl.when(c != sec)
        def _():
            route_away(kind, i).wait_send()

    def route_received(kind, i):
        @pl.when(c == routed(kind, i)[2])
        def _():
            route_away(kind, i).wait_recv()

    def gp_copy(i):
        return pltpu.make_async_copy(gpb, gp.at[i], gp_sem.at[i])

    cut = rows // 32 * 16

    def piece(p):
        return slice(0, cut) if p == 0 else slice(cut, rows)

    def x_copy(p, i):
        return remote(
            yd.at[i, piece(p)], x0.at[i, piece(p)], xs_sem.at[p, i], xr_sem.at[p, i], chip_peer
        )

    def pass_copy(p, i):
        return remote(
            x0.at[i, piece(p)], xo.at[i, piece(p)], fs_sem.at[p, i], fr_sem.at[p, i], core_peer
        )

    def mem_copy(which, i):
        return remote(
            yd.at[i, toks:rows, :], memin.at[which, i], ms_sem.at[which, i],
            mr_sem.at[which, i], cross_peer if which else chip_peer,
        )

    def gy_copy(i):
        return remote(yd.at[i], gy.at[i], gs_sem.at[i], gr_sem.at[i], chip_peer)

    def mg_copy(i):
        return remote(
            yd.at[i, toks:rows, :], mgin.at[i], hs_sem.at[i], hr_sem.at[i], chip_peer
        )

    def dkv_copy(j, i, slot):
        return remote(
            dkvs.at[1 - c, j], dkvin.at[slot, j], ds_sem.at[j, i], dr_sem.at[j, i], core_peer
        )

    head_lanes = group_of((rows, quad), 1, head_dim)
    mem_lanes = group_of((rows, 4 * mem_keys), 1, mem_keys)
    key_lane = lax.broadcasted_iota(jnp.int32, (rows, 4 * mem_keys), 1)
    mem_valid = lax.rem(key_lane, MEM_PAD) < M // 2
    diagonal = group_of((4 * mem_keys, quad), 0, mem_keys) == group_of(
        (4 * mem_keys, quad), 1, head_dim
    )
    stat_lane = lax.broadcasted_iota(jnp.int32, (rows, 128), 1)

    def stacked(block):
        return jnp.concatenate(
            [jnp.where(head_lanes == h, block, BF16(0)) for h in range(4)], axis=0
        )

    def head_rows(block):
        return [block[h * rows : (h + 1) * rows] for h in range(4)]

    def token_and_memory(i, low):
        cols = slice(low, low + quad)
        tok = jnp.concatenate([kv[i, 0, 0:toks, cols], kv[i, 1, 0:toks, cols]], axis=0)
        mem = jnp.concatenate([kv[i, 0, toks:, cols], kv[i, 1, toks:, cols]], axis=0)
        return tok, jnp.where(diagonal, jnp.concatenate([mem] * 4, axis=0), BF16(0))

    def only_same_document(s, i):
        mine = jnp.concatenate([qdoc[i]] * (seg_len // 128), axis=1)
        same = jnp.where(mine == kdoc[i], s[0:toks], MASKED_SCORE)
        return jnp.concatenate([same, s[toks:]], axis=0)

    def memory_scores(q4, mem_k):
        return jnp.where(mem_valid, dot(q4, mem_k, 1, 1), ABSENT_SCORE)

    def attend(i):
        st = jnp.zeros((rows, 128), F32)
        for j in range(quads):
            cols = slice(j * quad, (j + 1) * quad)
            q4 = q[i, :, cols]
            tok_k, mem_k = token_and_memory(i, j * quad)
            s = head_rows(dot(stacked(q4), tok_k, 1, 1))
            sm = memory_scores(q4, mem_k)
            peaks, totals, probs = [], [], []
            for h in range(4):
                sh = only_same_document(s[h], i)
                own_mem = jnp.where(mem_lanes == h, sm, ABSENT_SCORE)
                peak = jnp.maximum(
                    jnp.max(sh, axis=1, keepdims=True), jnp.max(own_mem, axis=1, keepdims=True)
                )
                p = jnp.exp(sh - peak)
                peaks.append(peak)
                totals.append(jnp.sum(p, axis=1, keepdims=True))
                probs.append(p.astype(BF16))
            pm = jnp.exp(sm - spread(peaks, mem_lanes))
            for h in range(4):
                totals[h] += jnp.sum(jnp.where(mem_lanes == h, pm, 0.0), axis=1, keepdims=True)
                lse = peaks[h] + jnp.log(totals[h])
                st = jnp.where(stat_lane == 4 * j + h, lse, st)
            tok_v, mem_v = token_and_memory(i, width + j * quad)
            o = spread(head_rows(dot(jnp.concatenate(probs, axis=0), tok_v)), head_lanes)
            o = o + dot(pm.astype(BF16), mem_v)
            inverse = spread([1.0 / total for total in totals], head_lanes)
            ctx[i, :, cols] = (o * inverse).astype(BF16)
        stats[i] = st

    def forward_tick(t, carry):
        i = t - x

        @pl.when((i >= 0) & (i < items))
        def _():
            @pl.when(x == 0)
            def _():
                for which, rows_ref in enumerate((x0, xo)):
                    token_copy(which, i).wait()

                    @pl.when(i < n)
                    def _():
                        rows_ref[i, toks:rows, :] = jnp.zeros((MEM_PAD, width), BF16)

                    @pl.when(i >= n)
                    def _():
                        mem_copy(which, i - n).wait_recv()
                        rows_ref[i, toks:rows, :] = jnp.where(
                            keep[i][:, 0:1] > 0.0, memin[which, i - n], jnp.zeros((), BF16)
                        )

            @pl.when(x == 1)
            def _():
                for p in range(2):
                    x_copy(p, i).wait_recv()
                    pass_copy(p, i).start()

            @pl.when(i == 0)
            def _():
                wait_first_of(0, (0,))

            kv[i, c] = dot(x0[i], wf[0, :, width:wide]).astype(BF16)

            @pl.when(i == 0)
            def _():
                wait_first_of(0, (1,))

            q[i] = dot(x0[i], wf[0, :, 0:width]).astype(BF16) * BF16(scale)

            @pl.when(x == 1)
            def _():
                for p in range(2):
                    pass_copy(p, i).wait_recv()

            kv[i, 1 - c] = dot(xo[i], wf[0, :, width:wide]).astype(BF16)
            attend(i)
            route(S_X0, i)
            route(S_CTX, i)

            @pl.when(i == 0)
            def _():
                wait_first_of(0, (2,))
                weight_remote(4).wait_recv()

            normed, inv = normalize(dot(ctx[i], wf[0, :, wide:]) + x0[i].astype(F32))
            natt[i] = normed.astype(BF16)
            stats[i] = jnp.where(stat_lane == heads, inv, stats[i])
            yatt[i] = (normed * nrm[0, 0:1, :] + nrm[0, 1:2, :]).astype(BF16)

            @pl.when(i == 0)
            def _():
                wait_first_of(1, (0, 1, 2))

            @pl.when(i > 0)
            def _():
                route_sent(S_GLO, i - 1)
                route_sent(S_GHI, i - 1)
                gp_copy(i - 1).wait()

            for part in range(2):
                cols = slice(part * hidden_half, (part + 1) * hidden_half)
                u = dot(yatt[i], wf[1, :, cols])
                cdf = 0.5 + 0.5 * lax.erf(u * 0.7071067811865476)
                pdf = 0.3989422804014327 * jnp.exp(-0.5 * u * u)
                g[:, cols] = (u * cdf).astype(BF16)
                gpb[:, cols] = (cdf + u * pdf).astype(BF16)
            gp_copy(i).start()
            route(OUT_ATT, i)
            route(S_Y1, i)
            route(S_Y2, i)
            route(S_GLO, i)
            route(S_GHI, i)

            @pl.when(i == 0)
            def _():
                wait_first_of(0, (3,))
                wait_first_of(1, (3,))

            normed, inv = normalize(
                dot(g[:, 0:hidden_half], wd[0])
                + dot(g[:, hidden_half:], wd[1])
                + yatt[i].astype(F32)
            )
            yd[i] = (normed * nrm[1, 0:1, :] + nrm[1, 1:2, :]).astype(BF16)

            @pl.when(x == 0)
            def _():
                for p in range(2):
                    x_copy(p, i).start()

            @pl.when((x == 1) & (i < items - n))
            def _():
                for which in range(2):
                    mem_copy(which, i).start()

            nff[i] = normed.astype(BF16)
            stats[i] = jnp.where(stat_lane == heads + 1, inv, stats[i])
            route(OUT_FF, i)

        return carry

    lax.fori_loop(0, items + 1, forward_tick, 0)

    def forward_drain(i, carry):
        route_sent(OUT_FF, i)

        @pl.when(x == 0)
        def _():
            for p in range(2):
                x_copy(p, i).wait_send()

        @pl.when(x == 1)
        def _():
            for p in range(2):
                pass_copy(p, i).wait_send()

        @pl.when((x == 1) & (i < items - n))
        def _():
            for which in range(2):
                mem_copy(which, i).wait_send()

        return carry

    lax.fori_loop(0, items, forward_drain, 0)
    route_sent(S_GLO, items - 1)
    route_sent(S_GHI, items - 1)
    gp_copy(items - 1).wait()
    acc[...] = jnp.zeros_like(acc)

    def norm_back(s, i, normed_ref):
        grad = gy[i].astype(F32)
        normed = normed_ref[i].astype(F32)
        inv = stats[i][:, heads + s : heads + s + 1]
        acc[s, 0:1, :] += jnp.sum(grad * normed, axis=0, keepdims=True)
        acc[s, 1:2, :] += jnp.sum(grad, axis=0, keepdims=True)
        scaled = grad * nrm[s, 0:1, :]
        row_term = jnp.mean(scaled, axis=1, keepdims=True)
        row_cross = jnp.mean(scaled * normed, axis=1, keepdims=True)
        dh = inv * (scaled - row_term - normed * row_cross)
        dhb[...] = dh
        normed_ref[i] = dh.astype(BF16)

    def attend_back(i, slot):
        for j in range(quads):
            cols = slice(j * quad, (j + 1) * quad)
            q4 = q[i, :, cols]
            c4 = dctx[:, cols]
            tok_k, mem_k = token_and_memory(i, j * quad)
            tok_v, mem_v = token_and_memory(i, width + j * quad)
            products = c4.astype(F32) * ctx[i, :, cols].astype(F32)
            qs, cs = stacked(q4), stacked(c4)
            s = head_rows(dot(qs, tok_k, 1, 1))
            dp = head_rows(dot(cs, tok_v, 1, 1))
            sm = memory_scores(q4, mem_k)
            dpm = dot(c4, mem_v, 1, 1)
            lse = [stats[i][:, 4 * j + h : 4 * j + h + 1] for h in range(4)]
            inner = [
                jnp.sum(jnp.where(head_lanes == h, products, 0.0), axis=1, keepdims=True)
                for h in range(4)
            ]
            probs, dscores = [], []
            for h in range(4):
                p = jnp.exp(only_same_document(s[h], i) - lse[h])
                probs.append(p.astype(BF16))
                dscores.append((p * (dp[h] - inner[h])).astype(BF16))
            pm = jnp.exp(sm - spread(lse, mem_lanes))
            dsm = (pm * (dpm - spread(inner, mem_lanes))).astype(BF16)
            probs = jnp.concatenate(probs, axis=0)
            dscores = jnp.concatenate(dscores, axis=0)
            dv = dot(probs, cs, 0, 0)
            dk = dot(dscores, qs, 0, 0)
            dq = spread(head_rows(dot(dscores, tok_k)), head_lanes) + dot(dsm, mem_k)
            q[i, :, cols] = (dq * scale).astype(BF16)
            dvm = jnp.where(diagonal, dot(pm.astype(BF16), c4, 0, 0), 0.0)
            dkm = jnp.where(diagonal, dot(dsm, q4, 0, 0), 0.0)
            dvm = sum(dvm[h * mem_keys : (h + 1) * mem_keys] for h in range(4))
            dkm = sum(dkm[h * mem_keys : (h + 1) * mem_keys] for h in range(4))
            for half, (tok_part, mem_part) in enumerate(((dk, dkm), (dv, dvm))):
                cols = slice(half * quad, (half + 1) * quad)
                for core in range(2):
                    dkvs[core, j, 0:toks, cols] = tok_part[
                        core * toks : (core + 1) * toks
                    ].astype(BF16)
                    dkvs[core, j, toks:rows, cols] = mem_part[
                        core * MEM_PAD : (core + 1) * MEM_PAD
                    ].astype(BF16)
            dkv_copy(j, i, slot).start()

    def gather_dkv(j, i, slot):
        dkv_copy(j, i, slot).wait_recv()
        both = (dkvs[c, j].astype(F32) + dkvin[slot, j].astype(F32)).astype(BF16)
        kv[i, c, :, j * quad : (j + 1) * quad] = both[:, 0:quad]
        kv[i, c, :, width + j * quad : width + (j + 1) * quad] = both[:, quad:]

    def dkv_back(i, low, high):
        return dot(kv[i, c, :, low:high], wf[0, :, width + low : width + high], 1, 1) + dot(
            kv[i, c, :, width + low : width + high],
            wf[0, :, 2 * width + low : 2 * width + high], 1, 1,
        )

    def backward_tick(t, carry):
        r = t - (1 - x)

        @pl.when((r >= 0) & (r < items))
        def _():
            i = (nseg - 1 - lax.div(r, n)) * n + lax.rem(r, n)
            slot = lax.rem(r, 2)

            @pl.when(x == 1)
            def _():
                cot_copy(i).wait()

                @pl.when(i >= items - n)
                def _():
                    gy[i, toks:rows, :] = jnp.zeros((MEM_PAD, width), BF16)

                @pl.when(i < items - n)
                def _():
                    mg_copy(i + n).wait_recv()
                    gy[i, toks:rows, :] = jnp.where(
                        keep[i + n][:, 0:1] > 0.0, mgin[i + n], jnp.zeros((), BF16)
                    )

            @pl.when(x == 0)
            def _():
                gy_copy(i).wait_recv()

            norm_back(1, i, nff)
            for part in range(2):
                cols = slice(part * hidden_half, (part + 1) * hidden_half)
                dg = dot(nff[i], wd[part], 1, 1)
                gp[i, :, cols] = (dg * gp[i, :, cols].astype(F32)).astype(BF16)
            gy[i] = (dot(gp[i], wf[1], 1, 1) + dhb[...]).astype(BF16)
            norm_back(0, i, natt)
            dctx[...] = dot(natt[i], wf[0, :, wide:], 1, 1).astype(BF16)
            route(S_DFF0, i)
            route(S_DFF1, i)
            route(S_DU, i)
            route(GIN_FF, i)
            route(S_DATT, i)
            attend_back(i, slot)
            for j in range(quads - 1):
                gather_dkv(j, i, slot)
            early = (quads - 1) * quad
            partial_sum = dot(q[i], wf[0, :, 0:width], 1, 1) + dhb[...]
            if early:
                partial_sum = partial_sum + dkv_back(i, 0, early)
            dhb[...] = partial_sum
            gather_dkv(quads - 1, i, slot)
            yd[i] = (dkv_back(i, early, width) + dhb[...]).astype(BF16)

            @pl.when(x == 1)
            def _():
                gy_copy(i).start()

            @pl.when((x == 0) & (i >= n))
            def _():
                mg_copy(i).start()

            route(S_DQ, i)
            route(S_DKV, i)
            route(GIN_ATT, i)
            for j in range(quads):
                dkv_copy(j, i, slot).wait_send()

        return carry

    lax.fori_loop(0, items + 1, backward_tick, 0)

    acc_copy = remote(acc.at[1 - c], accp, as_sem, ar_sem, core_peer)
    acc_copy.start()

    def backward_drain(i, carry):
        @pl.when(x == 1)
        def _():
            gy_copy(i).wait_send()

        @pl.when((x == 0) & (i >= n))
        def _():
            mg_copy(i).wait_send()

        for kind in range(KINDS):
            if kind not in (OUT_FF, S_GLO, S_GHI):
                route_sent(kind, i)
            route_received(kind, i)
        return carry

    lax.fori_loop(0, items, backward_drain, 0)
    for k in range(5):
        weight_remote(k).wait_send()
    acc_copy.wait()
    norm_grad[...] = acc[c] + accp[...]


def run_layers(n, nseg, heads, tokens, cotangent, first, down, docs, resets, gain, shift):
    length, width = tokens.shape[1:]
    toks = length // nseg // 2
    rows = toks + MEM_PAD
    items = n * nseg
    hidden_half = down.shape[1]
    quads = heads // 4
    quad = width // quads
    any_spec = pl.BlockSpec(memory_space=pl.ANY)
    vmem_spec = pl.BlockSpec(memory_space=pltpu.VMEM)
    dma = pltpu.SemaphoreType.DMA
    item_rows = pltpu.VMEM((items, rows, width), BF16)
    one, two = dma((items,)), dma((2, items))
    return pl.pallas_call(
        partial(layers_kernel, n, nseg, heads),
        out_shape=(
            jax.ShapeDtypeStruct((n, length, width), BF16),
            jax.ShapeDtypeStruct((n, length, width), BF16),
            jax.ShapeDtypeStruct((2 * items, rows, width), BF16),
            jax.ShapeDtypeStruct((2 * items, rows, width), BF16),
            jax.ShapeDtypeStruct((2 * items, rows, 4 * width), BF16),
            jax.ShapeDtypeStruct((2 * items, rows, hidden_half), BF16),
            jax.ShapeDtypeStruct((2 * items, rows, width), BF16),
            jax.ShapeDtypeStruct((2, width), F32),
        ),
        in_specs=[any_spec] * 4 + [vmem_spec] * 4,
        out_specs=[any_spec] * 7 + [vmem_spec],
        scratch_shapes=[
            pltpu.VMEM((2, width, 4 * width), BF16),
            pltpu.VMEM((2, hidden_half, width), BF16),
            pltpu.VMEM((2, 2, width), F32),
            item_rows,
            item_rows,
            item_rows,
            pltpu.VMEM((items, 2, rows, 2 * width), BF16),
            item_rows,
            item_rows,
            item_rows,
            item_rows,
            item_rows,
            item_rows,
            pltpu.VMEM((rows, 2 * hidden_half), BF16),
            pltpu.VMEM((rows, 2 * hidden_half), BF16),
            pltpu.VMEM((items, rows, 2 * hidden_half), BF16),
            pltpu.VMEM((items, rows, 128), F32),
            pltpu.VMEM((items, toks, 128), F32),
            pltpu.VMEM((items, 1, 2 * toks), F32),
            pltpu.VMEM((items, MEM_PAD, 128), F32),
            pltpu.VMEM((2, items, MEM_PAD, width), BF16),
            pltpu.VMEM((items, MEM_PAD, width), BF16),
            pltpu.VMEM((2, quads, rows, 2 * quad), BF16),
            pltpu.VMEM((2, quads, rows, 2 * quad), BF16),
            pltpu.VMEM((rows, width), F32),
            pltpu.VMEM((rows, width), BF16),
            pltpu.VMEM((2, 2, width), F32),
            pltpu.VMEM((2, width), F32),
            dma((4,)), dma((5,)), dma((5,)),
            two, one, one,
            two, two,
            two, two,
            two, two,
            one, one, one, one,
            dma((quads, items)), dma((quads, items)),
            dma(()), dma(()),
        ]
        + [dma((KINDS, items))] * 3,
        compiler_params=pltpu.CompilerParams(
            collective_id=0, has_side_effects=True, vmem_limit_bytes=61 * 1024 * 1024
        ),
    )(tokens, cotangent, first, down, docs, resets, gain, shift)


def reduce_kernel(
    chunks,
    sx1, sx2, sr, sg, sd, norm_part,
    first_out, down_out, norm_out,
    x1, x2, rr, gg, dd, work, done, got_u, got_uz, got_vz, got_vy, stage, norms,
    right_sem, left_sem, out_sem, u_s, u_r, uz_s, uz_r, vz_s, vz_r, vy_s, vy_r, vg_s, vg_r,
    uzg_s, uzg_r, vzg_s, vzg_r, ug_s, ug_r, n_s, n_r,
):
    lines = 4
    d = lax.axis_index("dp")
    y = lax.rem(d, 2)
    z = lax.div(d, 2)
    dp = lax.axis_size("dp")
    width = sd.shape[1]
    half = width // 2
    part = width // chunks
    hr = part // 2
    lane_group = 128
    per_group = lane_group // part
    y_peer = {"dp": z * 2 + (1 - y)}

    def remote(src, dst, send, recv, peer):
        return pltpu.make_async_remote_copy(
            src_ref=src, dst_ref=dst, send_sem=send, recv_sem=recv,
            device_id=peer, device_id_type=MESH,
        )

    def other(step):
        return {"dp": lax.rem(d + step, dp)}

    barrier = pltpu.get_barrier_semaphore()
    for step in range(1, dp):
        pl.semaphore_signal(barrier, inc=1, device_id=other(step), device_id_type=MESH)

    lane_groups = width // lane_group
    right_loads = [(sd, dd)] + [
        (sr.at[:, b * width : (b + 1) * width], rr.at[:, b * width : (b + 1) * width])
        for b in range(4)
    ]

    def right_load(k):
        src, dst = right_loads[k]
        return pltpu.make_async_copy(src, dst, right_sem.at[k])

    def left_load(which, group):
        src, dst, low = ((sg, gg, 0), (sg, gg, width), (sx2, x2, 0), (sx1, x1, 0))[which]
        cols = pl.ds(pl.multiple_of(low + group * lane_group, lane_group), lane_group)
        return pltpu.make_async_copy(src.at[:, cols], dst.at[:, cols], left_sem.at[which, group])

    right_load(0).start()
    left_load(0, 0).start()
    left_load(1, 0).start()
    left_load(2, 0).start()
    right_load(4).start()
    left_load(3, 0).start()
    for k in range(1, 4):
        right_load(k).start()
    for group in range(1, lane_groups):
        for which in range(4):
            left_load(which, group).start()

    norms[d] = norm_part[...]
    pl.semaphore_wait(barrier, dp - 1)

    def norm_copy(step):
        return remote(norms.at[d], norms.at[d], n_s.at[step - 1], n_r.at[step - 1], other(step))

    def norm_arrival(step):
        source = lax.rem(d + dp - step, dp)
        return remote(
            norms.at[source], norms.at[source], n_s.at[step - 1], n_r.at[step - 1], other(step)
        )

    for step in range(1, dp):
        norm_copy(step).start()

    def column_half(h):
        return pl.ds(pl.multiple_of(h * half, 128), half)

    mine, theirs = column_half(y), column_half(1 - y)

    def place(flow):
        return z if flow == 0 else lines - 1 - z

    def onward(flow):
        step = -1 if flow == 0 else 1
        return {"dp": (z + step) * 2 + y}

    def back(flow):
        step = 1 if flow == 0 else -1
        return {"dp": (z + step) * 2 + y}

    def rows_of(flow):
        return slice(flow * hr, (flow + 1) * hr)

    def u_copy(k):
        return remote(
            work.at[k, 0:3, :, theirs], got_u.at[k], u_s.at[k], u_r.at[k], y_peer
        )

    def uz_copy(flow, k):
        return remote(
            work.at[k, 0:3, rows_of(flow), mine], got_uz.at[flow, k],
            uz_s.at[flow, k], uz_r.at[flow, k], onward(flow),
        )

    def vz_copy(flow, k):
        return remote(
            work.at[k, 3:6, rows_of(flow), :], got_vz.at[flow, k],
            vz_s.at[flow, k], vz_r.at[flow, k], onward(flow),
        )

    def vy_copy(flow, k):
        return remote(
            work.at[k, 3:6, rows_of(flow), theirs], got_vy.at[k], vy_s.at[k], vy_r.at[k], y_peer
        )

    def vg_copy(flow, k, cols):
        spot = done.at[k, 3:6, rows_of(flow), cols]
        return remote(spot, spot, vg_s.at[k], vg_r.at[k], y_peer)

    def uzg_copy(flow, k):
        spot = done.at[k, 0:3, rows_of(flow), mine]
        return remote(spot, spot, uzg_s.at[flow, k], uzg_r.at[flow, k], back(flow))

    def vzg_copy(flow, k):
        spot = done.at[k, 3:6, rows_of(flow), :]
        return remote(spot, spot, vzg_s.at[flow, k], vzg_r.at[flow, k], back(flow))

    def ug_copy(flow, k, cols):
        spot = done.at[k, 0:3, rows_of(flow), cols]
        return remote(spot, spot, ug_s.at[flow, k], ug_r.at[flow, k], y_peer)

    def out_copies(k, slot):
        rows = pl.ds(pl.multiple_of(k * part, part), part)
        copies = []
        for b in range(6):
            if b < 4:
                dst = first_out.at[rows, b * width : (b + 1) * width]
            else:
                low = pl.ds(pl.multiple_of((b - 4) * width + k * part, part), part)
                dst = down_out.at[low, :]
            copies.append(
                pltpu.make_async_copy(stage.at[slot, b], dst, out_sem.at[slot, b])
            )
        return copies

    def plus(a, b):
        return (a.astype(F32) + b.astype(F32)).astype(BF16)

    def ready(k, low=0):
        return (k >= low) & (k < chunks)

    def store_chunks(group, block, value):
        for e in range(per_group):
            work[group * per_group + e, block] = value[e * part : (e + 1) * part]

    def round_step(r, carry):
        group = lax.div(r, per_group)

        @pl.when((lax.rem(r, per_group) == 0) & (r < chunks))
        def _():
            cols = pl.ds(pl.multiple_of(group * lane_group, lane_group), lane_group)
            gcols = pl.ds(pl.multiple_of(width + group * lane_group, lane_group), lane_group)

            @pl.when(r == 0)
            def _():
                right_load(0).wait()

            left_load(0, group).wait()
            store_chunks(group, 4, dot(gg[:, cols], dd[...], 0, 0).astype(BF16))
            left_load(1, group).wait()
            store_chunks(group, 5, dot(gg[:, gcols], dd[...], 0, 0).astype(BF16))
            left_load(2, group).wait()

            @pl.when(r == 0)
            def _():
                right_load(4).wait()

            store_chunks(group, 3, dot(x2[:, cols], rr[:, 3 * width :], 0, 0).astype(BF16))

        for flow in range(2):
            p = place(flow)
            k = r - (lines - 1 - p)
            rows = rows_of(flow)

            @pl.when(ready(k))
            def _():
                @pl.when(p < lines - 1)
                def _():
                    vz_copy(flow, k).wait_recv()
                    work[k, 3:6, rows, :] = plus(work[k, 3:6, rows, :], got_vz[flow, k])

                @pl.when(p > 0)
                def _():
                    vz_copy(flow, k).start()

                @pl.when(p == 0)
                def _():
                    vy_copy(flow, k).start()

        @pl.when((lax.rem(r, per_group) == 0) & (r < chunks))
        def _():
            cols = pl.ds(pl.multiple_of(group * lane_group, lane_group), lane_group)

            left_load(3, group).wait()
            for b in range(3):

                @pl.when(r == 0)
                def _():
                    right_load(1 + b).wait()

                store_chunks(
                    group, b,
                    dot(x1[:, cols], rr[:, b * width : (b + 1) * width], 0, 0).astype(BF16),
                )

        @pl.when(ready(r))
        def _():
            u_copy(r).start()

        @pl.when(ready(r - 1))
        def _():
            k = r - 1
            u_copy(k).wait_recv()
            work[k, 0:3, :, mine] = plus(work[k, 0:3, :, mine], got_u[k])

        for flow in range(2):
            p = place(flow)
            k = r - 1 - (lines - 1 - p)
            rows = rows_of(flow)

            @pl.when(ready(k))
            def _():
                @pl.when(p < lines - 1)
                def _():
                    uz_copy(flow, k).wait_recv()
                    total = plus(work[k, 0:3, rows, mine], got_uz[flow, k])

                    @pl.when(p > 0)
                    def _():
                        work[k, 0:3, rows, mine] = total

                    @pl.when(p == 0)
                    def _():
                        done[k, 0:3, rows, mine] = total

                @pl.when(p > 0)
                def _():
                    uz_copy(flow, k).start()

                @pl.when(p == 0)
                def _():
                    uzg_copy(flow, k).start()
                    ug_copy(flow, k, mine).start()

        for flow in range(2):
            p = place(flow)
            rows = rows_of(flow)

            @pl.when((p == 0) & ready(r - lines))
            def _():
                k = r - lines
                vy_copy(flow, k).wait_recv()
                done[k, 3:6, rows, mine] = plus(work[k, 3:6, rows, mine], got_vy[k])
                vg_copy(flow, k, mine).start()

            @pl.when((p == 0) & ready(r - lines - 1))
            def _():
                k = r - lines - 1
                vg_copy(flow, k, theirs).wait_recv()
                vzg_copy(flow, k).start()

        for flow in range(2):
            p = place(flow)
            k = r - lines - p

            @pl.when((p > 0) & ready(k))
            def _():
                uzg_copy(flow, k).wait_recv()

                @pl.when(p < lines - 1)
                def _():
                    uzg_copy(flow, k).start()

                ug_copy(flow, k, mine).start()

        for flow in range(2):
            p = place(flow)
            k = r - lines - 1 - p

            @pl.when((p > 0) & ready(k))
            def _():
                vzg_copy(flow, k).wait_recv()

                @pl.when(p < lines - 1)
                def _():
                    vzg_copy(flow, k).start()

            @pl.when(ready(k))
            def _():
                ug_copy(flow, k, theirs).wait_recv()

        k = r - 2 * lines

        @pl.when(ready(k))
        def _():
            slot = lax.rem(k, 2)

            @pl.when(k >= 2)
            def _():
                for copy in out_copies(k - 2, slot):
                    copy.wait()

            stage[slot] = done[k].astype(F32)
            for copy in out_copies(k, slot):
                copy.start()

        return carry

    lax.fori_loop(0, chunks + 2 * lines, round_step, 0)

    for step in range(1, dp):
        norm_arrival(step).wait_recv()
    total = norms[0]
    for e in range(1, dp):
        total = total + norms[e]
    norm_out[...] = total

    def drain(k, carry):
        u_copy(k).wait_send()
        for flow in range(2):
            p = place(flow)
            ug_copy(flow, k, mine).wait_send()

            @pl.when(p > 0)
            def _():
                vz_copy(flow, k).wait_send()
                uz_copy(flow, k).wait_send()

            @pl.when(p < lines - 1)
            def _():
                uzg_copy(flow, k).wait_send()
                vzg_copy(flow, k).wait_send()

            @pl.when(p == 0)
            def _():
                vy_copy(flow, k).wait_send()
                vg_copy(flow, k, mine).wait_send()

        return carry

    lax.fori_loop(0, chunks, drain, 0)
    for k in (chunks - 2, chunks - 1):
        for copy in out_copies(k, k % 2):
            copy.wait()
    for step in range(1, dp):
        norm_copy(step).wait_send()


def sum_weights(dp, sx1, sx2, sr, sg, sd, norm_part):
    total, width = sx1.shape
    chunks = 12
    part = width // chunks
    half = width // 2
    any_spec = pl.BlockSpec(memory_space=pl.ANY)
    vmem_spec = pl.BlockSpec(memory_space=pltpu.VMEM)
    dma = pltpu.SemaphoreType.DMA
    one, two = dma((chunks,)), dma((2, chunks))
    return pl.pallas_call(
        partial(reduce_kernel, chunks),
        out_shape=(
            jax.ShapeDtypeStruct((width, 4 * width), F32),
            jax.ShapeDtypeStruct((2 * width, width), F32),
            jax.ShapeDtypeStruct((2, width), F32),
        ),
        in_specs=[any_spec] * 5 + [vmem_spec],
        out_specs=[any_spec] * 2 + [vmem_spec],
        scratch_shapes=[
            pltpu.VMEM((total, width), BF16),
            pltpu.VMEM((total, width), BF16),
            pltpu.VMEM((total, 4 * width), BF16),
            pltpu.VMEM((total, 2 * width), BF16),
            pltpu.VMEM((total, width), BF16),
            pltpu.VMEM((chunks, 6, part, width), BF16),
            pltpu.VMEM((chunks, 6, part, width), BF16),
            pltpu.VMEM((chunks, 3, part, half), BF16),
            pltpu.VMEM((2, chunks, 3, part // 2, half), BF16),
            pltpu.VMEM((2, chunks, 3, part // 2, width), BF16),
            pltpu.VMEM((chunks, 3, part // 2, half), BF16),
            pltpu.VMEM((2, 6, part, width), F32),
            pltpu.VMEM((dp, 2, width), F32),
            dma((5,)),
            dma((4, width // 128)),
            dma((2, 6)),
            one, one,
            two, two,
            two, two,
            one, one,
            one, one,
            two, two,
            two, two,
            two, two,
            dma((dp - 1,)), dma((dp - 1,)),
        ],
        compiler_params=pltpu.CompilerParams(
            collective_id=1, has_side_effects=True, vmem_limit_bytes=60 * 1024 * 1024
        ),
    )(sx1, sx2, sr, sg, sd, norm_part)


def shards(
    tokens, doc_ids, reset_flags, first_weights, down_halves, norm_gain, norm_bias, cotangent
):
    n, length, width = tokens.shape
    items = n * NSEG
    rows = length // NSEG // 2 + MEM_PAD
    out, gin, sx1, sx2, sr, sg, sd, norm_grad = run_layers(
        n, NSEG, H, tokens, cotangent, first_weights, down_halves,
        doc_ids, reset_flags, norm_gain, norm_bias,
    )
    total = 2 * items * rows
    sx1, sx2, sd = (a.reshape(total, width) for a in (sx1, sx2, sd))
    sr = sr.reshape(total, 4 * width)
    sg = sg.reshape(total, -1)

    dp = lax.axis_size("dp")
    if dp == 8:
        first_grad, down_grad, norm_grad = sum_weights(dp, sx1, sx2, sr, sg, sd, norm_grad)
    else:

        def weight_grad(left, right):
            return jnp.einsum("rd,re->de", left, right, preferred_element_type=F32).astype(BF16)

        first_grad = jnp.concatenate(
            [weight_grad(sx1, sr[:, : 3 * width]), weight_grad(sx2, sr[:, 3 * width :])], axis=1
        )
        down_grad = weight_grad(sg, sd)
        first_grad, down_grad = lax.psum((first_grad, down_grad), "dp")
        norm_grad = lax.psum(norm_grad, "dp")
    return (
        out[None],
        gin[None],
        first_grad.astype(F32)[None],
        down_grad.astype(F32)[None],
        norm_grad[0:1],
        norm_grad[1:2],
    )


def solution(mesh):
    in_specs = (
        P("dp", None, None),
        P("dp", None),
        P("dp", None),
        P("section", None, None),
        P("section", None, None),
        P("section", None),
        P("section", None),
        P("dp", None, None),
    )
    out_specs = (
        P("section", "dp", None, None),
        P("section", "dp", None, None),
        P("section", None, None),
        P("section", None, None),
        P("section", None),
        P("section", None),
    )
    return jax.shard_map(shards, mesh=mesh, in_specs=in_specs, out_specs=out_specs, check_vma=False)
```

```python
from functools import partial

import jax
import jax.numpy as jnp
from jax import lax
from jax.experimental import pallas as pl
from jax.experimental.pallas import tpu as pltpu
from jax.sharding import PartitionSpec as P

H = 12
M = 20
NSEG = 2
MEM_PAD = 16
NORM_EPSILON = 1e-05
MASKED_SCORE = -1000000000.0
ABSENT_SCORE = -3e38
MESH = pl.DeviceIdType.MESH
BF16 = jnp.bfloat16
F32 = jnp.float32

OUT_ATT, OUT_FF, GIN_ATT, GIN_FF = 0, 1, 2, 3
S_X0, S_CTX, S_DQ, S_DKV, S_DATT, S_GLO, S_DFF0 = 4, 5, 6, 7, 8, 9, 10
S_Y1, S_Y2, S_DU, S_GHI, S_DFF1 = 11, 12, 13, 14, 15
KINDS = 16


def dot(a, b, lhs_dim=1, rhs_dim=0):
    return lax.dot_general(
        a, b, (((lhs_dim,), (rhs_dim,)), ((), ())), preferred_element_type=F32
    )


def normalize(summed):
    mean = jnp.mean(summed, axis=-1, keepdims=True)
    centered = summed - mean
    var = jnp.mean(centered * centered, axis=-1, keepdims=True)
    inv = lax.rsqrt(var + NORM_EPSILON)
    return centered * inv, inv


def group_of(shape, dim, size):
    index = lax.broadcasted_iota(jnp.int32, shape, dim)
    return lax.shift_right_logical(index, size.bit_length() - 1)


def spread(values, groups):
    result = values[-1]
    for h in range(len(values) - 1):
        result = jnp.where(groups == h, values[h], result)
    return result


def layers_kernel(
    n, nseg, heads,
    tokens, cotangent, first, down, docs, resets, gain, shift,
    out, gin, sx1, sx2, sr, sg, sd, norm_grad, ptok, pmem,
    wf, wd, nrm, x0, xo, q, kv, ctx, natt, yatt, nff, yd, gy, g, gpb, gp, stats, qdoc, kdoc, keep,
    memin, mgin, dkvs, dkvin, dhb, dctx, ctxb, dqb, gab, acc, accp, tprob, mprob,
    wl, ws, wr, tok_sem, cot_sem, gp_sem, pw_sem, pr_sem, fs_sem, fr_sem, xs_sem, xr_sem,
    ms_sem, mr_sem, gs_sem, gr_sem, hs_sem, hr_sem, ds_sem, dr_sem, as_sem, ar_sem,
    lsem, ssem, rsem,
):
    items = n * nseg
    section = lax.axis_index("section")
    c = lax.rem(section, 2)
    x = lax.div(section, 2)
    core_peer = {"section": x * 2 + (1 - c)}
    chip_peer = {"section": (1 - x) * 2 + c}
    cross_peer = {"section": (1 - x) * 2 + (1 - c)}
    rows, width = x0.shape[1:]
    toks = rows - MEM_PAD
    seg_len = 2 * toks
    hidden_half = wd.shape[1]
    wide = 3 * width
    head_dim = width // heads
    quad = 4 * head_dim
    quads = heads // 4
    mem_keys = 2 * MEM_PAD
    scale = head_dim ** (-0.5)

    def remote(src, dst, send, recv, peer):
        return pltpu.make_async_remote_copy(
            src_ref=src, dst_ref=dst, send_sem=send, recv_sem=recv,
            device_id=peer, device_id_type=MESH,
        )

    barrier = pltpu.get_barrier_semaphore()
    pl.semaphore_signal(barrier, inc=1, device_id=core_peer, device_id_type=MESH)
    pl.semaphore_signal(barrier, inc=1, device_id=chip_peer, device_id_type=MESH)
    pl.semaphore_signal(barrier, inc=1, device_id=cross_peer, device_id_type=MESH)

    def token_rows(ref, i, core=None):
        core = c if core is None else core
        return ref.at[lax.rem(i, n), pl.ds(lax.div(i, n) * seg_len + core * toks, toks), :]

    def token_copy(which, i):
        if which == 0:
            src, dst = token_rows(tokens, i), x0.at[i, 0:toks, :]
        else:
            src, dst = token_rows(tokens, i, 1 - c), xo.at[i, 0:toks, :]
        return pltpu.make_async_copy(src, dst, tok_sem.at[which, i])

    def cot_copy(i):
        return pltpu.make_async_copy(
            token_rows(cotangent, i), gy.at[i, 0:toks, :], cot_sem.at[i]
        )

    def weight_piece(k):
        if k == 0:
            return first.at[0, :, width:wide], wf.at[c, :, width:wide]
        if k == 1:
            return first.at[0, :, 0:width], wf.at[c, :, 0:width]
        if k == 2:
            return first.at[0, :, wide:], wf.at[c, :, wide:]
        return down.at[0], wd.at[c]

    def weight_local(k):
        src, dst = weight_piece(k)
        return pltpu.make_async_copy(src, dst, wl.at[k])

    def weight_remote(k):
        if k == 4:
            return remote(nrm.at[c], nrm.at[c], ws.at[4], wr.at[4], core_peer)
        src, dst = weight_piece(k)
        return remote(src, dst, ws.at[k], wr.at[k], core_peer)

    nrm[c, 0:1, :] = gain[...]
    nrm[c, 1:2, :] = shift[...]
    weight_local(0).start()

    @pl.when(x == 0)
    def _():
        token_copy(0, 0).start()
        token_copy(1, 0).start()

    pl.semaphore_wait(barrier, 3)
    for k in range(5):
        weight_remote(k).start()
    for k in range(1, 4):
        weight_local(k).start()
    for i in range(items):
        if i > 0:

            @pl.when(x == 0)
            def _():
                token_copy(0, i).start()
                token_copy(1, i).start()

        @pl.when(x == 1)
        def _():
            cot_copy(i).start()

    def wait_first_of(core, ks):
        @pl.when(c == core)
        def _():
            for k in ks:
                weight_local(k).wait()

        @pl.when(c != core)
        def _():
            for k in ks:
                weight_remote(k).wait_recv()

    for i in range(items):
        seq, seg = i % n, i // n
        kdoc[i] = docs[seq : seq + 1, seg * seg_len : (seg + 1) * seg_len].astype(F32)
        own = pl.ds(pl.multiple_of(seg * seg_len + c * toks, toks), toks)
        own_row = docs[seq : seq + 1, own].astype(F32)
        qdoc[i] = jnp.transpose(jnp.broadcast_to(own_row, (128, toks)))
        if seg > 0:
            flag = resets[seq : seq + 1, seg - 1 : seg].astype(F32)
            keep[i] = jnp.broadcast_to(1.0 - flag, (MEM_PAD, 128))

    def routed(kind, i):
        block = i * 2 + c
        sec = 0
        if kind == OUT_ATT:
            src, dst = yatt.at[i, 0:toks, :], token_rows(out, i)
        elif kind == OUT_FF:
            src, dst, sec = yd.at[i, 0:toks, :], token_rows(out, i), 1
        elif kind == GIN_ATT:
            src, dst = yd.at[i, 0:toks, :], token_rows(gin, i)
        elif kind == GIN_FF:
            src, dst, sec = gab.at[0:toks, :], token_rows(gin, i), 1
        elif kind == S_X0:
            src, dst = x0.at[i], sx1.at[block]
        elif kind == S_CTX:
            src, dst = ctx.at[i], sx2.at[block]
        elif kind == S_DQ:
            src, dst = dqb, sr.at[block, :, 0:width]
        elif kind == S_DKV:
            src, dst = kv.at[i, c], sr.at[block, :, width:wide]
        elif kind == S_DATT:
            src, dst = natt.at[i], sr.at[block, :, wide:]
        elif kind == S_GLO:
            src, dst = g.at[:, 0:hidden_half], sg.at[block]
        elif kind == S_DFF0:
            src, dst = nff.at[i], sd.at[block]
        elif kind == S_Y1:
            src, dst, sec = yatt.at[i], sx1.at[block], 1
        elif kind == S_Y2:
            src, dst, sec = yatt.at[i], sx2.at[block], 1
        elif kind == S_DU:
            src, dst, sec = gp.at[i], sr.at[block], 1
        elif kind == S_GHI:
            src, dst, sec = g.at[:, hidden_half:], sg.at[block], 1
        else:
            src, dst, sec = nff.at[i], sd.at[block], 1
        return src, dst, sec

    def route_local(kind, i):
        src, dst, _ = routed(kind, i)
        return pltpu.make_async_copy(src, dst, lsem.at[kind, i])

    def route_away(kind, i):
        src, dst, _ = routed(kind, i)
        return remote(src, dst, ssem.at[kind, i], rsem.at[kind, i], core_peer)

    def route(kind, i):
        sec = routed(kind, i)[2]

        @pl.when(c == sec)
        def _():
            route_local(kind, i).start()

        @pl.when(c != sec)
        def _():
            route_away(kind, i).start()

    def route_sent(kind, i):
        sec = routed(kind, i)[2]

        @pl.when(c == sec)
        def _():
            route_local(kind, i).wait()

        @pl.when(c != sec)
        def _():
            route_away(kind, i).wait_send()

    def route_received(kind, i):
        @pl.when(c == routed(kind, i)[2])
        def _():
            route_away(kind, i).wait_recv()

    def gp_copy(i):
        return pltpu.make_async_copy(gpb, gp.at[i], gp_sem.at[i])

    def prob_copies(i, back):
        pairs = ((tprob, ptok.at[i]), (mprob, pmem.at[i]))
        if back:
            return [
                pltpu.make_async_copy(dst, src, pr_sem.at[e, i])
                for e, (src, dst) in enumerate(pairs)
            ]
        return [
            pltpu.make_async_copy(src, dst, pw_sem.at[e, i]) for e, (src, dst) in enumerate(pairs)
        ]

    cut = rows // 32 * 16

    def piece(p):
        return slice(0, cut) if p == 0 else slice(cut, rows)

    def x_copy(p, i):
        return remote(
            yd.at[i, piece(p)], x0.at[i, piece(p)], xs_sem.at[p, i], xr_sem.at[p, i], chip_peer
        )

    def pass_copy(p, i):
        return remote(
            x0.at[i, piece(p)], xo.at[i, piece(p)], fs_sem.at[p, i], fr_sem.at[p, i], core_peer
        )

    def mem_copy(which, i):
        return remote(
            yd.at[i, toks:rows, :], memin.at[which, i], ms_sem.at[which, i],
            mr_sem.at[which, i], cross_peer if which else chip_peer,
        )

    def gy_copy(i):
        return remote(yd.at[i], gy.at[i], gs_sem.at[i], gr_sem.at[i], chip_peer)

    def mg_copy(i):
        return remote(
            yd.at[i, toks:rows, :], mgin.at[i], hs_sem.at[i], hr_sem.at[i], chip_peer
        )

    def dkv_copy(j, i, slot):
        return remote(
            dkvs.at[1 - c, j], dkvin.at[slot, j], ds_sem.at[j, i], dr_sem.at[j, i], core_peer
        )

    head_lanes = group_of((rows, quad), 1, head_dim)
    mem_lanes = group_of((rows, 4 * mem_keys), 1, mem_keys)
    key_lane = lax.broadcasted_iota(jnp.int32, (rows, 4 * mem_keys), 1)
    mem_valid = lax.rem(key_lane, MEM_PAD) < M // 2
    diagonal = group_of((4 * mem_keys, quad), 0, mem_keys) == group_of(
        (4 * mem_keys, quad), 1, head_dim
    )
    stat_lane = lax.broadcasted_iota(jnp.int32, (rows, 128), 1)

    def stacked(block):
        return jnp.concatenate(
            [jnp.where(head_lanes == h, block, BF16(0)) for h in range(4)], axis=0
        )

    def head_rows(block):
        return [block[h * rows : (h + 1) * rows] for h in range(4)]

    def token_and_memory(i, low):
        cols = slice(low, low + quad)
        tok = jnp.concatenate([kv[i, 0, 0:toks, cols], kv[i, 1, 0:toks, cols]], axis=0)
        mem = jnp.concatenate([kv[i, 0, toks:, cols], kv[i, 1, toks:, cols]], axis=0)
        return tok, jnp.where(diagonal, jnp.concatenate([mem] * 4, axis=0), BF16(0))

    def only_same_document(s, i):
        mine = jnp.concatenate([qdoc[i]] * (seg_len // 128), axis=1)
        same = jnp.where(mine == kdoc[i], s[0:toks], MASKED_SCORE)
        return jnp.concatenate([same, s[toks:]], axis=0)

    def memory_scores(q4, mem_k):
        return jnp.where(mem_valid, dot(q4, mem_k, 1, 1), ABSENT_SCORE)

    def attend(i):
        st = jnp.zeros((rows, 128), F32)
        for j in range(quads):
            cols = slice(j * quad, (j + 1) * quad)
            q4 = q[i, :, cols]
            tok_k, mem_k = token_and_memory(i, j * quad)
            s = head_rows(dot(stacked(q4), tok_k, 1, 1))
            sm = memory_scores(q4, mem_k)
            own = [mem_lanes == h for h in range(4)]
            s = [only_same_document(s[h], i) for h in range(4)]
            peaks = [
                jnp.max(
                    jnp.concatenate([s[h], jnp.where(own[h], sm, ABSENT_SCORE)], axis=1),
                    axis=1, keepdims=True,
                )
                for h in range(4)
            ]
            pm = jnp.exp(sm - spread(peaks, mem_lanes))
            mprob[j] = pm.astype(BF16)
            totals, probs = [], []
            for h in range(4):
                p = jnp.exp(s[h] - peaks[h])
                probs.append(p.astype(BF16))
                tprob[j, h * rows : (h + 1) * rows, :] = probs[h]
                both = jnp.concatenate([p, jnp.where(own[h], pm, 0.0)], axis=1)
                totals.append(1.0 / jnp.sum(both, axis=1, keepdims=True))
                st = jnp.where(stat_lane == 4 * j + h, totals[h], st)
            tok_v, mem_v = token_and_memory(i, width + j * quad)
            o = spread(head_rows(dot(jnp.concatenate(probs, axis=0), tok_v)), head_lanes)
            o = o + dot(pm.astype(BF16), mem_v)
            ctxb[:, cols] = (o * spread(totals, head_lanes)).astype(BF16)
        stats[i] = st
        ctx[i] = ctxb[...]

    def forward_tick(t, carry):
        i = t - x

        @pl.when((i >= 0) & (i < items))
        def _():
            @pl.when(x == 0)
            def _():
                for which, rows_ref in enumerate((x0, xo)):
                    token_copy(which, i).wait()

                    @pl.when(i < n)
                    def _():
                        rows_ref[i, toks:rows, :] = jnp.zeros((MEM_PAD, width), BF16)

                    @pl.when(i >= n)
                    def _():
                        mem_copy(which, i - n).wait_recv()
                        rows_ref[i, toks:rows, :] = jnp.where(
                            keep[i][:, 0:1] > 0.0, memin[which, i - n], jnp.zeros((), BF16)
                        )

            @pl.when(x == 1)
            def _():
                for p in range(2):
                    x_copy(p, i).wait_recv()
                    pass_copy(p, i).start()

            @pl.when(i == 0)
            def _():
                wait_first_of(0, (0,))

            kv[i, c] = dot(x0[i], wf[0, :, width:wide]).astype(BF16)

            @pl.when(i == 0)
            def _():
                wait_first_of(0, (1,))

            q[i] = dot(x0[i], wf[0, :, 0:width]).astype(BF16) * BF16(scale)

            @pl.when(x == 1)
            def _():
                for p in range(2):
                    pass_copy(p, i).wait_recv()

            kv[i, 1 - c] = dot(xo[i], wf[0, :, width:wide]).astype(BF16)
            @pl.when(i > 0)
            def _():
                for copy in prob_copies(i - 1, False):
                    copy.wait()

            attend(i)
            for copy in prob_copies(i, False):
                copy.start()
            route(S_X0, i)
            route(S_CTX, i)

            @pl.when(i == 0)
            def _():
                wait_first_of(0, (2,))
                weight_remote(4).wait_recv()

            normed, inv = normalize(dot(ctxb[...], wf[0, :, wide:]) + x0[i].astype(F32))
            natt[i] = normed.astype(BF16)
            stats[i] = jnp.where(stat_lane == heads, inv, stats[i])
            yatt[i] = (normed * nrm[0, 0:1, :] + nrm[0, 1:2, :]).astype(BF16)

            @pl.when(i == 0)
            def _():
                wait_first_of(1, (0, 1, 2))

            @pl.when(i > 0)
            def _():
                route_sent(S_GLO, i - 1)
                route_sent(S_GHI, i - 1)
                gp_copy(i - 1).wait()

            for part in range(2):
                cols = slice(part * hidden_half, (part + 1) * hidden_half)
                u = dot(yatt[i], wf[1, :, cols])
                cdf = 0.5 + 0.5 * lax.erf(u * 0.7071067811865476)
                pdf = 0.3989422804014327 * jnp.exp(-0.5 * u * u)
                g[:, cols] = (u * cdf).astype(BF16)
                gpb[:, cols] = (cdf + u * pdf).astype(BF16)
            gp_copy(i).start()
            route(OUT_ATT, i)
            route(S_Y1, i)
            route(S_Y2, i)
            route(S_GLO, i)
            route(S_GHI, i)

            @pl.when(i == 0)
            def _():
                wait_first_of(0, (3,))
                wait_first_of(1, (3,))

            normed, inv = normalize(
                dot(g[:, 0:hidden_half], wd[0])
                + dot(g[:, hidden_half:], wd[1])
                + yatt[i].astype(F32)
            )
            yd[i] = (normed * nrm[1, 0:1, :] + nrm[1, 1:2, :]).astype(BF16)

            @pl.when(x == 0)
            def _():
                for p in range(2):
                    x_copy(p, i).start()

            @pl.when((x == 1) & (i < items - n))
            def _():
                for which in range(2):
                    mem_copy(which, i).start()

            nff[i] = normed.astype(BF16)
            stats[i] = jnp.where(stat_lane == heads + 1, inv, stats[i])
            route(OUT_FF, i)

        return carry

    lax.fori_loop(0, items + 1, forward_tick, 0)

    def forward_sent(i):
        route_sent(OUT_FF, i)

        @pl.when(x == 0)
        def _():
            for p in range(2):
                x_copy(p, i).wait_send()

        @pl.when(x == 1)
        def _():
            for p in range(2):
                pass_copy(p, i).wait_send()

        @pl.when((x == 1) & (i < items - n))
        def _():
            for which in range(2):
                mem_copy(which, i).wait_send()

    for copy in prob_copies(items - 1, False):
        copy.wait()
    for copy in prob_copies(items - n, True):
        copy.start()
    gp_copy(items - 1).wait()
    acc[...] = jnp.zeros_like(acc)

    def norm_back(s, i, normed_ref):
        grad = (gy[i] if s else gab[...]).astype(F32)
        normed = normed_ref[i].astype(F32)
        inv = stats[i][:, heads + s : heads + s + 1]
        acc[s, 0:1, :] += jnp.sum(grad * normed, axis=0, keepdims=True)
        acc[s, 1:2, :] += jnp.sum(grad, axis=0, keepdims=True)
        scaled = grad * nrm[s, 0:1, :]
        row_term = jnp.mean(scaled, axis=1, keepdims=True)
        row_cross = jnp.mean(scaled * normed, axis=1, keepdims=True)
        dh = inv * (scaled - row_term - normed * row_cross)
        dhb[...] = dh
        normed_ref[i] = dh.astype(BF16)

    def attend_back(i, slot):
        for j in range(quads):
            cols = slice(j * quad, (j + 1) * quad)
            q4 = q[i, :, cols]
            c4 = dctx[:, cols]
            tok_k, mem_k = token_and_memory(i, j * quad)
            tok_v, mem_v = token_and_memory(i, width + j * quad)
            inverse = [stats[i][:, 4 * j + h : 4 * j + h + 1] for h in range(4)]
            c4 = (c4.astype(F32) * spread(inverse, head_lanes)).astype(BF16)
            products = c4.astype(F32) * ctx[i, :, cols].astype(F32)
            dp = head_rows(dot(stacked(c4), tok_v, 1, 1))
            dpm = dot(c4, mem_v, 1, 1)
            inner = [
                jnp.sum(jnp.where(head_lanes == h, products, 0.0), axis=1, keepdims=True)
                for h in range(4)
            ]
            dscores = [
                (tprob[j, h * rows : (h + 1) * rows, :].astype(F32) * (dp[h] - inner[h])).astype(BF16)
                for h in range(4)
            ]
            dsm = (mprob[j].astype(F32) * (dpm - spread(inner, mem_lanes))).astype(BF16)
            ct, qt = jnp.transpose(c4), jnp.transpose(q4)
            mine = [slice(h * head_dim, (h + 1) * head_dim) for h in range(4)]
            dv = [
                dot(ct[mine[h]], tprob[j, h * rows : (h + 1) * rows, :]).astype(BF16)
                for h in range(4)
            ]
            dk = [dot(qt[mine[h]], dscores[h]).astype(BF16) for h in range(4)]
            dv = jnp.transpose(jnp.concatenate(dv, axis=0))
            dk = jnp.transpose(jnp.concatenate(dk, axis=0))
            dscores = jnp.concatenate(dscores, axis=0)
            dq = spread(head_rows(dot(dscores, tok_k)), head_lanes) + dot(dsm, mem_k)
            dqb[:, cols] = (dq * scale).astype(BF16)
            dvm = jnp.where(diagonal, dot(mprob[j], c4, 0, 0), 0.0)
            dkm = jnp.where(diagonal, dot(dsm, q4, 0, 0), 0.0)
            dvm = sum(dvm[h * mem_keys : (h + 1) * mem_keys] for h in range(4))
            dkm = sum(dkm[h * mem_keys : (h + 1) * mem_keys] for h in range(4))
            for half, (tok_part, mem_part) in enumerate(((dk, dkm), (dv, dvm))):
                cols = slice(half * quad, (half + 1) * quad)
                for core in range(2):
                    dkvs[core, j, 0:toks, cols] = tok_part[
                        core * toks : (core + 1) * toks
                    ].astype(BF16)
                    dkvs[core, j, toks:rows, cols] = mem_part[
                        core * MEM_PAD : (core + 1) * MEM_PAD
                    ].astype(BF16)
            dkv_copy(j, i, slot).start()

    def gather_dkv(j, i, slot):
        dkv_copy(j, i, slot).wait_recv()
        both = (dkvs[c, j].astype(F32) + dkvin[slot, j].astype(F32)).astype(BF16)
        kv[i, c, :, j * quad : (j + 1) * quad] = both[:, 0:quad]
        kv[i, c, :, width + j * quad : width + (j + 1) * quad] = both[:, quad:]

    def dkv_back(i, low, high):
        return dot(kv[i, c, :, low:high], wf[0, :, width + low : width + high], 1, 1) + dot(
            kv[i, c, :, width + low : width + high],
            wf[0, :, 2 * width + low : 2 * width + high], 1, 1,
        )

    def item_of(r):
        return (nseg - 1 - lax.div(r, n)) * n + lax.rem(r, n)

    def backward_tick(t, carry):
        r = t - (1 - x)

        @pl.when((r >= 0) & (r < items))
        def _():
            i = item_of(r)
            slot = lax.rem(r, 2)

            @pl.when(x == 1)
            def _():
                cot_copy(i).wait()

                @pl.when(i >= items - n)
                def _():
                    gy[i, toks:rows, :] = jnp.zeros((MEM_PAD, width), BF16)

                @pl.when(i < items - n)
                def _():
                    mg_copy(i + n).wait_recv()
                    gy[i, toks:rows, :] = jnp.where(
                        keep[i + n][:, 0:1] > 0.0, mgin[i + n], jnp.zeros((), BF16)
                    )

            @pl.when(x == 0)
            def _():
                gy_copy(i).wait_recv()

            @pl.when(r > 0)
            def _():
                route_sent(S_DQ, item_of(r - 1))
                route_sent(GIN_FF, item_of(r - 1))

            norm_back(1, i, nff)
            for part in range(2):
                cols = slice(part * hidden_half, (part + 1) * hidden_half)
                dg = dot(nff[i], wd[part], 1, 1)
                gp[i, :, cols] = (dg * gp[i, :, cols].astype(F32)).astype(BF16)
            gab[...] = (dot(gp[i], wf[1], 1, 1) + dhb[...]).astype(BF16)
            norm_back(0, i, natt)
            dctx[...] = dot(natt[i], wf[0, :, wide:], 1, 1).astype(BF16)
            route(S_DFF0, i)
            route(S_DFF1, i)
            route(S_DU, i)
            route(GIN_FF, i)
            route(S_DATT, i)
            for copy in prob_copies(i, True):
                copy.wait()
            attend_back(i, slot)
            route(S_DQ, i)

            @pl.when(r + 1 < items)
            def _():
                for copy in prob_copies(item_of(r + 1), True):
                    copy.start()

            for j in range(quads - 1):
                gather_dkv(j, i, slot)
            early = (quads - 1) * quad
            partial_sum = dot(dqb[...], wf[0, :, 0:width], 1, 1) + dhb[...]
            if early:
                partial_sum = partial_sum + dkv_back(i, 0, early)
            dhb[...] = partial_sum
            gather_dkv(quads - 1, i, slot)
            route(S_DKV, i)
            forward_sent(i)
            yd[i] = (dkv_back(i, early, width) + dhb[...]).astype(BF16)

            @pl.when(x == 1)
            def _():
                gy_copy(i).start()

            @pl.when((x == 0) & (i >= n))
            def _():
                mg_copy(i).start()

            route(GIN_ATT, i)
            for j in range(quads):
                dkv_copy(j, i, slot).wait_send()

        return carry

    lax.fori_loop(0, items + 1, backward_tick, 0)

    acc_copy = remote(acc.at[1 - c], accp, as_sem, ar_sem, core_peer)
    acc_copy.start()

    def backward_drain(i, carry):
        @pl.when(x == 1)
        def _():
            gy_copy(i).wait_send()

        @pl.when((x == 0) & (i >= n))
        def _():
            mg_copy(i).wait_send()

        for kind in range(KINDS):
            if kind not in (OUT_FF, S_GLO, S_GHI, S_DQ, GIN_FF):
                route_sent(kind, i)
            route_received(kind, i)
        return carry

    lax.fori_loop(0, items, backward_drain, 0)
    route_sent(S_GLO, items - 1)
    route_sent(S_GHI, items - 1)
    route_sent(S_DQ, item_of(items - 1))
    route_sent(GIN_FF, item_of(items - 1))
    for k in range(5):
        weight_remote(k).wait_send()
    acc_copy.wait()
    norm_grad[...] = acc[c] + accp[...]


def run_layers(n, nseg, heads, tokens, cotangent, first, down, docs, resets, gain, shift):
    length, width = tokens.shape[1:]
    toks = length // nseg // 2
    rows = toks + MEM_PAD
    items = n * nseg
    hidden_half = down.shape[1]
    quads = heads // 4
    quad = width // quads
    any_spec = pl.BlockSpec(memory_space=pl.ANY)
    vmem_spec = pl.BlockSpec(memory_space=pltpu.VMEM)
    dma = pltpu.SemaphoreType.DMA
    item_rows = pltpu.VMEM((items, rows, width), BF16)
    one, two = dma((items,)), dma((2, items))
    return pl.pallas_call(
        partial(layers_kernel, n, nseg, heads),
        out_shape=(
            jax.ShapeDtypeStruct((n, length, width), BF16),
            jax.ShapeDtypeStruct((n, length, width), BF16),
            jax.ShapeDtypeStruct((2 * items, rows, width), BF16),
            jax.ShapeDtypeStruct((2 * items, rows, width), BF16),
            jax.ShapeDtypeStruct((2 * items, rows, 4 * width), BF16),
            jax.ShapeDtypeStruct((2 * items, rows, hidden_half), BF16),
            jax.ShapeDtypeStruct((2 * items, rows, width), BF16),
            jax.ShapeDtypeStruct((2, width), F32),
            jax.ShapeDtypeStruct((items, quads, 4 * rows, 2 * toks), BF16),
            jax.ShapeDtypeStruct((items, quads, rows, 8 * MEM_PAD), BF16),
        ),
        in_specs=[any_spec] * 4 + [vmem_spec] * 4,
        out_specs=[any_spec] * 7 + [vmem_spec] + [any_spec] * 2,
        scratch_shapes=[
            pltpu.VMEM((2, width, 4 * width), BF16),
            pltpu.VMEM((2, hidden_half, width), BF16),
            pltpu.VMEM((2, 2, width), F32),
            item_rows,
            item_rows,
            item_rows,
            pltpu.VMEM((items, 2, rows, 2 * width), BF16),
            item_rows,
            item_rows,
            item_rows,
            item_rows,
            item_rows,
            item_rows,
            pltpu.VMEM((rows, 2 * hidden_half), BF16),
            pltpu.VMEM((rows, 2 * hidden_half), BF16),
            pltpu.VMEM((items, rows, 2 * hidden_half), BF16),
            pltpu.VMEM((items, rows, 128), F32),
            pltpu.VMEM((items, toks, 128), F32),
            pltpu.VMEM((items, 1, 2 * toks), F32),
            pltpu.VMEM((items, MEM_PAD, 128), F32),
            pltpu.VMEM((2, items, MEM_PAD, width), BF16),
            pltpu.VMEM((items, MEM_PAD, width), BF16),
            pltpu.VMEM((2, quads, rows, 2 * quad), BF16),
            pltpu.VMEM((2, quads, rows, 2 * quad), BF16),
            pltpu.VMEM((rows, width), F32),
            pltpu.VMEM((rows, width), BF16),
            pltpu.VMEM((rows, width), BF16),
            pltpu.VMEM((rows, width), BF16),
            pltpu.VMEM((rows, width), BF16),
            pltpu.VMEM((2, 2, width), F32),
            pltpu.VMEM((2, width), F32),
            pltpu.VMEM((quads, 4 * rows, 2 * toks), BF16),
            pltpu.VMEM((quads, rows, 8 * MEM_PAD), BF16),
            dma((4,)), dma((5,)), dma((5,)),
            two, one, one, two, two,
            two, two,
            two, two,
            two, two,
            one, one, one, one,
            dma((quads, items)), dma((quads, items)),
            dma(()), dma(()),
        ]
        + [dma((KINDS, items))] * 3,
        compiler_params=pltpu.CompilerParams(
            collective_id=0, has_side_effects=True, vmem_limit_bytes=61 * 1024 * 1024
        ),
    )(tokens, cotangent, first, down, docs, resets, gain, shift)


def reduce_kernel(
    chunks,
    sx1, sx2, sr, sg, sd, norm_part,
    first_out, down_out, norm_out,
    x1, x2, rr, gg, dd, work, done, got_u, got_uz, got_vz, got_vy, stage, norms,
    right_sem, left_sem, out_sem, u_s, u_r, uz_s, uz_r, vz_s, vz_r, vy_s, vy_r, vg_s, vg_r,
    uzg_s, uzg_r, vzg_s, vzg_r, ug_s, ug_r, n_s, n_r,
):
    lines = 4
    d = lax.axis_index("dp")
    y = lax.rem(d, 2)
    z = lax.div(d, 2)
    dp = lax.axis_size("dp")
    width = sd.shape[1]
    half = width // 2
    part = width // chunks
    hr = part // 2
    lane_group = 128
    per_group = lane_group // part
    y_peer = {"dp": z * 2 + (1 - y)}

    def remote(src, dst, send, recv, peer):
        return pltpu.make_async_remote_copy(
            src_ref=src, dst_ref=dst, send_sem=send, recv_sem=recv,
            device_id=peer, device_id_type=MESH,
        )

    def other(step):
        return {"dp": lax.rem(d + step, dp)}

    barrier = pltpu.get_barrier_semaphore()
    for step in range(1, dp):
        pl.semaphore_signal(barrier, inc=1, device_id=other(step), device_id_type=MESH)

    lane_groups = width // lane_group
    right_loads = [(sd, dd)] + [
        (sr.at[:, b * width : (b + 1) * width], rr.at[:, b * width : (b + 1) * width])
        for b in range(4)
    ]

    def right_load(k):
        src, dst = right_loads[k]
        return pltpu.make_async_copy(src, dst, right_sem.at[k])

    def left_load(which, group):
        src, dst, low = ((sg, gg, 0), (sg, gg, width), (sx2, x2, 0), (sx1, x1, 0))[which]
        cols = pl.ds(pl.multiple_of(low + group * lane_group, lane_group), lane_group)
        return pltpu.make_async_copy(src.at[:, cols], dst.at[:, cols], left_sem.at[which, group])

    right_load(0).start()
    left_load(0, 0).start()
    left_load(1, 0).start()
    left_load(2, 0).start()
    right_load(4).start()
    left_load(3, 0).start()
    for k in range(1, 4):
        right_load(k).start()
    for group in range(1, lane_groups):
        for which in range(4):
            left_load(which, group).start()

    norms[d] = norm_part[...]
    pl.semaphore_wait(barrier, dp - 1)

    def norm_copy(step):
        return remote(norms.at[d], norms.at[d], n_s.at[step - 1], n_r.at[step - 1], other(step))

    def norm_arrival(step):
        source = lax.rem(d + dp - step, dp)
        return remote(
            norms.at[source], norms.at[source], n_s.at[step - 1], n_r.at[step - 1], other(step)
        )

    for step in range(1, dp):
        norm_copy(step).start()

    def column_half(h):
        return pl.ds(pl.multiple_of(h * half, 128), half)

    mine, theirs = column_half(y), column_half(1 - y)

    def place(flow):
        return z if flow == 0 else lines - 1 - z

    def onward(flow):
        step = -1 if flow == 0 else 1
        return {"dp": (z + step) * 2 + y}

    def back(flow):
        step = 1 if flow == 0 else -1
        return {"dp": (z + step) * 2 + y}

    def rows_of(flow):
        return slice(flow * hr, (flow + 1) * hr)

    def u_copy(k):
        return remote(
            work.at[k, 0:3, :, theirs], got_u.at[k], u_s.at[k], u_r.at[k], y_peer
        )

    def uz_copy(flow, k):
        return remote(
            work.at[k, 0:3, rows_of(flow), mine], got_uz.at[flow, k],
            uz_s.at[flow, k], uz_r.at[flow, k], onward(flow),
        )

    def vz_copy(flow, k):
        return remote(
            work.at[k, 3:6, rows_of(flow), :], got_vz.at[flow, k],
            vz_s.at[flow, k], vz_r.at[flow, k], onward(flow),
        )

    def vy_copy(flow, k):
        return remote(
            work.at[k, 3:6, rows_of(flow), theirs], got_vy.at[k], vy_s.at[k], vy_r.at[k], y_peer
        )

    def vg_copy(flow, k, cols):
        spot = done.at[k, 3:6, rows_of(flow), cols]
        return remote(spot, spot, vg_s.at[k], vg_r.at[k], y_peer)

    def uzg_copy(flow, k):
        spot = done.at[k, 0:3, rows_of(flow), mine]
        return remote(spot, spot, uzg_s.at[flow, k], uzg_r.at[flow, k], back(flow))

    def vzg_copy(flow, k):
        spot = done.at[k, 3:6, rows_of(flow), :]
        return remote(spot, spot, vzg_s.at[flow, k], vzg_r.at[flow, k], back(flow))

    def ug_copy(flow, k, cols):
        spot = done.at[k, 0:3, rows_of(flow), cols]
        return remote(spot, spot, ug_s.at[flow, k], ug_r.at[flow, k], y_peer)

    def out_copies(k, slot):
        rows = pl.ds(pl.multiple_of(k * part, part), part)
        copies = []
        for b in range(6):
            if b < 4:
                dst = first_out.at[rows, b * width : (b + 1) * width]
            else:
                low = pl.ds(pl.multiple_of((b - 4) * width + k * part, part), part)
                dst = down_out.at[low, :]
            copies.append(
                pltpu.make_async_copy(stage.at[slot, b], dst, out_sem.at[slot, b])
            )
        return copies

    def plus(a, b):
        return (a.astype(F32) + b.astype(F32)).astype(BF16)

    def ready(k, low=0):
        return (k >= low) & (k < chunks)

    def store_chunks(group, block, value):
        for e in range(per_group):
            work[group * per_group + e, block] = value[e * part : (e + 1) * part]

    def round_step(r, carry):
        group = lax.div(r, per_group)

        @pl.when((lax.rem(r, per_group) == 0) & (r < chunks))
        def _():
            cols = pl.ds(pl.multiple_of(group * lane_group, lane_group), lane_group)
            gcols = pl.ds(pl.multiple_of(width + group * lane_group, lane_group), lane_group)

            @pl.when(r == 0)
            def _():
                right_load(0).wait()

            left_load(0, group).wait()
            store_chunks(group, 4, dot(gg[:, cols], dd[...], 0, 0).astype(BF16))
            left_load(1, group).wait()
            store_chunks(group, 5, dot(gg[:, gcols], dd[...], 0, 0).astype(BF16))
            left_load(2, group).wait()

            @pl.when(r == 0)
            def _():
                right_load(4).wait()

            store_chunks(group, 3, dot(x2[:, cols], rr[:, 3 * width :], 0, 0).astype(BF16))

        for flow in range(2):
            p = place(flow)
            k = r - (lines - 1 - p)
            rows = rows_of(flow)

            @pl.when(ready(k))
            def _():
                @pl.when(p < lines - 1)
                def _():
                    vz_copy(flow, k).wait_recv()
                    work[k, 3:6, rows, :] = plus(work[k, 3:6, rows, :], got_vz[flow, k])

                @pl.when(p > 0)
                def _():
                    vz_copy(flow, k).start()

                @pl.when(p == 0)
                def _():
                    vy_copy(flow, k).start()

        @pl.when((lax.rem(r, per_group) == 0) & (r < chunks))
        def _():
            cols = pl.ds(pl.multiple_of(group * lane_group, lane_group), lane_group)

            left_load(3, group).wait()
            for b in range(3):

                @pl.when(r == 0)
                def _():
                    right_load(1 + b).wait()

                store_chunks(
                    group, b,
                    dot(x1[:, cols], rr[:, b * width : (b + 1) * width], 0, 0).astype(BF16),
                )

        @pl.when(ready(r))
        def _():
            u_copy(r).start()

        @pl.when(ready(r - 1))
        def _():
            k = r - 1
            u_copy(k).wait_recv()
            work[k, 0:3, :, mine] = plus(work[k, 0:3, :, mine], got_u[k])

        for flow in range(2):
            p = place(flow)
            k = r - 1 - (lines - 1 - p)
            rows = rows_of(flow)

            @pl.when(ready(k))
            def _():
                @pl.when(p < lines - 1)
                def _():
                    uz_copy(flow, k).wait_recv()
                    total = plus(work[k, 0:3, rows, mine], got_uz[flow, k])

                    @pl.when(p > 0)
                    def _():
                        work[k, 0:3, rows, mine] = total

                    @pl.when(p == 0)
                    def _():
                        done[k, 0:3, rows, mine] = total

                @pl.when(p > 0)
                def _():
                    uz_copy(flow, k).start()

                @pl.when(p == 0)
                def _():
                    uzg_copy(flow, k).start()
                    ug_copy(flow, k, mine).start()

        for flow in range(2):
            p = place(flow)
            rows = rows_of(flow)

            @pl.when((p == 0) & ready(r - lines))
            def _():
                k = r - lines
                vy_copy(flow, k).wait_recv()
                done[k, 3:6, rows, mine] = plus(work[k, 3:6, rows, mine], got_vy[k])
                vg_copy(flow, k, mine).start()

            @pl.when((p == 0) & ready(r - lines - 1))
            def _():
                k = r - lines - 1
                vg_copy(flow, k, theirs).wait_recv()
                vzg_copy(flow, k).start()

        for flow in range(2):
            p = place(flow)
            k = r - lines - p

            @pl.when((p > 0) & ready(k))
            def _():
                uzg_copy(flow, k).wait_recv()

                @pl.when(p < lines - 1)
                def _():
                    uzg_copy(flow, k).start()

                ug_copy(flow, k, mine).start()

        for flow in range(2):
            p = place(flow)
            k = r - lines - 1 - p

            @pl.when((p > 0) & ready(k))
            def _():
                vzg_copy(flow, k).wait_recv()

                @pl.when(p < lines - 1)
                def _():
                    vzg_copy(flow, k).start()

            @pl.when(ready(k))
            def _():
                ug_copy(flow, k, theirs).wait_recv()

        k = r - 2 * lines

        @pl.when(ready(k))
        def _():
            slot = lax.rem(k, 2)

            @pl.when(k >= 2)
            def _():
                for copy in out_copies(k - 2, slot):
                    copy.wait()

            stage[slot] = done[k].astype(F32)
            for copy in out_copies(k, slot):
                copy.start()

        return carry

    lax.fori_loop(0, chunks + 2 * lines, round_step, 0)

    for step in range(1, dp):
        norm_arrival(step).wait_recv()
    total = norms[0]
    for e in range(1, dp):
        total = total + norms[e]
    norm_out[...] = total

    def drain(k, carry):
        u_copy(k).wait_send()
        for flow in range(2):
            p = place(flow)
            ug_copy(flow, k, mine).wait_send()

            @pl.when(p > 0)
            def _():
                vz_copy(flow, k).wait_send()
                uz_copy(flow, k).wait_send()

            @pl.when(p < lines - 1)
            def _():
                uzg_copy(flow, k).wait_send()
                vzg_copy(flow, k).wait_send()

            @pl.when(p == 0)
            def _():
                vy_copy(flow, k).wait_send()
                vg_copy(flow, k, mine).wait_send()

        return carry

    lax.fori_loop(0, chunks, drain, 0)
    for k in (chunks - 2, chunks - 1):
        for copy in out_copies(k, k % 2):
            copy.wait()
    for step in range(1, dp):
        norm_copy(step).wait_send()


def sum_weights(dp, sx1, sx2, sr, sg, sd, norm_part):
    total, width = sx1.shape
    chunks = 12
    part = width // chunks
    half = width // 2
    any_spec = pl.BlockSpec(memory_space=pl.ANY)
    vmem_spec = pl.BlockSpec(memory_space=pltpu.VMEM)
    dma = pltpu.SemaphoreType.DMA
    one, two = dma((chunks,)), dma((2, chunks))
    return pl.pallas_call(
        partial(reduce_kernel, chunks),
        out_shape=(
            jax.ShapeDtypeStruct((width, 4 * width), F32),
            jax.ShapeDtypeStruct((2 * width, width), F32),
            jax.ShapeDtypeStruct((2, width), F32),
        ),
        in_specs=[any_spec] * 5 + [vmem_spec],
        out_specs=[any_spec] * 2 + [vmem_spec],
        scratch_shapes=[
            pltpu.VMEM((total, width), BF16),
            pltpu.VMEM((total, width), BF16),
            pltpu.VMEM((total, 4 * width), BF16),
            pltpu.VMEM((total, 2 * width), BF16),
            pltpu.VMEM((total, width), BF16),
            pltpu.VMEM((chunks, 6, part, width), BF16),
            pltpu.VMEM((chunks, 6, part, width), BF16),
            pltpu.VMEM((chunks, 3, part, half), BF16),
            pltpu.VMEM((2, chunks, 3, part // 2, half), BF16),
            pltpu.VMEM((2, chunks, 3, part // 2, width), BF16),
            pltpu.VMEM((chunks, 3, part // 2, half), BF16),
            pltpu.VMEM((2, 6, part, width), F32),
            pltpu.VMEM((dp, 2, width), F32),
            dma((5,)),
            dma((4, width // 128)),
            dma((2, 6)),
            one, one,
            two, two,
            two, two,
            one, one,
            one, one,
            two, two,
            two, two,
            two, two,
            dma((dp - 1,)), dma((dp - 1,)),
        ],
        compiler_params=pltpu.CompilerParams(
            collective_id=1, has_side_effects=True, vmem_limit_bytes=60 * 1024 * 1024
        ),
    )(sx1, sx2, sr, sg, sd, norm_part)


def shards(
    tokens, doc_ids, reset_flags, first_weights, down_halves, norm_gain, norm_bias, cotangent
):
    n, length, width = tokens.shape
    items = n * NSEG
    rows = length // NSEG // 2 + MEM_PAD
    out, gin, sx1, sx2, sr, sg, sd, norm_grad, _, _ = run_layers(
        n, NSEG, H, tokens, cotangent, first_weights, down_halves,
        doc_ids, reset_flags, norm_gain, norm_bias,
    )
    total = 2 * items * rows
    sx1, sx2, sd = (a.reshape(total, width) for a in (sx1, sx2, sd))
    sr = sr.reshape(total, 4 * width)
    sg = sg.reshape(total, -1)

    dp = lax.axis_size("dp")
    if dp == 8:
        first_grad, down_grad, norm_grad = sum_weights(dp, sx1, sx2, sr, sg, sd, norm_grad)
    else:

        def weight_grad(left, right):
            return jnp.einsum("rd,re->de", left, right, preferred_element_type=F32).astype(BF16)

        first_grad = jnp.concatenate(
            [weight_grad(sx1, sr[:, : 3 * width]), weight_grad(sx2, sr[:, 3 * width :])], axis=1
        )
        down_grad = weight_grad(sg, sd)
        first_grad, down_grad = lax.psum((first_grad, down_grad), "dp")
        norm_grad = lax.psum(norm_grad, "dp")
    return (
        out[None],
        gin[None],
        first_grad.astype(F32)[None],
        down_grad.astype(F32)[None],
        norm_grad[0:1],
        norm_grad[1:2],
    )


def solution(mesh):
    in_specs = (
        P("dp", None, None),
        P("dp", None),
        P("dp", None),
        P("section", None, None),
        P("section", None, None),
        P("section", None),
        P("section", None),
        P("dp", None, None),
    )
    out_specs = (
        P("section", "dp", None, None),
        P("section", "dp", None, None),
        P("section", None, None),
        P("section", None, None),
        P("section", None),
        P("section", None),
    )
    return jax.shard_map(shards, mesh=mesh, in_specs=in_specs, out_specs=out_specs, check_vma=False)
```

```python
from functools import partial

import jax
import jax.numpy as jnp
from jax import lax
from jax.experimental import pallas as pl
from jax.experimental.pallas import tpu as pltpu
from jax.sharding import PartitionSpec as P

H = 12
M = 20
NSEG = 2
MEM_PAD = 16
NORM_EPSILON = 1e-05
MASKED_SCORE = -1000000000.0
ABSENT_SCORE = -3e38
MESH = pl.DeviceIdType.MESH
BF16 = jnp.bfloat16
F32 = jnp.float32

OUT_ATT, OUT_FF, GIN_ATT, GIN_FF = 0, 1, 2, 3
S_X0, S_CTX, S_DQ, S_DKV, S_DATT, S_GLO, S_DFF0 = 4, 5, 6, 7, 8, 9, 10
S_Y1, S_Y2, S_DU, S_GHI, S_DFF1 = 11, 12, 13, 14, 15
KINDS = 16


def dot(a, b, lhs_dim=1, rhs_dim=0):
    return lax.dot_general(
        a, b, (((lhs_dim,), (rhs_dim,)), ((), ())), preferred_element_type=F32
    )


def normalize(summed):
    mean = jnp.mean(summed, axis=-1, keepdims=True)
    centered = summed - mean
    var = jnp.mean(centered * centered, axis=-1, keepdims=True)
    inv = lax.rsqrt(var + NORM_EPSILON)
    return centered * inv, inv


def group_of(shape, dim, size):
    index = lax.broadcasted_iota(jnp.int32, shape, dim)
    return lax.shift_right_logical(index, size.bit_length() - 1)


def spread(values, groups):
    result = values[-1]
    for h in range(len(values) - 1):
        result = jnp.where(groups == h, values[h], result)
    return result


def layers_kernel(
    n, nseg, heads,
    tokens, cotangent, first, down, docs, resets, gain, shift,
    out, gin, sx1, sx2, sr, sg, sd, norm_grad, ptok, pmem,
    wf, wd, nrm, x0, xo, q, kv, ctx, natt, yatt, nff, yd, gy, g, gpb, gp, stats, qdoc, kdoc, keep,
    memin, mgin, dkvs, dkvin, dhb, ctxb, acc, accp, tprob, mprob,
    wl, ws, wr, tok_sem, cot_sem, gp_sem, pw_sem, pr_sem, fs_sem, fr_sem, xs_sem, xr_sem,
    ms_sem, mr_sem, gs_sem, gr_sem, hs_sem, hr_sem, ds_sem, dr_sem, as_sem, ar_sem,
    lsem, ssem, rsem,
):
    items = n * nseg
    section = lax.axis_index("section")
    c = lax.rem(section, 2)
    x = lax.div(section, 2)
    core_peer = {"section": x * 2 + (1 - c)}
    chip_peer = {"section": (1 - x) * 2 + c}
    cross_peer = {"section": (1 - x) * 2 + (1 - c)}
    rows, width = x0.shape[1:]
    toks = rows - MEM_PAD
    seg_len = 2 * toks
    hidden_half = wd.shape[1]
    wide = 3 * width
    head_dim = width // heads
    quad = 4 * head_dim
    quads = heads // 4
    mem_keys = 2 * MEM_PAD
    scale = head_dim ** (-0.5)
    dqb = gpb.at[:, 0:width]
    gab = gpb.at[:, width : 2 * width]
    dctx = gpb.at[:, 2 * width : wide]

    def remote(src, dst, send, recv, peer):
        return pltpu.make_async_remote_copy(
            src_ref=src, dst_ref=dst, send_sem=send, recv_sem=recv,
            device_id=peer, device_id_type=MESH,
        )

    barrier = pltpu.get_barrier_semaphore()
    pl.semaphore_signal(barrier, inc=1, device_id=core_peer, device_id_type=MESH)
    pl.semaphore_signal(barrier, inc=1, device_id=chip_peer, device_id_type=MESH)
    pl.semaphore_signal(barrier, inc=1, device_id=cross_peer, device_id_type=MESH)

    def token_rows(ref, i, core=None):
        core = c if core is None else core
        return ref.at[lax.rem(i, n), pl.ds(lax.div(i, n) * seg_len + core * toks, toks), :]

    def token_copy(which, i):
        if which == 0:
            src, dst = token_rows(tokens, i), x0.at[i, 0:toks, :]
        else:
            src, dst = token_rows(tokens, i, 1 - c), xo.at[i, 0:toks, :]
        return pltpu.make_async_copy(src, dst, tok_sem.at[which, i])

    def cot_copy(i):
        return pltpu.make_async_copy(
            token_rows(cotangent, i), gy.at[i, 0:toks, :], cot_sem.at[i]
        )

    def weight_piece(k):
        if k == 0:
            return first.at[0, :, width:wide], wf.at[c, :, width:wide]
        if k == 1:
            return first.at[0, :, 0:width], wf.at[c, :, 0:width]
        if k == 2:
            return first.at[0, :, wide:], wf.at[c, :, wide:]
        return down.at[0], wd.at[c]

    def weight_local(k):
        src, dst = weight_piece(k)
        return pltpu.make_async_copy(src, dst, wl.at[k])

    def weight_remote(k):
        if k == 4:
            return remote(nrm.at[c], nrm.at[c], ws.at[4], wr.at[4], core_peer)
        src, dst = weight_piece(k)
        return remote(src, dst, ws.at[k], wr.at[k], core_peer)

    nrm[c, 0:1, :] = gain[...]
    nrm[c, 1:2, :] = shift[...]
    weight_local(0).start()

    @pl.when(x == 0)
    def _():
        token_copy(0, 0).start()
        token_copy(1, 0).start()

    pl.semaphore_wait(barrier, 3)
    for k in range(5):
        weight_remote(k).start()
    for k in range(1, 4):
        weight_local(k).start()
    for i in range(items):
        if i > 0:

            @pl.when(x == 0)
            def _():
                token_copy(0, i).start()
                token_copy(1, i).start()

        @pl.when(x == 1)
        def _():
            cot_copy(i).start()

    def wait_first_of(core, ks):
        @pl.when(c == core)
        def _():
            for k in ks:
                weight_local(k).wait()

        @pl.when(c != core)
        def _():
            for k in ks:
                weight_remote(k).wait_recv()

    for i in range(items):
        seq, seg = i % n, i // n
        kdoc[i] = docs[seq : seq + 1, seg * seg_len : (seg + 1) * seg_len].astype(F32)
        own = pl.ds(pl.multiple_of(seg * seg_len + c * toks, toks), toks)
        own_row = docs[seq : seq + 1, own].astype(F32)
        qdoc[i] = jnp.transpose(jnp.broadcast_to(own_row, (128, toks)))
        if seg > 0:
            flag = resets[seq : seq + 1, seg - 1 : seg].astype(F32)
            keep[i] = jnp.broadcast_to(1.0 - flag, (MEM_PAD, 128))

    def routed(kind, i):
        block = i * 2 + c
        sec = 0
        if kind == OUT_ATT:
            src, dst = yatt.at[i, 0:toks, :], token_rows(out, i)
        elif kind == OUT_FF:
            src, dst, sec = yd.at[i, 0:toks, :], token_rows(out, i), 1
        elif kind == GIN_ATT:
            src, dst = yd.at[i, 0:toks, :], token_rows(gin, i)
        elif kind == GIN_FF:
            src, dst, sec = gab.at[0:toks, :], token_rows(gin, i), 1
        elif kind == S_X0:
            src, dst = x0.at[i], sx1.at[block]
        elif kind == S_CTX:
            src, dst = ctx.at[i], sx2.at[block]
        elif kind == S_DQ:
            src, dst = dqb, sr.at[block, :, 0:width]
        elif kind == S_DKV:
            src, dst = kv.at[i, c], sr.at[block, :, width:wide]
        elif kind == S_DATT:
            src, dst = natt.at[i], sr.at[block, :, wide:]
        elif kind == S_GLO:
            src, dst = g.at[:, 0:hidden_half], sg.at[block]
        elif kind == S_DFF0:
            src, dst = nff.at[i], sd.at[block]
        elif kind == S_Y1:
            src, dst, sec = yatt.at[i], sx1.at[block], 1
        elif kind == S_Y2:
            src, dst, sec = yatt.at[i], sx2.at[block], 1
        elif kind == S_DU:
            src, dst, sec = gp.at[i], sr.at[block], 1
        elif kind == S_GHI:
            src, dst, sec = g.at[:, hidden_half:], sg.at[block], 1
        else:
            src, dst, sec = nff.at[i], sd.at[block], 1
        return src, dst, sec

    def route_local(kind, i):
        src, dst, _ = routed(kind, i)
        return pltpu.make_async_copy(src, dst, lsem.at[kind, i])

    def route_away(kind, i):
        src, dst, _ = routed(kind, i)
        return remote(src, dst, ssem.at[kind, i], rsem.at[kind, i], core_peer)

    def route(kind, i):
        sec = routed(kind, i)[2]

        @pl.when(c == sec)
        def _():
            route_local(kind, i).start()

        @pl.when(c != sec)
        def _():
            route_away(kind, i).start()

    def route_sent(kind, i):
        sec = routed(kind, i)[2]

        @pl.when(c == sec)
        def _():
            route_local(kind, i).wait()

        @pl.when(c != sec)
        def _():
            route_away(kind, i).wait_send()

    def route_received(kind, i):
        @pl.when(c == routed(kind, i)[2])
        def _():
            route_away(kind, i).wait_recv()

    def gp_copy(i):
        return pltpu.make_async_copy(gpb, gp.at[i], gp_sem.at[i])

    def prob_copies(i, back):
        pairs = ((tprob, ptok.at[i]), (mprob, pmem.at[i]))
        if back:
            return [
                pltpu.make_async_copy(dst, src, pr_sem.at[e, i])
                for e, (src, dst) in enumerate(pairs)
            ]
        return [
            pltpu.make_async_copy(src, dst, pw_sem.at[e, i]) for e, (src, dst) in enumerate(pairs)
        ]

    cut = rows // 32 * 16

    def piece(p):
        return slice(0, cut) if p == 0 else slice(cut, rows)

    def x_copy(p, i):
        return remote(
            yd.at[i, piece(p)], x0.at[i, piece(p)], xs_sem.at[p, i], xr_sem.at[p, i], chip_peer
        )

    def pass_copy(p, i):
        return remote(
            x0.at[i, piece(p)], xo.at[i, piece(p)], fs_sem.at[p, i], fr_sem.at[p, i], core_peer
        )

    def mem_copy(which, i):
        return remote(
            yd.at[i, toks:rows, :], memin.at[which, i], ms_sem.at[which, i],
            mr_sem.at[which, i], cross_peer if which else chip_peer,
        )

    def gy_copy(i):
        return remote(yd.at[i], gy.at[i], gs_sem.at[i], gr_sem.at[i], chip_peer)

    def mg_copy(i):
        return remote(
            yd.at[i, toks:rows, :], mgin.at[i], hs_sem.at[i], hr_sem.at[i], chip_peer
        )

    def dkv_copy(j, i, slot):
        return remote(
            dkvs.at[1 - c, j], dkvin.at[slot, j], ds_sem.at[j, i], dr_sem.at[j, i], core_peer
        )

    head_lanes = group_of((rows, quad), 1, head_dim)
    mem_lanes = group_of((rows, 4 * mem_keys), 1, mem_keys)
    key_lane = lax.broadcasted_iota(jnp.int32, (rows, 4 * mem_keys), 1)
    mem_valid = lax.rem(key_lane, MEM_PAD) < M // 2
    diagonal = group_of((4 * mem_keys, quad), 0, mem_keys) == group_of(
        (4 * mem_keys, quad), 1, head_dim
    )
    stat_lane = lax.broadcasted_iota(jnp.int32, (rows, 128), 1)

    def stacked(block):
        return jnp.concatenate(
            [jnp.where(head_lanes == h, block, BF16(0)) for h in range(4)], axis=0
        )

    def head_rows(block):
        return [block[h * rows : (h + 1) * rows] for h in range(4)]

    def token_and_memory(i, low):
        cols = slice(low, low + quad)
        tok = jnp.concatenate([kv[i, 0, 0:toks, cols], kv[i, 1, 0:toks, cols]], axis=0)
        mem = jnp.concatenate([kv[i, 0, toks:, cols], kv[i, 1, toks:, cols]], axis=0)
        return tok, jnp.where(diagonal, jnp.concatenate([mem] * 4, axis=0), BF16(0))

    def only_same_document(s, i):
        mine = jnp.concatenate([qdoc[i]] * (seg_len // 128), axis=1)
        same = jnp.where(mine == kdoc[i], s[0:toks], MASKED_SCORE)
        return jnp.concatenate([same, s[toks:]], axis=0)

    def memory_scores(q4, mem_k):
        return jnp.where(mem_valid, dot(q4, mem_k, 1, 1), ABSENT_SCORE)

    def attend(i):
        own = [mem_lanes == h for h in range(4)]

        def scores(j):
            q4 = q[i, :, j * quad : (j + 1) * quad]
            tok_k, mem_k = token_and_memory(i, j * quad)
            return dot(stacked(q4), tok_k, 1, 1), memory_scores(q4, mem_k)

        st = jnp.zeros((rows, 128), F32)
        following = scores(0)
        for j in range(quads):
            s, sm = following
            if j + 1 < quads:
                following = scores(j + 1)
            s = [only_same_document(part, i) for part in head_rows(s)]
            peaks = [
                jnp.max(
                    jnp.concatenate([s[h], jnp.where(own[h], sm, ABSENT_SCORE)], axis=1),
                    axis=1, keepdims=True,
                )
                for h in range(4)
            ]
            pm = jnp.exp(sm - spread(peaks, mem_lanes))
            mprob[j] = pm.astype(BF16)
            totals, probs = [], []
            for h in range(4):
                p = jnp.exp(s[h] - peaks[h])
                probs.append(p.astype(BF16))
                tprob[j, h * rows : (h + 1) * rows, :] = probs[h]
                both = jnp.concatenate([p, jnp.where(own[h], pm, 0.0)], axis=1)
                totals.append(1.0 / jnp.sum(both, axis=1, keepdims=True))
                st = jnp.where(stat_lane == 4 * j + h, totals[h], st)
            tok_v, mem_v = token_and_memory(i, width + j * quad)
            o = spread(head_rows(dot(jnp.concatenate(probs, axis=0), tok_v)), head_lanes)
            o = o + dot(pm.astype(BF16), mem_v)
            ctxb[:, j * quad : (j + 1) * quad] = (o * spread(totals, head_lanes)).astype(BF16)
        stats[i] = st
        ctx[i] = ctxb[...]

    def forward_tick(t, carry):
        i = t - x

        @pl.when((i >= 0) & (i < items))
        def _():
            @pl.when(x == 0)
            def _():
                for which, rows_ref in enumerate((x0, xo)):
                    token_copy(which, i).wait()

                    @pl.when(i < n)
                    def _():
                        rows_ref[i, toks:rows, :] = jnp.zeros((MEM_PAD, width), BF16)

                    @pl.when(i >= n)
                    def _():
                        mem_copy(which, i - n).wait_recv()
                        rows_ref[i, toks:rows, :] = jnp.where(
                            keep[i][:, 0:1] > 0.0, memin[which, i - n], jnp.zeros((), BF16)
                        )

            @pl.when(x == 1)
            def _():
                for p in range(2):
                    x_copy(p, i).wait_recv()
                    pass_copy(p, i).start()

            @pl.when(i == 0)
            def _():
                wait_first_of(0, (0,))

            kv[i, c] = dot(x0[i], wf[0, :, width:wide]).astype(BF16)

            @pl.when(i == 0)
            def _():
                wait_first_of(0, (1,))

            q[i] = dot(x0[i], wf[0, :, 0:width]).astype(BF16) * BF16(scale)

            @pl.when(x == 1)
            def _():
                for p in range(2):
                    pass_copy(p, i).wait_recv()

            kv[i, 1 - c] = dot(xo[i], wf[0, :, width:wide]).astype(BF16)
            @pl.when(i > 0)
            def _():
                for copy in prob_copies(i - 1, False):
                    copy.wait()

            attend(i)
            for copy in prob_copies(i, False):
                copy.start()
            route(S_X0, i)
            route(S_CTX, i)

            @pl.when(i == 0)
            def _():
                wait_first_of(0, (2,))
                weight_remote(4).wait_recv()

            normed, inv = normalize(dot(ctxb[...], wf[0, :, wide:]) + x0[i].astype(F32))
            natt[i] = normed.astype(BF16)
            stats[i] = jnp.where(stat_lane == heads, inv, stats[i])
            yatt[i] = (normed * nrm[0, 0:1, :] + nrm[0, 1:2, :]).astype(BF16)

            @pl.when(i == 0)
            def _():
                wait_first_of(1, (0, 1, 2))

            @pl.when(i > 0)
            def _():
                route_sent(S_GLO, i - 1)
                route_sent(S_GHI, i - 1)
                gp_copy(i - 1).wait()

            for part in range(2):
                cols = slice(part * hidden_half, (part + 1) * hidden_half)
                u = dot(yatt[i], wf[1, :, cols])
                cdf = 0.5 + 0.5 * lax.erf(u * 0.7071067811865476)
                pdf = 0.3989422804014327 * jnp.exp(-0.5 * u * u)
                g[:, cols] = (u * cdf).astype(BF16)
                gpb[:, cols] = (cdf + u * pdf).astype(BF16)
            gp_copy(i).start()
            route(OUT_ATT, i)
            route(S_Y1, i)
            route(S_Y2, i)
            route(S_GLO, i)
            route(S_GHI, i)

            @pl.when(i == 0)
            def _():
                wait_first_of(0, (3,))
                wait_first_of(1, (3,))

            normed, inv = normalize(
                dot(g[:, 0:hidden_half], wd[0])
                + dot(g[:, hidden_half:], wd[1])
                + yatt[i].astype(F32)
            )
            yd[i] = (normed * nrm[1, 0:1, :] + nrm[1, 1:2, :]).astype(BF16)

            @pl.when(x == 0)
            def _():
                for p in range(2):
                    x_copy(p, i).start()

            @pl.when((x == 1) & (i < items - n))
            def _():
                for which in range(2):
                    mem_copy(which, i).start()

            nff[i] = normed.astype(BF16)
            stats[i] = jnp.where(stat_lane == heads + 1, inv, stats[i])
            route(OUT_FF, i)

        return carry

    lax.fori_loop(0, items + 1, forward_tick, 0)

    def forward_sent(i):
        route_sent(OUT_FF, i)

        @pl.when(x == 0)
        def _():
            for p in range(2):
                x_copy(p, i).wait_send()

        @pl.when(x == 1)
        def _():
            for p in range(2):
                pass_copy(p, i).wait_send()

        @pl.when((x == 1) & (i < items - n))
        def _():
            for which in range(2):
                mem_copy(which, i).wait_send()

    for copy in prob_copies(items - 1, False):
        copy.wait()
    for copy in prob_copies(items - n, True):
        copy.start()
    gp_copy(items - 1).wait()
    acc[...] = jnp.zeros_like(acc)

    def norm_back(s, i, normed_ref):
        grad = (gy[i] if s else gab[...]).astype(F32)
        normed = normed_ref[i].astype(F32)
        inv = stats[i][:, heads + s : heads + s + 1]
        acc[s, 0:1, :] += jnp.sum(grad * normed, axis=0, keepdims=True)
        acc[s, 1:2, :] += jnp.sum(grad, axis=0, keepdims=True)
        scaled = grad * nrm[s, 0:1, :]
        row_term = jnp.mean(scaled, axis=1, keepdims=True)
        row_cross = jnp.mean(scaled * normed, axis=1, keepdims=True)
        dh = inv * (scaled - row_term - normed * row_cross)
        dhb[...] = dh
        normed_ref[i] = dh.astype(BF16)

    def attend_back(i, slot):
        def prob_grads(j):
            inverse = [stats[i][:, 4 * j + h : 4 * j + h + 1] for h in range(4)]
            c4 = dctx[:, j * quad : (j + 1) * quad].astype(F32) * spread(inverse, head_lanes)
            c4 = c4.astype(BF16)
            tok_v, mem_v = token_and_memory(i, width + j * quad)
            return c4, dot(stacked(c4), tok_v, 1, 1), dot(c4, mem_v, 1, 1)

        following = prob_grads(0)
        for j in range(quads):
            c4, dp, dpm = following
            if j + 1 < quads:
                following = prob_grads(j + 1)
            cols = slice(j * quad, (j + 1) * quad)
            q4 = q[i, :, cols]
            tok_k, mem_k = token_and_memory(i, j * quad)
            products = c4.astype(F32) * ctx[i, :, cols].astype(F32)
            dp = head_rows(dp)
            inner = [
                jnp.sum(jnp.where(head_lanes == h, products, 0.0), axis=1, keepdims=True)
                for h in range(4)
            ]
            dscores = [
                (tprob[j, h * rows : (h + 1) * rows, :].astype(F32) * (dp[h] - inner[h])).astype(BF16)
                for h in range(4)
            ]
            dsm = (mprob[j].astype(F32) * (dpm - spread(inner, mem_lanes))).astype(BF16)
            ct, qt = jnp.transpose(c4), jnp.transpose(q4)
            mine = [slice(h * head_dim, (h + 1) * head_dim) for h in range(4)]
            dv = [
                dot(ct[mine[h]], tprob[j, h * rows : (h + 1) * rows, :]).astype(BF16)
                for h in range(4)
            ]
            dk = [dot(qt[mine[h]], dscores[h]).astype(BF16) for h in range(4)]
            dv = jnp.transpose(jnp.concatenate(dv, axis=0))
            dk = jnp.transpose(jnp.concatenate(dk, axis=0))
            dscores = jnp.concatenate(dscores, axis=0)
            dq = spread(head_rows(dot(dscores, tok_k)), head_lanes) + dot(dsm, mem_k)
            dqb[:, cols] = (dq * scale).astype(BF16)
            dvm = jnp.where(diagonal, dot(mprob[j], c4, 0, 0), 0.0)
            dkm = jnp.where(diagonal, dot(dsm, q4, 0, 0), 0.0)
            dvm = sum(dvm[h * mem_keys : (h + 1) * mem_keys] for h in range(4))
            dkm = sum(dkm[h * mem_keys : (h + 1) * mem_keys] for h in range(4))
            for half, (tok_part, mem_part) in enumerate(((dk, dkm), (dv, dvm))):
                cols = slice(half * quad, (half + 1) * quad)
                for core in range(2):
                    dkvs[core, j, 0:toks, cols] = tok_part[
                        core * toks : (core + 1) * toks
                    ].astype(BF16)
                    dkvs[core, j, toks:rows, cols] = mem_part[
                        core * MEM_PAD : (core + 1) * MEM_PAD
                    ].astype(BF16)
            dkv_copy(j, i, slot).start()

    def gather_dkv(j, i, slot):
        dkv_copy(j, i, slot).wait_recv()
        both = (dkvs[c, j].astype(F32) + dkvin[slot, j].astype(F32)).astype(BF16)
        kv[i, c, :, j * quad : (j + 1) * quad] = both[:, 0:quad]
        kv[i, c, :, width + j * quad : width + (j + 1) * quad] = both[:, quad:]

    def dkv_back(i, low, high):
        return dot(kv[i, c, :, low:high], wf[0, :, width + low : width + high], 1, 1) + dot(
            kv[i, c, :, width + low : width + high],
            wf[0, :, 2 * width + low : 2 * width + high], 1, 1,
        )

    def item_of(r):
        return (nseg - 1 - lax.div(r, n)) * n + lax.rem(r, n)

    def backward_tick(t, carry):
        r = t - (1 - x)

        @pl.when((r >= 0) & (r < items))
        def _():
            i = item_of(r)
            slot = lax.rem(r, 2)

            @pl.when(x == 1)
            def _():
                cot_copy(i).wait()

                @pl.when(i >= items - n)
                def _():
                    gy[i, toks:rows, :] = jnp.zeros((MEM_PAD, width), BF16)

                @pl.when(i < items - n)
                def _():
                    mg_copy(i + n).wait_recv()
                    gy[i, toks:rows, :] = jnp.where(
                        keep[i + n][:, 0:1] > 0.0, mgin[i + n], jnp.zeros((), BF16)
                    )

            @pl.when(x == 0)
            def _():
                gy_copy(i).wait_recv()

            @pl.when(r > 0)
            def _():
                route_sent(S_DQ, item_of(r - 1))
                route_sent(GIN_FF, item_of(r - 1))

            norm_back(1, i, nff)
            for part in range(2):
                cols = slice(part * hidden_half, (part + 1) * hidden_half)
                dg = dot(nff[i], wd[part], 1, 1)
                gp[i, :, cols] = (dg * gp[i, :, cols].astype(F32)).astype(BF16)
            gab[...] = (dot(gp[i], wf[1], 1, 1) + dhb[...]).astype(BF16)
            norm_back(0, i, natt)
            dctx[...] = dot(natt[i], wf[0, :, wide:], 1, 1).astype(BF16)
            route(S_DFF0, i)
            route(S_DFF1, i)
            route(S_DU, i)
            route(GIN_FF, i)
            route(S_DATT, i)
            for copy in prob_copies(i, True):
                copy.wait()
            attend_back(i, slot)
            route(S_DQ, i)

            @pl.when(r + 1 < items)
            def _():
                for copy in prob_copies(item_of(r + 1), True):
                    copy.start()

            for j in range(quads - 1):
                gather_dkv(j, i, slot)
            early = (quads - 1) * quad
            partial_sum = dot(dqb[...], wf[0, :, 0:width], 1, 1) + dhb[...]
            if early:
                partial_sum = partial_sum + dkv_back(i, 0, early)
            dhb[...] = partial_sum
            gather_dkv(quads - 1, i, slot)
            route(S_DKV, i)
            forward_sent(i)
            yd[i] = (dkv_back(i, early, width) + dhb[...]).astype(BF16)

            @pl.when(x == 1)
            def _():
                gy_copy(i).start()

            @pl.when((x == 0) & (i >= n))
            def _():
                mg_copy(i).start()

            route(GIN_ATT, i)
            for j in range(quads):
                dkv_copy(j, i, slot).wait_send()

        return carry

    lax.fori_loop(0, items + 1, backward_tick, 0)

    acc_copy = remote(acc.at[1 - c], accp, as_sem, ar_sem, core_peer)
    acc_copy.start()

    def backward_drain(i, carry):
        @pl.when(x == 1)
        def _():
            gy_copy(i).wait_send()

        @pl.when((x == 0) & (i >= n))
        def _():
            mg_copy(i).wait_send()

        for kind in range(KINDS):
            if kind not in (OUT_FF, S_GLO, S_GHI, S_DQ, GIN_FF):
                route_sent(kind, i)
            route_received(kind, i)
        return carry

    lax.fori_loop(0, items, backward_drain, 0)
    route_sent(S_GLO, items - 1)
    route_sent(S_GHI, items - 1)
    route_sent(S_DQ, item_of(items - 1))
    route_sent(GIN_FF, item_of(items - 1))
    for k in range(5):
        weight_remote(k).wait_send()
    acc_copy.wait()
    norm_grad[...] = acc[c] + accp[...]


def run_layers(n, nseg, heads, tokens, cotangent, first, down, docs, resets, gain, shift):
    length, width = tokens.shape[1:]
    toks = length // nseg // 2
    rows = toks + MEM_PAD
    items = n * nseg
    hidden_half = down.shape[1]
    quads = heads // 4
    quad = width // quads
    any_spec = pl.BlockSpec(memory_space=pl.ANY)
    vmem_spec = pl.BlockSpec(memory_space=pltpu.VMEM)
    dma = pltpu.SemaphoreType.DMA
    item_rows = pltpu.VMEM((items, rows, width), BF16)
    one, two = dma((items,)), dma((2, items))
    return pl.pallas_call(
        partial(layers_kernel, n, nseg, heads),
        out_shape=(
            jax.ShapeDtypeStruct((n, length, width), BF16),
            jax.ShapeDtypeStruct((n, length, width), BF16),
            jax.ShapeDtypeStruct((2 * items, rows, width), BF16),
            jax.ShapeDtypeStruct((2 * items, rows, width), BF16),
            jax.ShapeDtypeStruct((2 * items, rows, 4 * width), BF16),
            jax.ShapeDtypeStruct((2 * items, rows, hidden_half), BF16),
            jax.ShapeDtypeStruct((2 * items, rows, width), BF16),
            jax.ShapeDtypeStruct((2, width), F32),
            jax.ShapeDtypeStruct((items, quads, 4 * rows, 2 * toks), BF16),
            jax.ShapeDtypeStruct((items, quads, rows, 8 * MEM_PAD), BF16),
        ),
        in_specs=[any_spec] * 4 + [vmem_spec] * 4,
        out_specs=[any_spec] * 7 + [vmem_spec] + [any_spec] * 2,
        scratch_shapes=[
            pltpu.VMEM((2, width, 4 * width), BF16),
            pltpu.VMEM((2, hidden_half, width), BF16),
            pltpu.VMEM((2, 2, width), F32),
            item_rows,
            item_rows,
            item_rows,
            pltpu.VMEM((items, 2, rows, 2 * width), BF16),
            item_rows,
            item_rows,
            item_rows,
            item_rows,
            item_rows,
            item_rows,
            pltpu.VMEM((rows, 2 * hidden_half), BF16),
            pltpu.VMEM((rows, 2 * hidden_half), BF16),
            pltpu.VMEM((items, rows, 2 * hidden_half), BF16),
            pltpu.VMEM((items, rows, 128), F32),
            pltpu.VMEM((items, toks, 128), F32),
            pltpu.VMEM((items, 1, 2 * toks), F32),
            pltpu.VMEM((items, MEM_PAD, 128), F32),
            pltpu.VMEM((2, items, MEM_PAD, width), BF16),
            pltpu.VMEM((items, MEM_PAD, width), BF16),
            pltpu.VMEM((2, quads, rows, 2 * quad), BF16),
            pltpu.VMEM((2, quads, rows, 2 * quad), BF16),
            pltpu.VMEM((rows, width), F32),
            pltpu.VMEM((rows, width), BF16),
            pltpu.VMEM((2, 2, width), F32),
            pltpu.VMEM((2, width), F32),
            pltpu.VMEM((quads, 4 * rows, 2 * toks), BF16),
            pltpu.VMEM((quads, rows, 8 * MEM_PAD), BF16),
            dma((4,)), dma((5,)), dma((5,)),
            two, one, one, two, two,
            two, two,
            two, two,
            two, two,
            one, one, one, one,
            dma((quads, items)), dma((quads, items)),
            dma(()), dma(()),
        ]
        + [dma((KINDS, items))] * 3,
        compiler_params=pltpu.CompilerParams(
            collective_id=0, has_side_effects=True, vmem_limit_bytes=61 * 1024 * 1024
        ),
    )(tokens, cotangent, first, down, docs, resets, gain, shift)


def reduce_kernel(
    chunks,
    sx1, sx2, sr, sg, sd, norm_part,
    sums, norm_out,
    x1, x2, rr, gg, dd, work, done, got_u, got_uz, got_vz, got_vy, norms,
    right_sem, left_sem, out_sem, u_s, u_r, uz_s, uz_r, vz_s, vz_r, vy_s, vy_r, vg_s, vg_r,
    uzg_s, uzg_r, vzg_s, vzg_r, ug_s, ug_r, n_s, n_r,
):
    lines = 4
    d = lax.axis_index("dp")
    y = lax.rem(d, 2)
    z = lax.div(d, 2)
    dp = lax.axis_size("dp")
    width = sd.shape[1]
    half = width // 2
    part = width // chunks
    hr = part // 2
    lane_group = 128
    per_group = lane_group // part
    y_peer = {"dp": z * 2 + (1 - y)}

    def remote(src, dst, send, recv, peer):
        return pltpu.make_async_remote_copy(
            src_ref=src, dst_ref=dst, send_sem=send, recv_sem=recv,
            device_id=peer, device_id_type=MESH,
        )

    def other(step):
        return {"dp": lax.rem(d + step, dp)}

    barrier = pltpu.get_barrier_semaphore()
    for step in range(1, dp):
        pl.semaphore_signal(barrier, inc=1, device_id=other(step), device_id_type=MESH)

    lane_groups = width // lane_group
    right_loads = [(sd, dd)] + [
        (sr.at[:, b * width : (b + 1) * width], rr.at[:, b * width : (b + 1) * width])
        for b in range(4)
    ]

    def right_load(k):
        src, dst = right_loads[k]
        return pltpu.make_async_copy(src, dst, right_sem.at[k])

    def left_load(which, group):
        src, dst, low = ((sg, gg, 0), (sg, gg, width), (sx2, x2, 0), (sx1, x1, 0))[which]
        cols = pl.ds(pl.multiple_of(low + group * lane_group, lane_group), lane_group)
        return pltpu.make_async_copy(src.at[:, cols], dst.at[:, cols], left_sem.at[which, group])

    right_load(0).start()
    left_load(0, 0).start()
    left_load(1, 0).start()
    left_load(2, 0).start()
    right_load(4).start()
    left_load(3, 0).start()
    for k in range(1, 4):
        right_load(k).start()
    for group in range(1, lane_groups):
        for which in range(4):
            left_load(which, group).start()

    norms[d] = norm_part[...]
    pl.semaphore_wait(barrier, dp - 1)

    def norm_copy(step):
        return remote(norms.at[d], norms.at[d], n_s.at[step - 1], n_r.at[step - 1], other(step))

    def norm_arrival(step):
        source = lax.rem(d + dp - step, dp)
        return remote(
            norms.at[source], norms.at[source], n_s.at[step - 1], n_r.at[step - 1], other(step)
        )

    for step in range(1, dp):
        norm_copy(step).start()

    def column_half(h):
        return pl.ds(pl.multiple_of(h * half, 128), half)

    mine, theirs = column_half(y), column_half(1 - y)

    def place(flow):
        return z if flow == 0 else lines - 1 - z

    def onward(flow):
        step = -1 if flow == 0 else 1
        return {"dp": (z + step) * 2 + y}

    def back(flow):
        step = 1 if flow == 0 else -1
        return {"dp": (z + step) * 2 + y}

    def rows_of(flow):
        return slice(flow * hr, (flow + 1) * hr)

    def u_copy(k):
        return remote(
            work.at[k, 0:3, :, theirs], got_u.at[k], u_s.at[k], u_r.at[k], y_peer
        )

    def uz_copy(flow, k):
        return remote(
            work.at[k, 0:3, rows_of(flow), mine], got_uz.at[flow, k],
            uz_s.at[flow, k], uz_r.at[flow, k], onward(flow),
        )

    def vz_copy(flow, k):
        return remote(
            work.at[k, 3:6, rows_of(flow), :], got_vz.at[flow, k],
            vz_s.at[flow, k], vz_r.at[flow, k], onward(flow),
        )

    def vy_copy(flow, k):
        return remote(
            work.at[k, 3:6, rows_of(flow), theirs], got_vy.at[k], vy_s.at[k], vy_r.at[k], y_peer
        )

    def vg_copy(flow, k, cols):
        spot = done.at[k, 3:6, rows_of(flow), cols]
        return remote(spot, spot, vg_s.at[k], vg_r.at[k], y_peer)

    def uzg_copy(flow, k):
        spot = done.at[k, 0:3, rows_of(flow), mine]
        return remote(spot, spot, uzg_s.at[flow, k], uzg_r.at[flow, k], back(flow))

    def vzg_copy(flow, k):
        spot = done.at[k, 3:6, rows_of(flow), :]
        return remote(spot, spot, vzg_s.at[flow, k], vzg_r.at[flow, k], back(flow))

    def ug_copy(flow, k, cols):
        spot = done.at[k, 0:3, rows_of(flow), cols]
        return remote(spot, spot, ug_s.at[flow, k], ug_r.at[flow, k], y_peer)

    def out_copy(k):
        return pltpu.make_async_copy(done.at[k], sums.at[k], out_sem.at[k])

    def plus(a, b):
        return (a.astype(F32) + b.astype(F32)).astype(BF16)

    def ready(k, low=0):
        return (k >= low) & (k < chunks)

    def store_chunks(group, block, value):
        for e in range(per_group):
            work[group * per_group + e, block] = value[e * part : (e + 1) * part]

    def second_half(r):
        group = lax.div(r + per_group - 1, per_group)
        cols = pl.ds(pl.multiple_of(group * lane_group, lane_group), lane_group)
        gcols = pl.ds(pl.multiple_of(width + group * lane_group, lane_group), lane_group)

        @pl.when(r == 0)
        def _():
            right_load(0).wait()

        left_load(0, group).wait()
        store_chunks(group, 4, dot(gg[:, cols], dd[...], 0, 0).astype(BF16))
        left_load(1, group).wait()
        store_chunks(group, 5, dot(gg[:, gcols], dd[...], 0, 0).astype(BF16))
        left_load(2, group).wait()

        @pl.when(r == 0)
        def _():
            right_load(4).wait()

        store_chunks(group, 3, dot(x2[:, cols], rr[:, 3 * width :], 0, 0).astype(BF16))

    def round_step(r, carry):
        @pl.when(r == 0)
        def _():
            second_half(r)

        for flow in range(2):
            p = place(flow)
            k = r - (lines - 1 - p)
            rows = rows_of(flow)

            @pl.when(ready(k))
            def _():
                @pl.when(p < lines - 1)
                def _():
                    vz_copy(flow, k).wait_recv()
                    work[k, 3:6, rows, :] = plus(work[k, 3:6, rows, :], got_vz[flow, k])

                @pl.when(p > 0)
                def _():
                    vz_copy(flow, k).start()

                @pl.when(p == 0)
                def _():
                    vy_copy(flow, k).start()

        @pl.when((lax.rem(r, per_group) == 0) & (r < chunks))
        def _():
            group = lax.div(r, per_group)
            cols = pl.ds(pl.multiple_of(group * lane_group, lane_group), lane_group)
            left_load(3, group).wait()
            for b in range(3):

                @pl.when(r == 0)
                def _():
                    right_load(1 + b).wait()

                store_chunks(
                    group, b,
                    dot(x1[:, cols], rr[:, b * width : (b + 1) * width], 0, 0).astype(BF16),
                )

        @pl.when(ready(r))
        def _():
            u_copy(r).start()

        @pl.when((lax.rem(r, per_group) == per_group - 1) & (r + 1 < chunks))
        def _():
            second_half(r)

        @pl.when(ready(r - 1))
        def _():
            k = r - 1
            u_copy(k).wait_recv()
            work[k, 0:3, :, mine] = plus(work[k, 0:3, :, mine], got_u[k])

        for flow in range(2):
            p = place(flow)
            k = r - 1 - (lines - 1 - p)
            rows = rows_of(flow)

            @pl.when(ready(k))
            def _():
                @pl.when(p < lines - 1)
                def _():
                    uz_copy(flow, k).wait_recv()
                    total = plus(work[k, 0:3, rows, mine], got_uz[flow, k])

                    @pl.when(p > 0)
                    def _():
                        work[k, 0:3, rows, mine] = total

                    @pl.when(p == 0)
                    def _():
                        done[k, 0:3, rows, mine] = total

                @pl.when(p > 0)
                def _():
                    uz_copy(flow, k).start()

                @pl.when(p == 0)
                def _():
                    uzg_copy(flow, k).start()
                    ug_copy(flow, k, mine).start()

        for flow in range(2):
            p = place(flow)
            rows = rows_of(flow)

            @pl.when((p == 0) & ready(r - lines))
            def _():
                k = r - lines
                vy_copy(flow, k).wait_recv()
                done[k, 3:6, rows, mine] = plus(work[k, 3:6, rows, mine], got_vy[k])
                vg_copy(flow, k, mine).start()

            @pl.when((p == 0) & ready(r - lines - 1))
            def _():
                k = r - lines - 1
                vg_copy(flow, k, theirs).wait_recv()
                vzg_copy(flow, k).start()

        for flow in range(2):
            p = place(flow)
            k = r - lines - p

            @pl.when((p > 0) & ready(k))
            def _():
                uzg_copy(flow, k).wait_recv()

                @pl.when(p < lines - 1)
                def _():
                    uzg_copy(flow, k).start()

                ug_copy(flow, k, mine).start()

        for flow in range(2):
            p = place(flow)
            k = r - lines - 1 - p

            @pl.when((p > 0) & ready(k))
            def _():
                vzg_copy(flow, k).wait_recv()

                @pl.when(p < lines - 1)
                def _():
                    vzg_copy(flow, k).start()

            @pl.when(ready(k))
            def _():
                ug_copy(flow, k, theirs).wait_recv()

        @pl.when(ready(r - 2 * lines))
        def _():
            out_copy(r - 2 * lines).start()

        return carry

    lax.fori_loop(0, chunks + 2 * lines, round_step, 0)

    for step in range(1, dp):
        norm_arrival(step).wait_recv()
    total = norms[0]
    for e in range(1, dp):
        total = total + norms[e]
    norm_out[...] = total

    def drain(k, carry):
        out_copy(k).wait()
        u_copy(k).wait_send()
        for flow in range(2):
            p = place(flow)
            ug_copy(flow, k, mine).wait_send()

            @pl.when(p > 0)
            def _():
                vz_copy(flow, k).wait_send()
                uz_copy(flow, k).wait_send()

            @pl.when(p < lines - 1)
            def _():
                uzg_copy(flow, k).wait_send()
                vzg_copy(flow, k).wait_send()

            @pl.when(p == 0)
            def _():
                vy_copy(flow, k).wait_send()
                vg_copy(flow, k, mine).wait_send()

        return carry

    lax.fori_loop(0, chunks, drain, 0)
    for step in range(1, dp):
        norm_copy(step).wait_send()


def sum_weights(dp, sx1, sx2, sr, sg, sd, norm_part):
    total, width = sx1.shape
    chunks = 12
    part = width // chunks
    half = width // 2
    any_spec = pl.BlockSpec(memory_space=pl.ANY)
    vmem_spec = pl.BlockSpec(memory_space=pltpu.VMEM)
    dma = pltpu.SemaphoreType.DMA
    one, two = dma((chunks,)), dma((2, chunks))
    return pl.pallas_call(
        partial(reduce_kernel, chunks),
        out_shape=(
            jax.ShapeDtypeStruct((chunks, 6, part, width), BF16),
            jax.ShapeDtypeStruct((2, width), F32),
        ),
        in_specs=[any_spec] * 5 + [vmem_spec],
        out_specs=[any_spec, vmem_spec],
        scratch_shapes=[
            pltpu.VMEM((total, width), BF16),
            pltpu.VMEM((total, width), BF16),
            pltpu.VMEM((total, 4 * width), BF16),
            pltpu.VMEM((total, 2 * width), BF16),
            pltpu.VMEM((total, width), BF16),
            pltpu.VMEM((chunks, 6, part, width), BF16),
            pltpu.VMEM((chunks, 6, part, width), BF16),
            pltpu.VMEM((chunks, 3, part, half), BF16),
            pltpu.VMEM((2, chunks, 3, part // 2, half), BF16),
            pltpu.VMEM((2, chunks, 3, part // 2, width), BF16),
            pltpu.VMEM((chunks, 3, part // 2, half), BF16),
            pltpu.VMEM((dp, 2, width), F32),
            dma((5,)),
            dma((4, width // 128)),
            one,
            one, one,
            two, two,
            two, two,
            one, one,
            one, one,
            two, two,
            two, two,
            two, two,
            dma((dp - 1,)), dma((dp - 1,)),
        ],
        compiler_params=pltpu.CompilerParams(
            collective_id=1, has_side_effects=True, vmem_limit_bytes=60 * 1024 * 1024
        ),
    )(sx1, sx2, sr, sg, sd, norm_part)


def finish_kernel(sums, out, gin, norms, first_grad, down_grad, out_copy, gin_copy, gain, shift):
    width = sums.shape[3]
    for b in range(4):
        first_grad[:, b * width : (b + 1) * width] = sums[0, b].astype(F32)
    for b in range(2):
        down_grad[b] = sums[0, 4 + b].astype(F32)
    out_copy[...] = out[...]
    gin_copy[...] = gin[...]
    gain[...] = norms[0:1]
    shift[...] = norms[1:2]


def finish(sums, out, gin, norms):
    chunks, _, part, width = sums.shape
    total = out.shape[0]
    blocks = 8
    tokens = pl.BlockSpec((total // blocks, width), lambda k: (jnp.minimum(k, blocks - 1), 0))
    whole = pl.BlockSpec((1, width), lambda k: (0, 0))
    return pl.pallas_call(
        finish_kernel,
        grid=(chunks,),
        out_shape=(
            jax.ShapeDtypeStruct((width, 4 * width), F32),
            jax.ShapeDtypeStruct((2, width, width), F32),
            jax.ShapeDtypeStruct(out.shape, BF16),
            jax.ShapeDtypeStruct(gin.shape, BF16),
            jax.ShapeDtypeStruct((1, width), F32),
            jax.ShapeDtypeStruct((1, width), F32),
        ),
        in_specs=[
            pl.BlockSpec((1, 6, part, width), lambda k: (k, 0, 0, 0)),
            tokens,
            tokens,
            pl.BlockSpec((2, width), lambda k: (0, 0)),
        ],
        out_specs=[
            pl.BlockSpec((part, 4 * width), lambda k: (k, 0)),
            pl.BlockSpec((2, part, width), lambda k: (0, k, 0)),
            tokens,
            tokens,
            whole,
            whole,
        ],
    )(sums, out, gin, norms)


def shards(
    tokens, doc_ids, reset_flags, first_weights, down_halves, norm_gain, norm_bias, cotangent
):
    n, length, width = tokens.shape
    items = n * NSEG
    rows = length // NSEG // 2 + MEM_PAD
    out, gin, sx1, sx2, sr, sg, sd, norm_grad, _, _ = run_layers(
        n, NSEG, H, tokens, cotangent, first_weights, down_halves,
        doc_ids, reset_flags, norm_gain, norm_bias,
    )
    total = 2 * items * rows
    sx1, sx2, sd = (a.reshape(total, width) for a in (sx1, sx2, sd))
    sr = sr.reshape(total, 4 * width)
    sg = sg.reshape(total, -1)

    dp = lax.axis_size("dp")
    if dp == 8:
        sums, norm_grad = sum_weights(dp, sx1, sx2, sr, sg, sd, norm_grad)
        first_grad, down_grad, out, gin, gain_grad, shift_grad = finish(
            sums, out.reshape(-1, width), gin.reshape(-1, width), norm_grad
        )
        down_grad = down_grad.reshape(-1, width)
        out, gin = (a.reshape(n, length, width) for a in (out, gin))
    else:

        def weight_grad(left, right):
            return jnp.einsum("rd,re->de", left, right, preferred_element_type=F32).astype(BF16)

        first_grad = jnp.concatenate(
            [weight_grad(sx1, sr[:, : 3 * width]), weight_grad(sx2, sr[:, 3 * width :])], axis=1
        )
        down_grad = weight_grad(sg, sd)
        first_grad, down_grad = lax.psum((first_grad, down_grad), "dp")
        norm_grad = lax.psum(norm_grad, "dp")
        gain_grad, shift_grad = norm_grad[0:1], norm_grad[1:2]
    return (
        out[None],
        gin[None],
        first_grad.astype(F32)[None],
        down_grad.astype(F32)[None],
        gain_grad,
        shift_grad,
    )


def solution(mesh):
    in_specs = (
        P("dp", None, None),
        P("dp", None),
        P("dp", None),
        P("section", None, None),
        P("section", None, None),
        P("section", None),
        P("section", None),
        P("dp", None, None),
    )
    out_specs = (
        P("section", "dp", None, None),
        P("section", "dp", None, None),
        P("section", None, None),
        P("section", None, None),
        P("section", None),
        P("section", None),
    )
    return jax.shard_map(shards, mesh=mesh, in_specs=in_specs, out_specs=out_specs, check_vma=False)
```

```python
from functools import partial

import jax
import jax.numpy as jnp
from jax import lax
from jax.experimental import pallas as pl
from jax.experimental.pallas import tpu as pltpu
from jax.sharding import PartitionSpec as P

H = 12
M = 20
NSEG = 2
MEM_PAD = 16
NORM_EPSILON = 1e-05
MASKED_SCORE = -1000000000.0
ABSENT_SCORE = -3e38
MESH = pl.DeviceIdType.MESH
BF16 = jnp.bfloat16
F32 = jnp.float32

OUT_ATT, OUT_FF, GIN_ATT, GIN_FF = 0, 1, 2, 3
S_X0, S_CTX, S_DQ, S_DKV, S_DATT, S_GLO, S_DFF0 = 4, 5, 6, 7, 8, 9, 10
S_Y1, S_Y2, S_DU, S_GHI, S_DFF1 = 11, 12, 13, 14, 15
KINDS = 16


def dot(a, b, lhs_dim=1, rhs_dim=0):
    return lax.dot_general(
        a, b, (((lhs_dim,), (rhs_dim,)), ((), ())), preferred_element_type=F32
    )


def normalize(summed):
    mean = jnp.mean(summed, axis=-1, keepdims=True)
    centered = summed - mean
    var = jnp.mean(centered * centered, axis=-1, keepdims=True)
    inv = lax.rsqrt(var + NORM_EPSILON)
    return centered * inv, inv


def group_of(shape, dim, size):
    index = lax.broadcasted_iota(jnp.int32, shape, dim)
    return lax.shift_right_logical(index, size.bit_length() - 1)


def spread(values, groups):
    result = values[-1]
    for h in range(len(values) - 1):
        result = jnp.where(groups == h, values[h], result)
    return result


def layers_kernel(
    n, nseg, heads,
    tokens, cotangent, first, down, docs, resets, gain, shift,
    out, gin, sx1, sx2, sr, sg, sd, norm_grad, ptok, pmem,
    wf, wd, nrm, x0, xo, q, kv, ctx, natt, yatt, nff, yd, gy, g, gpb, gp, stats, qdoc, kdoc, keep,
    memin, mgin, dkvs, dkvin, dhb, kvb, acc, accp, tprob, mprob,
    wl, ws, wr, tok_sem, cot_sem, gp_sem, qkv_sem, pw_sem, pr_sem, fs_sem, fr_sem, xs_sem, xr_sem,
    ms_sem, mr_sem, gs_sem, gr_sem, hs_sem, hr_sem, ds_sem, dr_sem, as_sem, ar_sem,
    lsem, ssem, rsem,
):
    items = n * nseg
    section = lax.axis_index("section")
    c = lax.rem(section, 2)
    x = lax.div(section, 2)
    core_peer = {"section": x * 2 + (1 - c)}
    chip_peer = {"section": (1 - x) * 2 + c}
    cross_peer = {"section": (1 - x) * 2 + (1 - c)}
    rows, width = x0.shape[1:]
    toks = rows - MEM_PAD
    seg_len = 2 * toks
    hidden_half = wd.shape[1]
    wide = 3 * width
    head_dim = width // heads
    quad = 4 * head_dim
    quads = heads // 4
    mem_keys = 2 * MEM_PAD
    scale = head_dim ** (-0.5)
    qb = gpb.at[:, 0:width]
    ctxb = gpb.at[:, width : 2 * width]
    dqb = gpb.at[:, 0:width]
    gab = gpb.at[:, width : 2 * width]
    dctx = gpb.at[:, 2 * width : wide]

    def remote(src, dst, send, recv, peer):
        return pltpu.make_async_remote_copy(
            src_ref=src, dst_ref=dst, send_sem=send, recv_sem=recv,
            device_id=peer, device_id_type=MESH,
        )

    barrier = pltpu.get_barrier_semaphore()
    pl.semaphore_signal(barrier, inc=1, device_id=core_peer, device_id_type=MESH)
    pl.semaphore_signal(barrier, inc=1, device_id=chip_peer, device_id_type=MESH)
    pl.semaphore_signal(barrier, inc=1, device_id=cross_peer, device_id_type=MESH)

    def token_rows(ref, i, core=None):
        core = c if core is None else core
        return ref.at[lax.rem(i, n), pl.ds(lax.div(i, n) * seg_len + core * toks, toks), :]

    def token_copy(which, i):
        if which == 0:
            src, dst = token_rows(tokens, i), x0.at[i, 0:toks, :]
        else:
            src, dst = token_rows(tokens, i, 1 - c), xo.at[lax.rem(i, n), 0:toks, :]
        return pltpu.make_async_copy(src, dst, tok_sem.at[which, i])

    def cot_copy(i):
        return pltpu.make_async_copy(
            token_rows(cotangent, i), gy.at[i, 0:toks, :], cot_sem.at[i]
        )

    def weight_piece(k):
        if k == 0:
            return first.at[0, :, width:wide], wf.at[c, :, width:wide]
        if k == 1:
            return first.at[0, :, 0:width], wf.at[c, :, 0:width]
        if k == 2:
            return first.at[0, :, wide:], wf.at[c, :, wide:]
        return down.at[0], wd.at[c]

    def weight_local(k):
        src, dst = weight_piece(k)
        return pltpu.make_async_copy(src, dst, wl.at[k])

    def weight_remote(k):
        if k == 4:
            return remote(nrm.at[c], nrm.at[c], ws.at[4], wr.at[4], core_peer)
        src, dst = weight_piece(k)
        return remote(src, dst, ws.at[k], wr.at[k], core_peer)

    nrm[c, 0:1, :] = gain[...]
    nrm[c, 1:2, :] = shift[...]
    weight_local(0).start()

    @pl.when(x == 0)
    def _():
        token_copy(0, 0).start()
        token_copy(1, 0).start()

    pl.semaphore_wait(barrier, 3)
    for k in range(5):
        weight_remote(k).start()
    for k in range(1, 4):
        weight_local(k).start()
    for i in range(items):
        if i > 0:

            @pl.when(x == 0)
            def _():
                token_copy(0, i).start()
                if i < n:
                    token_copy(1, i).start()

        @pl.when(x == 1)
        def _():
            cot_copy(i).start()

    def wait_first_of(core, ks):
        @pl.when(c == core)
        def _():
            for k in ks:
                weight_local(k).wait()

        @pl.when(c != core)
        def _():
            for k in ks:
                weight_remote(k).wait_recv()

    for i in range(items):
        seq, seg = i % n, i // n
        own = pl.ds(pl.multiple_of(seg * seg_len + c * toks, toks), toks)
        others = pl.ds(pl.multiple_of(seg * seg_len + (1 - c) * toks, toks), toks)
        own_row = docs[seq : seq + 1, own].astype(F32)
        kdoc[i, :, 0:toks] = own_row
        kdoc[i, :, toks:] = docs[seq : seq + 1, others].astype(F32)
        qdoc[i] = jnp.transpose(jnp.broadcast_to(own_row, (128, toks)))
        if seg > 0:
            flag = resets[seg - 1 : seg, seq : seq + 1].astype(F32)
            keep[i] = jnp.broadcast_to(1.0 - flag, (MEM_PAD, 128))

    def routed(kind, i):
        block = i * 2 + c
        sec = 0
        if kind == OUT_ATT:
            src, dst = yatt.at[i, 0:toks, :], token_rows(out, i)
        elif kind == OUT_FF:
            src, dst, sec = yd.at[i, 0:toks, :], token_rows(out, i), 1
        elif kind == GIN_ATT:
            src, dst = yd.at[i, 0:toks, :], token_rows(gin, i)
        elif kind == GIN_FF:
            src, dst, sec = gab.at[0:toks, :], token_rows(gin, i), 1
        elif kind == S_X0:
            src, dst = x0.at[i], sx1.at[block]
        elif kind == S_CTX:
            src, dst = ctx.at[i], sx2.at[block]
        elif kind == S_DQ:
            src, dst = dqb, sr.at[block, :, 0:width]
        elif kind == S_DKV:
            src, dst = kv.at[i, 0], sr.at[block, :, width:wide]
        elif kind == S_DATT:
            src, dst = natt.at[i], sr.at[block, :, wide:]
        elif kind == S_GLO:
            src, dst = g.at[:, 0:hidden_half], sg.at[block]
        elif kind == S_DFF0:
            src, dst = nff.at[i], sd.at[block]
        elif kind == S_Y1:
            src, dst, sec = yatt.at[i], sx1.at[block], 1
        elif kind == S_Y2:
            src, dst, sec = yatt.at[i], sx2.at[block], 1
        elif kind == S_DU:
            src, dst, sec = gp.at[i], sr.at[block], 1
        elif kind == S_GHI:
            src, dst, sec = g.at[:, hidden_half:], sg.at[block], 1
        else:
            src, dst, sec = nff.at[i], sd.at[block], 1
        return src, dst, sec

    def route_local(kind, i):
        src, dst, _ = routed(kind, i)
        return pltpu.make_async_copy(src, dst, lsem.at[kind, i])

    def route_away(kind, i):
        src, dst, _ = routed(kind, i)
        return remote(src, dst, ssem.at[kind, i], rsem.at[kind, i], core_peer)

    def route(kind, i):
        sec = routed(kind, i)[2]

        @pl.when(c == sec)
        def _():
            route_local(kind, i).start()

        @pl.when(c != sec)
        def _():
            route_away(kind, i).start()

    def route_sent(kind, i):
        sec = routed(kind, i)[2]

        @pl.when(c == sec)
        def _():
            route_local(kind, i).wait()

        @pl.when(c != sec)
        def _():
            route_away(kind, i).wait_send()

    def route_received(kind, i):
        @pl.when(c == routed(kind, i)[2])
        def _():
            route_away(kind, i).wait_recv()

    def qkv_copies(i):
        return [
            pltpu.make_async_copy(qb, q.at[i], qkv_sem.at[0, i]),
            pltpu.make_async_copy(kvb, kv.at[i], qkv_sem.at[1, i]),
        ]

    def gp_copy(i):
        return pltpu.make_async_copy(gpb, gp.at[i], gp_sem.at[i])

    def prob_copies(i, back):
        pairs = ((tprob, ptok.at[i]), (mprob, pmem.at[i]))
        if back:
            return [
                pltpu.make_async_copy(dst, src, pr_sem.at[e, i])
                for e, (src, dst) in enumerate(pairs)
            ]
        return [
            pltpu.make_async_copy(src, dst, pw_sem.at[e, i]) for e, (src, dst) in enumerate(pairs)
        ]

    cut = rows // 32 * 16

    def piece(p):
        return slice(0, cut) if p == 0 else slice(cut, rows)

    def x_copy(p, i):
        return remote(
            yd.at[i, piece(p)], x0.at[i, piece(p)], xs_sem.at[p, i], xr_sem.at[p, i], chip_peer
        )

    def pass_copy(p, i):
        return remote(
            x0.at[i, piece(p)], xo.at[lax.rem(i, n), piece(p)],
            fs_sem.at[p, i], fr_sem.at[p, i], core_peer,
        )

    def mem_copy(which, i):
        return remote(
            yd.at[i, toks:rows, :], memin.at[which, i], ms_sem.at[which, i],
            mr_sem.at[which, i], cross_peer if which else chip_peer,
        )

    def gy_copy(i):
        return remote(yd.at[i], gy.at[i], gs_sem.at[i], gr_sem.at[i], chip_peer)

    def mg_copy(i):
        return remote(
            yd.at[i, toks:rows, :], mgin.at[i], hs_sem.at[i], hr_sem.at[i], chip_peer
        )

    def dkv_copy(j, i, slot):
        return remote(
            dkvs.at[1, j], dkvin.at[slot, j], ds_sem.at[j, i], dr_sem.at[j, i], core_peer
        )

    head_lanes = group_of((rows, quad), 1, head_dim)
    mem_lanes = group_of((rows, 4 * mem_keys), 1, mem_keys)
    key_lane = lax.broadcasted_iota(jnp.int32, (rows, 4 * mem_keys), 1)
    mem_valid = lax.rem(key_lane, MEM_PAD) < M // 2
    diagonal = group_of((4 * mem_keys, quad), 0, mem_keys) == group_of(
        (4 * mem_keys, quad), 1, head_dim
    )
    stat_lane = lax.broadcasted_iota(jnp.int32, (rows, 128), 1)

    def stacked(block):
        return jnp.concatenate(
            [jnp.where(head_lanes == h, block, BF16(0)) for h in range(4)], axis=0
        )

    def head_rows(block):
        return [block[h * rows : (h + 1) * rows] for h in range(4)]

    def token_and_memory(ref, low):
        cols = slice(low, low + quad)
        tok = jnp.concatenate([ref[0, 0:toks, cols], ref[1, 0:toks, cols]], axis=0)
        mem = jnp.concatenate([ref[0, toks:, cols], ref[1, toks:, cols]], axis=0)
        return tok, jnp.where(diagonal, jnp.concatenate([mem] * 4, axis=0), BF16(0))

    def only_same_document(s, i):
        mine = jnp.concatenate([qdoc[i]] * (seg_len // 128), axis=1)
        same = jnp.where(mine == kdoc[i], s[0:toks], MASKED_SCORE)
        return jnp.concatenate([same, s[toks:]], axis=0)

    def memory_scores(q4, mem_k):
        return jnp.where(mem_valid, dot(q4, mem_k, 1, 1), ABSENT_SCORE)

    def attend(i):
        own = [mem_lanes == h for h in range(4)]

        def scores(j):
            q4 = qb[:, j * quad : (j + 1) * quad]
            tok_k, mem_k = token_and_memory(kvb, j * quad)
            return dot(stacked(q4), tok_k, 1, 1), memory_scores(q4, mem_k)

        st = jnp.zeros((rows, 128), F32)
        following = scores(0)
        for j in range(quads):
            s, sm = following
            if j + 1 < quads:
                following = scores(j + 1)
            s = [only_same_document(part, i) for part in head_rows(s)]
            peaks = [
                jnp.max(
                    jnp.concatenate([s[h], jnp.where(own[h], sm, ABSENT_SCORE)], axis=1),
                    axis=1, keepdims=True,
                )
                for h in range(4)
            ]
            pm = jnp.exp(sm - spread(peaks, mem_lanes))
            mprob[j] = pm.astype(BF16)
            totals, probs = [], []
            for h in range(4):
                p = jnp.exp(s[h] - peaks[h])
                probs.append(p.astype(BF16))
                tprob[j, h * rows : (h + 1) * rows, :] = probs[h]
                both = jnp.concatenate([p, jnp.where(own[h], pm, 0.0)], axis=1)
                totals.append(1.0 / jnp.sum(both, axis=1, keepdims=True))
                st = jnp.where(stat_lane == 4 * j + h, totals[h], st)
            tok_v, mem_v = token_and_memory(kvb, width + j * quad)
            o = spread(head_rows(dot(jnp.concatenate(probs, axis=0), tok_v)), head_lanes)
            o = o + dot(pm.astype(BF16), mem_v)
            ctxb[:, j * quad : (j + 1) * quad] = (o * spread(totals, head_lanes)).astype(BF16)
        stats[i] = st
        ctx[i] = ctxb[...]

    def forward_tick(t, carry):
        i = t - x

        @pl.when((i >= 0) & (i < items))
        def _():
            @pl.when(x == 0)
            def _():
                for which, rows_ref in enumerate((x0.at[i], xo.at[lax.rem(i, n)])):
                    token_copy(which, i).wait()

                    @pl.when(i < n)
                    def _():
                        rows_ref[toks:rows, :] = jnp.zeros((MEM_PAD, width), BF16)

                    @pl.when(i >= n)
                    def _():
                        mem_copy(which, i - n).wait_recv()
                        rows_ref[toks:rows, :] = jnp.where(
                            keep[i][:, 0:1] > 0.0, memin[which, i - n], jnp.zeros((), BF16)
                        )

            @pl.when(x == 1)
            def _():
                for p in range(2):
                    x_copy(p, i).wait_recv()
                    pass_copy(p, i).start()

            @pl.when(i == 0)
            def _():
                wait_first_of(0, (0,))

            @pl.when(i > 0)
            def _():
                qkv_copies(i - 1)[1].wait()
                gp_copy(i - 1).wait()

            kvb[0] = dot(x0[i], wf[0, :, width:wide]).astype(BF16)

            @pl.when(i == 0)
            def _():
                wait_first_of(0, (1,))

            qb[...] = dot(x0[i], wf[0, :, 0:width]).astype(BF16) * BF16(scale)

            @pl.when(x == 1)
            def _():
                for p in range(2):
                    pass_copy(p, i).wait_recv()

            kvb[1] = dot(xo[lax.rem(i, n)], wf[0, :, width:wide]).astype(BF16)
            for copy in qkv_copies(i):
                copy.start()

            @pl.when((x == 0) & (i < items - n))
            def _():
                token_copy(1, i + n).start()

            @pl.when(i > 0)
            def _():
                for copy in prob_copies(i - 1, False):
                    copy.wait()

            attend(i)
            for copy in prob_copies(i, False):
                copy.start()

            @pl.when(i == 0)
            def _():
                wait_first_of(0, (2,))
                weight_remote(4).wait_recv()

            normed, inv = normalize(dot(ctxb[...], wf[0, :, wide:]) + x0[i].astype(F32))
            natt[i] = normed.astype(BF16)
            stats[i] = jnp.where(stat_lane == heads, inv, stats[i])
            yatt[i] = (normed * nrm[0, 0:1, :] + nrm[0, 1:2, :]).astype(BF16)

            @pl.when(i == 0)
            def _():
                wait_first_of(1, (0, 1, 2))

            @pl.when(i > 0)
            def _():
                route_sent(S_GLO, i - 1)
                route_sent(S_GHI, i - 1)

            qkv_copies(i)[0].wait()

            for part in range(2):
                cols = slice(part * hidden_half, (part + 1) * hidden_half)
                u = dot(yatt[i], wf[1, :, cols])
                cdf = 0.5 + 0.5 * lax.erf(u * 0.7071067811865476)
                pdf = 0.3989422804014327 * jnp.exp(-0.5 * u * u)
                g[:, cols] = (u * cdf).astype(BF16)
                gpb[:, cols] = (cdf + u * pdf).astype(BF16)
            @pl.when(i == 0)
            def _():
                wait_first_of(0, (3,))
                wait_first_of(1, (3,))

            normed, inv = normalize(
                dot(g[:, 0:hidden_half], wd[0])
                + dot(g[:, hidden_half:], wd[1])
                + yatt[i].astype(F32)
            )
            yd[i] = (normed * nrm[1, 0:1, :] + nrm[1, 1:2, :]).astype(BF16)

            @pl.when(x == 0)
            def _():
                for p in range(2):
                    x_copy(p, i).start()

            @pl.when((x == 1) & (i < items - n))
            def _():
                for which in range(2):
                    mem_copy(which, i).start()

            gp_copy(i).start()
            for kind in (S_GLO, S_GHI, S_X0, S_CTX, OUT_ATT, S_Y1, S_Y2, OUT_FF):
                route(kind, i)
            nff[i] = normed.astype(BF16)
            stats[i] = jnp.where(stat_lane == heads + 1, inv, stats[i])

        return carry

    lax.fori_loop(0, items + 1, forward_tick, 0)

    def forward_sent(i):
        route_sent(OUT_FF, i)

        @pl.when(x == 0)
        def _():
            for p in range(2):
                x_copy(p, i).wait_send()

        @pl.when(x == 1)
        def _():
            for p in range(2):
                pass_copy(p, i).wait_send()

        @pl.when((x == 1) & (i < items - n))
        def _():
            for which in range(2):
                mem_copy(which, i).wait_send()

    for copy in prob_copies(items - 1, False) + qkv_copies(items - 1)[1:]:
        copy.wait()
    for copy in prob_copies(items - n, True):
        copy.start()
    gp_copy(items - 1).wait()
    acc[...] = jnp.zeros_like(acc)

    def norm_back(s, i, normed_ref):
        grad = (gy[i] if s else gab[...]).astype(F32)
        normed = normed_ref[i].astype(F32)
        inv = stats[i][:, heads + s : heads + s + 1]
        acc[s, 0:1, :] += jnp.sum(grad * normed, axis=0, keepdims=True)
        acc[s, 1:2, :] += jnp.sum(grad, axis=0, keepdims=True)
        scaled = grad * nrm[s, 0:1, :]
        row_term = jnp.mean(scaled, axis=1, keepdims=True)
        row_cross = jnp.mean(scaled * normed, axis=1, keepdims=True)
        dh = inv * (scaled - row_term - normed * row_cross)
        dhb[...] = dh
        normed_ref[i] = dh.astype(BF16)

    def attend_back(i, slot):
        def prob_grads(j):
            inverse = [stats[i][:, 4 * j + h : 4 * j + h + 1] for h in range(4)]
            c4 = dctx[:, j * quad : (j + 1) * quad].astype(F32) * spread(inverse, head_lanes)
            c4 = c4.astype(BF16)
            tok_v, mem_v = token_and_memory(kv.at[i], width + j * quad)
            return c4, dot(stacked(c4), tok_v, 1, 1), dot(c4, mem_v, 1, 1)

        following = prob_grads(0)
        for j in range(quads):
            c4, dp, dpm = following
            if j + 1 < quads:
                following = prob_grads(j + 1)
            cols = slice(j * quad, (j + 1) * quad)
            q4 = q[i, :, cols]
            tok_k, mem_k = token_and_memory(kv.at[i], j * quad)
            products = c4.astype(F32) * ctx[i, :, cols].astype(F32)
            dp = head_rows(dp)
            inner = [
                jnp.sum(jnp.where(head_lanes == h, products, 0.0), axis=1, keepdims=True)
                for h in range(4)
            ]
            dscores = [
                (tprob[j, h * rows : (h + 1) * rows, :].astype(F32) * (dp[h] - inner[h])).astype(BF16)
                for h in range(4)
            ]
            dsm = (mprob[j].astype(F32) * (dpm - spread(inner, mem_lanes))).astype(BF16)
            ct, qt = jnp.transpose(c4), jnp.transpose(q4)
            mine = [slice(h * head_dim, (h + 1) * head_dim) for h in range(4)]
            dv = [
                dot(ct[mine[h]], tprob[j, h * rows : (h + 1) * rows, :]).astype(BF16)
                for h in range(4)
            ]
            dk = [dot(qt[mine[h]], dscores[h]).astype(BF16) for h in range(4)]
            dv = jnp.transpose(jnp.concatenate(dv, axis=0))
            dk = jnp.transpose(jnp.concatenate(dk, axis=0))
            dscores = jnp.concatenate(dscores, axis=0)
            dq = spread(head_rows(dot(dscores, tok_k)), head_lanes) + dot(dsm, mem_k)
            dqb[:, cols] = (dq * scale).astype(BF16)
            dvm = jnp.where(diagonal, dot(mprob[j], c4, 0, 0), 0.0)
            dkm = jnp.where(diagonal, dot(dsm, q4, 0, 0), 0.0)
            dvm = sum(dvm[h * mem_keys : (h + 1) * mem_keys] for h in range(4))
            dkm = sum(dkm[h * mem_keys : (h + 1) * mem_keys] for h in range(4))
            for half, (tok_part, mem_part) in enumerate(((dk, dkm), (dv, dvm))):
                cols = slice(half * quad, (half + 1) * quad)
                for core in range(2):
                    dkvs[core, j, 0:toks, cols] = tok_part[
                        core * toks : (core + 1) * toks
                    ].astype(BF16)
                    dkvs[core, j, toks:rows, cols] = mem_part[
                        core * MEM_PAD : (core + 1) * MEM_PAD
                    ].astype(BF16)
            dkv_copy(j, i, slot).start()

    def gather_dkv(j, i, slot):
        dkv_copy(j, i, slot).wait_recv()
        both = (dkvs[0, j].astype(F32) + dkvin[slot, j].astype(F32)).astype(BF16)
        kv[i, 0, :, j * quad : (j + 1) * quad] = both[:, 0:quad]
        kv[i, 0, :, width + j * quad : width + (j + 1) * quad] = both[:, quad:]

    def dkv_back(i, low, high):
        return dot(kv[i, 0, :, low:high], wf[0, :, width + low : width + high], 1, 1) + dot(
            kv[i, 0, :, width + low : width + high],
            wf[0, :, 2 * width + low : 2 * width + high], 1, 1,
        )

    def item_of(r):
        return (nseg - 1 - lax.div(r, n)) * n + lax.rem(r, n)

    def backward_tick(t, carry):
        r = t - (1 - x)

        @pl.when((r >= 0) & (r < items))
        def _():
            i = item_of(r)
            slot = lax.rem(r, 2)

            @pl.when(x == 1)
            def _():
                cot_copy(i).wait()

                @pl.when(i >= items - n)
                def _():
                    gy[i, toks:rows, :] = jnp.zeros((MEM_PAD, width), BF16)

                @pl.when(i < items - n)
                def _():
                    mg_copy(i + n).wait_recv()
                    gy[i, toks:rows, :] = jnp.where(
                        keep[i + n][:, 0:1] > 0.0, mgin[i + n], jnp.zeros((), BF16)
                    )

            @pl.when(x == 0)
            def _():
                gy_copy(i).wait_recv()

            @pl.when(r > 0)
            def _():
                route_sent(S_DQ, item_of(r - 1))
                route_sent(GIN_FF, item_of(r - 1))

            norm_back(1, i, nff)
            for part in range(2):
                cols = slice(part * hidden_half, (part + 1) * hidden_half)
                dg = dot(nff[i], wd[part], 1, 1)
                gp[i, :, cols] = (dg * gp[i, :, cols].astype(F32)).astype(BF16)
            gab[...] = (dot(gp[i], wf[1], 1, 1) + dhb[...]).astype(BF16)
            norm_back(0, i, natt)
            dctx[...] = dot(natt[i], wf[0, :, wide:], 1, 1).astype(BF16)
            route(S_DFF0, i)
            route(S_DFF1, i)
            route(S_DU, i)
            route(GIN_FF, i)
            route(S_DATT, i)
            for copy in prob_copies(i, True):
                copy.wait()
            attend_back(i, slot)
            route(S_DQ, i)

            @pl.when(r + 1 < items)
            def _():
                for copy in prob_copies(item_of(r + 1), True):
                    copy.start()

            for j in range(quads - 1):
                gather_dkv(j, i, slot)
            early = (quads - 1) * quad
            partial_sum = dot(dqb[...], wf[0, :, 0:width], 1, 1) + dhb[...]
            if early:
                partial_sum = partial_sum + dkv_back(i, 0, early)
            dhb[...] = partial_sum
            gather_dkv(quads - 1, i, slot)
            route(S_DKV, i)
            forward_sent(i)
            yd[i] = (dkv_back(i, early, width) + dhb[...]).astype(BF16)

            @pl.when(x == 1)
            def _():
                gy_copy(i).start()

            @pl.when((x == 0) & (i >= n))
            def _():
                mg_copy(i).start()

            route(GIN_ATT, i)
            for j in range(quads):
                dkv_copy(j, i, slot).wait_send()

        return carry

    lax.fori_loop(0, items + 1, backward_tick, 0)

    acc_copy = remote(acc.at[1 - c], accp, as_sem, ar_sem, core_peer)
    acc_copy.start()

    def backward_drain(i, carry):
        @pl.when(x == 1)
        def _():
            gy_copy(i).wait_send()

        @pl.when((x == 0) & (i >= n))
        def _():
            mg_copy(i).wait_send()

        for kind in range(KINDS):
            if kind not in (OUT_FF, S_GLO, S_GHI, S_DQ, GIN_FF):
                route_sent(kind, i)
            route_received(kind, i)
        return carry

    lax.fori_loop(0, items, backward_drain, 0)
    route_sent(S_GLO, items - 1)
    route_sent(S_GHI, items - 1)
    route_sent(S_DQ, item_of(items - 1))
    route_sent(GIN_FF, item_of(items - 1))
    for k in range(5):
        weight_remote(k).wait_send()
    acc_copy.wait()
    norm_grad[...] = acc[c] + accp[...]


def run_layers(n, nseg, heads, tokens, cotangent, first, down, docs, resets, gain, shift):
    length, width = tokens.shape[1:]
    toks = length // nseg // 2
    rows = toks + MEM_PAD
    items = n * nseg
    hidden_half = down.shape[1]
    quads = heads // 4
    quad = width // quads
    any_spec = pl.BlockSpec(memory_space=pl.ANY)
    vmem_spec = pl.BlockSpec(memory_space=pltpu.VMEM)
    dma = pltpu.SemaphoreType.DMA
    item_rows = pltpu.VMEM((items, rows, width), BF16)
    one, two = dma((items,)), dma((2, items))
    return pl.pallas_call(
        partial(layers_kernel, n, nseg, heads),
        out_shape=(
            jax.ShapeDtypeStruct((n, length, width), BF16),
            jax.ShapeDtypeStruct((n, length, width), BF16),
            jax.ShapeDtypeStruct((2 * items, rows, width), BF16),
            jax.ShapeDtypeStruct((2 * items, rows, width), BF16),
            jax.ShapeDtypeStruct((2 * items, rows, 4 * width), BF16),
            jax.ShapeDtypeStruct((2 * items, rows, hidden_half), BF16),
            jax.ShapeDtypeStruct((2 * items, rows, width), BF16),
            jax.ShapeDtypeStruct((2, width), F32),
            jax.ShapeDtypeStruct((items, quads, 4 * rows, 2 * toks), BF16),
            jax.ShapeDtypeStruct((items, quads, rows, 8 * MEM_PAD), BF16),
        ),
        in_specs=[any_spec] * 4 + [vmem_spec] * 4,
        out_specs=[any_spec] * 7 + [vmem_spec] + [any_spec] * 2,
        scratch_shapes=[
            pltpu.VMEM((2, width, 4 * width), BF16),
            pltpu.VMEM((2, hidden_half, width), BF16),
            pltpu.VMEM((2, 2, width), F32),
            item_rows,
            pltpu.VMEM((n, rows, width), BF16),
            item_rows,
            pltpu.VMEM((items, 2, rows, 2 * width), BF16),
            item_rows,
            item_rows,
            item_rows,
            item_rows,
            item_rows,
            item_rows,
            pltpu.VMEM((rows, 2 * hidden_half), BF16),
            pltpu.VMEM((rows, 2 * hidden_half), BF16),
            pltpu.VMEM((items, rows, 2 * hidden_half), BF16),
            pltpu.VMEM((items, rows, 128), F32),
            pltpu.VMEM((items, toks, 128), F32),
            pltpu.VMEM((items, 1, 2 * toks), F32),
            pltpu.VMEM((items, MEM_PAD, 128), F32),
            pltpu.VMEM((2, items, MEM_PAD, width), BF16),
            pltpu.VMEM((items, MEM_PAD, width), BF16),
            pltpu.VMEM((2, quads, rows, 2 * quad), BF16),
            pltpu.VMEM((2, quads, rows, 2 * quad), BF16),
            pltpu.VMEM((rows, width), F32),
            pltpu.VMEM((2, rows, 2 * width), BF16),
            pltpu.VMEM((2, 2, width), F32),
            pltpu.VMEM((2, width), F32),
            pltpu.VMEM((quads, 4 * rows, 2 * toks), BF16),
            pltpu.VMEM((quads, rows, 8 * MEM_PAD), BF16),
            dma((4,)), dma((5,)), dma((5,)),
            two, one, one, two, two, two,
            two, two,
            two, two,
            two, two,
            one, one, one, one,
            dma((quads, items)), dma((quads, items)),
            dma(()), dma(()),
        ]
        + [dma((KINDS, items))] * 3,
        compiler_params=pltpu.CompilerParams(
            collective_id=0, has_side_effects=True, vmem_limit_bytes=61 * 1024 * 1024
        ),
    )(tokens, cotangent, first, down, docs, resets, gain, shift)


def reduce_kernel(
    chunks,
    sx1, sx2, sr, sg, sd, norm_part,
    sums, norm_out,
    x1, x2, rr, gg, dd, work, done, got_u, got_uz, got_vz, got_vy, norms,
    right_sem, left_sem, out_sem, u_s, u_r, uz_s, uz_r, vz_s, vz_r, vy_s, vy_r, vg_s, vg_r,
    uzg_s, uzg_r, vzg_s, vzg_r, ug_s, ug_r, n_s, n_r,
):
    lines = 4
    d = lax.axis_index("dp")
    y = lax.rem(d, 2)
    z = lax.div(d, 2)
    dp = lax.axis_size("dp")
    width = sd.shape[1]
    half = width // 2
    part = width // chunks
    hr = part // 2
    lane_group = 128
    per_group = lane_group // part
    y_peer = {"dp": z * 2 + (1 - y)}

    def remote(src, dst, send, recv, peer):
        return pltpu.make_async_remote_copy(
            src_ref=src, dst_ref=dst, send_sem=send, recv_sem=recv,
            device_id=peer, device_id_type=MESH,
        )

    def other(step):
        return {"dp": lax.rem(d + step, dp)}

    barrier = pltpu.get_barrier_semaphore()
    for step in range(1, dp):
        pl.semaphore_signal(barrier, inc=1, device_id=other(step), device_id_type=MESH)

    lane_groups = width // lane_group
    right_loads = [(sd, dd)] + [
        (sr.at[:, b * width : (b + 1) * width], rr.at[:, b * width : (b + 1) * width])
        for b in range(4)
    ]

    def right_load(k):
        src, dst = right_loads[k]
        return pltpu.make_async_copy(src, dst, right_sem.at[k])

    def left_load(which, group):
        src, dst, low = ((sg, gg, 0), (sg, gg, width), (sx2, x2, 0), (sx1, x1, 0))[which]
        cols = pl.ds(pl.multiple_of(low + group * lane_group, lane_group), lane_group)
        return pltpu.make_async_copy(src.at[:, cols], dst.at[:, cols], left_sem.at[which, group])

    right_load(0).start()
    left_load(0, 0).start()
    left_load(1, 0).start()
    left_load(2, 0).start()
    right_load(4).start()
    left_load(3, 0).start()
    for k in range(1, 4):
        right_load(k).start()
    for group in range(1, lane_groups):
        for which in range(4):
            left_load(which, group).start()

    norms[d] = norm_part[...]
    pl.semaphore_wait(barrier, dp - 1)

    def norm_copy(step):
        return remote(norms.at[d], norms.at[d], n_s.at[step - 1], n_r.at[step - 1], other(step))

    def norm_arrival(step):
        source = lax.rem(d + dp - step, dp)
        return remote(
            norms.at[source], norms.at[source], n_s.at[step - 1], n_r.at[step - 1], other(step)
        )

    for step in range(1, dp):
        norm_copy(step).start()

    def column_half(h):
        return pl.ds(pl.multiple_of(h * half, 128), half)

    mine, theirs = column_half(y), column_half(1 - y)

    def place(flow):
        return z if flow == 0 else lines - 1 - z

    def onward(flow):
        step = -1 if flow == 0 else 1
        return {"dp": (z + step) * 2 + y}

    def back(flow):
        step = 1 if flow == 0 else -1
        return {"dp": (z + step) * 2 + y}

    def rows_of(flow):
        return slice(flow * hr, (flow + 1) * hr)

    def u_copy(k):
        return remote(
            work.at[k, 0:3, :, theirs], got_u.at[k], u_s.at[k], u_r.at[k], y_peer
        )

    def uz_copy(flow, k):
        return remote(
            work.at[k, 0:3, rows_of(flow), mine], got_uz.at[flow, k],
            uz_s.at[flow, k], uz_r.at[flow, k], onward(flow),
        )

    def vz_copy(flow, k):
        return remote(
            work.at[k, 3:6, rows_of(flow), :], got_vz.at[flow, k],
            vz_s.at[flow, k], vz_r.at[flow, k], onward(flow),
        )

    def vy_copy(flow, k):
        return remote(
            work.at[k, 3:6, rows_of(flow), theirs], got_vy.at[k], vy_s.at[k], vy_r.at[k], y_peer
        )

    def vg_copy(flow, k, cols):
        spot = done.at[k, 3:6, rows_of(flow), cols]
        return remote(spot, spot, vg_s.at[k], vg_r.at[k], y_peer)

    def uzg_copy(flow, k):
        spot = done.at[k, 0:3, rows_of(flow), mine]
        return remote(spot, spot, uzg_s.at[flow, k], uzg_r.at[flow, k], back(flow))

    def vzg_copy(flow, k):
        spot = done.at[k, 3:6, rows_of(flow), :]
        return remote(spot, spot, vzg_s.at[flow, k], vzg_r.at[flow, k], back(flow))

    def ug_copy(flow, k, cols):
        spot = done.at[k, 0:3, rows_of(flow), cols]
        return remote(spot, spot, ug_s.at[flow, k], ug_r.at[flow, k], y_peer)

    def out_copy(k):
        return pltpu.make_async_copy(done.at[k], sums.at[k], out_sem.at[k])

    def plus(a, b):
        return (a.astype(F32) + b.astype(F32)).astype(BF16)

    def ready(k, low=0):
        return (k >= low) & (k < chunks)

    def store_chunks(group, block, value):
        for e in range(per_group):
            work[group * per_group + e, block] = value[e * part : (e + 1) * part]

    def second_half(r):
        group = lax.div(r + per_group - 1, per_group)
        cols = pl.ds(pl.multiple_of(group * lane_group, lane_group), lane_group)
        gcols = pl.ds(pl.multiple_of(width + group * lane_group, lane_group), lane_group)

        @pl.when(r == 0)
        def _():
            right_load(0).wait()

        left_load(0, group).wait()
        store_chunks(group, 4, dot(gg[:, cols], dd[...], 0, 0).astype(BF16))
        left_load(1, group).wait()
        store_chunks(group, 5, dot(gg[:, gcols], dd[...], 0, 0).astype(BF16))
        left_load(2, group).wait()

        @pl.when(r == 0)
        def _():
            right_load(4).wait()

        store_chunks(group, 3, dot(x2[:, cols], rr[:, 3 * width :], 0, 0).astype(BF16))

    def round_step(r, carry):
        @pl.when(r == 0)
        def _():
            second_half(r)

        for flow in range(2):
            p = place(flow)
            k = r - (lines - 1 - p)
            rows = rows_of(flow)

            @pl.when(ready(k))
            def _():
                @pl.when(p < lines - 1)
                def _():
                    vz_copy(flow, k).wait_recv()
                    work[k, 3:6, rows, :] = plus(work[k, 3:6, rows, :], got_vz[flow, k])

                @pl.when(p > 0)
                def _():
                    vz_copy(flow, k).start()

                @pl.when(p == 0)
                def _():
                    vy_copy(flow, k).start()

        @pl.when((lax.rem(r, per_group) == 0) & (r < chunks))
        def _():
            group = lax.div(r, per_group)
            cols = pl.ds(pl.multiple_of(group * lane_group, lane_group), lane_group)
            left_load(3, group).wait()
            for b in range(3):

                @pl.when(r == 0)
                def _():
                    right_load(1 + b).wait()

                store_chunks(
                    group, b,
                    dot(x1[:, cols], rr[:, b * width : (b + 1) * width], 0, 0).astype(BF16),
                )

        @pl.when(ready(r))
        def _():
            u_copy(r).start()

        @pl.when((lax.rem(r, per_group) == per_group - 1) & (r + 1 < chunks))
        def _():
            second_half(r)

        @pl.when(ready(r - 1))
        def _():
            k = r - 1
            u_copy(k).wait_recv()
            work[k, 0:3, :, mine] = plus(work[k, 0:3, :, mine], got_u[k])

        for flow in range(2):
            p = place(flow)
            k = r - 1 - (lines - 1 - p)
            rows = rows_of(flow)

            @pl.when(ready(k))
            def _():
                @pl.when(p < lines - 1)
                def _():
                    uz_copy(flow, k).wait_recv()
                    total = plus(work[k, 0:3, rows, mine], got_uz[flow, k])

                    @pl.when(p > 0)
                    def _():
                        work[k, 0:3, rows, mine] = total

                    @pl.when(p == 0)
                    def _():
                        done[k, 0:3, rows, mine] = total

                @pl.when(p > 0)
                def _():
                    uz_copy(flow, k).start()

                @pl.when(p == 0)
                def _():
                    uzg_copy(flow, k).start()
                    ug_copy(flow, k, mine).start()

        for flow in range(2):
            p = place(flow)
            rows = rows_of(flow)

            @pl.when((p == 0) & ready(r - lines))
            def _():
                k = r - lines
                vy_copy(flow, k).wait_recv()
                done[k, 3:6, rows, mine] = plus(work[k, 3:6, rows, mine], got_vy[k])
                vg_copy(flow, k, mine).start()

            @pl.when((p == 0) & ready(r - lines - 1))
            def _():
                k = r - lines - 1
                vg_copy(flow, k, theirs).wait_recv()
                vzg_copy(flow, k).start()

        for flow in range(2):
            p = place(flow)
            k = r - lines - p

            @pl.when((p > 0) & ready(k))
            def _():
                uzg_copy(flow, k).wait_recv()

                @pl.when(p < lines - 1)
                def _():
                    uzg_copy(flow, k).start()

                ug_copy(flow, k, mine).start()

        for flow in range(2):
            p = place(flow)
            k = r - lines - 1 - p

            @pl.when((p > 0) & ready(k))
            def _():
                vzg_copy(flow, k).wait_recv()

                @pl.when(p < lines - 1)
                def _():
                    vzg_copy(flow, k).start()

            @pl.when(ready(k))
            def _():
                ug_copy(flow, k, theirs).wait_recv()

        @pl.when(ready(r - 2 * lines))
        def _():
            out_copy(r - 2 * lines).start()

        return carry

    lax.fori_loop(0, chunks + 2 * lines, round_step, 0)

    for step in range(1, dp):
        norm_arrival(step).wait_recv()
    total = norms[0]
    for e in range(1, dp):
        total = total + norms[e]
    norm_out[...] = total

    def drain(k, carry):
        out_copy(k).wait()
        u_copy(k).wait_send()
        for flow in range(2):
            p = place(flow)
            ug_copy(flow, k, mine).wait_send()

            @pl.when(p > 0)
            def _():
                vz_copy(flow, k).wait_send()
                uz_copy(flow, k).wait_send()

            @pl.when(p < lines - 1)
            def _():
                uzg_copy(flow, k).wait_send()
                vzg_copy(flow, k).wait_send()

            @pl.when(p == 0)
            def _():
                vy_copy(flow, k).wait_send()
                vg_copy(flow, k, mine).wait_send()

        return carry

    lax.fori_loop(0, chunks, drain, 0)
    for step in range(1, dp):
        norm_copy(step).wait_send()


def sum_weights(dp, sx1, sx2, sr, sg, sd, norm_part):
    total, width = sx1.shape
    chunks = 12
    part = width // chunks
    half = width // 2
    any_spec = pl.BlockSpec(memory_space=pl.ANY)
    vmem_spec = pl.BlockSpec(memory_space=pltpu.VMEM)
    dma = pltpu.SemaphoreType.DMA
    one, two = dma((chunks,)), dma((2, chunks))
    return pl.pallas_call(
        partial(reduce_kernel, chunks),
        out_shape=(
            jax.ShapeDtypeStruct((chunks, 6, part, width), BF16),
            jax.ShapeDtypeStruct((2, width), F32),
        ),
        in_specs=[any_spec] * 5 + [vmem_spec],
        out_specs=[any_spec, vmem_spec],
        scratch_shapes=[
            pltpu.VMEM((total, width), BF16),
            pltpu.VMEM((total, width), BF16),
            pltpu.VMEM((total, 4 * width), BF16),
            pltpu.VMEM((total, 2 * width), BF16),
            pltpu.VMEM((total, width), BF16),
            pltpu.VMEM((chunks, 6, part, width), BF16),
            pltpu.VMEM((chunks, 6, part, width), BF16),
            pltpu.VMEM((chunks, 3, part, half), BF16),
            pltpu.VMEM((2, chunks, 3, part // 2, half), BF16),
            pltpu.VMEM((2, chunks, 3, part // 2, width), BF16),
            pltpu.VMEM((chunks, 3, part // 2, half), BF16),
            pltpu.VMEM((dp, 2, width), F32),
            dma((5,)),
            dma((4, width // 128)),
            one,
            one, one,
            two, two,
            two, two,
            one, one,
            one, one,
            two, two,
            two, two,
            two, two,
            dma((dp - 1,)), dma((dp - 1,)),
        ],
        compiler_params=pltpu.CompilerParams(
            collective_id=1, has_side_effects=True, vmem_limit_bytes=60 * 1024 * 1024
        ),
    )(sx1, sx2, sr, sg, sd, norm_part)


def finish_kernel(sums, out, gin, norms, first_grad, down_grad, out_copy, gin_copy, gain, shift):
    group, _, part, width = sums.shape
    for e in range(group):
        rows = slice(e * part, (e + 1) * part)
        for b in range(4):
            first_grad[rows, b * width : (b + 1) * width] = sums[e, b].astype(F32)
        for b in range(2):
            down_grad[b, rows] = sums[e, 4 + b].astype(F32)
    out_copy[...] = out[...]
    gin_copy[...] = gin[...]
    gain[...] = norms[0:1]
    shift[...] = norms[1:2]


def finish(sums, out, gin, norms):
    chunks, _, part, width = sums.shape
    total = out.shape[0]
    group, blocks = chunks // 3, 2
    tokens = pl.BlockSpec((total // blocks, width), lambda k: (jnp.minimum(k, blocks - 1), 0))
    whole = pl.BlockSpec((1, width), lambda k: (0, 0))
    return pl.pallas_call(
        finish_kernel,
        grid=(chunks // group,),
        out_shape=(
            jax.ShapeDtypeStruct((width, 4 * width), F32),
            jax.ShapeDtypeStruct((2, width, width), F32),
            jax.ShapeDtypeStruct(out.shape, BF16),
            jax.ShapeDtypeStruct(gin.shape, BF16),
            jax.ShapeDtypeStruct((1, width), F32),
            jax.ShapeDtypeStruct((1, width), F32),
        ),
        in_specs=[
            pl.BlockSpec((group, 6, part, width), lambda k: (k, 0, 0, 0)),
            tokens,
            tokens,
            pl.BlockSpec((2, width), lambda k: (0, 0)),
        ],
        out_specs=[
            pl.BlockSpec((group * part, 4 * width), lambda k: (k, 0)),
            pl.BlockSpec((2, group * part, width), lambda k: (0, k, 0)),
            tokens,
            tokens,
            whole,
            whole,
        ],
        compiler_params=pltpu.CompilerParams(vmem_limit_bytes=40 * 1024 * 1024),
    )(sums, out, gin, norms)


def shards(
    tokens, doc_ids, reset_flags, first_weights, down_halves, norm_gain, norm_bias, cotangent
):
    n, length, width = tokens.shape
    items = n * NSEG
    rows = length // NSEG // 2 + MEM_PAD
    out, gin, sx1, sx2, sr, sg, sd, norm_grad, _, _ = run_layers(
        n, NSEG, H, tokens, cotangent, first_weights, down_halves,
        doc_ids, reset_flags.T, norm_gain, norm_bias,
    )
    total = 2 * items * rows
    sx1, sx2, sd = (a.reshape(total, width) for a in (sx1, sx2, sd))
    sr = sr.reshape(total, 4 * width)
    sg = sg.reshape(total, -1)

    dp = lax.axis_size("dp")
    if dp == 8:
        sums, norm_grad = sum_weights(dp, sx1, sx2, sr, sg, sd, norm_grad)
        first_grad, down_grad, out, gin, gain_grad, shift_grad = finish(
            sums, out.reshape(-1, width), gin.reshape(-1, width), norm_grad
        )
        down_grad = down_grad.reshape(-1, width)
        out, gin = (a.reshape(n, length, width) for a in (out, gin))
    else:

        def weight_grad(left, right):
            return jnp.einsum("rd,re->de", left, right, preferred_element_type=F32).astype(BF16)

        first_grad = jnp.concatenate(
            [weight_grad(sx1, sr[:, : 3 * width]), weight_grad(sx2, sr[:, 3 * width :])], axis=1
        )
        down_grad = weight_grad(sg, sd)
        first_grad, down_grad = lax.psum((first_grad, down_grad), "dp")
        norm_grad = lax.psum(norm_grad, "dp")
        gain_grad, shift_grad = norm_grad[0:1], norm_grad[1:2]
    return (
        out[None],
        gin[None],
        first_grad.astype(F32)[None],
        down_grad.astype(F32)[None],
        gain_grad,
        shift_grad,
    )


def solution(mesh):
    in_specs = (
        P("dp", None, None),
        P("dp", None),
        P("dp", None),
        P("section", None, None),
        P("section", None, None),
        P("section", None),
        P("section", None),
        P("dp", None, None),
    )
    out_specs = (
        P("section", "dp", None, None),
        P("section", "dp", None, None),
        P("section", None, None),
        P("section", None, None),
        P("section", None),
        P("section", None),
    )
    return jax.shard_map(shards, mesh=mesh, in_specs=in_specs, out_specs=out_specs, check_vma=False)
```

```python
from functools import partial

import jax
import jax.numpy as jnp
from jax import lax
from jax.experimental import pallas as pl
from jax.experimental.pallas import tpu as pltpu
from jax.sharding import PartitionSpec as P

H = 12
M = 20
NSEG = 2
MEM_PAD = 16
NORM_EPSILON = 1e-05
MASKED_SCORE = -1000000000.0
ABSENT_SCORE = -3e38
MESH = pl.DeviceIdType.MESH
BF16 = jnp.bfloat16
F32 = jnp.float32

OUT_ATT, OUT_FF, GIN_ATT, GIN_FF = 0, 1, 2, 3
S_X0, S_CTX, S_DQ, S_DKV, S_DATT, S_GLO, S_DFF0 = 4, 5, 6, 7, 8, 9, 10
S_Y1, S_Y2, S_DU, S_GHI, S_DFF1 = 11, 12, 13, 14, 15
KINDS = 16


def dot(a, b, lhs_dim=1, rhs_dim=0):
    return lax.dot_general(
        a, b, (((lhs_dim,), (rhs_dim,)), ((), ())), preferred_element_type=F32
    )


def normalize(summed):
    mean = jnp.mean(summed, axis=-1, keepdims=True)
    centered = summed - mean
    var = jnp.mean(centered * centered, axis=-1, keepdims=True)
    inv = lax.rsqrt(var + NORM_EPSILON)
    return centered * inv, inv


def group_of(shape, dim, size):
    index = lax.broadcasted_iota(jnp.int32, shape, dim)
    return lax.shift_right_logical(index, size.bit_length() - 1)


def spread(values, groups):
    result = values[-1]
    for h in range(len(values) - 1):
        result = jnp.where(groups == h, values[h], result)
    return result


def layers_kernel(
    n, nseg, heads,
    tokens, cotangent, first, down, docs, resets, gain, shift,
    out, gin, sx1, sx2, sr, sg, sd, norm_grad, ptok, pmem,
    wf, wd, nrm, x0, xo, q, kv, ctx, natt, yatt, nff, yd, gy, g, gpb, gp, stats, qdoc, kdoc, keep,
    memin, mgin, dkvs, dkvin, dhb, kvb, acc, accp, tprob, mprob,
    wl, ws, wr, tok_sem, cot_sem, gp_sem, qkv_sem, pw_sem, pr_sem, fs_sem, fr_sem, xs_sem, xr_sem,
    ms_sem, mr_sem, gs_sem, gr_sem, hs_sem, hr_sem, ds_sem, dr_sem, as_sem, ar_sem,
    lsem, ssem, rsem,
):
    items = n * nseg
    section = lax.axis_index("section")
    c = lax.rem(section, 2)
    x = lax.div(section, 2)
    core_peer = {"section": x * 2 + (1 - c)}
    chip_peer = {"section": (1 - x) * 2 + c}
    cross_peer = {"section": (1 - x) * 2 + (1 - c)}
    rows, width = x0.shape[1:]
    toks = rows - MEM_PAD
    seg_len = 2 * toks
    hidden_half = wd.shape[1]
    wide = 3 * width
    head_dim = width // heads
    quad = 4 * head_dim
    quads = heads // 4
    mem_keys = 2 * MEM_PAD
    scale = head_dim ** (-0.5)
    qb = gpb.at[:, 0:width]
    ctxb = gpb.at[:, width : 2 * width]
    dqb = gpb.at[:, 0:width]
    gab = gpb.at[:, width : 2 * width]
    dctx = gpb.at[:, 2 * width : wide]

    def remote(src, dst, send, recv, peer):
        return pltpu.make_async_remote_copy(
            src_ref=src, dst_ref=dst, send_sem=send, recv_sem=recv,
            device_id=peer, device_id_type=MESH,
        )

    barrier = pltpu.get_barrier_semaphore()
    pl.semaphore_signal(barrier, inc=1, device_id=core_peer, device_id_type=MESH)
    pl.semaphore_signal(barrier, inc=1, device_id=chip_peer, device_id_type=MESH)
    pl.semaphore_signal(barrier, inc=1, device_id=cross_peer, device_id_type=MESH)

    def token_rows(ref, i, core=None):
        core = c if core is None else core
        return ref.at[lax.rem(i, n), pl.ds(lax.div(i, n) * seg_len + core * toks, toks), :]

    def token_copy(which, i):
        if which == 0:
            src, dst = token_rows(tokens, i), x0.at[i, 0:toks, :]
        else:
            src, dst = token_rows(tokens, i, 1 - c), xo.at[lax.rem(i, n), 0:toks, :]
        return pltpu.make_async_copy(src, dst, tok_sem.at[which, i])

    def cot_copy(i):
        return pltpu.make_async_copy(
            token_rows(cotangent, i), gy.at[i, 0:toks, :], cot_sem.at[i]
        )

    def weight_piece(k):
        if k == 0:
            return first.at[0, :, width:wide], wf.at[c, :, width:wide]
        if k == 1:
            return first.at[0, :, 0:width], wf.at[c, :, 0:width]
        if k == 2:
            return first.at[0, :, wide:], wf.at[c, :, wide:]
        return down.at[0], wd.at[c]

    def weight_local(k):
        src, dst = weight_piece(k)
        return pltpu.make_async_copy(src, dst, wl.at[k])

    def weight_remote(k):
        if k == 4:
            return remote(nrm.at[c], nrm.at[c], ws.at[4], wr.at[4], core_peer)
        src, dst = weight_piece(k)
        return remote(src, dst, ws.at[k], wr.at[k], core_peer)

    nrm[c, 0:1, :] = gain[...]
    nrm[c, 1:2, :] = shift[...]
    weight_local(0).start()

    @pl.when(x == 0)
    def _():
        token_copy(0, 0).start()
        token_copy(1, 0).start()

    pl.semaphore_wait(barrier, 3)
    for k in range(5):
        weight_remote(k).start()
    for k in range(1, 4):
        weight_local(k).start()
    for i in range(items):
        if i > 0:

            @pl.when(x == 0)
            def _():
                token_copy(0, i).start()
                if i < n:
                    token_copy(1, i).start()

        @pl.when(x == 1)
        def _():
            cot_copy(i).start()

    def wait_first_of(core, ks):
        @pl.when(c == core)
        def _():
            for k in ks:
                weight_local(k).wait()

        @pl.when(c != core)
        def _():
            for k in ks:
                weight_remote(k).wait_recv()

    for i in range(items):
        seq, seg = i % n, i // n
        own = pl.ds(pl.multiple_of(seg * seg_len + c * toks, toks), toks)
        others = pl.ds(pl.multiple_of(seg * seg_len + (1 - c) * toks, toks), toks)
        own_row = docs[seq : seq + 1, own].astype(F32)
        kdoc[i, :, 0:toks] = own_row
        kdoc[i, :, toks:] = docs[seq : seq + 1, others].astype(F32)
        qdoc[i] = jnp.transpose(jnp.broadcast_to(own_row, (128, toks)))
        if seg > 0:
            flag = resets[seg - 1 : seg, seq : seq + 1].astype(F32)
            keep[i] = jnp.broadcast_to(1.0 - flag, (MEM_PAD, 128))

    def routed(kind, i):
        block = i * 2 + c
        sec = 0
        if kind == OUT_ATT:
            src, dst = yatt.at[i, 0:toks, :], token_rows(out, i)
        elif kind == OUT_FF:
            src, dst, sec = yd.at[i, 0:toks, :], token_rows(out, i), 1
        elif kind == GIN_ATT:
            src, dst = yd.at[i, 0:toks, :], token_rows(gin, i)
        elif kind == GIN_FF:
            src, dst, sec = gab.at[0:toks, :], token_rows(gin, i), 1
        elif kind == S_X0:
            src, dst = x0.at[i], sx1.at[block]
        elif kind == S_CTX:
            src, dst = ctx.at[i], sx2.at[block]
        elif kind == S_DQ:
            src, dst = dqb, sr.at[block, :, 0:width]
        elif kind == S_DKV:
            src, dst = kv.at[i, 0], sr.at[block, :, width:wide]
        elif kind == S_DATT:
            src, dst = natt.at[i], sr.at[block, :, wide:]
        elif kind == S_GLO:
            src, dst = g.at[:, 0:hidden_half], sg.at[block]
        elif kind == S_DFF0:
            src, dst = nff.at[i], sd.at[block]
        elif kind == S_Y1:
            src, dst, sec = yatt.at[i], sx1.at[block], 1
        elif kind == S_Y2:
            src, dst, sec = yatt.at[i], sx2.at[block], 1
        elif kind == S_DU:
            src, dst, sec = gp.at[i], sr.at[block], 1
        elif kind == S_GHI:
            src, dst, sec = g.at[:, hidden_half:], sg.at[block], 1
        else:
            src, dst, sec = nff.at[i], sd.at[block], 1
        return src, dst, sec

    def route_local(kind, i):
        src, dst, _ = routed(kind, i)
        return pltpu.make_async_copy(src, dst, lsem.at[kind, i])

    def route_away(kind, i):
        src, dst, _ = routed(kind, i)
        return remote(src, dst, ssem.at[kind, i], rsem.at[kind, i], core_peer)

    def route(kind, i):
        sec = routed(kind, i)[2]

        @pl.when(c == sec)
        def _():
            route_local(kind, i).start()

        @pl.when(c != sec)
        def _():
            route_away(kind, i).start()

    def route_sent(kind, i):
        sec = routed(kind, i)[2]

        @pl.when(c == sec)
        def _():
            route_local(kind, i).wait()

        @pl.when(c != sec)
        def _():
            route_away(kind, i).wait_send()

    def route_received(kind, i):
        @pl.when(c == routed(kind, i)[2])
        def _():
            route_away(kind, i).wait_recv()

    def qkv_copies(i):
        return [
            pltpu.make_async_copy(qb, q.at[i], qkv_sem.at[0, i]),
            pltpu.make_async_copy(kvb, kv.at[i], qkv_sem.at[1, i]),
        ]

    def gp_copy(i):
        return pltpu.make_async_copy(gpb, gp.at[i], gp_sem.at[i])

    def prob_copies(i, back):
        pairs = ((tprob, ptok.at[i]), (mprob, pmem.at[i]))
        if back:
            return [
                pltpu.make_async_copy(dst, src, pr_sem.at[e, i])
                for e, (src, dst) in enumerate(pairs)
            ]
        return [
            pltpu.make_async_copy(src, dst, pw_sem.at[e, i]) for e, (src, dst) in enumerate(pairs)
        ]

    cut = rows // 32 * 16

    def piece(p):
        return slice(0, cut) if p == 0 else slice(cut, rows)

    def x_copy(p, i):
        return remote(
            yd.at[i, piece(p)], x0.at[i, piece(p)], xs_sem.at[p, i], xr_sem.at[p, i], chip_peer
        )

    def pass_copy(p, i):
        return remote(
            x0.at[i, piece(p)], xo.at[lax.rem(i, n), piece(p)],
            fs_sem.at[p, i], fr_sem.at[p, i], core_peer,
        )

    def mem_copy(which, i):
        return remote(
            yd.at[i, toks:rows, :], memin.at[which, i], ms_sem.at[which, i],
            mr_sem.at[which, i], cross_peer if which else chip_peer,
        )

    def gy_copy(i):
        return remote(yd.at[i], gy.at[i], gs_sem.at[i], gr_sem.at[i], chip_peer)

    def mg_copy(i):
        return remote(
            yd.at[i, toks:rows, :], mgin.at[i], hs_sem.at[i], hr_sem.at[i], chip_peer
        )

    def dkv_copy(j, i, slot):
        return remote(
            dkvs.at[1, j], dkvin.at[slot, j], ds_sem.at[j, i], dr_sem.at[j, i], core_peer
        )

    head_lanes = group_of((rows, quad), 1, head_dim)
    mem_lanes = group_of((rows, 4 * mem_keys), 1, mem_keys)
    key_lane = lax.broadcasted_iota(jnp.int32, (rows, 4 * mem_keys), 1)
    mem_valid = lax.rem(key_lane, MEM_PAD) < M // 2
    diagonal = group_of((4 * mem_keys, quad), 0, mem_keys) == group_of(
        (4 * mem_keys, quad), 1, head_dim
    )
    stat_lane = lax.broadcasted_iota(jnp.int32, (rows, 128), 1)

    def stacked(block):
        return jnp.concatenate(
            [jnp.where(head_lanes == h, block, BF16(0)) for h in range(4)], axis=0
        )

    def head_rows(block):
        return [block[h * rows : (h + 1) * rows] for h in range(4)]

    def token_and_memory(ref, low):
        cols = slice(low, low + quad)
        tok = jnp.concatenate([ref[0, 0:toks, cols], ref[1, 0:toks, cols]], axis=0)
        mem = jnp.concatenate([ref[0, toks:, cols], ref[1, toks:, cols]], axis=0)
        return tok, jnp.where(diagonal, jnp.concatenate([mem] * 4, axis=0), BF16(0))

    def only_same_document(s, i):
        mine = jnp.concatenate([qdoc[i]] * (seg_len // 128), axis=1)
        same = jnp.where(mine == kdoc[i], s[0:toks], MASKED_SCORE)
        return jnp.concatenate([same, s[toks:]], axis=0)

    def memory_scores(q4, mem_k):
        return jnp.where(mem_valid, dot(q4, mem_k, 1, 1), ABSENT_SCORE)

    def attend(i):
        own = [mem_lanes == h for h in range(4)]

        def scores(j):
            q4 = qb[:, j * quad : (j + 1) * quad]
            tok_k, mem_k = token_and_memory(kvb, j * quad)
            return dot(stacked(q4), tok_k, 1, 1), memory_scores(q4, mem_k)

        st = jnp.zeros((rows, 128), F32)
        following = scores(0)
        for j in range(quads):
            s, sm = following
            if j + 1 < quads:
                following = scores(j + 1)
            s = [only_same_document(part, i) for part in head_rows(s)]
            peaks = [
                jnp.max(
                    jnp.concatenate([s[h], jnp.where(own[h], sm, ABSENT_SCORE)], axis=1),
                    axis=1, keepdims=True,
                )
                for h in range(4)
            ]
            pm = jnp.exp(sm - spread(peaks, mem_lanes))
            mprob[j] = pm.astype(BF16)
            totals, probs = [], []
            for h in range(4):
                p = jnp.exp(s[h] - peaks[h])
                probs.append(p.astype(BF16))
                tprob[j, h * rows : (h + 1) * rows, :] = probs[h]
                both = jnp.concatenate([p, jnp.where(own[h], pm, 0.0)], axis=1)
                totals.append(1.0 / jnp.sum(both, axis=1, keepdims=True))
                st = jnp.where(stat_lane == 4 * j + h, totals[h], st)
            tok_v, mem_v = token_and_memory(kvb, width + j * quad)
            o = spread(head_rows(dot(jnp.concatenate(probs, axis=0), tok_v)), head_lanes)
            o = o + dot(pm.astype(BF16), mem_v)
            ctxb[:, j * quad : (j + 1) * quad] = (o * spread(totals, head_lanes)).astype(BF16)
        stats[i] = st
        ctx[i] = ctxb[...]

    def forward_tick(t, carry):
        i = t - x

        @pl.when((i >= 0) & (i < items))
        def _():
            @pl.when(x == 0)
            def _():
                for which, rows_ref in enumerate((x0.at[i], xo.at[lax.rem(i, n)])):
                    token_copy(which, i).wait()

                    @pl.when(i < n)
                    def _():
                        rows_ref[toks:rows, :] = jnp.zeros((MEM_PAD, width), BF16)

                    @pl.when(i >= n)
                    def _():
                        mem_copy(which, i - n).wait_recv()
                        rows_ref[toks:rows, :] = jnp.where(
                            keep[i][:, 0:1] > 0.0, memin[which, i - n], jnp.zeros((), BF16)
                        )

            @pl.when(x == 1)
            def _():
                for p in range(2):
                    x_copy(p, i).wait_recv()
                    pass_copy(p, i).start()

            @pl.when(i == 0)
            def _():
                wait_first_of(0, (0,))

            @pl.when(i > 0)
            def _():
                qkv_copies(i - 1)[1].wait()
                gp_copy(i - 1).wait()

            kvb[0] = dot(x0[i], wf[0, :, width:wide]).astype(BF16)

            @pl.when(i == 0)
            def _():
                wait_first_of(0, (1,))

            qb[...] = dot(x0[i], wf[0, :, 0:width]).astype(BF16) * BF16(scale)

            @pl.when(x == 1)
            def _():
                for p in range(2):
                    pass_copy(p, i).wait_recv()

            kvb[1] = dot(xo[lax.rem(i, n)], wf[0, :, width:wide]).astype(BF16)
            for copy in qkv_copies(i):
                copy.start()

            @pl.when((x == 0) & (i < items - n))
            def _():
                token_copy(1, i + n).start()

            @pl.when(i > 0)
            def _():
                for copy in prob_copies(i - 1, False):
                    copy.wait()

            attend(i)
            for copy in prob_copies(i, False):
                copy.start()

            @pl.when(i == 0)
            def _():
                wait_first_of(0, (2,))
                weight_remote(4).wait_recv()

            normed, inv = normalize(dot(ctxb[...], wf[0, :, wide:]) + x0[i].astype(F32))
            natt[i] = normed.astype(BF16)
            stats[i] = jnp.where(stat_lane == heads, inv, stats[i])
            yatt[i] = (normed * nrm[0, 0:1, :] + nrm[0, 1:2, :]).astype(BF16)

            @pl.when(i == 0)
            def _():
                wait_first_of(1, (0, 1, 2))

            @pl.when(i > 0)
            def _():
                route_sent(S_GLO, i - 1)
                route_sent(S_GHI, i - 1)

            qkv_copies(i)[0].wait()

            for part in range(2):
                cols = slice(part * hidden_half, (part + 1) * hidden_half)
                u = dot(yatt[i], wf[1, :, cols])
                cdf = 0.5 + 0.5 * lax.erf(u * 0.7071067811865476)
                pdf = 0.3989422804014327 * jnp.exp(-0.5 * u * u)
                g[:, cols] = (u * cdf).astype(BF16)
                gpb[:, cols] = (cdf + u * pdf).astype(BF16)
            @pl.when(i == 0)
            def _():
                wait_first_of(0, (3,))
                wait_first_of(1, (3,))

            normed, inv = normalize(
                dot(g[:, 0:hidden_half], wd[0])
                + dot(g[:, hidden_half:], wd[1])
                + yatt[i].astype(F32)
            )
            yd[i] = (normed * nrm[1, 0:1, :] + nrm[1, 1:2, :]).astype(BF16)

            @pl.when(x == 0)
            def _():
                for p in range(2):
                    x_copy(p, i).start()

            @pl.when((x == 1) & (i < items - n))
            def _():
                for which in range(2):
                    mem_copy(which, i).start()

            gp_copy(i).start()
            for kind in (S_GLO, S_GHI, S_X0, S_CTX, OUT_ATT, S_Y1, S_Y2, OUT_FF):
                route(kind, i)
            nff[i] = normed.astype(BF16)
            stats[i] = jnp.where(stat_lane == heads + 1, inv, stats[i])

        return carry

    lax.fori_loop(0, items + 1, forward_tick, 0)

    def forward_sent(i):
        route_sent(OUT_FF, i)

        @pl.when(x == 0)
        def _():
            for p in range(2):
                x_copy(p, i).wait_send()

        @pl.when(x == 1)
        def _():
            for p in range(2):
                pass_copy(p, i).wait_send()

        @pl.when((x == 1) & (i < items - n))
        def _():
            for which in range(2):
                mem_copy(which, i).wait_send()

    for copy in prob_copies(items - 1, False) + qkv_copies(items - 1)[1:]:
        copy.wait()
    for copy in prob_copies(items - n, True):
        copy.start()
    gp_copy(items - 1).wait()
    acc[...] = jnp.zeros_like(acc)

    def norm_back(s, i, normed_ref):
        grad = (gy[i] if s else gab[...]).astype(F32)
        normed = normed_ref[i].astype(F32)
        inv = stats[i][:, heads + s : heads + s + 1]
        acc[s, 0:1, :] += jnp.sum(grad * normed, axis=0, keepdims=True)
        acc[s, 1:2, :] += jnp.sum(grad, axis=0, keepdims=True)
        scaled = grad * nrm[s, 0:1, :]
        row_term = jnp.mean(scaled, axis=1, keepdims=True)
        row_cross = jnp.mean(scaled * normed, axis=1, keepdims=True)
        dh = inv * (scaled - row_term - normed * row_cross)
        dhb[...] = dh
        normed_ref[i] = dh.astype(BF16)

    def attend_back(i, slot):
        def prob_grads(j):
            inverse = [stats[i][:, 4 * j + h : 4 * j + h + 1] for h in range(4)]
            c4 = dctx[:, j * quad : (j + 1) * quad].astype(F32) * spread(inverse, head_lanes)
            c4 = c4.astype(BF16)
            tok_v, mem_v = token_and_memory(kv.at[i], width + j * quad)
            return c4, dot(stacked(c4), tok_v, 1, 1), dot(c4, mem_v, 1, 1)

        following = prob_grads(0)
        for j in range(quads):
            c4, dp, dpm = following
            if j + 1 < quads:
                following = prob_grads(j + 1)
            cols = slice(j * quad, (j + 1) * quad)
            q4 = q[i, :, cols]
            tok_k, mem_k = token_and_memory(kv.at[i], j * quad)
            products = c4.astype(F32) * ctx[i, :, cols].astype(F32)
            dp = head_rows(dp)
            inner = [
                jnp.sum(jnp.where(head_lanes == h, products, 0.0), axis=1, keepdims=True)
                for h in range(4)
            ]
            dscores = [
                (tprob[j, h * rows : (h + 1) * rows, :].astype(F32) * (dp[h] - inner[h])).astype(BF16)
                for h in range(4)
            ]
            dsm = (mprob[j].astype(F32) * (dpm - spread(inner, mem_lanes))).astype(BF16)
            ct, qt = jnp.transpose(c4), jnp.transpose(q4)
            mine = [slice(h * head_dim, (h + 1) * head_dim) for h in range(4)]
            dv = [
                dot(ct[mine[h]], tprob[j, h * rows : (h + 1) * rows, :]).astype(BF16)
                for h in range(4)
            ]
            dk = [dot(qt[mine[h]], dscores[h]).astype(BF16) for h in range(4)]
            dv = jnp.transpose(jnp.concatenate(dv, axis=0))
            dk = jnp.transpose(jnp.concatenate(dk, axis=0))
            dscores = jnp.concatenate(dscores, axis=0)
            dq = spread(head_rows(dot(dscores, tok_k)), head_lanes) + dot(dsm, mem_k)
            dqb[:, cols] = (dq * scale).astype(BF16)
            dvm = jnp.where(diagonal, dot(mprob[j], c4, 0, 0), 0.0)
            dkm = jnp.where(diagonal, dot(dsm, q4, 0, 0), 0.0)
            dvm = sum(dvm[h * mem_keys : (h + 1) * mem_keys] for h in range(4))
            dkm = sum(dkm[h * mem_keys : (h + 1) * mem_keys] for h in range(4))
            for half, (tok_part, mem_part) in enumerate(((dk, dkm), (dv, dvm))):
                cols = slice(half * quad, (half + 1) * quad)
                for core in range(2):
                    dkvs[core, j, 0:toks, cols] = tok_part[
                        core * toks : (core + 1) * toks
                    ].astype(BF16)
                    dkvs[core, j, toks:rows, cols] = mem_part[
                        core * MEM_PAD : (core + 1) * MEM_PAD
                    ].astype(BF16)
            if j == quads - 1:
                dkv_copy(j, i, slot).start()
            elif j == quads - 2:
                for ready in range(quads - 1):
                    dkv_copy(ready, i, slot).start()

    def gather_dkv(j, i, slot):
        dkv_copy(j, i, slot).wait_recv()
        both = (dkvs[0, j].astype(F32) + dkvin[slot, j].astype(F32)).astype(BF16)
        kv[i, 0, :, j * quad : (j + 1) * quad] = both[:, 0:quad]
        kv[i, 0, :, width + j * quad : width + (j + 1) * quad] = both[:, quad:]

    def dkv_back(i, low, high):
        return dot(kv[i, 0, :, low:high], wf[0, :, width + low : width + high], 1, 1) + dot(
            kv[i, 0, :, width + low : width + high],
            wf[0, :, 2 * width + low : 2 * width + high], 1, 1,
        )

    def item_of(r):
        return (nseg - 1 - lax.div(r, n)) * n + lax.rem(r, n)

    def backward_tick(t, carry):
        r = t - (1 - x)

        @pl.when((r >= 0) & (r < items))
        def _():
            i = item_of(r)
            slot = lax.rem(r, 2)

            @pl.when(x == 1)
            def _():
                cot_copy(i).wait()

                @pl.when(i >= items - n)
                def _():
                    gy[i, toks:rows, :] = jnp.zeros((MEM_PAD, width), BF16)

                @pl.when(i < items - n)
                def _():
                    mg_copy(i + n).wait_recv()
                    gy[i, toks:rows, :] = jnp.where(
                        keep[i + n][:, 0:1] > 0.0, mgin[i + n], jnp.zeros((), BF16)
                    )

            @pl.when(x == 0)
            def _():
                gy_copy(i).wait_recv()

            @pl.when(r > 0)
            def _():
                route_sent(S_DQ, item_of(r - 1))
                route_sent(GIN_FF, item_of(r - 1))

            norm_back(1, i, nff)
            for part in range(2):
                cols = slice(part * hidden_half, (part + 1) * hidden_half)
                dg = dot(nff[i], wd[part], 1, 1)
                gp[i, :, cols] = (dg * gp[i, :, cols].astype(F32)).astype(BF16)
            gab[...] = (dot(gp[i], wf[1], 1, 1) + dhb[...]).astype(BF16)
            norm_back(0, i, natt)
            dctx[...] = dot(natt[i], wf[0, :, wide:], 1, 1).astype(BF16)
            route(S_DFF0, i)
            route(S_DFF1, i)
            route(S_DU, i)
            route(GIN_FF, i)
            route(S_DATT, i)
            for copy in prob_copies(i, True):
                copy.wait()
            attend_back(i, slot)
            route(S_DQ, i)

            @pl.when(r + 1 < items)
            def _():
                for copy in prob_copies(item_of(r + 1), True):
                    copy.start()

            for j in range(quads - 1):
                gather_dkv(j, i, slot)
            early = (quads - 1) * quad
            partial_sum = dot(dqb[...], wf[0, :, 0:width], 1, 1) + dhb[...]
            if early:
                partial_sum = partial_sum + dkv_back(i, 0, early)
            dhb[...] = partial_sum
            gather_dkv(quads - 1, i, slot)
            route(S_DKV, i)
            forward_sent(i)
            yd[i] = (dkv_back(i, early, width) + dhb[...]).astype(BF16)

            @pl.when(x == 1)
            def _():
                gy_copy(i).start()

            @pl.when((x == 0) & (i >= n))
            def _():
                mg_copy(i).start()

            route(GIN_ATT, i)
            for j in range(quads):
                dkv_copy(j, i, slot).wait_send()

        return carry

    lax.fori_loop(0, items + 1, backward_tick, 0)

    acc_copy = remote(acc.at[1 - c], accp, as_sem, ar_sem, core_peer)
    acc_copy.start()

    def backward_drain(i, carry):
        @pl.when(x == 1)
        def _():
            gy_copy(i).wait_send()

        @pl.when((x == 0) & (i >= n))
        def _():
            mg_copy(i).wait_send()

        for kind in range(KINDS):
            if kind not in (OUT_FF, S_GLO, S_GHI, S_DQ, GIN_FF):
                route_sent(kind, i)
            route_received(kind, i)
        return carry

    lax.fori_loop(0, items, backward_drain, 0)
    route_sent(S_GLO, items - 1)
    route_sent(S_GHI, items - 1)
    route_sent(S_DQ, item_of(items - 1))
    route_sent(GIN_FF, item_of(items - 1))
    for k in range(5):
        weight_remote(k).wait_send()
    acc_copy.wait()
    norm_grad[...] = acc[c] + accp[...]


def run_layers(n, nseg, heads, tokens, cotangent, first, down, docs, resets, gain, shift):
    length, width = tokens.shape[1:]
    toks = length // nseg // 2
    rows = toks + MEM_PAD
    items = n * nseg
    hidden_half = down.shape[1]
    quads = heads // 4
    quad = width // quads
    any_spec = pl.BlockSpec(memory_space=pl.ANY)
    vmem_spec = pl.BlockSpec(memory_space=pltpu.VMEM)
    dma = pltpu.SemaphoreType.DMA
    item_rows = pltpu.VMEM((items, rows, width), BF16)
    one, two = dma((items,)), dma((2, items))
    return pl.pallas_call(
        partial(layers_kernel, n, nseg, heads),
        out_shape=(
            jax.ShapeDtypeStruct((n, length, width), BF16),
            jax.ShapeDtypeStruct((n, length, width), BF16),
            jax.ShapeDtypeStruct((2 * items, rows, width), BF16),
            jax.ShapeDtypeStruct((2 * items, rows, width), BF16),
            jax.ShapeDtypeStruct((2 * items, rows, 4 * width), BF16),
            jax.ShapeDtypeStruct((2 * items, rows, hidden_half), BF16),
            jax.ShapeDtypeStruct((2 * items, rows, width), BF16),
            jax.ShapeDtypeStruct((2, width), F32),
            jax.ShapeDtypeStruct((items, quads, 4 * rows, 2 * toks), BF16),
            jax.ShapeDtypeStruct((items, quads, rows, 8 * MEM_PAD), BF16),
        ),
        in_specs=[any_spec] * 4 + [vmem_spec] * 4,
        out_specs=[any_spec] * 7 + [vmem_spec] + [any_spec] * 2,
        scratch_shapes=[
            pltpu.VMEM((2, width, 4 * width), BF16),
            pltpu.VMEM((2, hidden_half, width), BF16),
            pltpu.VMEM((2, 2, width), F32),
            item_rows,
            pltpu.VMEM((n, rows, width), BF16),
            item_rows,
            pltpu.VMEM((items, 2, rows, 2 * width), BF16),
            item_rows,
            item_rows,
            item_rows,
            item_rows,
            item_rows,
            item_rows,
            pltpu.VMEM((rows, 2 * hidden_half), BF16),
            pltpu.VMEM((rows, 2 * hidden_half), BF16),
            pltpu.VMEM((items, rows, 2 * hidden_half), BF16),
            pltpu.VMEM((items, rows, 128), F32),
            pltpu.VMEM((items, toks, 128), F32),
            pltpu.VMEM((items, 1, 2 * toks), F32),
            pltpu.VMEM((items, MEM_PAD, 128), F32),
            pltpu.VMEM((2, items, MEM_PAD, width), BF16),
            pltpu.VMEM((items, MEM_PAD, width), BF16),
            pltpu.VMEM((2, quads, rows, 2 * quad), BF16),
            pltpu.VMEM((2, quads, rows, 2 * quad), BF16),
            pltpu.VMEM((rows, width), F32),
            pltpu.VMEM((2, rows, 2 * width), BF16),
            pltpu.VMEM((2, 2, width), F32),
            pltpu.VMEM((2, width), F32),
            pltpu.VMEM((quads, 4 * rows, 2 * toks), BF16),
            pltpu.VMEM((quads, rows, 8 * MEM_PAD), BF16),
            dma((4,)), dma((5,)), dma((5,)),
            two, one, one, two, two, two,
            two, two,
            two, two,
            two, two,
            one, one, one, one,
            dma((quads, items)), dma((quads, items)),
            dma(()), dma(()),
        ]
        + [dma((KINDS, items))] * 3,
        compiler_params=pltpu.CompilerParams(
            collective_id=0, has_side_effects=True, vmem_limit_bytes=61 * 1024 * 1024
        ),
    )(tokens, cotangent, first, down, docs, resets, gain, shift)


def reduce_kernel(
    chunks,
    sx1, sx2, sr, sg, sd, norm_part,
    sums, norm_out,
    x1, x2, rr, gg, dd, work, done, got_u, got_uz, got_vz, got_vy, norms,
    right_sem, left_sem, out_sem, u_s, u_r, uz_s, uz_r, vz_s, vz_r, vy_s, vy_r, vg_s, vg_r,
    uzg_s, uzg_r, vzg_s, vzg_r, ug_s, ug_r, n_s, n_r,
):
    lines = 4
    d = lax.axis_index("dp")
    y = lax.rem(d, 2)
    z = lax.div(d, 2)
    dp = lax.axis_size("dp")
    width = sd.shape[1]
    half = width // 2
    part = width // chunks
    hr = part // 2
    lane_group = 128
    per_group = lane_group // part
    y_peer = {"dp": z * 2 + (1 - y)}

    def remote(src, dst, send, recv, peer):
        return pltpu.make_async_remote_copy(
            src_ref=src, dst_ref=dst, send_sem=send, recv_sem=recv,
            device_id=peer, device_id_type=MESH,
        )

    def other(step):
        return {"dp": lax.rem(d + step, dp)}

    barrier = pltpu.get_barrier_semaphore()
    for step in range(1, dp):
        pl.semaphore_signal(barrier, inc=1, device_id=other(step), device_id_type=MESH)

    lane_groups = width // lane_group
    right_loads = [(sd, dd)] + [
        (sr.at[:, b * width : (b + 1) * width], rr.at[:, b * width : (b + 1) * width])
        for b in range(4)
    ]

    def right_load(k):
        src, dst = right_loads[k]
        return pltpu.make_async_copy(src, dst, right_sem.at[k])

    def left_load(which, group):
        src, dst, low = ((sg, gg, 0), (sg, gg, width), (sx2, x2, 0), (sx1, x1, 0))[which]
        cols = pl.ds(pl.multiple_of(low + group * lane_group, lane_group), lane_group)
        return pltpu.make_async_copy(src.at[:, cols], dst.at[:, cols], left_sem.at[which, group])

    right_load(0).start()
    left_load(0, 0).start()
    left_load(1, 0).start()
    left_load(2, 0).start()
    right_load(4).start()

    norms[d] = norm_part[...]
    pl.semaphore_wait(barrier, dp - 1)

    def norm_copy(step):
        return remote(norms.at[d], norms.at[d], n_s.at[step - 1], n_r.at[step - 1], other(step))

    def norm_arrival(step):
        source = lax.rem(d + dp - step, dp)
        return remote(
            norms.at[source], norms.at[source], n_s.at[step - 1], n_r.at[step - 1], other(step)
        )

    for step in range(1, dp):
        norm_copy(step).start()

    def column_half(h):
        return pl.ds(pl.multiple_of(h * half, 128), half)

    mine, theirs = column_half(y), column_half(1 - y)

    def place(flow):
        return z if flow == 0 else lines - 1 - z

    def onward(flow):
        step = -1 if flow == 0 else 1
        return {"dp": (z + step) * 2 + y}

    def back(flow):
        step = 1 if flow == 0 else -1
        return {"dp": (z + step) * 2 + y}

    def rows_of(flow):
        return slice(flow * hr, (flow + 1) * hr)

    def u_copy(k):
        return remote(
            work.at[k, 0:3, :, theirs], got_u.at[k], u_s.at[k], u_r.at[k], y_peer
        )

    def uz_copy(flow, k):
        return remote(
            work.at[k, 0:3, rows_of(flow), mine], got_uz.at[flow, k],
            uz_s.at[flow, k], uz_r.at[flow, k], onward(flow),
        )

    def vz_copy(flow, k):
        return remote(
            work.at[k, 3:6, rows_of(flow), :], got_vz.at[flow, k],
            vz_s.at[flow, k], vz_r.at[flow, k], onward(flow),
        )

    def vy_copy(flow, k):
        return remote(
            work.at[k, 3:6, rows_of(flow), theirs], got_vy.at[k], vy_s.at[k], vy_r.at[k], y_peer
        )

    def vg_copy(flow, k, cols):
        spot = done.at[k, 3:6, rows_of(flow), cols]
        return remote(spot, spot, vg_s.at[k], vg_r.at[k], y_peer)

    def uzg_copy(flow, k):
        spot = done.at[k, 0:3, rows_of(flow), mine]
        return remote(spot, spot, uzg_s.at[flow, k], uzg_r.at[flow, k], back(flow))

    def vzg_copy(flow, k):
        spot = done.at[k, 3:6, rows_of(flow), :]
        return remote(spot, spot, vzg_s.at[flow, k], vzg_r.at[flow, k], back(flow))

    def ug_copy(flow, k, cols):
        spot = done.at[k, 0:3, rows_of(flow), cols]
        return remote(spot, spot, ug_s.at[flow, k], ug_r.at[flow, k], y_peer)

    def out_copy(k):
        return pltpu.make_async_copy(done.at[k], sums.at[k], out_sem.at[k])

    def plus(a, b):
        return (a.astype(F32) + b.astype(F32)).astype(BF16)

    def ready(k, low=0):
        return (k >= low) & (k < chunks)

    def store_chunks(group, block, value):
        for e in range(per_group):
            work[group * per_group + e, block] = value[e * part : (e + 1) * part]

    def second_half(r):
        group = lax.div(r + per_group - 1, per_group)
        cols = pl.ds(pl.multiple_of(group * lane_group, lane_group), lane_group)
        gcols = pl.ds(pl.multiple_of(width + group * lane_group, lane_group), lane_group)

        @pl.when(r == 0)
        def _():
            right_load(0).wait()

        left_load(0, group).wait()
        store_chunks(group, 4, dot(gg[:, cols], dd[...], 0, 0).astype(BF16))
        left_load(1, group).wait()
        store_chunks(group, 5, dot(gg[:, gcols], dd[...], 0, 0).astype(BF16))
        left_load(2, group).wait()

        @pl.when(r == 0)
        def _():
            right_load(4).wait()
            left_load(3, 0).start()
            for k in range(1, 4):
                right_load(k).start()
            for later in range(1, lane_groups):
                for which in range(4):
                    left_load(which, later).start()

        store_chunks(group, 3, dot(x2[:, cols], rr[:, 3 * width :], 0, 0).astype(BF16))

    def round_step(r, carry):
        @pl.when(r == 0)
        def _():
            second_half(r)

        for flow in range(2):
            p = place(flow)
            k = r - (lines - 1 - p)
            rows = rows_of(flow)

            @pl.when(ready(k))
            def _():
                @pl.when(p < lines - 1)
                def _():
                    vz_copy(flow, k).wait_recv()
                    work[k, 3:6, rows, :] = plus(work[k, 3:6, rows, :], got_vz[flow, k])

                @pl.when(p > 0)
                def _():
                    vz_copy(flow, k).start()

                @pl.when(p == 0)
                def _():
                    vy_copy(flow, k).start()

        @pl.when((lax.rem(r, per_group) == 0) & (r < chunks))
        def _():
            group = lax.div(r, per_group)
            cols = pl.ds(pl.multiple_of(group * lane_group, lane_group), lane_group)
            left_load(3, group).wait()
            for b in range(3):

                @pl.when(r == 0)
                def _():
                    right_load(1 + b).wait()

                store_chunks(
                    group, b,
                    dot(x1[:, cols], rr[:, b * width : (b + 1) * width], 0, 0).astype(BF16),
                )

        @pl.when(ready(r))
        def _():
            u_copy(r).start()

        @pl.when((lax.rem(r, per_group) == per_group - 1) & (r + 1 < chunks))
        def _():
            second_half(r)

        @pl.when(ready(r - 1))
        def _():
            k = r - 1
            u_copy(k).wait_recv()
            work[k, 0:3, :, mine] = plus(work[k, 0:3, :, mine], got_u[k])

        for flow in range(2):
            p = place(flow)
            k = r - 1 - (lines - 1 - p)
            rows = rows_of(flow)

            @pl.when(ready(k))
            def _():
                @pl.when(p < lines - 1)
                def _():
                    uz_copy(flow, k).wait_recv()
                    total = plus(work[k, 0:3, rows, mine], got_uz[flow, k])

                    @pl.when(p > 0)
                    def _():
                        work[k, 0:3, rows, mine] = total

                    @pl.when(p == 0)
                    def _():
                        done[k, 0:3, rows, mine] = total

                @pl.when(p > 0)
                def _():
                    uz_copy(flow, k).start()

                @pl.when(p == 0)
                def _():
                    uzg_copy(flow, k).start()
                    ug_copy(flow, k, mine).start()

        for flow in range(2):
            p = place(flow)
            rows = rows_of(flow)

            @pl.when((p == 0) & ready(r - lines))
            def _():
                k = r - lines
                vy_copy(flow, k).wait_recv()
                done[k, 3:6, rows, mine] = plus(work[k, 3:6, rows, mine], got_vy[k])
                vg_copy(flow, k, mine).start()

            @pl.when((p == 0) & ready(r - lines - 1))
            def _():
                k = r - lines - 1
                vg_copy(flow, k, theirs).wait_recv()
                vzg_copy(flow, k).start()

        for flow in range(2):
            p = place(flow)
            k = r - lines - p

            @pl.when((p > 0) & ready(k))
            def _():
                uzg_copy(flow, k).wait_recv()

                @pl.when(p < lines - 1)
                def _():
                    uzg_copy(flow, k).start()

                ug_copy(flow, k, mine).start()

        for flow in range(2):
            p = place(flow)
            k = r - lines - 1 - p

            @pl.when((p > 0) & ready(k))
            def _():
                vzg_copy(flow, k).wait_recv()

                @pl.when(p < lines - 1)
                def _():
                    vzg_copy(flow, k).start()

            @pl.when(ready(k))
            def _():
                ug_copy(flow, k, theirs).wait_recv()

        @pl.when(ready(r - 2 * lines))
        def _():
            out_copy(r - 2 * lines).start()

        return carry

    lax.fori_loop(0, chunks + 2 * lines, round_step, 0)

    for step in range(1, dp):
        norm_arrival(step).wait_recv()
    total = norms[0]
    for e in range(1, dp):
        total = total + norms[e]
    norm_out[...] = total

    def drain(k, carry):
        out_copy(k).wait()
        u_copy(k).wait_send()
        for flow in range(2):
            p = place(flow)
            ug_copy(flow, k, mine).wait_send()

            @pl.when(p > 0)
            def _():
                vz_copy(flow, k).wait_send()
                uz_copy(flow, k).wait_send()

            @pl.when(p < lines - 1)
            def _():
                uzg_copy(flow, k).wait_send()
                vzg_copy(flow, k).wait_send()

            @pl.when(p == 0)
            def _():
                vy_copy(flow, k).wait_send()
                vg_copy(flow, k, mine).wait_send()

        return carry

    lax.fori_loop(0, chunks, drain, 0)
    for step in range(1, dp):
        norm_copy(step).wait_send()


def sum_weights(dp, sx1, sx2, sr, sg, sd, norm_part):
    total, width = sx1.shape
    chunks = 12
    part = width // chunks
    half = width // 2
    any_spec = pl.BlockSpec(memory_space=pl.ANY)
    vmem_spec = pl.BlockSpec(memory_space=pltpu.VMEM)
    dma = pltpu.SemaphoreType.DMA
    one, two = dma((chunks,)), dma((2, chunks))
    return pl.pallas_call(
        partial(reduce_kernel, chunks),
        out_shape=(
            jax.ShapeDtypeStruct((chunks, 6, part, width), BF16),
            jax.ShapeDtypeStruct((2, width), F32),
        ),
        in_specs=[any_spec] * 5 + [vmem_spec],
        out_specs=[any_spec, vmem_spec],
        scratch_shapes=[
            pltpu.VMEM((total, width), BF16),
            pltpu.VMEM((total, width), BF16),
            pltpu.VMEM((total, 4 * width), BF16),
            pltpu.VMEM((total, 2 * width), BF16),
            pltpu.VMEM((total, width), BF16),
            pltpu.VMEM((chunks, 6, part, width), BF16),
            pltpu.VMEM((chunks, 6, part, width), BF16),
            pltpu.VMEM((chunks, 3, part, half), BF16),
            pltpu.VMEM((2, chunks, 3, part // 2, half), BF16),
            pltpu.VMEM((2, chunks, 3, part // 2, width), BF16),
            pltpu.VMEM((chunks, 3, part // 2, half), BF16),
            pltpu.VMEM((dp, 2, width), F32),
            dma((5,)),
            dma((4, width // 128)),
            one,
            one, one,
            two, two,
            two, two,
            one, one,
            one, one,
            two, two,
            two, two,
            two, two,
            dma((dp - 1,)), dma((dp - 1,)),
        ],
        compiler_params=pltpu.CompilerParams(
            collective_id=1, has_side_effects=True, vmem_limit_bytes=60 * 1024 * 1024
        ),
    )(sx1, sx2, sr, sg, sd, norm_part)


def finish_kernel(sums, out, gin, norms, first_grad, down_grad, out_copy, gin_copy, gain, shift):
    group, _, part, width = sums.shape
    for e in range(group):
        rows = slice(e * part, (e + 1) * part)
        for b in range(4):
            first_grad[rows, b * width : (b + 1) * width] = sums[e, b].astype(F32)
        for b in range(2):
            down_grad[b, rows] = sums[e, 4 + b].astype(F32)
    out_copy[...] = out[...]
    gin_copy[...] = gin[...]
    gain[...] = norms[0:1]
    shift[...] = norms[1:2]


def finish(sums, out, gin, norms):
    chunks, _, part, width = sums.shape
    total = out.shape[0]
    group, blocks = chunks // 3, 2
    tokens = pl.BlockSpec((total // blocks, width), lambda k: (jnp.minimum(k, blocks - 1), 0))
    whole = pl.BlockSpec((1, width), lambda k: (0, 0))
    return pl.pallas_call(
        finish_kernel,
        grid=(chunks // group,),
        out_shape=(
            jax.ShapeDtypeStruct((width, 4 * width), F32),
            jax.ShapeDtypeStruct((2, width, width), F32),
            jax.ShapeDtypeStruct(out.shape, BF16),
            jax.ShapeDtypeStruct(gin.shape, BF16),
            jax.ShapeDtypeStruct((1, width), F32),
            jax.ShapeDtypeStruct((1, width), F32),
        ),
        in_specs=[
            pl.BlockSpec((group, 6, part, width), lambda k: (k, 0, 0, 0)),
            tokens,
            tokens,
            pl.BlockSpec((2, width), lambda k: (0, 0)),
        ],
        out_specs=[
            pl.BlockSpec((group * part, 4 * width), lambda k: (k, 0)),
            pl.BlockSpec((2, group * part, width), lambda k: (0, k, 0)),
            tokens,
            tokens,
            whole,
            whole,
        ],
        compiler_params=pltpu.CompilerParams(vmem_limit_bytes=61 * 1024 * 1024),
    )(sums, out, gin, norms)


def shards(
    tokens, doc_ids, reset_flags, first_weights, down_halves, norm_gain, norm_bias, cotangent
):
    n, length, width = tokens.shape
    items = n * NSEG
    rows = length // NSEG // 2 + MEM_PAD
    out, gin, sx1, sx2, sr, sg, sd, norm_grad, _, _ = run_layers(
        n, NSEG, H, tokens, cotangent, first_weights, down_halves,
        doc_ids, reset_flags.T, norm_gain, norm_bias,
    )
    total = 2 * items * rows
    sx1, sx2, sd = (a.reshape(total, width) for a in (sx1, sx2, sd))
    sr = sr.reshape(total, 4 * width)
    sg = sg.reshape(total, -1)

    dp = lax.axis_size("dp")
    if dp == 8:
        sums, norm_grad = sum_weights(dp, sx1, sx2, sr, sg, sd, norm_grad)
        first_grad, down_grad, out, gin, gain_grad, shift_grad = finish(
            sums, out.reshape(-1, width), gin.reshape(-1, width), norm_grad
        )
        down_grad = down_grad.reshape(-1, width)
        out, gin = (a.reshape(n, length, width) for a in (out, gin))
    else:

        def weight_grad(left, right):
            return jnp.einsum("rd,re->de", left, right, preferred_element_type=F32).astype(BF16)

        first_grad = jnp.concatenate(
            [weight_grad(sx1, sr[:, : 3 * width]), weight_grad(sx2, sr[:, 3 * width :])], axis=1
        )
        down_grad = weight_grad(sg, sd)
        first_grad, down_grad = lax.psum((first_grad, down_grad), "dp")
        norm_grad = lax.psum(norm_grad, "dp")
        gain_grad, shift_grad = norm_grad[0:1], norm_grad[1:2]
    return (
        out[None],
        gin[None],
        first_grad.astype(F32)[None],
        down_grad.astype(F32)[None],
        gain_grad,
        shift_grad,
    )


def solution(mesh):
    in_specs = (
        P("dp", None, None),
        P("dp", None),
        P("dp", None),
        P("section", None, None),
        P("section", None, None),
        P("section", None),
        P("section", None),
        P("dp", None, None),
    )
    out_specs = (
        P("section", "dp", None, None),
        P("section", "dp", None, None),
        P("section", None, None),
        P("section", None, None),
        P("section", None),
        P("section", None),
    )
    return jax.shard_map(shards, mesh=mesh, in_specs=in_specs, out_specs=out_specs, check_vma=False)
```

```python
from functools import partial

import jax
import jax.numpy as jnp
from jax import lax
from jax.experimental import pallas as pl
from jax.experimental.pallas import tpu as pltpu
from jax.sharding import PartitionSpec as P

H = 12
M = 20
NSEG = 2
MEM_PAD = 16
NORM_EPSILON = 1e-05
MASKED_SCORE = -1000000000.0
ABSENT_SCORE = -3e38
MESH = pl.DeviceIdType.MESH
BF16 = jnp.bfloat16
F32 = jnp.float32

OUT_ATT, OUT_FF, GIN_ATT, GIN_FF = 0, 1, 2, 3
S_X0, S_CTX, S_DQ, S_DKV, S_DATT, S_GLO, S_DFF0 = 4, 5, 6, 7, 8, 9, 10
S_Y1, S_Y2, S_DU, S_GHI, S_DFF1 = 11, 12, 13, 14, 15
S_DV, S_LASTK, S_LASTV = 16, 17, 18
KINDS = 19


def dot(a, b, lhs_dim=1, rhs_dim=0):
    return lax.dot_general(
        a, b, (((lhs_dim,), (rhs_dim,)), ((), ())), preferred_element_type=F32
    )


def normalize(summed):
    mean = jnp.mean(summed, axis=-1, keepdims=True)
    centered = summed - mean
    var = jnp.mean(centered * centered, axis=-1, keepdims=True)
    inv = lax.rsqrt(var + NORM_EPSILON)
    return centered * inv, inv


def group_of(shape, dim, size):
    index = lax.broadcasted_iota(jnp.int32, shape, dim)
    return lax.shift_right_logical(index, size.bit_length() - 1)


def spread(values, groups):
    result = values[-1]
    for h in range(len(values) - 1):
        result = jnp.where(groups == h, values[h], result)
    return result


def layers_kernel(
    n, nseg, heads,
    tokens, cotangent, first, down, docs, resets, gain, shift,
    out, gin, sx1, sx2, sr, sg, sd, norm_grad, ptok, pmem,
    wf, wd, nrm, x0, xo, q, kv, ctx, natt, yatt, nff, yd, gy, g, gpb, gp, stats, qdoc, kdoc, keep,
    memin, mgin, dkvs, dkvin, dhb, kvb, acc, accp, tprob, mprob,
    wl, ws, wr, tok_sem, cot_sem, gp_sem, qkv_sem, pw_sem, pr_sem, fs_sem, fr_sem, xs_sem, xr_sem,
    ms_sem, mr_sem, gs_sem, gr_sem, hs_sem, hr_sem, ds_sem, dr_sem, as_sem, ar_sem,
    lsem, ssem, rsem,
):
    items = n * nseg
    section = lax.axis_index("section")
    c = lax.rem(section, 2)
    x = lax.div(section, 2)
    core_peer = {"section": x * 2 + (1 - c)}
    chip_peer = {"section": (1 - x) * 2 + c}
    cross_peer = {"section": (1 - x) * 2 + (1 - c)}
    rows, width = x0.shape[1:]
    toks = rows - MEM_PAD
    seg_len = 2 * toks
    hidden_half = wd.shape[1]
    wide = 3 * width
    head_dim = width // heads
    quad = 4 * head_dim
    quads = heads // 4
    mem_keys = 2 * MEM_PAD
    scale = head_dim ** (-0.5)
    qb = gpb.at[:, 0:width]
    ctxb = gpb.at[:, width : 2 * width]
    dqb = gpb.at[:, 0:width]
    gab = gpb.at[:, width : 2 * width]
    dctx = gpb.at[:, 2 * width : wide]

    def remote(src, dst, send, recv, peer):
        return pltpu.make_async_remote_copy(
            src_ref=src, dst_ref=dst, send_sem=send, recv_sem=recv,
            device_id=peer, device_id_type=MESH,
        )

    barrier = pltpu.get_barrier_semaphore()
    pl.semaphore_signal(barrier, inc=1, device_id=core_peer, device_id_type=MESH)
    pl.semaphore_signal(barrier, inc=1, device_id=chip_peer, device_id_type=MESH)
    pl.semaphore_signal(barrier, inc=1, device_id=cross_peer, device_id_type=MESH)

    def token_rows(ref, i, core=None):
        core = c if core is None else core
        return ref.at[lax.rem(i, n), pl.ds(lax.div(i, n) * seg_len + core * toks, toks), :]

    def token_copy(which, i):
        if which == 0:
            src, dst = token_rows(tokens, i), x0.at[i, 0:toks, :]
        else:
            src, dst = token_rows(tokens, i, 1 - c), xo.at[lax.rem(i, n), 0:toks, :]
        return pltpu.make_async_copy(src, dst, tok_sem.at[which, i])

    def cot_copy(i):
        return pltpu.make_async_copy(
            token_rows(cotangent, i), gy.at[i, 0:toks, :], cot_sem.at[i]
        )

    def weight_piece(k):
        if k == 0:
            return first.at[0, :, width:wide], wf.at[c, :, width:wide]
        if k == 1:
            return first.at[0, :, 0:width], wf.at[c, :, 0:width]
        if k == 2:
            return first.at[0, :, wide:], wf.at[c, :, wide:]
        return down.at[0], wd.at[c]

    def weight_local(k):
        src, dst = weight_piece(k)
        return pltpu.make_async_copy(src, dst, wl.at[k])

    def weight_remote(k):
        if k == 4:
            return remote(nrm.at[c], nrm.at[c], ws.at[4], wr.at[4], core_peer)
        src, dst = weight_piece(k)
        return remote(src, dst, ws.at[k], wr.at[k], core_peer)

    nrm[c, 0:1, :] = gain[...]
    nrm[c, 1:2, :] = shift[...]
    weight_local(0).start()

    @pl.when(x == 0)
    def _():
        token_copy(0, 0).start()
        token_copy(1, 0).start()

    pl.semaphore_wait(barrier, 3)
    for k in range(5):
        weight_remote(k).start()
    for k in range(1, 4):
        weight_local(k).start()
    for i in range(items):
        if i > 0:

            @pl.when(x == 0)
            def _():
                token_copy(0, i).start()
                if i < n:
                    token_copy(1, i).start()

        @pl.when(x == 1)
        def _():
            cot_copy(i).start()

    def wait_first_of(core, ks):
        @pl.when(c == core)
        def _():
            for k in ks:
                weight_local(k).wait()

        @pl.when(c != core)
        def _():
            for k in ks:
                weight_remote(k).wait_recv()

    for i in range(items):
        seq, seg = i % n, i // n
        own = pl.ds(pl.multiple_of(seg * seg_len + c * toks, toks), toks)
        others = pl.ds(pl.multiple_of(seg * seg_len + (1 - c) * toks, toks), toks)
        own_row = docs[seq : seq + 1, own].astype(F32)
        kdoc[i, :, 0:toks] = own_row
        kdoc[i, :, toks:] = docs[seq : seq + 1, others].astype(F32)
        qdoc[i] = jnp.transpose(jnp.broadcast_to(own_row, (128, toks)))
        if seg > 0:
            flag = resets[seg - 1 : seg, seq : seq + 1].astype(F32)
            keep[i] = jnp.broadcast_to(1.0 - flag, (MEM_PAD, 128))

    def routed(kind, i):
        block = i * 2 + c
        sec = 0
        if kind == OUT_ATT:
            src, dst = yatt.at[i, 0:toks, :], token_rows(out, i)
        elif kind == OUT_FF:
            src, dst, sec = yd.at[i, 0:toks, :], token_rows(out, i), 1
        elif kind == GIN_ATT:
            src, dst = yd.at[i, 0:toks, :], token_rows(gin, i)
        elif kind == GIN_FF:
            src, dst, sec = gab.at[0:toks, :], token_rows(gin, i), 1
        elif kind == S_X0:
            src, dst = x0.at[i], sx1.at[block]
        elif kind == S_CTX:
            src, dst = ctx.at[i], sx2.at[block]
        elif kind == S_DQ:
            src, dst = dqb, sr.at[block, :, 0:width]
        elif kind in (S_DKV, S_DV, S_LASTK, S_LASTV):
            last = width - width // quads
            low, high = (0, last) if kind in (S_DKV, S_DV) else (last, width)
            if kind in (S_DV, S_LASTV):
                low, high = low + width, high + width
            src, dst = kv.at[i, 0, :, low:high], sr.at[block, :, width + low : width + high]
        elif kind == S_DATT:
            src, dst = natt.at[i], sr.at[block, :, wide:]
        elif kind == S_GLO:
            src, dst = g.at[:, 0:hidden_half], sg.at[block]
        elif kind == S_DFF0:
            src, dst = nff.at[i], sd.at[block]
        elif kind == S_Y1:
            src, dst, sec = yatt.at[i], sx1.at[block], 1
        elif kind == S_Y2:
            src, dst, sec = yatt.at[i], sx2.at[block], 1
        elif kind == S_DU:
            src, dst, sec = gp.at[i], sr.at[block], 1
        elif kind == S_GHI:
            src, dst, sec = g.at[:, hidden_half:], sg.at[block], 1
        else:
            src, dst, sec = nff.at[i], sd.at[block], 1
        return src, dst, sec

    def route_local(kind, i):
        src, dst, _ = routed(kind, i)
        return pltpu.make_async_copy(src, dst, lsem.at[kind, i])

    def route_away(kind, i):
        src, dst, _ = routed(kind, i)
        return remote(src, dst, ssem.at[kind, i], rsem.at[kind, i], core_peer)

    def route(kind, i):
        sec = routed(kind, i)[2]

        @pl.when(c == sec)
        def _():
            route_local(kind, i).start()

        @pl.when(c != sec)
        def _():
            route_away(kind, i).start()

    def route_sent(kind, i):
        sec = routed(kind, i)[2]

        @pl.when(c == sec)
        def _():
            route_local(kind, i).wait()

        @pl.when(c != sec)
        def _():
            route_away(kind, i).wait_send()

    def route_received(kind, i):
        @pl.when(c == routed(kind, i)[2])
        def _():
            route_away(kind, i).wait_recv()

    def qkv_copies(i):
        return [
            pltpu.make_async_copy(qb, q.at[i], qkv_sem.at[0, i]),
            pltpu.make_async_copy(kvb, kv.at[i], qkv_sem.at[1, i]),
        ]

    def gp_copy(i):
        return pltpu.make_async_copy(gpb, gp.at[i], gp_sem.at[i])

    def prob_copies(i, back):
        pairs = ((tprob, ptok.at[i]), (mprob, pmem.at[i]))
        if back:
            return [
                pltpu.make_async_copy(dst, src, pr_sem.at[e, i])
                for e, (src, dst) in enumerate(pairs)
            ]
        return [
            pltpu.make_async_copy(src, dst, pw_sem.at[e, i]) for e, (src, dst) in enumerate(pairs)
        ]

    cut = rows // 32 * 16

    def piece(p):
        return slice(0, cut) if p == 0 else slice(cut, rows)

    def x_copy(p, i):
        return remote(
            yd.at[i, piece(p)], x0.at[i, piece(p)], xs_sem.at[p, i], xr_sem.at[p, i], chip_peer
        )

    def pass_copy(p, i):
        return remote(
            x0.at[i, piece(p)], xo.at[lax.rem(i, n), piece(p)],
            fs_sem.at[p, i], fr_sem.at[p, i], core_peer,
        )

    def mem_copy(which, i):
        return remote(
            yd.at[i, toks:rows, :], memin.at[which, i], ms_sem.at[which, i],
            mr_sem.at[which, i], cross_peer if which else chip_peer,
        )

    def gy_copy(i):
        return remote(yd.at[i], gy.at[i], gs_sem.at[i], gr_sem.at[i], chip_peer)

    def mg_copy(i):
        return remote(
            yd.at[i, toks:rows, :], mgin.at[i], hs_sem.at[i], hr_sem.at[i], chip_peer
        )

    def dkv_copy(j, i, slot):
        return remote(
            dkvs.at[1, j], dkvin.at[slot, j], ds_sem.at[j, i], dr_sem.at[j, i], core_peer
        )

    head_lanes = group_of((rows, quad), 1, head_dim)
    mem_lanes = group_of((rows, 4 * mem_keys), 1, mem_keys)
    key_lane = lax.broadcasted_iota(jnp.int32, (rows, 4 * mem_keys), 1)
    mem_valid = lax.rem(key_lane, MEM_PAD) < M // 2
    diagonal = group_of((4 * mem_keys, quad), 0, mem_keys) == group_of(
        (4 * mem_keys, quad), 1, head_dim
    )
    stat_lane = lax.broadcasted_iota(jnp.int32, (rows, 128), 1)

    def stacked(block):
        return jnp.concatenate(
            [jnp.where(head_lanes == h, block, BF16(0)) for h in range(4)], axis=0
        )

    def head_rows(block):
        return [block[h * rows : (h + 1) * rows] for h in range(4)]

    def token_and_memory(ref, low):
        cols = slice(low, low + quad)
        tok = jnp.concatenate([ref[0, 0:toks, cols], ref[1, 0:toks, cols]], axis=0)
        mem = jnp.concatenate([ref[0, toks:, cols], ref[1, toks:, cols]], axis=0)
        return tok, jnp.where(diagonal, jnp.concatenate([mem] * 4, axis=0), BF16(0))

    def only_same_document(s, i):
        mine = jnp.concatenate([qdoc[i]] * (seg_len // 128), axis=1)
        same = jnp.where(mine == kdoc[i], s[0:toks], MASKED_SCORE)
        return jnp.concatenate([same, s[toks:]], axis=0)

    def memory_scores(q4, mem_k):
        return jnp.where(mem_valid, dot(q4, mem_k, 1, 1), ABSENT_SCORE)

    def attend(i):
        own = [mem_lanes == h for h in range(4)]

        def scores(j):
            q4 = qb[:, j * quad : (j + 1) * quad]
            tok_k, mem_k = token_and_memory(kvb, j * quad)
            return dot(stacked(q4), tok_k, 1, 1), memory_scores(q4, mem_k)

        st = jnp.zeros((rows, 128), F32)
        following = scores(0)
        for j in range(quads):
            s, sm = following
            if j + 1 < quads:
                following = scores(j + 1)
            s = [only_same_document(part, i) for part in head_rows(s)]
            peaks = [
                jnp.max(
                    jnp.concatenate([s[h], jnp.where(own[h], sm, ABSENT_SCORE)], axis=1),
                    axis=1, keepdims=True,
                )
                for h in range(4)
            ]
            pm = jnp.exp(sm - spread(peaks, mem_lanes))
            mprob[j] = pm.astype(BF16)
            totals, probs = [], []
            for h in range(4):
                p = jnp.exp(s[h] - peaks[h])
                probs.append(p.astype(BF16))
                tprob[j, h * rows : (h + 1) * rows, :] = probs[h]
                both = jnp.concatenate([p, jnp.where(own[h], pm, 0.0)], axis=1)
                totals.append(1.0 / jnp.sum(both, axis=1, keepdims=True))
                st = jnp.where(stat_lane == 4 * j + h, totals[h], st)
            tok_v, mem_v = token_and_memory(kvb, width + j * quad)
            o = spread(head_rows(dot(jnp.concatenate(probs, axis=0), tok_v)), head_lanes)
            o = o + dot(pm.astype(BF16), mem_v)
            ctxb[:, j * quad : (j + 1) * quad] = (o * spread(totals, head_lanes)).astype(BF16)
        stats[i] = st
        ctx[i] = ctxb[...]

    def to_queries(product):
        return product.astype(BF16) * BF16(scale)

    def forward_tick(t, carry):
        i = t - x

        @pl.when((i >= 0) & (i < items))
        def _():
            ahead = (x == 0) & (i >= n) & (lax.rem(i, n) == 0)

            @pl.when(i > 0)
            def _():
                qkv_copies(i - 1)[1].wait()
                gp_copy(i - 1).wait()

            @pl.when(x == 0)
            def _():
                token_copy(0, i).wait()
                token_copy(1, i).wait()

            @pl.when(ahead)
            def _():
                kvb[0, 0:toks, :] = dot(x0[i, 0:toks, :], wf[0, :, width:wide]).astype(BF16)
                kvb[1, 0:toks, :] = dot(
                    xo[lax.rem(i, n), 0:toks, :], wf[0, :, width:wide]
                ).astype(BF16)
                qb[0:toks, :] = to_queries(dot(x0[i, 0:toks, :], wf[0, :, 0:width]))

            @pl.when(x == 0)
            def _():
                for which, rows_ref in enumerate((x0.at[i], xo.at[lax.rem(i, n)])):

                    @pl.when(i < n)
                    def _():
                        rows_ref[toks:rows, :] = jnp.zeros((MEM_PAD, width), BF16)

                    @pl.when(i >= n)
                    def _():
                        mem_copy(which, i - n).wait_recv()
                        rows_ref[toks:rows, :] = jnp.where(
                            keep[i][:, 0:1] > 0.0, memin[which, i - n], jnp.zeros((), BF16)
                        )

            @pl.when(x == 1)
            def _():
                for p in range(2):
                    x_copy(p, i).wait_recv()
                    pass_copy(p, i).start()

            @pl.when(i == 0)
            def _():
                wait_first_of(0, (0,))

            @pl.when(ahead)
            def _():
                memory = jnp.concatenate(
                    [x0[i, toks:rows, :], xo[lax.rem(i, n), toks:rows, :]], axis=0
                )
                both = dot(memory, wf[0, :, width:wide]).astype(BF16)
                kvb[0, toks:rows, :] = both[0:MEM_PAD]
                kvb[1, toks:rows, :] = both[MEM_PAD:]
                qb[toks:rows, :] = to_queries(dot(memory, wf[0, :, 0:width])[0:MEM_PAD])

            @pl.when(jnp.logical_not(ahead))
            def _():
                kvb[0] = dot(x0[i], wf[0, :, width:wide]).astype(BF16)

                @pl.when(i == 0)
                def _():
                    wait_first_of(0, (1,))

                qb[...] = to_queries(dot(x0[i], wf[0, :, 0:width]))

                @pl.when(x == 1)
                def _():
                    for p in range(2):
                        pass_copy(p, i).wait_recv()

                kvb[1] = dot(xo[lax.rem(i, n)], wf[0, :, width:wide]).astype(BF16)

            for copy in qkv_copies(i):
                copy.start()

            @pl.when((x == 0) & (i < items - n))
            def _():
                token_copy(1, i + n).start()

            @pl.when(i > 0)
            def _():
                for copy in prob_copies(i - 1, False):
                    copy.wait()

            attend(i)
            for copy in prob_copies(i, False):
                copy.start()

            @pl.when(i == 0)
            def _():
                wait_first_of(0, (2,))
                weight_remote(4).wait_recv()

            normed, inv = normalize(dot(ctxb[...], wf[0, :, wide:]) + x0[i].astype(F32))
            natt[i] = normed.astype(BF16)
            stats[i] = jnp.where(stat_lane == heads, inv, stats[i])
            yatt[i] = (normed * nrm[0, 0:1, :] + nrm[0, 1:2, :]).astype(BF16)

            @pl.when(i == 0)
            def _():
                wait_first_of(1, (0, 1, 2))

            @pl.when(i > 0)
            def _():
                route_sent(S_GLO, i - 1)
                route_sent(S_GHI, i - 1)

            qkv_copies(i)[0].wait()

            for part in range(2):
                cols = slice(part * hidden_half, (part + 1) * hidden_half)
                u = dot(yatt[i], wf[1, :, cols])
                cdf = 0.5 + 0.5 * lax.erf(u * 0.7071067811865476)
                pdf = 0.3989422804014327 * jnp.exp(-0.5 * u * u)
                g[:, cols] = (u * cdf).astype(BF16)
                gpb[:, cols] = (cdf + u * pdf).astype(BF16)
            @pl.when(i == 0)
            def _():
                wait_first_of(0, (3,))
                wait_first_of(1, (3,))

            normed, inv = normalize(
                dot(g[:, 0:hidden_half], wd[0])
                + dot(g[:, hidden_half:], wd[1])
                + yatt[i].astype(F32)
            )
            yd[i] = (normed * nrm[1, 0:1, :] + nrm[1, 1:2, :]).astype(BF16)

            @pl.when(x == 0)
            def _():
                for p in range(2):
                    x_copy(p, i).start()

            @pl.when((x == 1) & (i < items - n))
            def _():
                for which in range(2):
                    mem_copy(which, i).start()

            gp_copy(i).start()
            for kind in (S_GLO, S_GHI, S_X0, S_CTX, OUT_ATT, S_Y1, S_Y2, OUT_FF):
                route(kind, i)
            nff[i] = normed.astype(BF16)
            stats[i] = jnp.where(stat_lane == heads + 1, inv, stats[i])

        return carry

    lax.fori_loop(0, items + 1, forward_tick, 0)

    def forward_sent(i):
        route_sent(OUT_FF, i)

        @pl.when(x == 0)
        def _():
            for p in range(2):
                x_copy(p, i).wait_send()

        @pl.when(x == 1)
        def _():
            for p in range(2):
                pass_copy(p, i).wait_send()

        @pl.when((x == 1) & (i < items - n))
        def _():
            for which in range(2):
                mem_copy(which, i).wait_send()

    for copy in prob_copies(items - 1, False) + qkv_copies(items - 1)[1:]:
        copy.wait()
    for copy in prob_copies(items - n, True):
        copy.start()
    gp_copy(items - 1).wait()
    acc[...] = jnp.zeros_like(acc)

    def norm_back(s, i, normed_ref):
        grad = (gy[i] if s else gab[...]).astype(F32)
        normed = normed_ref[i].astype(F32)
        inv = stats[i][:, heads + s : heads + s + 1]
        acc[s, 0:1, :] += jnp.sum(grad * normed, axis=0, keepdims=True)
        acc[s, 1:2, :] += jnp.sum(grad, axis=0, keepdims=True)
        scaled = grad * nrm[s, 0:1, :]
        row_term = jnp.mean(scaled, axis=1, keepdims=True)
        row_cross = jnp.mean(scaled * normed, axis=1, keepdims=True)
        dh = inv * (scaled - row_term - normed * row_cross)
        dhb[...] = dh
        normed_ref[i] = dh.astype(BF16)

    def attend_back(i, slot):
        def prob_grads(j):
            inverse = [stats[i][:, 4 * j + h : 4 * j + h + 1] for h in range(4)]
            c4 = dctx[:, j * quad : (j + 1) * quad].astype(F32) * spread(inverse, head_lanes)
            c4 = c4.astype(BF16)
            tok_v, mem_v = token_and_memory(kv.at[i], width + j * quad)
            return c4, dot(stacked(c4), tok_v, 1, 1), dot(c4, mem_v, 1, 1)

        following = prob_grads(0)
        for j in range(quads):
            c4, dp, dpm = following
            if j + 1 < quads:
                following = prob_grads(j + 1)
            cols = slice(j * quad, (j + 1) * quad)
            q4 = q[i, :, cols]
            tok_k, mem_k = token_and_memory(kv.at[i], j * quad)
            products = c4.astype(F32) * ctx[i, :, cols].astype(F32)
            dp = head_rows(dp)
            inner = [
                jnp.sum(jnp.where(head_lanes == h, products, 0.0), axis=1, keepdims=True)
                for h in range(4)
            ]
            dscores = [
                (tprob[j, h * rows : (h + 1) * rows, :].astype(F32) * (dp[h] - inner[h])).astype(BF16)
                for h in range(4)
            ]
            dsm = (mprob[j].astype(F32) * (dpm - spread(inner, mem_lanes))).astype(BF16)
            ct, qt = jnp.transpose(c4), jnp.transpose(q4)
            mine = [slice(h * head_dim, (h + 1) * head_dim) for h in range(4)]
            dv = [
                dot(ct[mine[h]], tprob[j, h * rows : (h + 1) * rows, :]).astype(BF16)
                for h in range(4)
            ]
            dk = [dot(qt[mine[h]], dscores[h]).astype(BF16) for h in range(4)]
            dv = jnp.transpose(jnp.concatenate(dv, axis=0))
            dk = jnp.transpose(jnp.concatenate(dk, axis=0))
            dscores = jnp.concatenate(dscores, axis=0)
            dq = spread(head_rows(dot(dscores, tok_k)), head_lanes) + dot(dsm, mem_k)
            dqb[:, cols] = (dq * scale).astype(BF16)
            dvm = jnp.where(diagonal, dot(mprob[j], c4, 0, 0), 0.0)
            dkm = jnp.where(diagonal, dot(dsm, q4, 0, 0), 0.0)
            dvm = sum(dvm[h * mem_keys : (h + 1) * mem_keys] for h in range(4))
            dkm = sum(dkm[h * mem_keys : (h + 1) * mem_keys] for h in range(4))
            for half, (tok_part, mem_part) in enumerate(((dk, dkm), (dv, dvm))):
                cols = slice(half * quad, (half + 1) * quad)
                for core in range(2):
                    dkvs[core, j, 0:toks, cols] = tok_part[
                        core * toks : (core + 1) * toks
                    ].astype(BF16)
                    dkvs[core, j, toks:rows, cols] = mem_part[
                        core * MEM_PAD : (core + 1) * MEM_PAD
                    ].astype(BF16)
            if j == quads - 1:
                dkv_copy(j, i, slot).start()
            elif j == quads - 2:
                for ready in range(quads - 1):
                    dkv_copy(ready, i, slot).start()

    def gather_dkv(j, i, slot):
        dkv_copy(j, i, slot).wait_recv()
        both = (dkvs[0, j].astype(F32) + dkvin[slot, j].astype(F32)).astype(BF16)
        kv[i, 0, :, j * quad : (j + 1) * quad] = both[:, 0:quad]
        kv[i, 0, :, width + j * quad : width + (j + 1) * quad] = both[:, quad:]

    def dkv_back(i, low, high):
        return dot(kv[i, 0, :, low:high], wf[0, :, width + low : width + high], 1, 1) + dot(
            kv[i, 0, :, width + low : width + high],
            wf[0, :, 2 * width + low : 2 * width + high], 1, 1,
        )

    def item_of(r):
        return (nseg - 1 - lax.div(r, n)) * n + lax.rem(r, n)

    def backward_tick(t, carry):
        r = t - (1 - x)

        @pl.when((r >= 0) & (r < items))
        def _():
            i = item_of(r)
            slot = lax.rem(r, 2)

            @pl.when(x == 1)
            def _():
                cot_copy(i).wait()

                @pl.when(i >= items - n)
                def _():
                    gy[i, toks:rows, :] = jnp.zeros((MEM_PAD, width), BF16)

                @pl.when(i < items - n)
                def _():
                    mg_copy(i + n).wait_recv()
                    gy[i, toks:rows, :] = jnp.where(
                        keep[i + n][:, 0:1] > 0.0, mgin[i + n], jnp.zeros((), BF16)
                    )

            @pl.when(x == 0)
            def _():
                gy_copy(i).wait_recv()

            @pl.when(r > 0)
            def _():
                route_sent(S_DQ, item_of(r - 1))
                route_sent(GIN_FF, item_of(r - 1))

            norm_back(1, i, nff)
            for part in range(2):
                cols = slice(part * hidden_half, (part + 1) * hidden_half)
                dg = dot(nff[i], wd[part], 1, 1)
                gp[i, :, cols] = (dg * gp[i, :, cols].astype(F32)).astype(BF16)
            gab[...] = (dot(gp[i], wf[1], 1, 1) + dhb[...]).astype(BF16)
            norm_back(0, i, natt)
            dctx[...] = dot(natt[i], wf[0, :, wide:], 1, 1).astype(BF16)
            route(S_DFF0, i)
            route(S_DFF1, i)
            route(S_DU, i)
            route(GIN_FF, i)
            route(S_DATT, i)
            for copy in prob_copies(i, True):
                copy.wait()
            attend_back(i, slot)
            route(S_DQ, i)

            @pl.when(r + 1 < items)
            def _():
                for copy in prob_copies(item_of(r + 1), True):
                    copy.start()

            for j in range(quads - 1):
                gather_dkv(j, i, slot)
            if quads > 1:
                route(S_DKV, i)
                route(S_DV, i)
            early = (quads - 1) * quad
            partial_sum = dot(dqb[...], wf[0, :, 0:width], 1, 1) + dhb[...]
            if early:
                partial_sum = partial_sum + dkv_back(i, 0, early)
            dhb[...] = partial_sum
            gather_dkv(quads - 1, i, slot)
            route(S_LASTK, i)
            route(S_LASTV, i)
            forward_sent(i)
            yd[i] = (dkv_back(i, early, width) + dhb[...]).astype(BF16)

            @pl.when(x == 1)
            def _():
                gy_copy(i).start()

            @pl.when((x == 0) & (i >= n))
            def _():
                mg_copy(i).start()

            route(GIN_ATT, i)
            for j in range(quads):
                dkv_copy(j, i, slot).wait_send()

        return carry

    lax.fori_loop(0, items + 1, backward_tick, 0)

    acc_copy = remote(acc.at[1 - c], accp, as_sem, ar_sem, core_peer)
    acc_copy.start()

    def backward_drain(i, carry):
        @pl.when(x == 1)
        def _():
            gy_copy(i).wait_send()

        @pl.when((x == 0) & (i >= n))
        def _():
            mg_copy(i).wait_send()

        for kind in range(KINDS):
            if quads == 1 and kind in (S_DKV, S_DV):
                continue
            if kind not in (OUT_FF, S_GLO, S_GHI, S_DQ, GIN_FF):
                route_sent(kind, i)
            route_received(kind, i)
        return carry

    lax.fori_loop(0, items, backward_drain, 0)
    route_sent(S_GLO, items - 1)
    route_sent(S_GHI, items - 1)
    route_sent(S_DQ, item_of(items - 1))
    route_sent(GIN_FF, item_of(items - 1))
    for k in range(5):
        weight_remote(k).wait_send()
    acc_copy.wait()
    norm_grad[...] = acc[c] + accp[...]


def run_layers(n, nseg, heads, tokens, cotangent, first, down, docs, resets, gain, shift):
    length, width = tokens.shape[1:]
    toks = length // nseg // 2
    rows = toks + MEM_PAD
    items = n * nseg
    hidden_half = down.shape[1]
    quads = heads // 4
    quad = width // quads
    any_spec = pl.BlockSpec(memory_space=pl.ANY)
    vmem_spec = pl.BlockSpec(memory_space=pltpu.VMEM)
    dma = pltpu.SemaphoreType.DMA
    item_rows = pltpu.VMEM((items, rows, width), BF16)
    one, two = dma((items,)), dma((2, items))
    return pl.pallas_call(
        partial(layers_kernel, n, nseg, heads),
        out_shape=(
            jax.ShapeDtypeStruct((n, length, width), BF16),
            jax.ShapeDtypeStruct((n, length, width), BF16),
            jax.ShapeDtypeStruct((2 * items, rows, width), BF16),
            jax.ShapeDtypeStruct((2 * items, rows, width), BF16),
            jax.ShapeDtypeStruct((2 * items, rows, 4 * width), BF16),
            jax.ShapeDtypeStruct((2 * items, rows, hidden_half), BF16),
            jax.ShapeDtypeStruct((2 * items, rows, width), BF16),
            jax.ShapeDtypeStruct((2, width), F32),
            jax.ShapeDtypeStruct((items, quads, 4 * rows, 2 * toks), BF16),
            jax.ShapeDtypeStruct((items, quads, rows, 8 * MEM_PAD), BF16),
        ),
        in_specs=[any_spec] * 4 + [vmem_spec] * 4,
        out_specs=[any_spec] * 7 + [vmem_spec] + [any_spec] * 2,
        scratch_shapes=[
            pltpu.VMEM((2, width, 4 * width), BF16),
            pltpu.VMEM((2, hidden_half, width), BF16),
            pltpu.VMEM((2, 2, width), F32),
            item_rows,
            pltpu.VMEM((n, rows, width), BF16),
            item_rows,
            pltpu.VMEM((items, 2, rows, 2 * width), BF16),
            item_rows,
            item_rows,
            item_rows,
            item_rows,
            item_rows,
            item_rows,
            pltpu.VMEM((rows, 2 * hidden_half), BF16),
            pltpu.VMEM((rows, 2 * hidden_half), BF16),
            pltpu.VMEM((items, rows, 2 * hidden_half), BF16),
            pltpu.VMEM((items, rows, 128), F32),
            pltpu.VMEM((items, toks, 128), F32),
            pltpu.VMEM((items, 1, 2 * toks), F32),
            pltpu.VMEM((items, MEM_PAD, 128), F32),
            pltpu.VMEM((2, items, MEM_PAD, width), BF16),
            pltpu.VMEM((items, MEM_PAD, width), BF16),
            pltpu.VMEM((2, quads, rows, 2 * quad), BF16),
            pltpu.VMEM((2, quads, rows, 2 * quad), BF16),
            pltpu.VMEM((rows, width), F32),
            pltpu.VMEM((2, rows, 2 * width), BF16),
            pltpu.VMEM((2, 2, width), F32),
            pltpu.VMEM((2, width), F32),
            pltpu.VMEM((quads, 4 * rows, 2 * toks), BF16),
            pltpu.VMEM((quads, rows, 8 * MEM_PAD), BF16),
            dma((4,)), dma((5,)), dma((5,)),
            two, one, one, two, two, two,
            two, two,
            two, two,
            two, two,
            one, one, one, one,
            dma((quads, items)), dma((quads, items)),
            dma(()), dma(()),
        ]
        + [dma((KINDS, items))] * 3,
        compiler_params=pltpu.CompilerParams(
            collective_id=0, has_side_effects=True, vmem_limit_bytes=61 * 1024 * 1024
        ),
    )(tokens, cotangent, first, down, docs, resets, gain, shift)


def reduce_kernel(
    chunks,
    sx1, sx2, sr, sg, sd, norm_part,
    sums, norm_out,
    x1, x2, rr, gg, dd, work, done, got_u, got_uz, got_vz, got_vy, norms,
    right_sem, left_sem, out_sem, u_s, u_r, uz_s, uz_r, vz_s, vz_r, vy_s, vy_r, vg_s, vg_r,
    uzg_s, uzg_r, vzg_s, vzg_r, ug_s, ug_r, n_s, n_r,
):
    lines = 4
    d = lax.axis_index("dp")
    y = lax.rem(d, 2)
    z = lax.div(d, 2)
    dp = lax.axis_size("dp")
    width = sd.shape[1]
    half = width // 2
    part = width // chunks
    hr = part // 2
    lane_group = 128
    per_group = lane_group // part
    y_peer = {"dp": z * 2 + (1 - y)}

    def remote(src, dst, send, recv, peer):
        return pltpu.make_async_remote_copy(
            src_ref=src, dst_ref=dst, send_sem=send, recv_sem=recv,
            device_id=peer, device_id_type=MESH,
        )

    def other(step):
        return {"dp": lax.rem(d + step, dp)}

    barrier = pltpu.get_barrier_semaphore()
    for step in range(1, dp):
        pl.semaphore_signal(barrier, inc=1, device_id=other(step), device_id_type=MESH)

    lane_groups = width // lane_group
    right_loads = [(sd, dd)] + [
        (sr.at[:, b * width : (b + 1) * width], rr.at[:, b * width : (b + 1) * width])
        for b in range(4)
    ]

    def right_load(k):
        src, dst = right_loads[k]
        return pltpu.make_async_copy(src, dst, right_sem.at[k])

    def left_load(which, group):
        src, dst, low = ((sg, gg, 0), (sg, gg, width), (sx2, x2, 0), (sx1, x1, 0))[which]
        cols = pl.ds(pl.multiple_of(low + group * lane_group, lane_group), lane_group)
        return pltpu.make_async_copy(src.at[:, cols], dst.at[:, cols], left_sem.at[which, group])

    right_load(0).start()
    left_load(0, 0).start()
    left_load(1, 0).start()
    left_load(2, 0).start()
    right_load(4).start()

    norms[d] = norm_part[...]
    pl.semaphore_wait(barrier, dp - 1)

    def norm_copy(step):
        return remote(norms.at[d], norms.at[d], n_s.at[step - 1], n_r.at[step - 1], other(step))

    def norm_arrival(step):
        source = lax.rem(d + dp - step, dp)
        return remote(
            norms.at[source], norms.at[source], n_s.at[step - 1], n_r.at[step - 1], other(step)
        )

    for step in range(1, dp):
        norm_copy(step).start()

    def column_half(h):
        return pl.ds(pl.multiple_of(h * half, 128), half)

    mine, theirs = column_half(y), column_half(1 - y)

    def place(flow):
        return z if flow == 0 else lines - 1 - z

    def onward(flow):
        step = -1 if flow == 0 else 1
        return {"dp": (z + step) * 2 + y}

    def back(flow):
        step = 1 if flow == 0 else -1
        return {"dp": (z + step) * 2 + y}

    def rows_of(flow):
        return slice(flow * hr, (flow + 1) * hr)

    def u_copy(k):
        return remote(
            work.at[k, 0:3, :, theirs], got_u.at[k], u_s.at[k], u_r.at[k], y_peer
        )

    def uz_copy(flow, k):
        return remote(
            work.at[k, 0:3, rows_of(flow), mine], got_uz.at[flow, k],
            uz_s.at[flow, k], uz_r.at[flow, k], onward(flow),
        )

    def vz_copy(flow, k):
        return remote(
            work.at[k, 3:6, rows_of(flow), :], got_vz.at[flow, k],
            vz_s.at[flow, k], vz_r.at[flow, k], onward(flow),
        )

    def vy_copy(flow, k):
        return remote(
            work.at[k, 3:6, rows_of(flow), theirs], got_vy.at[k], vy_s.at[k], vy_r.at[k], y_peer
        )

    def vg_copy(flow, k, cols):
        spot = done.at[k, 3:6, rows_of(flow), cols]
        return remote(spot, spot, vg_s.at[k], vg_r.at[k], y_peer)

    def uzg_copy(flow, k):
        spot = done.at[k, 0:3, rows_of(flow), mine]
        return remote(spot, spot, uzg_s.at[flow, k], uzg_r.at[flow, k], back(flow))

    def vzg_copy(flow, k):
        spot = done.at[k, 3:6, rows_of(flow), :]
        return remote(spot, spot, vzg_s.at[flow, k], vzg_r.at[flow, k], back(flow))

    def ug_copy(flow, k, cols):
        spot = done.at[k, 0:3, rows_of(flow), cols]
        return remote(spot, spot, ug_s.at[flow, k], ug_r.at[flow, k], y_peer)

    def out_copy(k):
        return pltpu.make_async_copy(done.at[k], sums.at[k], out_sem.at[k])

    def plus(a, b):
        return (a.astype(F32) + b.astype(F32)).astype(BF16)

    def ready(k, low=0):
        return (k >= low) & (k < chunks)

    def store_chunks(group, block, value):
        for e in range(per_group):
            work[group * per_group + e, block] = value[e * part : (e + 1) * part]

    def second_half(r):
        group = lax.div(r + per_group - 1, per_group)
        cols = pl.ds(pl.multiple_of(group * lane_group, lane_group), lane_group)
        gcols = pl.ds(pl.multiple_of(width + group * lane_group, lane_group), lane_group)

        @pl.when(r == 0)
        def _():
            right_load(0).wait()

        left_load(0, group).wait()
        store_chunks(group, 4, dot(gg[:, cols], dd[...], 0, 0).astype(BF16))
        left_load(1, group).wait()
        store_chunks(group, 5, dot(gg[:, gcols], dd[...], 0, 0).astype(BF16))
        left_load(2, group).wait()

        @pl.when(r == 0)
        def _():
            right_load(4).wait()
            left_load(3, 0).start()
            for k in range(1, 4):
                right_load(k).start()
            for later in range(1, lane_groups):
                for which in range(4):
                    left_load(which, later).start()

        store_chunks(group, 3, dot(x2[:, cols], rr[:, 3 * width :], 0, 0).astype(BF16))

    def round_step(r, carry):
        @pl.when(r == 0)
        def _():
            second_half(r)

        for flow in range(2):
            p = place(flow)
            k = r - (lines - 1 - p)
            rows = rows_of(flow)

            @pl.when(ready(k))
            def _():
                @pl.when(p < lines - 1)
                def _():
                    vz_copy(flow, k).wait_recv()
                    work[k, 3:6, rows, :] = plus(work[k, 3:6, rows, :], got_vz[flow, k])

                @pl.when(p > 0)
                def _():
                    vz_copy(flow, k).start()

                @pl.when(p == 0)
                def _():
                    vy_copy(flow, k).start()

        @pl.when((lax.rem(r, per_group) == 0) & (r < chunks))
        def _():
            group = lax.div(r, per_group)
            cols = pl.ds(pl.multiple_of(group * lane_group, lane_group), lane_group)
            left_load(3, group).wait()
            for b in range(3):

                @pl.when(r == 0)
                def _():
                    right_load(1 + b).wait()

                store_chunks(
                    group, b,
                    dot(x1[:, cols], rr[:, b * width : (b + 1) * width], 0, 0).astype(BF16),
                )

        @pl.when(ready(r))
        def _():
            u_copy(r).start()

        @pl.when((lax.rem(r, per_group) == per_group - 1) & (r + 1 < chunks))
        def _():
            second_half(r)

        @pl.when(ready(r - 1))
        def _():
            k = r - 1
            u_copy(k).wait_recv()
            work[k, 0:3, :, mine] = plus(work[k, 0:3, :, mine], got_u[k])

        for flow in range(2):
            p = place(flow)
            k = r - 1 - (lines - 1 - p)
            rows = rows_of(flow)

            @pl.when(ready(k))
            def _():
                @pl.when(p < lines - 1)
                def _():
                    uz_copy(flow, k).wait_recv()
                    total = plus(work[k, 0:3, rows, mine], got_uz[flow, k])

                    @pl.when(p > 0)
                    def _():
                        work[k, 0:3, rows, mine] = total

                    @pl.when(p == 0)
                    def _():
                        done[k, 0:3, rows, mine] = total

                @pl.when(p > 0)
                def _():
                    uz_copy(flow, k).start()

                @pl.when(p == 0)
                def _():
                    uzg_copy(flow, k).start()
                    ug_copy(flow, k, mine).start()

        for flow in range(2):
            p = place(flow)
            rows = rows_of(flow)

            @pl.when((p == 0) & ready(r - lines))
            def _():
                k = r - lines
                vy_copy(flow, k).wait_recv()
                done[k, 3:6, rows, mine] = plus(work[k, 3:6, rows, mine], got_vy[k])
                vg_copy(flow, k, mine).start()

            @pl.when((p == 0) & ready(r - lines - 1))
            def _():
                k = r - lines - 1
                vg_copy(flow, k, theirs).wait_recv()
                vzg_copy(flow, k).start()

        for flow in range(2):
            p = place(flow)
            k = r - lines - p

            @pl.when((p > 0) & ready(k))
            def _():
                uzg_copy(flow, k).wait_recv()

                @pl.when(p < lines - 1)
                def _():
                    uzg_copy(flow, k).start()

                ug_copy(flow, k, mine).start()

        for flow in range(2):
            p = place(flow)
            k = r - lines - 1 - p

            @pl.when((p > 0) & ready(k))
            def _():
                vzg_copy(flow, k).wait_recv()

                @pl.when(p < lines - 1)
                def _():
                    vzg_copy(flow, k).start()

            @pl.when(ready(k))
            def _():
                ug_copy(flow, k, theirs).wait_recv()

        @pl.when(ready(r - 2 * lines))
        def _():
            out_copy(r - 2 * lines).start()

        return carry

    lax.fori_loop(0, chunks + 2 * lines, round_step, 0)

    for step in range(1, dp):
        norm_arrival(step).wait_recv()
    total = norms[0]
    for e in range(1, dp):
        total = total + norms[e]
    norm_out[...] = total

    def drain(k, carry):
        out_copy(k).wait()
        u_copy(k).wait_send()
        for flow in range(2):
            p = place(flow)
            ug_copy(flow, k, mine).wait_send()

            @pl.when(p > 0)
            def _():
                vz_copy(flow, k).wait_send()
                uz_copy(flow, k).wait_send()

            @pl.when(p < lines - 1)
            def _():
                uzg_copy(flow, k).wait_send()
                vzg_copy(flow, k).wait_send()

            @pl.when(p == 0)
            def _():
                vy_copy(flow, k).wait_send()
                vg_copy(flow, k, mine).wait_send()

        return carry

    lax.fori_loop(0, chunks, drain, 0)
    for step in range(1, dp):
        norm_copy(step).wait_send()


def sum_weights(dp, sx1, sx2, sr, sg, sd, norm_part):
    total, width = sx1.shape
    chunks = 12
    part = width // chunks
    half = width // 2
    any_spec = pl.BlockSpec(memory_space=pl.ANY)
    vmem_spec = pl.BlockSpec(memory_space=pltpu.VMEM)
    dma = pltpu.SemaphoreType.DMA
    one, two = dma((chunks,)), dma((2, chunks))
    return pl.pallas_call(
        partial(reduce_kernel, chunks),
        out_shape=(
            jax.ShapeDtypeStruct((chunks, 6, part, width), BF16),
            jax.ShapeDtypeStruct((2, width), F32),
        ),
        in_specs=[any_spec] * 5 + [vmem_spec],
        out_specs=[any_spec, vmem_spec],
        scratch_shapes=[
            pltpu.VMEM((total, width), BF16),
            pltpu.VMEM((total, width), BF16),
            pltpu.VMEM((total, 4 * width), BF16),
            pltpu.VMEM((total, 2 * width), BF16),
            pltpu.VMEM((total, width), BF16),
            pltpu.VMEM((chunks, 6, part, width), BF16),
            pltpu.VMEM((chunks, 6, part, width), BF16),
            pltpu.VMEM((chunks, 3, part, half), BF16),
            pltpu.VMEM((2, chunks, 3, part // 2, half), BF16),
            pltpu.VMEM((2, chunks, 3, part // 2, width), BF16),
            pltpu.VMEM((chunks, 3, part // 2, half), BF16),
            pltpu.VMEM((dp, 2, width), F32),
            dma((5,)),
            dma((4, width // 128)),
            one,
            one, one,
            two, two,
            two, two,
            one, one,
            one, one,
            two, two,
            two, two,
            two, two,
            dma((dp - 1,)), dma((dp - 1,)),
        ],
        compiler_params=pltpu.CompilerParams(
            collective_id=1, has_side_effects=True, vmem_limit_bytes=60 * 1024 * 1024
        ),
    )(sx1, sx2, sr, sg, sd, norm_part)


def finish_kernel(sums, out, gin, norms, first_grad, down_grad, out_copy, gin_copy, gain, shift):
    group, _, part, width = sums.shape
    for e in range(group):
        rows = slice(e * part, (e + 1) * part)
        for b in range(4):
            first_grad[rows, b * width : (b + 1) * width] = sums[e, b].astype(F32)
        for b in range(2):
            down_grad[b, rows] = sums[e, 4 + b].astype(F32)
    out_copy[...] = out[...]
    gin_copy[...] = gin[...]
    gain[...] = norms[0:1]
    shift[...] = norms[1:2]


def finish(sums, out, gin, norms):
    chunks, _, part, width = sums.shape
    total = out.shape[0]
    group, blocks = chunks // 3, 2
    tokens = pl.BlockSpec((total // blocks, width), lambda k: (jnp.minimum(k, blocks - 1), 0))
    whole = pl.BlockSpec((1, width), lambda k: (0, 0))
    return pl.pallas_call(
        finish_kernel,
        grid=(chunks // group,),
        out_shape=(
            jax.ShapeDtypeStruct((width, 4 * width), F32),
            jax.ShapeDtypeStruct((2, width, width), F32),
            jax.ShapeDtypeStruct(out.shape, BF16),
            jax.ShapeDtypeStruct(gin.shape, BF16),
            jax.ShapeDtypeStruct((1, width), F32),
            jax.ShapeDtypeStruct((1, width), F32),
        ),
        in_specs=[
            pl.BlockSpec((group, 6, part, width), lambda k: (k, 0, 0, 0)),
            tokens,
            tokens,
            pl.BlockSpec((2, width), lambda k: (0, 0)),
        ],
        out_specs=[
            pl.BlockSpec((group * part, 4 * width), lambda k: (k, 0)),
            pl.BlockSpec((2, group * part, width), lambda k: (0, k, 0)),
            tokens,
            tokens,
            whole,
            whole,
        ],
        compiler_params=pltpu.CompilerParams(vmem_limit_bytes=61 * 1024 * 1024),
    )(sums, out, gin, norms)


def shards(
    tokens, doc_ids, reset_flags, first_weights, down_halves, norm_gain, norm_bias, cotangent
):
    n, length, width = tokens.shape
    items = n * NSEG
    rows = length // NSEG // 2 + MEM_PAD
    out, gin, sx1, sx2, sr, sg, sd, norm_grad, _, _ = run_layers(
        n, NSEG, H, tokens, cotangent, first_weights, down_halves,
        doc_ids, reset_flags.T, norm_gain, norm_bias,
    )
    total = 2 * items * rows
    sx1, sx2, sd = (a.reshape(total, width) for a in (sx1, sx2, sd))
    sr = sr.reshape(total, 4 * width)
    sg = sg.reshape(total, -1)

    dp = lax.axis_size("dp")
    if dp == 8:
        sums, norm_grad = sum_weights(dp, sx1, sx2, sr, sg, sd, norm_grad)
        first_grad, down_grad, out, gin, gain_grad, shift_grad = finish(
            sums, out.reshape(-1, width), gin.reshape(-1, width), norm_grad
        )
        down_grad = down_grad.reshape(-1, width)
        out, gin = (a.reshape(n, length, width) for a in (out, gin))
    else:

        def weight_grad(left, right):
            return jnp.einsum("rd,re->de", left, right, preferred_element_type=F32).astype(BF16)

        first_grad = jnp.concatenate(
            [weight_grad(sx1, sr[:, : 3 * width]), weight_grad(sx2, sr[:, 3 * width :])], axis=1
        )
        down_grad = weight_grad(sg, sd)
        first_grad, down_grad = lax.psum((first_grad, down_grad), "dp")
        norm_grad = lax.psum(norm_grad, "dp")
        gain_grad, shift_grad = norm_grad[0:1], norm_grad[1:2]
    return (
        out[None],
        gin[None],
        first_grad.astype(F32)[None],
        down_grad.astype(F32)[None],
        gain_grad,
        shift_grad,
    )


def solution(mesh):
    in_specs = (
        P("dp", None, None),
        P("dp", None),
        P("dp", None),
        P("section", None, None),
        P("section", None, None),
        P("section", None),
        P("section", None),
        P("dp", None, None),
    )
    out_specs = (
        P("section", "dp", None, None),
        P("section", "dp", None, None),
        P("section", None, None),
        P("section", None, None),
        P("section", None),
        P("section", None),
    )
    return jax.shard_map(shards, mesh=mesh, in_specs=in_specs, out_specs=out_specs, check_vma=False)
```

```python
from functools import partial

import jax
import jax.numpy as jnp
from jax import lax
from jax.experimental import pallas as pl
from jax.experimental.pallas import tpu as pltpu
from jax.sharding import PartitionSpec as P

H = 12
M = 20
NSEG = 2
MEM_PAD = 16
NORM_EPSILON = 1e-05
MASKED_SCORE = -1000000000.0
ABSENT_SCORE = -3e38
MESH = pl.DeviceIdType.MESH
BF16 = jnp.bfloat16
F32 = jnp.float32

OUT_ATT, OUT_FF, GIN_ATT, GIN_FF = 0, 1, 2, 3
S_X0, S_CTX, S_DQ, S_DKV, S_DATT, S_GLO, S_DFF0 = 4, 5, 6, 7, 8, 9, 10
S_Y1, S_Y2, S_DU, S_GHI, S_DFF1 = 11, 12, 13, 14, 15
S_DV, S_LASTK, S_LASTV = 16, 17, 18
KINDS = 19


def dot(a, b, lhs_dim=1, rhs_dim=0):
    return lax.dot_general(
        a, b, (((lhs_dim,), (rhs_dim,)), ((), ())), preferred_element_type=F32
    )


def normalize(summed):
    mean = jnp.mean(summed, axis=-1, keepdims=True)
    centered = summed - mean
    var = jnp.mean(centered * centered, axis=-1, keepdims=True)
    inv = lax.rsqrt(var + NORM_EPSILON)
    return centered * inv, inv


def group_of(shape, dim, size):
    index = lax.broadcasted_iota(jnp.int32, shape, dim)
    return lax.shift_right_logical(index, size.bit_length() - 1)


def spread(values, groups):
    result = values[-1]
    for h in range(len(values) - 1):
        result = jnp.where(groups == h, values[h], result)
    return result


def layers_kernel(
    n, nseg, heads,
    tokens, cotangent, first, down, docs, resets, gain, shift,
    out, gin, sx1, sx2, sr, sg, sd, norm_grad, ptok, pmem,
    wf, wd, nrm, x0, xo, q, kv, ctx, natt, yatt, nff, yd, gy, g, gpb, gp, stats, qdoc, kdoc, keep,
    memin, mgin, dkvs, dkvin, dhb, kvb, acc, accp, tprob, mprob,
    wl, ws, wr, tok_sem, cot_sem, gp_sem, qkv_sem, pw_sem, pr_sem, fs_sem, fr_sem, xs_sem, xr_sem,
    ms_sem, mr_sem, gs_sem, gr_sem, hs_sem, hr_sem, ds_sem, dr_sem, as_sem, ar_sem,
    lsem, ssem, rsem,
):
    items = n * nseg
    section = lax.axis_index("section")
    c = lax.rem(section, 2)
    x = lax.div(section, 2)
    core_peer = {"section": x * 2 + (1 - c)}
    chip_peer = {"section": (1 - x) * 2 + c}
    cross_peer = {"section": (1 - x) * 2 + (1 - c)}
    rows, width = x0.shape[1:]
    toks = rows - MEM_PAD
    seg_len = 2 * toks
    hidden_half = wd.shape[1]
    wide = 3 * width
    head_dim = width // heads
    quad = 4 * head_dim
    quads = heads // 4
    mem_keys = 2 * MEM_PAD
    scale = head_dim ** (-0.5)
    qb = gpb.at[:, 0:width]
    ctxb = gpb.at[:, width : 2 * width]
    dqb = gpb.at[:, 0:width]
    gab = gpb.at[:, width : 2 * width]
    dctx = gpb.at[:, 2 * width : wide]

    def remote(src, dst, send, recv, peer):
        return pltpu.make_async_remote_copy(
            src_ref=src, dst_ref=dst, send_sem=send, recv_sem=recv,
            device_id=peer, device_id_type=MESH,
        )

    barrier = pltpu.get_barrier_semaphore()
    pl.semaphore_signal(barrier, inc=1, device_id=core_peer, device_id_type=MESH)
    pl.semaphore_signal(barrier, inc=1, device_id=chip_peer, device_id_type=MESH)
    pl.semaphore_signal(barrier, inc=1, device_id=cross_peer, device_id_type=MESH)

    def token_rows(ref, i, core=None):
        core = c if core is None else core
        return ref.at[lax.rem(i, n), pl.ds(lax.div(i, n) * seg_len + core * toks, toks), :]

    def token_copy(which, i):
        if which == 0:
            src, dst = token_rows(tokens, i), x0.at[i, 0:toks, :]
        else:
            src, dst = token_rows(tokens, i, 1 - c), xo.at[lax.rem(i, n), 0:toks, :]
        return pltpu.make_async_copy(src, dst, tok_sem.at[which, i])

    def cot_copy(i):
        return pltpu.make_async_copy(
            token_rows(cotangent, i), gy.at[i, 0:toks, :], cot_sem.at[i]
        )

    def weight_piece(k):
        if k == 0:
            return first.at[0, :, width:wide], wf.at[c, :, width:wide]
        if k == 1:
            return first.at[0, :, 0:width], wf.at[c, :, 0:width]
        if k == 2:
            return first.at[0, :, wide:], wf.at[c, :, wide:]
        return down.at[0], wd.at[c]

    def weight_local(k):
        src, dst = weight_piece(k)
        return pltpu.make_async_copy(src, dst, wl.at[k])

    def weight_remote(k):
        if k == 4:
            return remote(nrm.at[c], nrm.at[c], ws.at[4], wr.at[4], core_peer)
        src, dst = weight_piece(k)
        return remote(src, dst, ws.at[k], wr.at[k], core_peer)

    nrm[c, 0:1, :] = gain[...]
    nrm[c, 1:2, :] = shift[...]
    weight_local(0).start()

    @pl.when(x == 0)
    def _():
        token_copy(0, 0).start()
        token_copy(1, 0).start()

    pl.semaphore_wait(barrier, 3)
    for k in range(5):
        weight_remote(k).start()
    for k in range(1, 4):
        weight_local(k).start()
    for i in range(items):
        if i > 0:

            @pl.when(x == 0)
            def _():
                token_copy(0, i).start()
                if i < n:
                    token_copy(1, i).start()

        @pl.when(x == 1)
        def _():
            cot_copy(i).start()

    def wait_first_of(core, ks):
        @pl.when(c == core)
        def _():
            for k in ks:
                weight_local(k).wait()

        @pl.when(c != core)
        def _():
            for k in ks:
                weight_remote(k).wait_recv()

    for i in range(items):
        seq, seg = i % n, i // n
        own = pl.ds(pl.multiple_of(seg * seg_len + c * toks, toks), toks)
        others = pl.ds(pl.multiple_of(seg * seg_len + (1 - c) * toks, toks), toks)
        own_row = docs[seq : seq + 1, own].astype(F32)
        kdoc[i, :, 0:toks] = own_row
        kdoc[i, :, toks:] = docs[seq : seq + 1, others].astype(F32)
        qdoc[i] = jnp.transpose(jnp.broadcast_to(own_row, (128, toks)))
        if seg > 0:
            flag = resets[seg - 1 : seg, seq : seq + 1].astype(F32)
            keep[i] = jnp.broadcast_to(1.0 - flag, (MEM_PAD, 128))

    def routed(kind, i):
        block = i * 2 + c
        sec = 0
        if kind == OUT_ATT:
            src, dst = yatt.at[i, 0:toks, :], token_rows(out, i)
        elif kind == OUT_FF:
            src, dst, sec = yd.at[i, 0:toks, :], token_rows(out, i), 1
        elif kind == GIN_ATT:
            src, dst = yd.at[i, 0:toks, :], token_rows(gin, i)
        elif kind == GIN_FF:
            src, dst, sec = gab.at[0:toks, :], token_rows(gin, i), 1
        elif kind == S_X0:
            src, dst = x0.at[i], sx1.at[block]
        elif kind == S_CTX:
            src, dst = ctx.at[i], sx2.at[block]
        elif kind == S_DQ:
            src, dst = dqb, sr.at[block, :, 0:width]
        elif kind in (S_DKV, S_DV, S_LASTK, S_LASTV):
            last = width - width // quads
            low, high = (0, last) if kind in (S_DKV, S_DV) else (last, width)
            if kind in (S_DV, S_LASTV):
                low, high = low + width, high + width
            src, dst = kv.at[i, 0, :, low:high], sr.at[block, :, width + low : width + high]
        elif kind == S_DATT:
            src, dst = natt.at[i], sr.at[block, :, wide:]
        elif kind == S_GLO:
            src, dst = g.at[:, 0:hidden_half], sg.at[block]
        elif kind == S_DFF0:
            src, dst = nff.at[i], sd.at[block]
        elif kind == S_Y1:
            src, dst, sec = yatt.at[i], sx1.at[block], 1
        elif kind == S_Y2:
            src, dst, sec = yatt.at[i], sx2.at[block], 1
        elif kind == S_DU:
            src, dst, sec = gp.at[i], sr.at[block], 1
        elif kind == S_GHI:
            src, dst, sec = g.at[:, hidden_half:], sg.at[block], 1
        else:
            src, dst, sec = nff.at[i], sd.at[block], 1
        return src, dst, sec

    def route_local(kind, i):
        src, dst, _ = routed(kind, i)
        return pltpu.make_async_copy(src, dst, lsem.at[kind, i])

    def route_away(kind, i):
        src, dst, _ = routed(kind, i)
        return remote(src, dst, ssem.at[kind, i], rsem.at[kind, i], core_peer)

    def route(kind, i):
        sec = routed(kind, i)[2]

        @pl.when(c == sec)
        def _():
            route_local(kind, i).start()

        @pl.when(c != sec)
        def _():
            route_away(kind, i).start()

    def route_sent(kind, i):
        sec = routed(kind, i)[2]

        @pl.when(c == sec)
        def _():
            route_local(kind, i).wait()

        @pl.when(c != sec)
        def _():
            route_away(kind, i).wait_send()

    def route_received(kind, i):
        @pl.when(c == routed(kind, i)[2])
        def _():
            route_away(kind, i).wait_recv()

    def qkv_copies(i):
        return [
            pltpu.make_async_copy(qb, q.at[i], qkv_sem.at[0, i]),
            pltpu.make_async_copy(kvb, kv.at[i], qkv_sem.at[1, i]),
        ]

    def gp_copy(i):
        return pltpu.make_async_copy(gpb, gp.at[i], gp_sem.at[i])

    def prob_copies(i, back):
        pairs = ((tprob, ptok.at[i]), (mprob, pmem.at[i]))
        if back:
            return [
                pltpu.make_async_copy(dst, src, pr_sem.at[e, i])
                for e, (src, dst) in enumerate(pairs)
            ]
        return [
            pltpu.make_async_copy(src, dst, pw_sem.at[e, i]) for e, (src, dst) in enumerate(pairs)
        ]

    cut = rows // 32 * 16

    def piece(p):
        return slice(0, cut) if p == 0 else slice(cut, rows)

    def x_copy(p, i):
        return remote(
            yd.at[i, piece(p)], x0.at[i, piece(p)], xs_sem.at[p, i], xr_sem.at[p, i], chip_peer
        )

    def pass_copy(p, i):
        return remote(
            x0.at[i, piece(p)], xo.at[lax.rem(i, n), piece(p)],
            fs_sem.at[p, i], fr_sem.at[p, i], core_peer,
        )

    def mem_copy(which, i):
        return remote(
            yd.at[i, toks:rows, :], memin.at[which, i], ms_sem.at[which, i],
            mr_sem.at[which, i], cross_peer if which else chip_peer,
        )

    def gy_copy(i):
        return remote(yd.at[i], gy.at[i], gs_sem.at[i], gr_sem.at[i], chip_peer)

    def mg_copy(i):
        return remote(
            yd.at[i, toks:rows, :], mgin.at[i], hs_sem.at[i], hr_sem.at[i], chip_peer
        )

    def dkv_copy(j, i, slot):
        return remote(
            dkvs.at[1, j], dkvin.at[slot, j], ds_sem.at[j, i], dr_sem.at[j, i], core_peer
        )

    head_lanes = group_of((rows, quad), 1, head_dim)
    mem_lanes = group_of((rows, 4 * mem_keys), 1, mem_keys)
    key_lane = lax.broadcasted_iota(jnp.int32, (rows, 4 * mem_keys), 1)
    mem_valid = lax.rem(key_lane, MEM_PAD) < M // 2
    diagonal = group_of((4 * mem_keys, quad), 0, mem_keys) == group_of(
        (4 * mem_keys, quad), 1, head_dim
    )
    stat_lane = lax.broadcasted_iota(jnp.int32, (rows, 128), 1)

    def stacked(block):
        return jnp.concatenate(
            [jnp.where(head_lanes == h, block, BF16(0)) for h in range(4)], axis=0
        )

    def head_rows(block):
        return [block[h * rows : (h + 1) * rows] for h in range(4)]

    def token_and_memory(ref, low):
        cols = slice(low, low + quad)
        tok = jnp.concatenate([ref[0, 0:toks, cols], ref[1, 0:toks, cols]], axis=0)
        mem = jnp.concatenate([ref[0, toks:, cols], ref[1, toks:, cols]], axis=0)
        return tok, jnp.where(diagonal, jnp.concatenate([mem] * 4, axis=0), BF16(0))

    def only_same_document(s, i):
        mine = jnp.concatenate([qdoc[i]] * (seg_len // 128), axis=1)
        same = jnp.where(mine == kdoc[i], s[0:toks], MASKED_SCORE)
        return jnp.concatenate([same, s[toks:]], axis=0)

    def memory_scores(q4, mem_k):
        return jnp.where(mem_valid, dot(q4, mem_k, 1, 1), ABSENT_SCORE)

    def attend(i):
        own = [mem_lanes == h for h in range(4)]

        def scores(j):
            q4 = qb[:, j * quad : (j + 1) * quad]
            tok_k, mem_k = token_and_memory(kvb, j * quad)
            return dot(stacked(q4), tok_k, 1, 1), memory_scores(q4, mem_k)

        st = jnp.zeros((rows, 128), F32)
        following = scores(0)
        for j in range(quads):
            s, sm = following
            if j + 1 < quads:
                following = scores(j + 1)
            s = [only_same_document(part, i) for part in head_rows(s)]
            peaks = [
                jnp.max(
                    jnp.concatenate([s[h], jnp.where(own[h], sm, ABSENT_SCORE)], axis=1),
                    axis=1, keepdims=True,
                )
                for h in range(4)
            ]
            pm = jnp.exp(sm - spread(peaks, mem_lanes))
            mprob[j] = pm.astype(BF16)
            totals, probs = [], []
            for h in range(4):
                p = jnp.exp(s[h] - peaks[h])
                probs.append(p.astype(BF16))
                tprob[j, h * rows : (h + 1) * rows, :] = probs[h]
                both = jnp.concatenate([p, jnp.where(own[h], pm, 0.0)], axis=1)
                totals.append(1.0 / jnp.sum(both, axis=1, keepdims=True))
                st = jnp.where(stat_lane == 4 * j + h, totals[h], st)
            tok_v, mem_v = token_and_memory(kvb, width + j * quad)
            o = spread(head_rows(dot(jnp.concatenate(probs, axis=0), tok_v)), head_lanes)
            o = o + dot(pm.astype(BF16), mem_v)
            ctxb[:, j * quad : (j + 1) * quad] = (o * spread(totals, head_lanes)).astype(BF16)
        stats[i] = st
        ctx[i] = ctxb[...]

    def to_queries(product):
        return product.astype(BF16) * BF16(scale)

    def forward_tick(t, carry):
        i = t - x

        @pl.when((i >= 0) & (i < items))
        def _():
            ahead = (x == 0) & (i >= n) & (lax.rem(i, n) == 0)

            @pl.when(i > 0)
            def _():
                qkv_copies(i - 1)[1].wait()
                gp_copy(i - 1).wait()

            @pl.when(x == 0)
            def _():
                token_copy(0, i).wait()
                token_copy(1, i).wait()

            @pl.when(ahead)
            def _():
                kvb[0, 0:toks, :] = dot(x0[i, 0:toks, :], wf[0, :, width:wide]).astype(BF16)
                kvb[1, 0:toks, :] = dot(
                    xo[lax.rem(i, n), 0:toks, :], wf[0, :, width:wide]
                ).astype(BF16)
                qb[0:toks, :] = to_queries(dot(x0[i, 0:toks, :], wf[0, :, 0:width]))

            @pl.when(x == 0)
            def _():
                for which, rows_ref in enumerate((x0.at[i], xo.at[lax.rem(i, n)])):

                    @pl.when(i < n)
                    def _():
                        rows_ref[toks:rows, :] = jnp.zeros((MEM_PAD, width), BF16)

                    @pl.when(i >= n)
                    def _():
                        mem_copy(which, i - n).wait_recv()
                        rows_ref[toks:rows, :] = jnp.where(
                            keep[i][:, 0:1] > 0.0, memin[which, i - n], jnp.zeros((), BF16)
                        )

            @pl.when(x == 1)
            def _():
                for p in range(2):
                    x_copy(p, i).wait_recv()
                    pass_copy(p, i).start()

            @pl.when(i == 0)
            def _():
                wait_first_of(0, (0,))

            @pl.when(ahead)
            def _():
                memory = jnp.concatenate(
                    [x0[i, toks:rows, :], xo[lax.rem(i, n), toks:rows, :]], axis=0
                )
                both = dot(memory, wf[0, :, width:wide]).astype(BF16)
                kvb[0, toks:rows, :] = both[0:MEM_PAD]
                kvb[1, toks:rows, :] = both[MEM_PAD:]
                qb[toks:rows, :] = to_queries(dot(memory, wf[0, :, 0:width])[0:MEM_PAD])

            @pl.when(jnp.logical_not(ahead))
            def _():
                kvb[0] = dot(x0[i], wf[0, :, width:wide]).astype(BF16)

                @pl.when(i == 0)
                def _():
                    wait_first_of(0, (1,))

                qb[...] = to_queries(dot(x0[i], wf[0, :, 0:width]))

                @pl.when(x == 1)
                def _():
                    for p in range(2):
                        pass_copy(p, i).wait_recv()

                kvb[1] = dot(xo[lax.rem(i, n)], wf[0, :, width:wide]).astype(BF16)

            for copy in qkv_copies(i):
                copy.start()

            @pl.when((x == 0) & (i < items - n))
            def _():
                token_copy(1, i + n).start()

            @pl.when(i > 0)
            def _():
                for copy in prob_copies(i - 1, False):
                    copy.wait()

            attend(i)
            for copy in prob_copies(i, False):
                copy.start()

            @pl.when(i == 0)
            def _():
                wait_first_of(0, (2,))
                weight_remote(4).wait_recv()

            normed, inv = normalize(dot(ctxb[...], wf[0, :, wide:]) + x0[i].astype(F32))
            natt[i] = normed.astype(BF16)
            stats[i] = jnp.where(stat_lane == heads, inv, stats[i])
            yatt[i] = (normed * nrm[0, 0:1, :] + nrm[0, 1:2, :]).astype(BF16)

            @pl.when(i == 0)
            def _():
                wait_first_of(1, (0, 1, 2))

            @pl.when(i > 0)
            def _():
                route_sent(S_GLO, i - 1)
                route_sent(S_GHI, i - 1)

            qkv_copies(i)[0].wait()

            for part in range(2):
                cols = slice(part * hidden_half, (part + 1) * hidden_half)
                u = dot(yatt[i], wf[1, :, cols])
                cdf = 0.5 + 0.5 * lax.erf(u * 0.7071067811865476)
                pdf = 0.3989422804014327 * jnp.exp(-0.5 * u * u)
                g[:, cols] = (u * cdf).astype(BF16)
                gpb[:, cols] = (cdf + u * pdf).astype(BF16)
            @pl.when(i == 0)
            def _():
                wait_first_of(0, (3,))
                wait_first_of(1, (3,))

            def finish_rows(part):
                normed, inv = normalize(
                    dot(g[part, 0:hidden_half], wd[0])
                    + dot(g[part, hidden_half:], wd[1])
                    + yatt[i, part].astype(F32)
                )
                yd[i, part] = (normed * nrm[1, 0:1, :] + nrm[1, 1:2, :]).astype(BF16)
                nff[i, part] = normed.astype(BF16)
                stats[i, part] = jnp.where(stat_lane[part] == heads + 1, inv, stats[i, part])

            @pl.when(x == 0)
            def _():
                for p in range(2):
                    finish_rows(piece(p))
                    x_copy(p, i).start()

            @pl.when(x == 1)
            def _():
                finish_rows(slice(0, rows))

            @pl.when((x == 1) & (i < items - n))
            def _():
                for which in range(2):
                    mem_copy(which, i).start()

            gp_copy(i).start()
            for kind in (S_GLO, S_GHI, S_X0, S_CTX, OUT_ATT, S_Y1, S_Y2, OUT_FF):
                route(kind, i)

        return carry

    lax.fori_loop(0, items + 1, forward_tick, 0)

    def forward_sent(i):
        route_sent(OUT_FF, i)

        @pl.when(x == 0)
        def _():
            for p in range(2):
                x_copy(p, i).wait_send()

        @pl.when(x == 1)
        def _():
            for p in range(2):
                pass_copy(p, i).wait_send()

        @pl.when((x == 1) & (i < items - n))
        def _():
            for which in range(2):
                mem_copy(which, i).wait_send()

    for copy in prob_copies(items - 1, False) + qkv_copies(items - 1)[1:]:
        copy.wait()
    for copy in prob_copies(items - n, True):
        copy.start()
    gp_copy(items - 1).wait()
    acc[...] = jnp.zeros_like(acc)

    def norm_back(s, i, normed_ref):
        grad = (gy[i] if s else gab[...]).astype(F32)
        normed = normed_ref[i].astype(F32)
        inv = stats[i][:, heads + s : heads + s + 1]
        acc[s, 0:1, :] += jnp.sum(grad * normed, axis=0, keepdims=True)
        acc[s, 1:2, :] += jnp.sum(grad, axis=0, keepdims=True)
        scaled = grad * nrm[s, 0:1, :]
        row_term = jnp.mean(scaled, axis=1, keepdims=True)
        row_cross = jnp.mean(scaled * normed, axis=1, keepdims=True)
        dh = inv * (scaled - row_term - normed * row_cross)
        dhb[...] = dh
        normed_ref[i] = dh.astype(BF16)

    def attend_back(i, slot):
        def prob_grads(j):
            inverse = [stats[i][:, 4 * j + h : 4 * j + h + 1] for h in range(4)]
            c4 = dctx[:, j * quad : (j + 1) * quad].astype(F32) * spread(inverse, head_lanes)
            c4 = c4.astype(BF16)
            tok_v, mem_v = token_and_memory(kv.at[i], width + j * quad)
            return c4, dot(stacked(c4), tok_v, 1, 1), dot(c4, mem_v, 1, 1)

        following = prob_grads(0)
        for j in range(quads):
            c4, dp, dpm = following
            if j + 1 < quads:
                following = prob_grads(j + 1)
            cols = slice(j * quad, (j + 1) * quad)
            q4 = q[i, :, cols]
            tok_k, mem_k = token_and_memory(kv.at[i], j * quad)
            products = c4.astype(F32) * ctx[i, :, cols].astype(F32)
            dp = head_rows(dp)
            inner = [
                jnp.sum(jnp.where(head_lanes == h, products, 0.0), axis=1, keepdims=True)
                for h in range(4)
            ]
            dscores = [
                (tprob[j, h * rows : (h + 1) * rows, :].astype(F32) * (dp[h] - inner[h])).astype(BF16)
                for h in range(4)
            ]
            dsm = (mprob[j].astype(F32) * (dpm - spread(inner, mem_lanes))).astype(BF16)
            ct, qt = jnp.transpose(c4), jnp.transpose(q4)
            mine = [slice(h * head_dim, (h + 1) * head_dim) for h in range(4)]
            dv = [
                dot(ct[mine[h]], tprob[j, h * rows : (h + 1) * rows, :]).astype(BF16)
                for h in range(4)
            ]
            dk = [dot(qt[mine[h]], dscores[h]).astype(BF16) for h in range(4)]
            dv = jnp.transpose(jnp.concatenate(dv, axis=0))
            dk = jnp.transpose(jnp.concatenate(dk, axis=0))
            dscores = jnp.concatenate(dscores, axis=0)
            dq = spread(head_rows(dot(dscores, tok_k)), head_lanes) + dot(dsm, mem_k)
            dqb[:, cols] = (dq * scale).astype(BF16)
            dvm = jnp.where(diagonal, dot(mprob[j], c4, 0, 0), 0.0)
            dkm = jnp.where(diagonal, dot(dsm, q4, 0, 0), 0.0)
            dvm = sum(dvm[h * mem_keys : (h + 1) * mem_keys] for h in range(4))
            dkm = sum(dkm[h * mem_keys : (h + 1) * mem_keys] for h in range(4))
            for half, (tok_part, mem_part) in enumerate(((dk, dkm), (dv, dvm))):
                cols = slice(half * quad, (half + 1) * quad)
                for core in range(2):
                    dkvs[core, j, 0:toks, cols] = tok_part[
                        core * toks : (core + 1) * toks
                    ].astype(BF16)
                    dkvs[core, j, toks:rows, cols] = mem_part[
                        core * MEM_PAD : (core + 1) * MEM_PAD
                    ].astype(BF16)
            if j == quads - 1:
                dkv_copy(j, i, slot).start()
            elif j == quads - 2:
                for ready in range(quads - 1):
                    dkv_copy(ready, i, slot).start()

    def gather_dkv(j, i, slot):
        dkv_copy(j, i, slot).wait_recv()
        both = (dkvs[0, j].astype(F32) + dkvin[slot, j].astype(F32)).astype(BF16)
        kv[i, 0, :, j * quad : (j + 1) * quad] = both[:, 0:quad]
        kv[i, 0, :, width + j * quad : width + (j + 1) * quad] = both[:, quad:]

    def dkv_back(i, low, high):
        return dot(kv[i, 0, :, low:high], wf[0, :, width + low : width + high], 1, 1) + dot(
            kv[i, 0, :, width + low : width + high],
            wf[0, :, 2 * width + low : 2 * width + high], 1, 1,
        )

    def item_of(r):
        return (nseg - 1 - lax.div(r, n)) * n + lax.rem(r, n)

    def backward_tick(t, carry):
        r = t - (1 - x)

        @pl.when((r >= 0) & (r < items))
        def _():
            i = item_of(r)
            slot = lax.rem(r, 2)

            @pl.when(x == 1)
            def _():
                cot_copy(i).wait()

                @pl.when(i >= items - n)
                def _():
                    gy[i, toks:rows, :] = jnp.zeros((MEM_PAD, width), BF16)

                @pl.when(i < items - n)
                def _():
                    mg_copy(i + n).wait_recv()
                    gy[i, toks:rows, :] = jnp.where(
                        keep[i + n][:, 0:1] > 0.0, mgin[i + n], jnp.zeros((), BF16)
                    )

            @pl.when(x == 0)
            def _():
                gy_copy(i).wait_recv()

            @pl.when(r > 0)
            def _():
                route_sent(S_DQ, item_of(r - 1))
                route_sent(GIN_FF, item_of(r - 1))

            norm_back(1, i, nff)
            for part in range(2):
                cols = slice(part * hidden_half, (part + 1) * hidden_half)
                dg = dot(nff[i], wd[part], 1, 1)
                gp[i, :, cols] = (dg * gp[i, :, cols].astype(F32)).astype(BF16)
            gab[...] = (dot(gp[i], wf[1], 1, 1) + dhb[...]).astype(BF16)
            norm_back(0, i, natt)
            dctx[...] = dot(natt[i], wf[0, :, wide:], 1, 1).astype(BF16)
            route(S_DFF0, i)
            route(S_DFF1, i)
            route(S_DU, i)
            route(GIN_FF, i)
            route(S_DATT, i)
            for copy in prob_copies(i, True):
                copy.wait()
            attend_back(i, slot)
            route(S_DQ, i)

            @pl.when(r + 1 < items)
            def _():
                for copy in prob_copies(item_of(r + 1), True):
                    copy.start()

            for j in range(quads - 1):
                gather_dkv(j, i, slot)
            if quads > 1:
                route(S_DKV, i)
                route(S_DV, i)
            early = (quads - 1) * quad
            partial_sum = dot(dqb[...], wf[0, :, 0:width], 1, 1) + dhb[...]
            if early:
                partial_sum = partial_sum + dkv_back(i, 0, early)
            dhb[...] = partial_sum
            gather_dkv(quads - 1, i, slot)
            route(S_LASTK, i)
            route(S_LASTV, i)
            forward_sent(i)
            yd[i] = (dkv_back(i, early, width) + dhb[...]).astype(BF16)

            @pl.when(x == 1)
            def _():
                gy_copy(i).start()

            @pl.when((x == 0) & (i >= n))
            def _():
                mg_copy(i).start()

            route(GIN_ATT, i)
            for j in range(quads):
                dkv_copy(j, i, slot).wait_send()

        return carry

    lax.fori_loop(0, items + 1, backward_tick, 0)

    acc_copy = remote(acc.at[1 - c], accp, as_sem, ar_sem, core_peer)
    acc_copy.start()

    def backward_drain(i, carry):
        @pl.when(x == 1)
        def _():
            gy_copy(i).wait_send()

        @pl.when((x == 0) & (i >= n))
        def _():
            mg_copy(i).wait_send()

        for kind in range(KINDS):
            if quads == 1 and kind in (S_DKV, S_DV):
                continue
            if kind not in (OUT_FF, S_GLO, S_GHI, S_DQ, GIN_FF):
                route_sent(kind, i)
            route_received(kind, i)
        return carry

    lax.fori_loop(0, items, backward_drain, 0)
    route_sent(S_GLO, items - 1)
    route_sent(S_GHI, items - 1)
    route_sent(S_DQ, item_of(items - 1))
    route_sent(GIN_FF, item_of(items - 1))
    for k in range(5):
        weight_remote(k).wait_send()
    acc_copy.wait()
    norm_grad[...] = acc[c] + accp[...]


def run_layers(n, nseg, heads, tokens, cotangent, first, down, docs, resets, gain, shift):
    length, width = tokens.shape[1:]
    toks = length // nseg // 2
    rows = toks + MEM_PAD
    items = n * nseg
    hidden_half = down.shape[1]
    quads = heads // 4
    quad = width // quads
    any_spec = pl.BlockSpec(memory_space=pl.ANY)
    vmem_spec = pl.BlockSpec(memory_space=pltpu.VMEM)
    dma = pltpu.SemaphoreType.DMA
    item_rows = pltpu.VMEM((items, rows, width), BF16)
    one, two = dma((items,)), dma((2, items))
    return pl.pallas_call(
        partial(layers_kernel, n, nseg, heads),
        out_shape=(
            jax.ShapeDtypeStruct((n, length, width), BF16),
            jax.ShapeDtypeStruct((n, length, width), BF16),
            jax.ShapeDtypeStruct((2 * items, rows, width), BF16),
            jax.ShapeDtypeStruct((2 * items, rows, width), BF16),
            jax.ShapeDtypeStruct((2 * items, rows, 4 * width), BF16),
            jax.ShapeDtypeStruct((2 * items, rows, hidden_half), BF16),
            jax.ShapeDtypeStruct((2 * items, rows, width), BF16),
            jax.ShapeDtypeStruct((2, width), F32),
            jax.ShapeDtypeStruct((items, quads, 4 * rows, 2 * toks), BF16),
            jax.ShapeDtypeStruct((items, quads, rows, 8 * MEM_PAD), BF16),
        ),
        in_specs=[any_spec] * 4 + [vmem_spec] * 4,
        out_specs=[any_spec] * 7 + [vmem_spec] + [any_spec] * 2,
        scratch_shapes=[
            pltpu.VMEM((2, width, 4 * width), BF16),
            pltpu.VMEM((2, hidden_half, width), BF16),
            pltpu.VMEM((2, 2, width), F32),
            item_rows,
            pltpu.VMEM((n, rows, width), BF16),
            item_rows,
            pltpu.VMEM((items, 2, rows, 2 * width), BF16),
            item_rows,
            item_rows,
            item_rows,
            item_rows,
            item_rows,
            item_rows,
            pltpu.VMEM((rows, 2 * hidden_half), BF16),
            pltpu.VMEM((rows, 2 * hidden_half), BF16),
            pltpu.VMEM((items, rows, 2 * hidden_half), BF16),
            pltpu.VMEM((items, rows, 128), F32),
            pltpu.VMEM((items, toks, 128), F32),
            pltpu.VMEM((items, 1, 2 * toks), F32),
            pltpu.VMEM((items, MEM_PAD, 128), F32),
            pltpu.VMEM((2, items, MEM_PAD, width), BF16),
            pltpu.VMEM((items, MEM_PAD, width), BF16),
            pltpu.VMEM((2, quads, rows, 2 * quad), BF16),
            pltpu.VMEM((2, quads, rows, 2 * quad), BF16),
            pltpu.VMEM((rows, width), F32),
            pltpu.VMEM((2, rows, 2 * width), BF16),
            pltpu.VMEM((2, 2, width), F32),
            pltpu.VMEM((2, width), F32),
            pltpu.VMEM((quads, 4 * rows, 2 * toks), BF16),
            pltpu.VMEM((quads, rows, 8 * MEM_PAD), BF16),
            dma((4,)), dma((5,)), dma((5,)),
            two, one, one, two, two, two,
            two, two,
            two, two,
            two, two,
            one, one, one, one,
            dma((quads, items)), dma((quads, items)),
            dma(()), dma(()),
        ]
        + [dma((KINDS, items))] * 3,
        compiler_params=pltpu.CompilerParams(
            collective_id=0, has_side_effects=True, vmem_limit_bytes=61 * 1024 * 1024
        ),
    )(tokens, cotangent, first, down, docs, resets, gain, shift)


def reduce_kernel(
    chunks,
    sx1, sx2, sr, sg, sd, norm_part,
    sums, norm_out,
    x1, x2, rr, gg, dd, work, done, got_u, got_uz, got_vz, got_vy, norms,
    right_sem, left_sem, out_sem, u_s, u_r, uz_s, uz_r, vz_s, vz_r, vy_s, vy_r, vg_s, vg_r,
    uzg_s, uzg_r, vzg_s, vzg_r, ug_s, ug_r, n_s, n_r,
):
    lines = 4
    d = lax.axis_index("dp")
    y = lax.rem(d, 2)
    z = lax.div(d, 2)
    dp = lax.axis_size("dp")
    width = sd.shape[1]
    half = width // 2
    part = width // chunks
    hr = part // 2
    lane_group = 128
    per_group = lane_group // part
    y_peer = {"dp": z * 2 + (1 - y)}

    def remote(src, dst, send, recv, peer):
        return pltpu.make_async_remote_copy(
            src_ref=src, dst_ref=dst, send_sem=send, recv_sem=recv,
            device_id=peer, device_id_type=MESH,
        )

    def other(step):
        return {"dp": lax.rem(d + step, dp)}

    barrier = pltpu.get_barrier_semaphore()
    for step in range(1, dp):
        pl.semaphore_signal(barrier, inc=1, device_id=other(step), device_id_type=MESH)

    lane_groups = width // lane_group
    right_loads = [(sd, dd)] + [
        (sr.at[:, b * width : (b + 1) * width], rr.at[:, b * width : (b + 1) * width])
        for b in range(4)
    ]

    def right_load(k):
        src, dst = right_loads[k]
        return pltpu.make_async_copy(src, dst, right_sem.at[k])

    def left_load(which, group):
        src, dst, low = ((sg, gg, 0), (sg, gg, width), (sx2, x2, 0), (sx1, x1, 0))[which]
        cols = pl.ds(pl.multiple_of(low + group * lane_group, lane_group), lane_group)
        return pltpu.make_async_copy(src.at[:, cols], dst.at[:, cols], left_sem.at[which, group])

    right_load(0).start()
    left_load(0, 0).start()
    left_load(1, 0).start()
    left_load(2, 0).start()
    right_load(4).start()

    norms[d] = norm_part[...]
    pl.semaphore_wait(barrier, dp - 1)

    def norm_copy(step):
        return remote(norms.at[d], norms.at[d], n_s.at[step - 1], n_r.at[step - 1], other(step))

    def norm_arrival(step):
        source = lax.rem(d + dp - step, dp)
        return remote(
            norms.at[source], norms.at[source], n_s.at[step - 1], n_r.at[step - 1], other(step)
        )

    for step in range(1, dp):
        norm_copy(step).start()

    def column_half(h):
        return pl.ds(pl.multiple_of(h * half, 128), half)

    mine, theirs = column_half(y), column_half(1 - y)

    def place(flow):
        return z if flow == 0 else lines - 1 - z

    def onward(flow):
        step = -1 if flow == 0 else 1
        return {"dp": (z + step) * 2 + y}

    def back(flow):
        step = 1 if flow == 0 else -1
        return {"dp": (z + step) * 2 + y}

    def rows_of(flow):
        return slice(flow * hr, (flow + 1) * hr)

    def u_copy(k):
        return remote(
            work.at[k, 0:3, :, theirs], got_u.at[k], u_s.at[k], u_r.at[k], y_peer
        )

    def uz_copy(flow, k):
        return remote(
            work.at[k, 0:3, rows_of(flow), mine], got_uz.at[flow, k],
            uz_s.at[flow, k], uz_r.at[flow, k], onward(flow),
        )

    def vz_copy(flow, k):
        return remote(
            work.at[k, 3:6, rows_of(flow), :], got_vz.at[flow, k],
            vz_s.at[flow, k], vz_r.at[flow, k], onward(flow),
        )

    def vy_copy(flow, k):
        return remote(
            work.at[k, 3:6, rows_of(flow), theirs], got_vy.at[k], vy_s.at[k], vy_r.at[k], y_peer
        )

    def vg_copy(flow, k, cols):
        spot = done.at[k, 3:6, rows_of(flow), cols]
        return remote(spot, spot, vg_s.at[k], vg_r.at[k], y_peer)

    def uzg_copy(flow, k):
        spot = done.at[k, 0:3, rows_of(flow), mine]
        return remote(spot, spot, uzg_s.at[flow, k], uzg_r.at[flow, k], back(flow))

    def vzg_copy(flow, k):
        spot = done.at[k, 3:6, rows_of(flow), :]
        return remote(spot, spot, vzg_s.at[flow, k], vzg_r.at[flow, k], back(flow))

    def ug_copy(flow, k, cols):
        spot = done.at[k, 0:3, rows_of(flow), cols]
        return remote(spot, spot, ug_s.at[flow, k], ug_r.at[flow, k], y_peer)

    def out_copy(k):
        return pltpu.make_async_copy(done.at[k], sums.at[k], out_sem.at[k])

    def plus(a, b):
        return (a.astype(F32) + b.astype(F32)).astype(BF16)

    def ready(k, low=0):
        return (k >= low) & (k < chunks)

    def store_chunks(group, block, value):
        for e in range(per_group):
            work[group * per_group + e, block] = value[e * part : (e + 1) * part]

    def second_half(r):
        group = lax.div(r + per_group - 1, per_group)
        cols = pl.ds(pl.multiple_of(group * lane_group, lane_group), lane_group)
        gcols = pl.ds(pl.multiple_of(width + group * lane_group, lane_group), lane_group)

        @pl.when(r == 0)
        def _():
            right_load(0).wait()

        left_load(0, group).wait()
        store_chunks(group, 4, dot(gg[:, cols], dd[...], 0, 0).astype(BF16))
        left_load(1, group).wait()
        store_chunks(group, 5, dot(gg[:, gcols], dd[...], 0, 0).astype(BF16))
        left_load(2, group).wait()

        @pl.when(r == 0)
        def _():
            right_load(4).wait()
            left_load(3, 0).start()
            for k in range(1, 4):
                right_load(k).start()
            for later in range(1, lane_groups):
                for which in range(4):
                    left_load(which, later).start()

        store_chunks(group, 3, dot(x2[:, cols], rr[:, 3 * width :], 0, 0).astype(BF16))

    def round_step(r, carry):
        @pl.when(r == 0)
        def _():
            second_half(r)

        for flow in range(2):
            p = place(flow)
            k = r - (lines - 1 - p)
            rows = rows_of(flow)

            @pl.when(ready(k))
            def _():
                @pl.when(p < lines - 1)
                def _():
                    vz_copy(flow, k).wait_recv()
                    work[k, 3:6, rows, :] = plus(work[k, 3:6, rows, :], got_vz[flow, k])

                @pl.when(p > 0)
                def _():
                    vz_copy(flow, k).start()

                @pl.when(p == 0)
                def _():
                    vy_copy(flow, k).start()

        @pl.when((lax.rem(r, per_group) == 0) & (r < chunks))
        def _():
            group = lax.div(r, per_group)
            cols = pl.ds(pl.multiple_of(group * lane_group, lane_group), lane_group)
            left_load(3, group).wait()
            for b in range(3):

                @pl.when(r == 0)
                def _():
                    right_load(1 + b).wait()

                store_chunks(
                    group, b,
                    dot(x1[:, cols], rr[:, b * width : (b + 1) * width], 0, 0).astype(BF16),
                )

        @pl.when(ready(r))
        def _():
            u_copy(r).start()

        @pl.when((lax.rem(r, per_group) == per_group - 1) & (r + 1 < chunks))
        def _():
            second_half(r)

        @pl.when(ready(r - 1))
        def _():
            k = r - 1
            u_copy(k).wait_recv()
            work[k, 0:3, :, mine] = plus(work[k, 0:3, :, mine], got_u[k])

        for flow in range(2):
            p = place(flow)
            k = r - 1 - (lines - 1 - p)
            rows = rows_of(flow)

            @pl.when(ready(k))
            def _():
                @pl.when(p < lines - 1)
                def _():
                    uz_copy(flow, k).wait_recv()
                    total = plus(work[k, 0:3, rows, mine], got_uz[flow, k])

                    @pl.when(p > 0)
                    def _():
                        work[k, 0:3, rows, mine] = total

                    @pl.when(p == 0)
                    def _():
                        done[k, 0:3, rows, mine] = total

                @pl.when(p > 0)
                def _():
                    uz_copy(flow, k).start()

                @pl.when(p == 0)
                def _():
                    uzg_copy(flow, k).start()
                    ug_copy(flow, k, mine).start()

        for flow in range(2):
            p = place(flow)
            rows = rows_of(flow)

            @pl.when((p == 0) & ready(r - lines))
            def _():
                k = r - lines
                vy_copy(flow, k).wait_recv()
                done[k, 3:6, rows, mine] = plus(work[k, 3:6, rows, mine], got_vy[k])
                vg_copy(flow, k, mine).start()

            @pl.when((p == 0) & ready(r - lines - 1))
            def _():
                k = r - lines - 1
                vg_copy(flow, k, theirs).wait_recv()
                vzg_copy(flow, k).start()

        for flow in range(2):
            p = place(flow)
            k = r - lines - p

            @pl.when((p > 0) & ready(k))
            def _():
                uzg_copy(flow, k).wait_recv()

                @pl.when(p < lines - 1)
                def _():
                    uzg_copy(flow, k).start()

                ug_copy(flow, k, mine).start()

        for flow in range(2):
            p = place(flow)
            k = r - lines - 1 - p

            @pl.when((p > 0) & ready(k))
            def _():
                vzg_copy(flow, k).wait_recv()

                @pl.when(p < lines - 1)
                def _():
                    vzg_copy(flow, k).start()

            @pl.when(ready(k))
            def _():
                ug_copy(flow, k, theirs).wait_recv()

        @pl.when(ready(r - 2 * lines))
        def _():
            out_copy(r - 2 * lines).start()

        return carry

    lax.fori_loop(0, chunks + 2 * lines, round_step, 0)

    for step in range(1, dp):
        norm_arrival(step).wait_recv()
    total = norms[0]
    for e in range(1, dp):
        total = total + norms[e]
    norm_out[...] = total

    def drain(k, carry):
        out_copy(k).wait()
        u_copy(k).wait_send()
        for flow in range(2):
            p = place(flow)
            ug_copy(flow, k, mine).wait_send()

            @pl.when(p > 0)
            def _():
                vz_copy(flow, k).wait_send()
                uz_copy(flow, k).wait_send()

            @pl.when(p < lines - 1)
            def _():
                uzg_copy(flow, k).wait_send()
                vzg_copy(flow, k).wait_send()

            @pl.when(p == 0)
            def _():
                vy_copy(flow, k).wait_send()
                vg_copy(flow, k, mine).wait_send()

        return carry

    lax.fori_loop(0, chunks, drain, 0)
    for step in range(1, dp):
        norm_copy(step).wait_send()


def sum_weights(dp, sx1, sx2, sr, sg, sd, norm_part):
    total, width = sx1.shape
    chunks = 12
    part = width // chunks
    half = width // 2
    any_spec = pl.BlockSpec(memory_space=pl.ANY)
    vmem_spec = pl.BlockSpec(memory_space=pltpu.VMEM)
    dma = pltpu.SemaphoreType.DMA
    one, two = dma((chunks,)), dma((2, chunks))
    return pl.pallas_call(
        partial(reduce_kernel, chunks),
        out_shape=(
            jax.ShapeDtypeStruct((chunks, 6, part, width), BF16),
            jax.ShapeDtypeStruct((2, width), F32),
        ),
        in_specs=[any_spec] * 5 + [vmem_spec],
        out_specs=[any_spec, vmem_spec],
        scratch_shapes=[
            pltpu.VMEM((total, width), BF16),
            pltpu.VMEM((total, width), BF16),
            pltpu.VMEM((total, 4 * width), BF16),
            pltpu.VMEM((total, 2 * width), BF16),
            pltpu.VMEM((total, width), BF16),
            pltpu.VMEM((chunks, 6, part, width), BF16),
            pltpu.VMEM((chunks, 6, part, width), BF16),
            pltpu.VMEM((chunks, 3, part, half), BF16),
            pltpu.VMEM((2, chunks, 3, part // 2, half), BF16),
            pltpu.VMEM((2, chunks, 3, part // 2, width), BF16),
            pltpu.VMEM((chunks, 3, part // 2, half), BF16),
            pltpu.VMEM((dp, 2, width), F32),
            dma((5,)),
            dma((4, width // 128)),
            one,
            one, one,
            two, two,
            two, two,
            one, one,
            one, one,
            two, two,
            two, two,
            two, two,
            dma((dp - 1,)), dma((dp - 1,)),
        ],
        compiler_params=pltpu.CompilerParams(
            collective_id=1, has_side_effects=True, vmem_limit_bytes=60 * 1024 * 1024
        ),
    )(sx1, sx2, sr, sg, sd, norm_part)


def finish_kernel(sums, out, gin, norms, first_grad, down_grad, out_copy, gin_copy, gain, shift):
    group, _, part, width = sums.shape
    for e in range(group):
        rows = slice(e * part, (e + 1) * part)
        for b in range(4):
            first_grad[rows, b * width : (b + 1) * width] = sums[e, b].astype(F32)
        for b in range(2):
            down_grad[b, rows] = sums[e, 4 + b].astype(F32)
    out_copy[...] = out[...]
    gin_copy[...] = gin[...]
    gain[...] = norms[0:1]
    shift[...] = norms[1:2]


def finish(sums, out, gin, norms):
    chunks, _, part, width = sums.shape
    total = out.shape[0]
    group, blocks = chunks // 3, 2
    tokens = pl.BlockSpec((total // blocks, width), lambda k: (jnp.minimum(k, blocks - 1), 0))
    whole = pl.BlockSpec((1, width), lambda k: (0, 0))
    return pl.pallas_call(
        finish_kernel,
        grid=(chunks // group,),
        out_shape=(
            jax.ShapeDtypeStruct((width, 4 * width), F32),
            jax.ShapeDtypeStruct((2, width, width), F32),
            jax.ShapeDtypeStruct(out.shape, BF16),
            jax.ShapeDtypeStruct(gin.shape, BF16),
            jax.ShapeDtypeStruct((1, width), F32),
            jax.ShapeDtypeStruct((1, width), F32),
        ),
        in_specs=[
            pl.BlockSpec((group, 6, part, width), lambda k: (k, 0, 0, 0)),
            tokens,
            tokens,
            pl.BlockSpec((2, width), lambda k: (0, 0)),
        ],
        out_specs=[
            pl.BlockSpec((group * part, 4 * width), lambda k: (k, 0)),
            pl.BlockSpec((2, group * part, width), lambda k: (0, k, 0)),
            tokens,
            tokens,
            whole,
            whole,
        ],
        compiler_params=pltpu.CompilerParams(vmem_limit_bytes=61 * 1024 * 1024),
    )(sums, out, gin, norms)


def shards(
    tokens, doc_ids, reset_flags, first_weights, down_halves, norm_gain, norm_bias, cotangent
):
    n, length, width = tokens.shape
    items = n * NSEG
    rows = length // NSEG // 2 + MEM_PAD
    out, gin, sx1, sx2, sr, sg, sd, norm_grad, _, _ = run_layers(
        n, NSEG, H, tokens, cotangent, first_weights, down_halves,
        doc_ids, reset_flags.T, norm_gain, norm_bias,
    )
    total = 2 * items * rows
    sx1, sx2, sd = (a.reshape(total, width) for a in (sx1, sx2, sd))
    sr = sr.reshape(total, 4 * width)
    sg = sg.reshape(total, -1)

    dp = lax.axis_size("dp")
    if dp == 8:
        sums, norm_grad = sum_weights(dp, sx1, sx2, sr, sg, sd, norm_grad)
        first_grad, down_grad, out, gin, gain_grad, shift_grad = finish(
            sums, out.reshape(-1, width), gin.reshape(-1, width), norm_grad
        )
        down_grad = down_grad.reshape(-1, width)
        out, gin = (a.reshape(n, length, width) for a in (out, gin))
    else:

        def weight_grad(left, right):
            return jnp.einsum("rd,re->de", left, right, preferred_element_type=F32).astype(BF16)

        first_grad = jnp.concatenate(
            [weight_grad(sx1, sr[:, : 3 * width]), weight_grad(sx2, sr[:, 3 * width :])], axis=1
        )
        down_grad = weight_grad(sg, sd)
        first_grad, down_grad = lax.psum((first_grad, down_grad), "dp")
        norm_grad = lax.psum(norm_grad, "dp")
        gain_grad, shift_grad = norm_grad[0:1], norm_grad[1:2]
    return (
        out[None],
        gin[None],
        first_grad.astype(F32)[None],
        down_grad.astype(F32)[None],
        gain_grad,
        shift_grad,
    )


def solution(mesh):
    in_specs = (
        P("dp", None, None),
        P("dp", None),
        P("dp", None),
        P("section", None, None),
        P("section", None, None),
        P("section", None),
        P("section", None),
        P("dp", None, None),
    )
    out_specs = (
        P("section", "dp", None, None),
        P("section", "dp", None, None),
        P("section", None, None),
        P("section", None, None),
        P("section", None),
        P("section", None),
    )
    return jax.shard_map(shards, mesh=mesh, in_specs=in_specs, out_specs=out_specs, check_vma=False)
```

```python
from functools import partial

import jax
import jax.numpy as jnp
from jax import lax
from jax.experimental import pallas as pl
from jax.experimental.pallas import tpu as pltpu
from jax.sharding import PartitionSpec as P

H = 12
M = 20
NSEG = 2
MEM_PAD = 16
NORM_EPSILON = 1e-05
MASKED_SCORE = -1000000000.0
ABSENT_SCORE = -3e38
MESH = pl.DeviceIdType.MESH
BF16 = jnp.bfloat16
F32 = jnp.float32

OUT_ATT, OUT_FF, GIN_ATT, GIN_FF = 0, 1, 2, 3
S_X0, S_CTX, S_DQ, S_DKV, S_DATT, S_GLO, S_DFF0 = 4, 5, 6, 7, 8, 9, 10
S_Y1, S_Y2, S_DU, S_GHI, S_DFF1 = 11, 12, 13, 14, 15
S_DV, S_LASTK, S_LASTV = 16, 17, 18
KINDS = 19


def dot(a, b, lhs_dim=1, rhs_dim=0):
    return lax.dot_general(
        a, b, (((lhs_dim,), (rhs_dim,)), ((), ())), preferred_element_type=F32
    )


def normalize(summed):
    mean = jnp.mean(summed, axis=-1, keepdims=True)
    centered = summed - mean
    var = jnp.mean(centered * centered, axis=-1, keepdims=True)
    inv = lax.rsqrt(var + NORM_EPSILON)
    return centered * inv, inv


def group_of(shape, dim, size):
    index = lax.broadcasted_iota(jnp.int32, shape, dim)
    return lax.shift_right_logical(index, size.bit_length() - 1)


def spread(values, groups):
    result = values[-1]
    for h in range(len(values) - 1):
        result = jnp.where(groups == h, values[h], result)
    return result


def layers_kernel(
    n, nseg, heads,
    tokens, cotangent, first, down, docs, resets, gain, shift,
    out, gin, sx1, sx2, sr, sg, sd, norm_grad, ptok, pmem,
    wf, wd, nrm, x0, xo, q, kv, ctx, natt, yatt, nff, yd, gy, g, gpb, gp, stats, qdoc, kdoc, keep,
    memin, mgin, dkvs, dkvin, dhb, kvb, acc, accp, tprob, mprob,
    wl, ws, wr, tok_sem, cot_sem, gp_sem, qkv_sem, pw_sem, pr_sem, fs_sem, fr_sem, xs_sem, xr_sem,
    ms_sem, mr_sem, gs_sem, gr_sem, hs_sem, hr_sem, ds_sem, dr_sem, as_sem, ar_sem,
    lsem, ssem, rsem,
):
    items = n * nseg
    section = lax.axis_index("section")
    c = lax.rem(section, 2)
    x = lax.div(section, 2)
    core_peer = {"section": x * 2 + (1 - c)}
    chip_peer = {"section": (1 - x) * 2 + c}
    cross_peer = {"section": (1 - x) * 2 + (1 - c)}
    rows, width = x0.shape[1:]
    toks = rows - MEM_PAD
    seg_len = 2 * toks
    hidden_half = wd.shape[1]
    wide = 3 * width
    head_dim = width // heads
    quad = 4 * head_dim
    quads = heads // 4
    mem_keys = 2 * MEM_PAD
    scale = head_dim ** (-0.5)
    qb = gpb.at[:, 0:width]
    ctxb = gpb.at[:, width : 2 * width]
    dqb = gpb.at[:, 0:width]
    gab = gpb.at[:, width : 2 * width]
    dctx = gpb.at[:, 2 * width : wide]

    def remote(src, dst, send, recv, peer):
        return pltpu.make_async_remote_copy(
            src_ref=src, dst_ref=dst, send_sem=send, recv_sem=recv,
            device_id=peer, device_id_type=MESH,
        )

    barrier = pltpu.get_barrier_semaphore()
    pl.semaphore_signal(barrier, inc=1, device_id=core_peer, device_id_type=MESH)
    pl.semaphore_signal(barrier, inc=1, device_id=chip_peer, device_id_type=MESH)
    pl.semaphore_signal(barrier, inc=1, device_id=cross_peer, device_id_type=MESH)

    def token_rows(ref, i, core=None):
        core = c if core is None else core
        return ref.at[lax.rem(i, n), pl.ds(lax.div(i, n) * seg_len + core * toks, toks), :]

    def token_copy(which, i):
        if which == 0:
            src, dst = token_rows(tokens, i), x0.at[i, 0:toks, :]
        else:
            src, dst = token_rows(tokens, i, 1 - c), xo.at[lax.rem(i, n), 0:toks, :]
        return pltpu.make_async_copy(src, dst, tok_sem.at[which, i])

    def cot_copy(i):
        return pltpu.make_async_copy(
            token_rows(cotangent, i), gy.at[i, 0:toks, :], cot_sem.at[i]
        )

    def weight_piece(k):
        if k == 0:
            return first.at[0, :, width:wide], wf.at[c, :, width:wide]
        if k == 1:
            return first.at[0, :, 0:width], wf.at[c, :, 0:width]
        if k == 2:
            return first.at[0, :, wide:], wf.at[c, :, wide:]
        return down.at[0], wd.at[c]

    def weight_local(k):
        src, dst = weight_piece(k)
        return pltpu.make_async_copy(src, dst, wl.at[k])

    def weight_remote(k):
        if k == 4:
            return remote(nrm.at[c], nrm.at[c], ws.at[4], wr.at[4], core_peer)
        src, dst = weight_piece(k)
        return remote(src, dst, ws.at[k], wr.at[k], core_peer)

    nrm[c, 0:1, :] = gain[...]
    nrm[c, 1:2, :] = shift[...]
    weight_local(0).start()

    @pl.when(x == 0)
    def _():
        token_copy(0, 0).start()
        token_copy(1, 0).start()

    pl.semaphore_wait(barrier, 3)
    for k in range(5):
        weight_remote(k).start()
    for k in range(1, 4):
        weight_local(k).start()
    for i in range(items):
        if i > 0:

            @pl.when(x == 0)
            def _():
                token_copy(0, i).start()
                if i < n:
                    token_copy(1, i).start()

        @pl.when(x == 1)
        def _():
            cot_copy(i).start()

    def wait_first_of(core, ks):
        @pl.when(c == core)
        def _():
            for k in ks:
                weight_local(k).wait()

        @pl.when(c != core)
        def _():
            for k in ks:
                weight_remote(k).wait_recv()

    for i in range(items):
        seq, seg = i % n, i // n
        own = pl.ds(pl.multiple_of(seg * seg_len + c * toks, toks), toks)
        others = pl.ds(pl.multiple_of(seg * seg_len + (1 - c) * toks, toks), toks)
        own_row = docs[seq : seq + 1, own].astype(F32)
        kdoc[i, :, 0:toks] = own_row
        kdoc[i, :, toks:] = docs[seq : seq + 1, others].astype(F32)
        qdoc[i] = jnp.transpose(jnp.broadcast_to(own_row, (128, toks)))
        if seg > 0:
            flag = resets[seg - 1 : seg, seq : seq + 1].astype(F32)
            keep[i] = jnp.broadcast_to(1.0 - flag, (MEM_PAD, 128))

    def routed(kind, i):
        block = i * 2 + c
        sec = 0
        if kind == OUT_ATT:
            src, dst = yatt.at[i, 0:toks, :], token_rows(out, i)
        elif kind == OUT_FF:
            src, dst, sec = yd.at[i, 0:toks, :], token_rows(out, i), 1
        elif kind == GIN_ATT:
            src, dst = yd.at[i, 0:toks, :], token_rows(gin, i)
        elif kind == GIN_FF:
            src, dst, sec = gab.at[0:toks, :], token_rows(gin, i), 1
        elif kind == S_X0:
            src, dst = x0.at[i], sx1.at[block]
        elif kind == S_CTX:
            src, dst = ctx.at[i], sx2.at[block]
        elif kind == S_DQ:
            src, dst = dqb, sr.at[block, :, 0:width]
        elif kind in (S_DKV, S_DV, S_LASTK, S_LASTV):
            last = width - width // quads
            low, high = (0, last) if kind in (S_DKV, S_DV) else (last, width)
            if kind in (S_DV, S_LASTV):
                low, high = low + width, high + width
            src, dst = kv.at[i, 0, :, low:high], sr.at[block, :, width + low : width + high]
        elif kind == S_DATT:
            src, dst = natt.at[i], sr.at[block, :, wide:]
        elif kind == S_GLO:
            src, dst = g.at[:, 0:hidden_half], sg.at[block]
        elif kind == S_DFF0:
            src, dst = nff.at[i], sd.at[block]
        elif kind == S_Y1:
            src, dst, sec = yatt.at[i], sx1.at[block], 1
        elif kind == S_Y2:
            src, dst, sec = yatt.at[i], sx2.at[block], 1
        elif kind == S_DU:
            src, dst, sec = gp.at[i], sr.at[block], 1
        elif kind == S_GHI:
            src, dst, sec = g.at[:, hidden_half:], sg.at[block], 1
        else:
            src, dst, sec = nff.at[i], sd.at[block], 1
        return src, dst, sec

    def route_local(kind, i):
        src, dst, _ = routed(kind, i)
        return pltpu.make_async_copy(src, dst, lsem.at[kind, i])

    def route_away(kind, i):
        src, dst, _ = routed(kind, i)
        return remote(src, dst, ssem.at[kind, i], rsem.at[kind, i], core_peer)

    def route(kind, i):
        sec = routed(kind, i)[2]

        @pl.when(c == sec)
        def _():
            route_local(kind, i).start()

        @pl.when(c != sec)
        def _():
            route_away(kind, i).start()

    def route_sent(kind, i):
        sec = routed(kind, i)[2]

        @pl.when(c == sec)
        def _():
            route_local(kind, i).wait()

        @pl.when(c != sec)
        def _():
            route_away(kind, i).wait_send()

    def route_received(kind, i):
        @pl.when(c == routed(kind, i)[2])
        def _():
            route_away(kind, i).wait_recv()

    def qkv_copies(i):
        return [
            pltpu.make_async_copy(qb, q.at[i], qkv_sem.at[0, i]),
            pltpu.make_async_copy(kvb, kv.at[i], qkv_sem.at[1, i]),
        ]

    def gp_copy(i):
        return pltpu.make_async_copy(gpb, gp.at[i], gp_sem.at[i])

    def prob_copies(i, back):
        pairs = ((tprob, ptok.at[i]), (mprob, pmem.at[i]))
        if back:
            return [
                pltpu.make_async_copy(dst, src, pr_sem.at[e, i])
                for e, (src, dst) in enumerate(pairs)
            ]
        return [
            pltpu.make_async_copy(src, dst, pw_sem.at[e, i]) for e, (src, dst) in enumerate(pairs)
        ]

    cut = rows // 32 * 16

    def piece(p):
        return slice(0, cut) if p == 0 else slice(cut, rows)

    def x_copy(p, i):
        return remote(
            yd.at[i, piece(p)], x0.at[i, piece(p)], xs_sem.at[p, i], xr_sem.at[p, i], chip_peer
        )

    def pass_copy(p, i):
        return remote(
            x0.at[i, piece(p)], xo.at[lax.rem(i, n), piece(p)],
            fs_sem.at[p, i], fr_sem.at[p, i], core_peer,
        )

    def mem_copy(which, i):
        return remote(
            yd.at[i, toks:rows, :], memin.at[which, i], ms_sem.at[which, i],
            mr_sem.at[which, i], cross_peer if which else chip_peer,
        )

    def gy_copy(p, i):
        return remote(
            yd.at[i, piece(p)], gy.at[i, piece(p)], gs_sem.at[p, i], gr_sem.at[p, i], chip_peer
        )

    def mg_copy(i):
        return remote(
            yd.at[i, toks:rows, :], mgin.at[i], hs_sem.at[i], hr_sem.at[i], chip_peer
        )

    def dkv_copy(j, i, slot):
        return remote(
            dkvs.at[1, j], dkvin.at[slot, j], ds_sem.at[j, i], dr_sem.at[j, i], core_peer
        )

    head_lanes = group_of((rows, quad), 1, head_dim)
    mem_lanes = group_of((rows, 4 * mem_keys), 1, mem_keys)
    key_lane = lax.broadcasted_iota(jnp.int32, (rows, 4 * mem_keys), 1)
    mem_valid = lax.rem(key_lane, MEM_PAD) < M // 2
    diagonal = group_of((4 * mem_keys, quad), 0, mem_keys) == group_of(
        (4 * mem_keys, quad), 1, head_dim
    )
    stat_lane = lax.broadcasted_iota(jnp.int32, (rows, 128), 1)

    def stacked(block):
        return jnp.concatenate(
            [jnp.where(head_lanes == h, block, BF16(0)) for h in range(4)], axis=0
        )

    def head_rows(block):
        return [block[h * rows : (h + 1) * rows] for h in range(4)]

    def token_and_memory(ref, low):
        cols = slice(low, low + quad)
        tok = jnp.concatenate([ref[0, 0:toks, cols], ref[1, 0:toks, cols]], axis=0)
        mem = jnp.concatenate([ref[0, toks:, cols], ref[1, toks:, cols]], axis=0)
        return tok, jnp.where(diagonal, jnp.concatenate([mem] * 4, axis=0), BF16(0))

    def only_same_document(s, i):
        mine = jnp.concatenate([qdoc[i]] * (seg_len // 128), axis=1)
        same = jnp.where(mine == kdoc[i], s[0:toks], MASKED_SCORE)
        return jnp.concatenate([same, s[toks:]], axis=0)

    def memory_scores(q4, mem_k):
        return jnp.where(mem_valid, dot(q4, mem_k, 1, 1), ABSENT_SCORE)

    def attend(i):
        own = [mem_lanes == h for h in range(4)]

        def scores(j):
            q4 = qb[:, j * quad : (j + 1) * quad]
            tok_k, mem_k = token_and_memory(kvb, j * quad)
            return dot(stacked(q4), tok_k, 1, 1), memory_scores(q4, mem_k)

        st = jnp.zeros((rows, 128), F32)
        following = scores(0)
        for j in range(quads):
            s, sm = following
            if j + 1 < quads:
                following = scores(j + 1)
            s = [only_same_document(part, i) for part in head_rows(s)]
            peaks = [
                jnp.max(
                    jnp.concatenate([s[h], jnp.where(own[h], sm, ABSENT_SCORE)], axis=1),
                    axis=1, keepdims=True,
                )
                for h in range(4)
            ]
            pm = jnp.exp(sm - spread(peaks, mem_lanes))
            mprob[j] = pm.astype(BF16)
            totals, probs = [], []
            for h in range(4):
                p = jnp.exp(s[h] - peaks[h])
                probs.append(p.astype(BF16))
                tprob[j, h * rows : (h + 1) * rows, :] = probs[h]
                both = jnp.concatenate([p, jnp.where(own[h], pm, 0.0)], axis=1)
                totals.append(1.0 / jnp.sum(both, axis=1, keepdims=True))
                st = jnp.where(stat_lane == 4 * j + h, totals[h], st)
            tok_v, mem_v = token_and_memory(kvb, width + j * quad)
            o = spread(head_rows(dot(jnp.concatenate(probs, axis=0), tok_v)), head_lanes)
            o = o + dot(pm.astype(BF16), mem_v)
            ctxb[:, j * quad : (j + 1) * quad] = (o * spread(totals, head_lanes)).astype(BF16)
        stats[i] = st
        ctx[i] = ctxb[...]

    def to_queries(product):
        return product.astype(BF16) * BF16(scale)

    def forward_tick(t, carry):
        i = t - x

        @pl.when((i >= 0) & (i < items))
        def _():
            ahead = (x == 0) & (i >= n) & (lax.rem(i, n) == 0)

            @pl.when(i > 0)
            def _():
                qkv_copies(i - 1)[1].wait()
                gp_copy(i - 1).wait()

            @pl.when(x == 0)
            def _():
                token_copy(0, i).wait()
                token_copy(1, i).wait()

            @pl.when(ahead)
            def _():
                kvb[0, 0:toks, :] = dot(x0[i, 0:toks, :], wf[0, :, width:wide]).astype(BF16)
                kvb[1, 0:toks, :] = dot(
                    xo[lax.rem(i, n), 0:toks, :], wf[0, :, width:wide]
                ).astype(BF16)
                qb[0:toks, :] = to_queries(dot(x0[i, 0:toks, :], wf[0, :, 0:width]))

            @pl.when(x == 0)
            def _():
                for which, rows_ref in enumerate((x0.at[i], xo.at[lax.rem(i, n)])):

                    @pl.when(i < n)
                    def _():
                        rows_ref[toks:rows, :] = jnp.zeros((MEM_PAD, width), BF16)

                    @pl.when(i >= n)
                    def _():
                        mem_copy(which, i - n).wait_recv()
                        rows_ref[toks:rows, :] = jnp.where(
                            keep[i][:, 0:1] > 0.0, memin[which, i - n], jnp.zeros((), BF16)
                        )

            @pl.when(x == 1)
            def _():
                for p in range(2):
                    x_copy(p, i).wait_recv()
                    pass_copy(p, i).start()

            @pl.when(i == 0)
            def _():
                wait_first_of(0, (0,))

            @pl.when(ahead)
            def _():
                memory = jnp.concatenate(
                    [x0[i, toks:rows, :], xo[lax.rem(i, n), toks:rows, :]], axis=0
                )
                both = dot(memory, wf[0, :, width:wide]).astype(BF16)
                kvb[0, toks:rows, :] = both[0:MEM_PAD]
                kvb[1, toks:rows, :] = both[MEM_PAD:]
                qb[toks:rows, :] = to_queries(dot(memory, wf[0, :, 0:width])[0:MEM_PAD])

            @pl.when(jnp.logical_not(ahead))
            def _():
                kvb[0] = dot(x0[i], wf[0, :, width:wide]).astype(BF16)

                @pl.when(i == 0)
                def _():
                    wait_first_of(0, (1,))

                qb[...] = to_queries(dot(x0[i], wf[0, :, 0:width]))

                @pl.when(x == 1)
                def _():
                    for p in range(2):
                        pass_copy(p, i).wait_recv()

                kvb[1] = dot(xo[lax.rem(i, n)], wf[0, :, width:wide]).astype(BF16)

            for copy in qkv_copies(i):
                copy.start()

            @pl.when((x == 0) & (i < items - n))
            def _():
                token_copy(1, i + n).start()

            @pl.when(i > 0)
            def _():
                for copy in prob_copies(i - 1, False):
                    copy.wait()

            attend(i)
            for copy in prob_copies(i, False):
                copy.start()

            @pl.when(i == 0)
            def _():
                wait_first_of(0, (2,))
                weight_remote(4).wait_recv()

            normed, inv = normalize(dot(ctxb[...], wf[0, :, wide:]) + x0[i].astype(F32))
            natt[i] = normed.astype(BF16)
            stats[i] = jnp.where(stat_lane == heads, inv, stats[i])
            yatt[i] = (normed * nrm[0, 0:1, :] + nrm[0, 1:2, :]).astype(BF16)

            @pl.when(i == 0)
            def _():
                wait_first_of(1, (0, 1, 2))

            @pl.when(i > 0)
            def _():
                route_sent(S_GLO, i - 1)
                route_sent(S_GHI, i - 1)

            qkv_copies(i)[0].wait()

            for part in range(2):
                cols = slice(part * hidden_half, (part + 1) * hidden_half)
                u = dot(yatt[i], wf[1, :, cols])
                cdf = 0.5 + 0.5 * lax.erf(u * 0.7071067811865476)
                pdf = 0.3989422804014327 * jnp.exp(-0.5 * u * u)
                g[:, cols] = (u * cdf).astype(BF16)
                gpb[:, cols] = (cdf + u * pdf).astype(BF16)
            @pl.when(i == 0)
            def _():
                wait_first_of(0, (3,))
                wait_first_of(1, (3,))

            def finish_rows(part):
                normed, inv = normalize(
                    dot(g[part, 0:hidden_half], wd[0])
                    + dot(g[part, hidden_half:], wd[1])
                    + yatt[i, part].astype(F32)
                )
                yd[i, part] = (normed * nrm[1, 0:1, :] + nrm[1, 1:2, :]).astype(BF16)
                nff[i, part] = normed.astype(BF16)
                stats[i, part] = jnp.where(stat_lane[part] == heads + 1, inv, stats[i, part])

            @pl.when(x == 0)
            def _():
                for p in range(2):
                    finish_rows(piece(p))
                    x_copy(p, i).start()

            @pl.when(x == 1)
            def _():
                finish_rows(slice(0, rows))

            @pl.when((x == 1) & (i < items - n))
            def _():
                for which in range(2):
                    mem_copy(which, i).start()

            gp_copy(i).start()
            for kind in (S_GLO, S_GHI, S_X0, S_CTX, OUT_ATT, S_Y1, S_Y2, OUT_FF):
                route(kind, i)

        return carry

    lax.fori_loop(0, items + 1, forward_tick, 0)

    def forward_sent(i):
        route_sent(OUT_FF, i)

        @pl.when(x == 0)
        def _():
            for p in range(2):
                x_copy(p, i).wait_send()

        @pl.when(x == 1)
        def _():
            for p in range(2):
                pass_copy(p, i).wait_send()

        @pl.when((x == 1) & (i < items - n))
        def _():
            for which in range(2):
                mem_copy(which, i).wait_send()

    for copy in prob_copies(items - 1, False) + qkv_copies(items - 1)[1:]:
        copy.wait()
    for copy in prob_copies(items - n, True):
        copy.start()
    gp_copy(items - 1).wait()
    acc[...] = jnp.zeros_like(acc)

    def norm_back(s, i, normed_ref):
        grad = (gy[i] if s else gab[...]).astype(F32)
        normed = normed_ref[i].astype(F32)
        inv = stats[i][:, heads + s : heads + s + 1]
        acc[s, 0:1, :] += jnp.sum(grad * normed, axis=0, keepdims=True)
        acc[s, 1:2, :] += jnp.sum(grad, axis=0, keepdims=True)
        scaled = grad * nrm[s, 0:1, :]
        row_term = jnp.mean(scaled, axis=1, keepdims=True)
        row_cross = jnp.mean(scaled * normed, axis=1, keepdims=True)
        dh = inv * (scaled - row_term - normed * row_cross)
        dhb[...] = dh
        normed_ref[i] = dh.astype(BF16)

    def attend_back(i, slot):
        def prob_grads(j):
            inverse = [stats[i][:, 4 * j + h : 4 * j + h + 1] for h in range(4)]
            c4 = dctx[:, j * quad : (j + 1) * quad].astype(F32) * spread(inverse, head_lanes)
            c4 = c4.astype(BF16)
            tok_v, mem_v = token_and_memory(kv.at[i], width + j * quad)
            return c4, dot(stacked(c4), tok_v, 1, 1), dot(c4, mem_v, 1, 1)

        following = prob_grads(0)
        for j in range(quads):
            c4, dp, dpm = following
            if j + 1 < quads:
                following = prob_grads(j + 1)
            cols = slice(j * quad, (j + 1) * quad)
            q4 = q[i, :, cols]
            tok_k, mem_k = token_and_memory(kv.at[i], j * quad)
            products = c4.astype(F32) * ctx[i, :, cols].astype(F32)
            dp = head_rows(dp)
            inner = [
                jnp.sum(jnp.where(head_lanes == h, products, 0.0), axis=1, keepdims=True)
                for h in range(4)
            ]
            dscores = [
                (tprob[j, h * rows : (h + 1) * rows, :].astype(F32) * (dp[h] - inner[h])).astype(BF16)
                for h in range(4)
            ]
            dsm = (mprob[j].astype(F32) * (dpm - spread(inner, mem_lanes))).astype(BF16)
            ct, qt = jnp.transpose(c4), jnp.transpose(q4)
            mine = [slice(h * head_dim, (h + 1) * head_dim) for h in range(4)]
            dv = [
                dot(ct[mine[h]], tprob[j, h * rows : (h + 1) * rows, :]).astype(BF16)
                for h in range(4)
            ]
            dk = [dot(qt[mine[h]], dscores[h]).astype(BF16) for h in range(4)]
            dv = jnp.transpose(jnp.concatenate(dv, axis=0))
            dk = jnp.transpose(jnp.concatenate(dk, axis=0))
            dscores = jnp.concatenate(dscores, axis=0)
            dq = spread(head_rows(dot(dscores, tok_k)), head_lanes) + dot(dsm, mem_k)
            dqb[:, cols] = (dq * scale).astype(BF16)
            dvm = jnp.where(diagonal, dot(mprob[j], c4, 0, 0), 0.0)
            dkm = jnp.where(diagonal, dot(dsm, q4, 0, 0), 0.0)
            dvm = sum(dvm[h * mem_keys : (h + 1) * mem_keys] for h in range(4))
            dkm = sum(dkm[h * mem_keys : (h + 1) * mem_keys] for h in range(4))
            for half, (tok_part, mem_part) in enumerate(((dk, dkm), (dv, dvm))):
                cols = slice(half * quad, (half + 1) * quad)
                for core in range(2):
                    dkvs[core, j, 0:toks, cols] = tok_part[
                        core * toks : (core + 1) * toks
                    ].astype(BF16)
                    dkvs[core, j, toks:rows, cols] = mem_part[
                        core * MEM_PAD : (core + 1) * MEM_PAD
                    ].astype(BF16)
            if j == quads - 1:
                dkv_copy(j, i, slot).start()
            elif j == quads - 2:
                for ready in range(quads - 1):
                    dkv_copy(ready, i, slot).start()

    def gather_dkv(j, i, slot):
        dkv_copy(j, i, slot).wait_recv()
        both = (dkvs[0, j].astype(F32) + dkvin[slot, j].astype(F32)).astype(BF16)
        kv[i, 0, :, j * quad : (j + 1) * quad] = both[:, 0:quad]
        kv[i, 0, :, width + j * quad : width + (j + 1) * quad] = both[:, quad:]

    def dkv_back(i, low, high, part):
        return dot(kv[i, 0, part, low:high], wf[0, :, width + low : width + high], 1, 1) + dot(
            kv[i, 0, part, width + low : width + high],
            wf[0, :, 2 * width + low : 2 * width + high], 1, 1,
        )

    def item_of(r):
        return (nseg - 1 - lax.div(r, n)) * n + lax.rem(r, n)

    def backward_tick(t, carry):
        r = t - (1 - x)

        @pl.when((r >= 0) & (r < items))
        def _():
            i = item_of(r)
            slot = lax.rem(r, 2)

            @pl.when(x == 1)
            def _():
                cot_copy(i).wait()

                @pl.when(i >= items - n)
                def _():
                    gy[i, toks:rows, :] = jnp.zeros((MEM_PAD, width), BF16)

                @pl.when(i < items - n)
                def _():
                    mg_copy(i + n).wait_recv()
                    gy[i, toks:rows, :] = jnp.where(
                        keep[i + n][:, 0:1] > 0.0, mgin[i + n], jnp.zeros((), BF16)
                    )

            @pl.when(x == 0)
            def _():
                for p in range(2):
                    gy_copy(p, i).wait_recv()

            @pl.when(r > 0)
            def _():
                route_sent(S_DQ, item_of(r - 1))
                route_sent(GIN_FF, item_of(r - 1))

            norm_back(1, i, nff)
            for part in range(2):
                cols = slice(part * hidden_half, (part + 1) * hidden_half)
                dg = dot(nff[i], wd[part], 1, 1)
                gp[i, :, cols] = (dg * gp[i, :, cols].astype(F32)).astype(BF16)
            gab[...] = (dot(gp[i], wf[1], 1, 1) + dhb[...]).astype(BF16)
            norm_back(0, i, natt)
            dctx[...] = dot(natt[i], wf[0, :, wide:], 1, 1).astype(BF16)
            route(S_DFF0, i)
            route(S_DFF1, i)
            route(S_DU, i)
            route(GIN_FF, i)
            route(S_DATT, i)
            for copy in prob_copies(i, True):
                copy.wait()
            attend_back(i, slot)
            route(S_DQ, i)

            @pl.when(r + 1 < items)
            def _():
                for copy in prob_copies(item_of(r + 1), True):
                    copy.start()

            for j in range(quads - 1):
                gather_dkv(j, i, slot)
            if quads > 1:
                route(S_DKV, i)
                route(S_DV, i)
            early = (quads - 1) * quad
            partial_sum = dot(dqb[...], wf[0, :, 0:width], 1, 1) + dhb[...]
            if early:
                partial_sum = partial_sum + dkv_back(i, 0, early, slice(0, rows))
            dhb[...] = partial_sum
            gather_dkv(quads - 1, i, slot)
            route(S_LASTK, i)
            route(S_LASTV, i)
            forward_sent(i)
            for p in range(2):
                part = piece(p)
                yd[i, part] = (dkv_back(i, early, width, part) + dhb[part, :]).astype(BF16)

                @pl.when(x == 1)
                def _():
                    gy_copy(p, i).start()

            @pl.when((x == 0) & (i >= n))
            def _():
                mg_copy(i).start()

            route(GIN_ATT, i)
            for j in range(quads):
                dkv_copy(j, i, slot).wait_send()

        return carry

    lax.fori_loop(0, items + 1, backward_tick, 0)

    acc_copy = remote(acc.at[1 - c], accp, as_sem, ar_sem, core_peer)
    acc_copy.start()

    def backward_drain(i, carry):
        @pl.when(x == 1)
        def _():
            for p in range(2):
                gy_copy(p, i).wait_send()

        @pl.when((x == 0) & (i >= n))
        def _():
            mg_copy(i).wait_send()

        for kind in range(KINDS):
            if quads == 1 and kind in (S_DKV, S_DV):
                continue
            if kind not in (OUT_FF, S_GLO, S_GHI, S_DQ, GIN_FF):
                route_sent(kind, i)
            route_received(kind, i)
        return carry

    lax.fori_loop(0, items, backward_drain, 0)
    route_sent(S_GLO, items - 1)
    route_sent(S_GHI, items - 1)
    route_sent(S_DQ, item_of(items - 1))
    route_sent(GIN_FF, item_of(items - 1))
    for k in range(5):
        weight_remote(k).wait_send()
    acc_copy.wait()
    norm_grad[...] = acc[c] + accp[...]


def run_layers(n, nseg, heads, tokens, cotangent, first, down, docs, resets, gain, shift):
    length, width = tokens.shape[1:]
    toks = length // nseg // 2
    rows = toks + MEM_PAD
    items = n * nseg
    hidden_half = down.shape[1]
    quads = heads // 4
    quad = width // quads
    any_spec = pl.BlockSpec(memory_space=pl.ANY)
    vmem_spec = pl.BlockSpec(memory_space=pltpu.VMEM)
    dma = pltpu.SemaphoreType.DMA
    item_rows = pltpu.VMEM((items, rows, width), BF16)
    one, two = dma((items,)), dma((2, items))
    return pl.pallas_call(
        partial(layers_kernel, n, nseg, heads),
        out_shape=(
            jax.ShapeDtypeStruct((n, length, width), BF16),
            jax.ShapeDtypeStruct((n, length, width), BF16),
            jax.ShapeDtypeStruct((2 * items, rows, width), BF16),
            jax.ShapeDtypeStruct((2 * items, rows, width), BF16),
            jax.ShapeDtypeStruct((2 * items, rows, 4 * width), BF16),
            jax.ShapeDtypeStruct((2 * items, rows, hidden_half), BF16),
            jax.ShapeDtypeStruct((2 * items, rows, width), BF16),
            jax.ShapeDtypeStruct((2, width), F32),
            jax.ShapeDtypeStruct((items, quads, 4 * rows, 2 * toks), BF16),
            jax.ShapeDtypeStruct((items, quads, rows, 8 * MEM_PAD), BF16),
        ),
        in_specs=[any_spec] * 4 + [vmem_spec] * 4,
        out_specs=[any_spec] * 7 + [vmem_spec] + [any_spec] * 2,
        scratch_shapes=[
            pltpu.VMEM((2, width, 4 * width), BF16),
            pltpu.VMEM((2, hidden_half, width), BF16),
            pltpu.VMEM((2, 2, width), F32),
            item_rows,
            pltpu.VMEM((n, rows, width), BF16),
            item_rows,
            pltpu.VMEM((items, 2, rows, 2 * width), BF16),
            item_rows,
            item_rows,
            item_rows,
            item_rows,
            item_rows,
            item_rows,
            pltpu.VMEM((rows, 2 * hidden_half), BF16),
            pltpu.VMEM((rows, 2 * hidden_half), BF16),
            pltpu.VMEM((items, rows, 2 * hidden_half), BF16),
            pltpu.VMEM((items, rows, 128), F32),
            pltpu.VMEM((items, toks, 128), F32),
            pltpu.VMEM((items, 1, 2 * toks), F32),
            pltpu.VMEM((items, MEM_PAD, 128), F32),
            pltpu.VMEM((2, items, MEM_PAD, width), BF16),
            pltpu.VMEM((items, MEM_PAD, width), BF16),
            pltpu.VMEM((2, quads, rows, 2 * quad), BF16),
            pltpu.VMEM((2, quads, rows, 2 * quad), BF16),
            pltpu.VMEM((rows, width), F32),
            pltpu.VMEM((2, rows, 2 * width), BF16),
            pltpu.VMEM((2, 2, width), F32),
            pltpu.VMEM((2, width), F32),
            pltpu.VMEM((quads, 4 * rows, 2 * toks), BF16),
            pltpu.VMEM((quads, rows, 8 * MEM_PAD), BF16),
            dma((4,)), dma((5,)), dma((5,)),
            two, one, one, two, two, two,
            two, two,
            two, two,
            two, two,
            two, two, one, one,
            dma((quads, items)), dma((quads, items)),
            dma(()), dma(()),
        ]
        + [dma((KINDS, items))] * 3,
        compiler_params=pltpu.CompilerParams(
            collective_id=0, has_side_effects=True, vmem_limit_bytes=61 * 1024 * 1024
        ),
    )(tokens, cotangent, first, down, docs, resets, gain, shift)


def reduce_kernel(
    chunks,
    sx1, sx2, sr, sg, sd, norm_part,
    sums, norm_out,
    x1, x2, rr, gg, dd, work, done, got_u, got_uz, got_vz, got_vy, norms,
    right_sem, left_sem, out_sem, u_s, u_r, uz_s, uz_r, vz_s, vz_r, vy_s, vy_r, vg_s, vg_r,
    uzg_s, uzg_r, vzg_s, vzg_r, ug_s, ug_r, n_s, n_r,
):
    lines = 4
    d = lax.axis_index("dp")
    y = lax.rem(d, 2)
    z = lax.div(d, 2)
    dp = lax.axis_size("dp")
    width = sd.shape[1]
    half = width // 2
    part = width // chunks
    hr = part // 2
    lane_group = 128
    per_group = lane_group // part
    y_peer = {"dp": z * 2 + (1 - y)}

    def remote(src, dst, send, recv, peer):
        return pltpu.make_async_remote_copy(
            src_ref=src, dst_ref=dst, send_sem=send, recv_sem=recv,
            device_id=peer, device_id_type=MESH,
        )

    def other(step):
        return {"dp": lax.rem(d + step, dp)}

    barrier = pltpu.get_barrier_semaphore()
    for step in range(1, dp):
        pl.semaphore_signal(barrier, inc=1, device_id=other(step), device_id_type=MESH)

    lane_groups = width // lane_group
    right_loads = [(sd, dd)] + [
        (sr.at[:, b * width : (b + 1) * width], rr.at[:, b * width : (b + 1) * width])
        for b in range(4)
    ]

    def right_load(k):
        src, dst = right_loads[k]
        return pltpu.make_async_copy(src, dst, right_sem.at[k])

    def left_load(which, group):
        src, dst, low = ((sg, gg, 0), (sg, gg, width), (sx2, x2, 0), (sx1, x1, 0))[which]
        cols = pl.ds(pl.multiple_of(low + group * lane_group, lane_group), lane_group)
        return pltpu.make_async_copy(src.at[:, cols], dst.at[:, cols], left_sem.at[which, group])

    right_load(0).start()
    left_load(0, 0).start()
    left_load(1, 0).start()
    left_load(2, 0).start()
    right_load(4).start()

    norms[d] = norm_part[...]
    pl.semaphore_wait(barrier, dp - 1)

    def norm_copy(step):
        return remote(norms.at[d], norms.at[d], n_s.at[step - 1], n_r.at[step - 1], other(step))

    def norm_arrival(step):
        source = lax.rem(d + dp - step, dp)
        return remote(
            norms.at[source], norms.at[source], n_s.at[step - 1], n_r.at[step - 1], other(step)
        )

    for step in range(1, dp):
        norm_copy(step).start()

    def column_half(h):
        return pl.ds(pl.multiple_of(h * half, 128), half)

    mine, theirs = column_half(y), column_half(1 - y)

    def place(flow):
        return z if flow == 0 else lines - 1 - z

    def onward(flow):
        step = -1 if flow == 0 else 1
        return {"dp": (z + step) * 2 + y}

    def back(flow):
        step = 1 if flow == 0 else -1
        return {"dp": (z + step) * 2 + y}

    def rows_of(flow):
        return slice(flow * hr, (flow + 1) * hr)

    def u_copy(k):
        return remote(
            work.at[k, 0:3, :, theirs], got_u.at[k], u_s.at[k], u_r.at[k], y_peer
        )

    def uz_copy(flow, k):
        return remote(
            work.at[k, 0:3, rows_of(flow), mine], got_uz.at[flow, k],
            uz_s.at[flow, k], uz_r.at[flow, k], onward(flow),
        )

    def vz_copy(flow, k):
        return remote(
            work.at[k, 3:6, rows_of(flow), :], got_vz.at[flow, k],
            vz_s.at[flow, k], vz_r.at[flow, k], onward(flow),
        )

    def vy_copy(flow, k):
        return remote(
            work.at[k, 3:6, rows_of(flow), theirs], got_vy.at[k], vy_s.at[k], vy_r.at[k], y_peer
        )

    def vg_copy(flow, k, cols):
        spot = done.at[k, 3:6, rows_of(flow), cols]
        return remote(spot, spot, vg_s.at[k], vg_r.at[k], y_peer)

    def uzg_copy(flow, k):
        spot = done.at[k, 0:3, rows_of(flow), mine]
        return remote(spot, spot, uzg_s.at[flow, k], uzg_r.at[flow, k], back(flow))

    def vzg_copy(flow, k):
        spot = done.at[k, 3:6, rows_of(flow), :]
        return remote(spot, spot, vzg_s.at[flow, k], vzg_r.at[flow, k], back(flow))

    def ug_copy(flow, k, cols):
        spot = done.at[k, 0:3, rows_of(flow), cols]
        return remote(spot, spot, ug_s.at[flow, k], ug_r.at[flow, k], y_peer)

    def out_copy(k):
        return pltpu.make_async_copy(done.at[k], sums.at[k], out_sem.at[k])

    def plus(a, b):
        return (a.astype(F32) + b.astype(F32)).astype(BF16)

    def ready(k, low=0):
        return (k >= low) & (k < chunks)

    def store_chunks(group, block, value):
        for e in range(per_group):
            work[group * per_group + e, block] = value[e * part : (e + 1) * part]

    def second_half(r):
        group = lax.div(r + per_group - 1, per_group)
        cols = pl.ds(pl.multiple_of(group * lane_group, lane_group), lane_group)
        gcols = pl.ds(pl.multiple_of(width + group * lane_group, lane_group), lane_group)

        @pl.when(r == 0)
        def _():
            right_load(0).wait()

        left_load(0, group).wait()
        store_chunks(group, 4, dot(gg[:, cols], dd[...], 0, 0).astype(BF16))
        left_load(1, group).wait()
        store_chunks(group, 5, dot(gg[:, gcols], dd[...], 0, 0).astype(BF16))
        left_load(2, group).wait()

        @pl.when(r == 0)
        def _():
            right_load(4).wait()
            left_load(3, 0).start()
            for k in range(1, 4):
                right_load(k).start()
            for later in range(1, lane_groups):
                for which in range(4):
                    left_load(which, later).start()

        store_chunks(group, 3, dot(x2[:, cols], rr[:, 3 * width :], 0, 0).astype(BF16))

    def round_step(r, carry):
        @pl.when(r == 0)
        def _():
            second_half(r)

        for flow in range(2):
            p = place(flow)
            k = r - (lines - 1 - p)
            rows = rows_of(flow)

            @pl.when(ready(k))
            def _():
                @pl.when(p < lines - 1)
                def _():
                    vz_copy(flow, k).wait_recv()
                    work[k, 3:6, rows, :] = plus(work[k, 3:6, rows, :], got_vz[flow, k])

                @pl.when(p > 0)
                def _():
                    vz_copy(flow, k).start()

                @pl.when(p == 0)
                def _():
                    vy_copy(flow, k).start()

        @pl.when((lax.rem(r, per_group) == 0) & (r < chunks))
        def _():
            group = lax.div(r, per_group)
            cols = pl.ds(pl.multiple_of(group * lane_group, lane_group), lane_group)
            left_load(3, group).wait()
            for b in range(3):

                @pl.when(r == 0)
                def _():
                    right_load(1 + b).wait()

                store_chunks(
                    group, b,
                    dot(x1[:, cols], rr[:, b * width : (b + 1) * width], 0, 0).astype(BF16),
                )

        @pl.when(ready(r))
        def _():
            u_copy(r).start()

        @pl.when((lax.rem(r, per_group) == per_group - 1) & (r + 1 < chunks))
        def _():
            second_half(r)

        @pl.when(ready(r - 1))
        def _():
            k = r - 1
            u_copy(k).wait_recv()
            work[k, 0:3, :, mine] = plus(work[k, 0:3, :, mine], got_u[k])

        for flow in range(2):
            p = place(flow)
            k = r - 1 - (lines - 1 - p)
            rows = rows_of(flow)

            @pl.when(ready(k))
            def _():
                @pl.when(p < lines - 1)
                def _():
                    uz_copy(flow, k).wait_recv()
                    total = plus(work[k, 0:3, rows, mine], got_uz[flow, k])

                    @pl.when(p > 0)
                    def _():
                        work[k, 0:3, rows, mine] = total

                    @pl.when(p == 0)
                    def _():
                        done[k, 0:3, rows, mine] = total

                @pl.when(p > 0)
                def _():
                    uz_copy(flow, k).start()

                @pl.when(p == 0)
                def _():
                    uzg_copy(flow, k).start()
                    ug_copy(flow, k, mine).start()

        for flow in range(2):
            p = place(flow)
            rows = rows_of(flow)

            @pl.when((p == 0) & ready(r - lines))
            def _():
                k = r - lines
                vy_copy(flow, k).wait_recv()
                done[k, 3:6, rows, mine] = plus(work[k, 3:6, rows, mine], got_vy[k])
                vg_copy(flow, k, mine).start()

            @pl.when((p == 0) & ready(r - lines - 1))
            def _():
                k = r - lines - 1
                vg_copy(flow, k, theirs).wait_recv()
                vzg_copy(flow, k).start()

        for flow in range(2):
            p = place(flow)
            k = r - lines - p

            @pl.when((p > 0) & ready(k))
            def _():
                uzg_copy(flow, k).wait_recv()

                @pl.when(p < lines - 1)
                def _():
                    uzg_copy(flow, k).start()

                ug_copy(flow, k, mine).start()

        for flow in range(2):
            p = place(flow)
            k = r - lines - 1 - p

            @pl.when((p > 0) & ready(k))
            def _():
                vzg_copy(flow, k).wait_recv()

                @pl.when(p < lines - 1)
                def _():
                    vzg_copy(flow, k).start()

            @pl.when(ready(k))
            def _():
                ug_copy(flow, k, theirs).wait_recv()

        @pl.when(ready(r - 2 * lines))
        def _():
            out_copy(r - 2 * lines).start()

        return carry

    lax.fori_loop(0, chunks + 2 * lines, round_step, 0)

    for step in range(1, dp):
        norm_arrival(step).wait_recv()
    total = norms[0]
    for e in range(1, dp):
        total = total + norms[e]
    norm_out[...] = total

    def drain(k, carry):
        out_copy(k).wait()
        u_copy(k).wait_send()
        for flow in range(2):
            p = place(flow)
            ug_copy(flow, k, mine).wait_send()

            @pl.when(p > 0)
            def _():
                vz_copy(flow, k).wait_send()
                uz_copy(flow, k).wait_send()

            @pl.when(p < lines - 1)
            def _():
                uzg_copy(flow, k).wait_send()
                vzg_copy(flow, k).wait_send()

            @pl.when(p == 0)
            def _():
                vy_copy(flow, k).wait_send()
                vg_copy(flow, k, mine).wait_send()

        return carry

    lax.fori_loop(0, chunks, drain, 0)
    for step in range(1, dp):
        norm_copy(step).wait_send()


def sum_weights(dp, sx1, sx2, sr, sg, sd, norm_part):
    total, width = sx1.shape
    chunks = 12
    part = width // chunks
    half = width // 2
    any_spec = pl.BlockSpec(memory_space=pl.ANY)
    vmem_spec = pl.BlockSpec(memory_space=pltpu.VMEM)
    dma = pltpu.SemaphoreType.DMA
    one, two = dma((chunks,)), dma((2, chunks))
    return pl.pallas_call(
        partial(reduce_kernel, chunks),
        out_shape=(
            jax.ShapeDtypeStruct((chunks, 6, part, width), BF16),
            jax.ShapeDtypeStruct((2, width), F32),
        ),
        in_specs=[any_spec] * 5 + [vmem_spec],
        out_specs=[any_spec, vmem_spec],
        scratch_shapes=[
            pltpu.VMEM((total, width), BF16),
            pltpu.VMEM((total, width), BF16),
            pltpu.VMEM((total, 4 * width), BF16),
            pltpu.VMEM((total, 2 * width), BF16),
            pltpu.VMEM((total, width), BF16),
            pltpu.VMEM((chunks, 6, part, width), BF16),
            pltpu.VMEM((chunks, 6, part, width), BF16),
            pltpu.VMEM((chunks, 3, part, half), BF16),
            pltpu.VMEM((2, chunks, 3, part // 2, half), BF16),
            pltpu.VMEM((2, chunks, 3, part // 2, width), BF16),
            pltpu.VMEM((chunks, 3, part // 2, half), BF16),
            pltpu.VMEM((dp, 2, width), F32),
            dma((5,)),
            dma((4, width // 128)),
            one,
            one, one,
            two, two,
            two, two,
            one, one,
            one, one,
            two, two,
            two, two,
            two, two,
            dma((dp - 1,)), dma((dp - 1,)),
        ],
        compiler_params=pltpu.CompilerParams(
            collective_id=1, has_side_effects=True, vmem_limit_bytes=60 * 1024 * 1024
        ),
    )(sx1, sx2, sr, sg, sd, norm_part)


def finish_kernel(sums, out, gin, norms, first_grad, down_grad, out_copy, gin_copy, gain, shift):
    group, _, part, width = sums.shape
    for e in range(group):
        rows = slice(e * part, (e + 1) * part)
        for b in range(4):
            first_grad[rows, b * width : (b + 1) * width] = sums[e, b].astype(F32)
        for b in range(2):
            down_grad[b, rows] = sums[e, 4 + b].astype(F32)
    out_copy[...] = out[...]
    gin_copy[...] = gin[...]
    gain[...] = norms[0:1]
    shift[...] = norms[1:2]


def finish(sums, out, gin, norms):
    chunks, _, part, width = sums.shape
    total = out.shape[0]
    group, blocks = chunks // 3, 2
    tokens = pl.BlockSpec((total // blocks, width), lambda k: (jnp.minimum(k, blocks - 1), 0))
    whole = pl.BlockSpec((1, width), lambda k: (0, 0))
    return pl.pallas_call(
        finish_kernel,
        grid=(chunks // group,),
        out_shape=(
            jax.ShapeDtypeStruct((width, 4 * width), F32),
            jax.ShapeDtypeStruct((2, width, width), F32),
            jax.ShapeDtypeStruct(out.shape, BF16),
            jax.ShapeDtypeStruct(gin.shape, BF16),
            jax.ShapeDtypeStruct((1, width), F32),
            jax.ShapeDtypeStruct((1, width), F32),
        ),
        in_specs=[
            pl.BlockSpec((group, 6, part, width), lambda k: (k, 0, 0, 0)),
            tokens,
            tokens,
            pl.BlockSpec((2, width), lambda k: (0, 0)),
        ],
        out_specs=[
            pl.BlockSpec((group * part, 4 * width), lambda k: (k, 0)),
            pl.BlockSpec((2, group * part, width), lambda k: (0, k, 0)),
            tokens,
            tokens,
            whole,
            whole,
        ],
        compiler_params=pltpu.CompilerParams(vmem_limit_bytes=61 * 1024 * 1024),
    )(sums, out, gin, norms)


def shards(
    tokens, doc_ids, reset_flags, first_weights, down_halves, norm_gain, norm_bias, cotangent
):
    n, length, width = tokens.shape
    items = n * NSEG
    rows = length // NSEG // 2 + MEM_PAD
    out, gin, sx1, sx2, sr, sg, sd, norm_grad, _, _ = run_layers(
        n, NSEG, H, tokens, cotangent, first_weights, down_halves,
        doc_ids, reset_flags.T, norm_gain, norm_bias,
    )
    total = 2 * items * rows
    sx1, sx2, sd = (a.reshape(total, width) for a in (sx1, sx2, sd))
    sr = sr.reshape(total, 4 * width)
    sg = sg.reshape(total, -1)

    dp = lax.axis_size("dp")
    if dp == 8:
        sums, norm_grad = sum_weights(dp, sx1, sx2, sr, sg, sd, norm_grad)
        first_grad, down_grad, out, gin, gain_grad, shift_grad = finish(
            sums, out.reshape(-1, width), gin.reshape(-1, width), norm_grad
        )
        down_grad = down_grad.reshape(-1, width)
        out, gin = (a.reshape(n, length, width) for a in (out, gin))
    else:

        def weight_grad(left, right):
            return jnp.einsum("rd,re->de", left, right, preferred_element_type=F32).astype(BF16)

        first_grad = jnp.concatenate(
            [weight_grad(sx1, sr[:, : 3 * width]), weight_grad(sx2, sr[:, 3 * width :])], axis=1
        )
        down_grad = weight_grad(sg, sd)
        first_grad, down_grad = lax.psum((first_grad, down_grad), "dp")
        norm_grad = lax.psum(norm_grad, "dp")
        gain_grad, shift_grad = norm_grad[0:1], norm_grad[1:2]
    return (
        out[None],
        gin[None],
        first_grad.astype(F32)[None],
        down_grad.astype(F32)[None],
        gain_grad,
        shift_grad,
    )


def solution(mesh):
    in_specs = (
        P("dp", None, None),
        P("dp", None),
        P("dp", None),
        P("section", None, None),
        P("section", None, None),
        P("section", None),
        P("section", None),
        P("dp", None, None),
    )
    out_specs = (
        P("section", "dp", None, None),
        P("section", "dp", None, None),
        P("section", None, None),
        P("section", None, None),
        P("section", None),
        P("section", None),
    )
    return jax.shard_map(shards, mesh=mesh, in_specs=in_specs, out_specs=out_specs, check_vma=False)
```
